32 devices in a mesh: dp: 16 (over z, y, core), mp: 2 (over x).
Axes of the slice: x: 2, y: 2, z: 4, core: 2. Of those that a mesh axis runs over, the one named last changes fastest.
Arguments:
- chars: bfloat16 [32768, 768], P(('dp', 'mp')), may hold values from -6 to 6
- segment_ids: int32 [32, 1024], P(('dp', 'mp')), may hold values from 0 to 5, never falling along the last dimension, each value on 1 to 512 neighbouring positions
- window_offsets: int32 [32], P(('dp', 'mp')), may hold values from 0 to 127
- ln1_gain: bfloat16 [768], P(('dp', 'mp')), may hold values from 0.25 to 1.75
- ln1_bias: bfloat16 [768], P(('dp', 'mp')), may hold values from -3 to 3
- w_qkv: bfloat16 [768, 2304], P(('dp', 'mp')), may hold values from -0.21875 to 0.21875
- qv_bias: bfloat16 [1536], P(('dp', 'mp')), may hold values from -3 to 3
- w_attn_out: bfloat16 [768, 768], P(('dp', 'mp')), may hold values from -0.875 to 0.875
- attn_out_bias: bfloat16 [768], P(('dp', 'mp')), may hold values from -2 to 2
- ln2_gain: bfloat16 [768], P(('dp', 'mp')), may hold values from 0.25 to 1.75
- ln2_bias: bfloat16 [768], P(('dp', 'mp')), may hold values from -3 to 3
- w_ff_in: bfloat16 [768, 3072], P('dp', 'mp'), may hold values from -0.21875 to 0.21875
- ff_in_bias: bfloat16 [3072], P(('dp', 'mp')), may hold values from -3 to 3
- w_ff_out: bfloat16 [3072, 768], P('mp', 'dp'), may hold values from -0.109375 to 0.109375
- ff_out_bias: bfloat16 [768], P(('dp', 'mp')), may hold values from -2 to 2
- conv_weight: bfloat16 [3072, 768], P('dp', 'mp'), may hold values from -0.109375 to 0.109375
- conv_bias: bfloat16 [768], P(('dp', 'mp')), may hold values from -3 to 3
- ln3_gain: bfloat16 [768], P(('dp', 'mp')), may hold values from 0.25 to 1.75
- ln3_bias: bfloat16 [768], P(('dp', 'mp')), may hold values from -3 to 3
- d_molecules: bfloat16 [8192, 768], P(('dp', 'mp')), may hold values from -6 to 6
Outputs:
- molecules: float32 [8192, 768], P(('dp', 'mp'))
- d_chars: float32 [32768, 768], P(('dp', 'mp'))
- d_ln1_gain: float32 [768], P(('dp', 'mp'))
- d_ln1_bias: float32 [768], P(('dp', 'mp'))
- d_w_qkv: float32 [768, 2304], P(('dp', 'mp'))
- d_qv_bias: float32 [1536], P(('dp', 'mp'))
- d_w_attn_out: float32 [768, 768], P(('dp', 'mp'))
- d_attn_out_bias: float32 [768], P(('dp', 'mp'))
- d_ln2_gain: float32 [768], P(('dp', 'mp'))
- d_ln2_bias: float32 [768], P(('dp', 'mp'))
- d_w_ff_in: float32 [768, 3072], P('dp', 'mp')
- d_ff_in_bias: float32 [3072], P(('dp', 'mp'))
- d_w_ff_out: float32 [3072, 768], P('mp', 'dp')
- d_ff_out_bias: float32 [768], P(('dp', 'mp'))
- d_conv_weight: float32 [3072, 768], P('dp', 'mp')
- d_conv_bias: float32 [768], P(('dp', 'mp'))
- d_ln3_gain: float32 [768], P(('dp', 'mp'))
- d_ln3_bias: float32 [768], P(('dp', 'mp'))
The draws below stay inside these ranges and needn't reach their ends.
Inputs may be any that keep to these rules, and one draw needn't show every extreme that they name: `segment_ids`: in each packed sequence segment numbers never fall; each segment is a run of 1 to 512 characters, one of exactly 512.
All inputs are finite; a program needn't handle non-finite values.
Results may differ from the reference program's by a relative error of at most 0.023.
Values may be sent and summed in bfloat16 or wider, within the bound.
A program may use at most 256 MiB of HBM per device.

```python
import math
import jax
import jax.numpy as jnp
import numpy as np
from jax import lax

D = 768
HEADS = 12
HDIM = 64
FF = 3072
KER = 4
WIN = 128
LEN = 1024
NSEQ = 32
TOKENS = 32768
MOLS = 8192


def with_ends(drawn, key, smallest, top_value):
    longest = drawn.shape.index(max(drawn.shape))
    spots = []
    for shift in (0, 1):
        where = [jax.random.randint(jax.random.fold_in(key, axis), (), 0, length) for axis, length in enumerate(drawn.shape)]
        where[longest] = (where[longest] + shift) % drawn.shape[longest]
        spots.append(tuple(where))
    return drawn.at[spots[0]].set(smallest).at[spots[1]].set(top_value)


def levels(key, extent, pieces, smallest, largest):
    factor_of = 1.0
    for dim, blocks in pieces:
        draws = jax.random.uniform(jax.random.fold_in(jax.random.fold_in(key, 6), dim), (blocks,), jnp.float32, smallest / len(pieces), largest / len(pieces))
        factor_of = factor_of * jnp.repeat(jnp.exp(draws), extent[dim] // blocks).reshape((-1,) + (1,) * (len(extent) - 1 - dim))
    return factor_of


def split_up(number_of, total, limit, lean):
    portions = [(1 << 20) // math.isqrt(rank ** lean) + 1 for rank in range(2, number_of + 1)]
    spare, holding = total - limit - (number_of - 1), [1] * (number_of - 1)
    while spare > 0:
        candidates = [i for i in range(number_of - 1) if holding[i] < limit]
        pool, remaining = sum([portions[i] for i in candidates]), spare
        for i in candidates:
            more = min(limit - holding[i], max(1, remaining * portions[i] // pool), spare)
            holding[i] = holding[i] + more
            spare = spare - more
    return np.array([limit] + holding)


def ragged_sizes(rng, amount, total, bound, slope):
    if amount == 2:
        one = jax.random.randint(rng, (), max(1, total - bound), min(bound, total - 1) + 1)
        return jnp.stack([one, total - one])
    tallies = jnp.asarray(split_up(amount, total, bound, slope), jnp.int32)
    couples = (amount - 1) // 2
    source_of, taker = tallies[1:1 + 2 * couples:2], tallies[2:2 + 2 * couples:2]
    room = jnp.minimum(source_of - 1, bound - taker)
    moved = jax.random.randint(jax.random.fold_in(rng, 1), (couples,), 0, 1 << 20) % (room + 1)
    tallies = tallies.at[1:1 + 2 * couples:2].set(source_of - moved).at[2:2 + 2 * couples:2].set(taker + moved)
    return tallies[jax.random.permutation(jax.random.fold_in(rng, 2), amount)]


def bell_draw(key, shape, width, bound, split=(), held_as=jnp.bfloat16):
    result = jax.random.normal(key, shape, jnp.float32) * width
    if len(split) > 0:
        result = levels(key, shape, split, -0.22, 0.18) * result
    return jnp.clip(result, min=-bound, max=bound).astype(held_as)


def setup_inputs(seed: int = 0) -> dict:
    streams_of = jax.random.split(jax.random.key(seed), 21)
    chars = bell_draw(streams_of[0], (TOKENS, D), 1.0, 6.0, ((0, 32),))
    segment_ids = jax.vmap(lambda own: jnp.searchsorted(jnp.cumsum(ragged_sizes(own, 6, LEN, LEN // 2, 0)), jnp.arange(LEN), side="right"))(jax.random.split(streams_of[1], NSEQ)).reshape((NSEQ, LEN)).astype(jnp.int32)
    window_offsets = with_ends(jax.random.randint(streams_of[2], (NSEQ,), 0, WIN), jax.random.fold_in(streams_of[2], 1), 0, WIN - 1).astype(jnp.int32)
    ln1_gain = jnp.clip(1.0 + 0.15 * jax.random.normal(streams_of[3], (D,), jnp.float32), 0.25, 1.75).astype(jnp.bfloat16)
    ln1_bias = bell_draw(streams_of[4], (D,), 0.5, 3.0, ((0, 32),))
    w_qkv = bell_draw(streams_of[5], (D, 3 * D), D ** -0.5, 0.21875, ((0, 32),))
    qv_bias = bell_draw(streams_of[6], (2 * D,), 0.5, 3.0, ((0, 32),))
    w_attn_out = bell_draw(streams_of[7], (D, D), (D // 16) ** -0.5, 0.875, ((0, 32),))
    attn_out_bias = bell_draw(streams_of[8], (D,), 0.3, 2.0, ((0, 32),))
    ln2_gain = jnp.clip(1.0 + 0.15 * jax.random.normal(streams_of[9], (D,), jnp.float32), 0.25, 1.75).astype(jnp.bfloat16)
    ln2_bias = bell_draw(streams_of[10], (D,), 0.5, 3.0, ((0, 32),))
    w_ff_in = bell_draw(streams_of[11], (D, FF), D ** -0.5, 0.21875, ((0, 16), (1, 2)))
    ff_in_bias = bell_draw(streams_of[12], (FF,), 0.5, 3.0, ((0, 32),))
    w_ff_out = bell_draw(streams_of[13], (FF, D), FF ** -0.5, 0.109375, ((0, 2), (1, 16)))
    ff_out_bias = bell_draw(streams_of[14], (D,), 0.3, 2.0, ((0, 32),))
    conv_weight = bell_draw(streams_of[15], (KER * D, D), (KER * D) ** -0.5, 0.109375, ((0, 16), (1, 2)))
    conv_bias = bell_draw(streams_of[16], (D,), 0.5, 3.0, ((0, 32),))
    ln3_gain = jnp.clip(1.0 + 0.15 * jax.random.normal(streams_of[17], (D,), jnp.float32), 0.25, 1.75).astype(jnp.bfloat16)
    ln3_bias = bell_draw(streams_of[18], (D,), 0.5, 3.0, ((0, 32),))
    d_molecules = bell_draw(streams_of[19], (MOLS, D), 1.0, 6.0, ((0, 32),))
    return dict(chars=chars, segment_ids=segment_ids, window_offsets=window_offsets, ln1_gain=ln1_gain, ln1_bias=ln1_bias, w_qkv=w_qkv, qv_bias=qv_bias, w_attn_out=w_attn_out, attn_out_bias=attn_out_bias, ln2_gain=ln2_gain, ln2_bias=ln2_bias, w_ff_in=w_ff_in, ff_in_bias=ff_in_bias, w_ff_out=w_ff_out, ff_out_bias=ff_out_bias, conv_weight=conv_weight, conv_bias=conv_bias, ln3_gain=ln3_gain, ln3_bias=ln3_bias, d_molecules=d_molecules)


layer_eps = 1e-06
highest = lax.Precision.HIGHEST

@jax.custom_vjp
def low(v):
    return lax.optimization_barrier(v.astype(jnp.bfloat16)).astype(jnp.float32)

@jax.custom_vjp
def low_back(v):
    return v

def low_keep(v):
    return (low(v), None)

def low_pass(kept, grad):
    return (grad,)

def back_keep(v):
    return (v, None)

def back_low(kept, grad):
    return (low(grad),)
low.defvjp(low_keep, low_pass)
low_back.defvjp(back_keep, back_low)

def layer_norm(row_values, gain_vec, shift_vec):
    centred = row_values - lax.optimization_barrier(jnp.mean(row_values, axis=-1, keepdims=True))
    spread = lax.optimization_barrier(jnp.mean(centred * centred, axis=-1, keepdims=True))
    return centred * lax.rsqrt(spread + layer_eps) * gain_vec + shift_vec

def gelu_exact(values):
    return jax.nn.gelu(values, approximate=False)

def group_forward(weights, chars_grp, seg_grp, offset_grp):
    ln1_gain, ln1_bias, w_qkv, qv_bias, w_attn_out, attn_out_bias, ln2_gain, ln2_bias, w_ff_in, ff_in_bias, w_ff_out, ff_out_bias, conv_weight, conv_bias, ln3_gain, ln3_bias = weights
    groups, seq_len, model_width = chars_grp.shape
    normed_one = low(layer_norm(chars_grp, ln1_gain, ln1_bias))
    qkv_shift = jnp.concatenate([qv_bias[:model_width], jnp.zeros((model_width,), jnp.float32), qv_bias[model_width:]])
    projected = low(low_back(jnp.einsum('gtd,de->gte', normed_one, w_qkv, precision=highest) + qkv_shift))
    split_qkv = projected.reshape(groups, seq_len, 3, HEADS, HDIM)
    queries = split_qkv[:, :, 0]
    key_rows = split_qkv[:, :, 1]
    value_rows = split_qkv[:, :, 2]
    raw_scores = low_back(jnp.einsum('gqhd,gkhd->ghqk', queries, key_rows, precision=highest) * HDIM ** (-0.5))
    positions = jnp.arange(seq_len, dtype=jnp.int32)
    blocks = (positions[None, :] + offset_grp[:, None].astype(jnp.int32)) // WIN
    allowed = (seg_grp[:, :, None] == seg_grp[:, None, :]) & (blocks[:, :, None] == blocks[:, None, :])
    scores = jnp.where(allowed[:, None], raw_scores, -1e+30)
    row_peak = lax.optimization_barrier(jnp.max(scores, axis=-1, keepdims=True))
    exp_scores = jnp.exp(scores - row_peak)
    probs = exp_scores / lax.optimization_barrier(jnp.sum(exp_scores, axis=-1, keepdims=True))
    head_out = jnp.einsum('ghqk,gkhd->gqhd', low(probs), value_rows, precision=highest)
    head_out = low(low_back(head_out.reshape(groups, seq_len, model_width)))
    attn_branch = low_back(jnp.einsum('gte,ec->gtc', head_out, w_attn_out, precision=highest) + attn_out_bias)
    resid_one = chars_grp + attn_branch
    normed_two = low(layer_norm(resid_one, ln2_gain, ln2_bias))
    hidden_pre = low_back(jnp.einsum('gtd,df->gtf', normed_two, w_ff_in, precision=highest) + ff_in_bias)
    hidden_act = low(gelu_exact(hidden_pre))
    ff_branch = low_back(jnp.einsum('gtf,fc->gtc', hidden_act, w_ff_out, precision=highest) + ff_out_bias)
    resid_two = resid_one + ff_branch
    mol_in = low(resid_two).reshape(groups, seq_len // KER, KER * model_width)
    conv_pre = low_back(jnp.einsum('gmk,kc->gmc', mol_in, conv_weight, precision=highest) + conv_bias)
    conv_act = low(low_back(gelu_exact(conv_pre)))
    return layer_norm(conv_act, ln3_gain, ln3_bias)

def reference(chars, segment_ids, window_offsets, ln1_gain, ln1_bias, w_qkv, qv_bias, w_attn_out, attn_out_bias, ln2_gain, ln2_bias, w_ff_in, ff_in_bias, w_ff_out, ff_out_bias, conv_weight, conv_bias, ln3_gain, ln3_bias, d_molecules):
    weights = tuple((weight_arg.astype(jnp.float32) for weight_arg in (ln1_gain, ln1_bias, w_qkv, qv_bias, w_attn_out, attn_out_bias, ln2_gain, ln2_bias, w_ff_in, ff_in_bias, w_ff_out, ff_out_bias, conv_weight, conv_bias, ln3_gain, ln3_bias)))
    inputs = chars.astype(jnp.float32)
    seq_pair = 2
    steps_count = NSEQ // seq_pair

    def forward(inputs_now, weights_now):

        def scan_body(running, seq_item):
            return (running, jax.checkpoint(group_forward)(weights_now, seq_item[0], seq_item[1], seq_item[2]))
        stacked = (inputs_now.reshape(steps_count, seq_pair, LEN, D), segment_ids.reshape(steps_count, seq_pair, LEN), window_offsets.reshape(steps_count, seq_pair))
        _, results = lax.scan(scan_body, jnp.zeros((), jnp.float32), stacked)
        return results.reshape(MOLS, D)
    molecules, pullback = jax.vjp(forward, inputs, weights)
    d_chars, d_weights = pullback(d_molecules.astype(jnp.float32))
    d_ln1_gain, d_ln1_bias, d_w_qkv, d_qv_bias, d_w_attn_out, d_attn_out_bias, d_ln2_gain, d_ln2_bias, d_w_ff_in, d_ff_in_bias, d_w_ff_out, d_ff_out_bias, d_conv_weight, d_conv_bias, d_ln3_gain, d_ln3_bias = d_weights
    return (molecules, d_chars, d_ln1_gain, d_ln1_bias, d_w_qkv, d_qv_bias, d_w_attn_out, d_attn_out_bias, d_ln2_gain, d_ln2_bias, d_w_ff_in, d_ff_in_bias, d_w_ff_out, d_ff_out_bias, d_conv_weight, d_conv_bias, d_ln3_gain, d_ln3_bias)
```

```python
import functools

import jax
import jax.numpy as jnp
from jax import lax
from jax.experimental import pallas as pl
from jax.experimental.pallas import tpu as pltpu
from jax.sharding import PartitionSpec as P

HEADS = 12
HDIM = 64
KER = 4
WIN = 128


layer_eps = 1e-06


def layer_norm(row_values, gain_vec, shift_vec):
    centred = row_values - jnp.mean(row_values, axis=-1, keepdims=True)
    spread = jnp.mean(centred * centred, axis=-1, keepdims=True)
    return centred * lax.rsqrt(spread + layer_eps) * gain_vec + shift_vec


def gelu_exact(values):
    return jax.nn.gelu(values, approximate=False)


def norm_backward(row_values, gain_vec, shift_vec, grad_out):
    _, pullback = jax.vjp(layer_norm, row_values, gain_vec, shift_vec)
    return pullback(grad_out)


def gelu_backward(values, grad_out):
    _, pullback = jax.vjp(gelu_exact, values)
    return pullback(grad_out)[0]


def three_blocks(rows, fill_value):
    edge = jnp.full_like(rows[:1], fill_value)
    before = jnp.concatenate([edge, rows[:-1]], axis=0)
    after = jnp.concatenate([rows[1:], edge], axis=0)
    return jnp.concatenate([before, rows, after], axis=1)


def fold_blocks(band_grad):
    edge = jnp.zeros_like(band_grad[:1, :WIN])
    from_next = jnp.concatenate([band_grad[1:, :WIN], edge], axis=0)
    from_prev = jnp.concatenate([edge, band_grad[:-1, 2 * WIN :]], axis=0)
    return band_grad[:, WIN : 2 * WIN] + from_next + from_prev


def band_inputs(queries, key_rows, value_rows, seg_row, offset):
    seq_len = queries.shape[0]
    block_count = seq_len // WIN
    win_row = (jnp.arange(seq_len, dtype=jnp.int32) + offset) // WIN
    seg_blk = seg_row.reshape(block_count, WIN)
    win_blk = win_row.reshape(block_count, WIN)
    return (
        queries.reshape(block_count, WIN, HEADS, HDIM),
        three_blocks(key_rows.reshape(block_count, WIN, HEADS, HDIM), 0),
        three_blocks(value_rows.reshape(block_count, WIN, HEADS, HDIM), 0),
        seg_blk,
        win_blk,
        three_blocks(seg_blk, 0),
        three_blocks(win_blk, -1),
    )


def band_scores(query_blk, key_band, seg_blk, win_blk, seg_band, win_band):
    raw_scores = jnp.einsum(
        "bqhd,bkhd->bhqk", query_blk, key_band, preferred_element_type=jnp.float32
    ) * HDIM ** (-0.5)
    allowed = (seg_blk[:, :, None] == seg_band[:, None, :]) & (
        win_blk[:, :, None] == win_band[:, None, :]
    )
    return jnp.where(allowed[:, None], raw_scores, -1e30)


def attend_forward(seq_item):
    queries, key_rows, value_rows, seg_row, offset = seq_item
    seq_len = queries.shape[0]
    query_blk, key_band, val_band, seg_blk, win_blk, seg_band, win_band = band_inputs(
        queries, key_rows, value_rows, seg_row, offset
    )
    scores = band_scores(query_blk, key_band, seg_blk, win_blk, seg_band, win_band)
    row_peak = jnp.max(scores, axis=-1, keepdims=True)
    exp_scores = jnp.exp(scores - row_peak)
    row_total = jnp.sum(exp_scores, axis=-1, keepdims=True)
    prob_low = (exp_scores / row_total).astype(jnp.bfloat16)
    merged = jnp.einsum("bhqk,bkhd->bqhd", prob_low, val_band, preferred_element_type=jnp.float32)
    return (merged.reshape(seq_len, HEADS * HDIM), (row_peak + jnp.log(row_total))[..., 0])


def attend_backward(seq_item):
    queries, key_rows, value_rows, seg_row, offset, log_norm, d_heads = seq_item
    seq_len = queries.shape[0]
    block_count = seq_len // WIN
    score_scale = HDIM ** (-0.5)
    query_blk, key_band, val_band, seg_blk, win_blk, seg_band, win_band = band_inputs(
        queries, key_rows, value_rows, seg_row, offset
    )
    grad_blk = d_heads.reshape(block_count, WIN, HEADS, HDIM)
    scores = band_scores(query_blk, key_band, seg_blk, win_blk, seg_band, win_band)
    prob_blk = jnp.exp(scores - log_norm[..., None])
    d_probs = jnp.einsum("bqhd,bkhd->bhqk", grad_blk, val_band, preferred_element_type=jnp.float32)
    row_dot = jnp.sum(prob_blk * d_probs, axis=-1, keepdims=True)
    d_scores = (prob_blk * (d_probs - row_dot)).astype(jnp.bfloat16)
    d_query = (
        jnp.einsum("bhqk,bkhd->bqhd", d_scores, key_band, preferred_element_type=jnp.float32)
        * score_scale
    )
    d_key_band = (
        jnp.einsum("bhqk,bqhd->bkhd", d_scores, query_blk, preferred_element_type=jnp.float32)
        * score_scale
    )
    d_val_band = jnp.einsum(
        "bhqk,bqhd->bkhd",
        prob_blk.astype(jnp.bfloat16),
        grad_blk,
        preferred_element_type=jnp.float32,
    )
    d_keys = fold_blocks(d_key_band)
    d_vals = fold_blocks(d_val_band)
    return (
        d_query.reshape(seq_len, HEADS * HDIM),
        d_keys.reshape(seq_len, HEADS * HDIM),
        d_vals.reshape(seq_len, HEADS * HDIM),
    )


def shards(
    chars,
    segment_ids,
    window_offsets,
    ln1_gain,
    ln1_bias,
    w_qkv,
    qv_bias,
    w_attn_out,
    attn_out_bias,
    ln2_gain,
    ln2_bias,
    w_ff_in,
    ff_in_bias,
    w_ff_out,
    ff_out_bias,
    conv_weight,
    conv_bias,
    ln3_gain,
    ln3_bias,
    d_molecules,
):
    gathered = (
        lax.all_gather(w_qkv, ("dp", "mp"), axis=0, tiled=True),
        lax.all_gather(w_attn_out, ("dp", "mp"), axis=0, tiled=True),
        lax.all_gather(ln1_gain, ("dp", "mp"), axis=0, tiled=True),
        lax.all_gather(ln1_bias, ("dp", "mp"), axis=0, tiled=True),
        lax.all_gather(qv_bias, ("dp", "mp"), axis=0, tiled=True),
        lax.all_gather(attn_out_bias, ("dp", "mp"), axis=0, tiled=True),
        lax.all_gather(ln2_gain, ("dp", "mp"), axis=0, tiled=True),
        lax.all_gather(ln2_bias, ("dp", "mp"), axis=0, tiled=True),
        lax.all_gather(ff_in_bias, ("dp", "mp"), axis=0, tiled=True),
        lax.all_gather(ff_out_bias, ("dp", "mp"), axis=0, tiled=True),
        lax.all_gather(conv_bias, ("dp", "mp"), axis=0, tiled=True),
        lax.all_gather(ln3_gain, ("dp", "mp"), axis=0, tiled=True),
        lax.all_gather(ln3_bias, ("dp", "mp"), axis=0, tiled=True),
    )
    qkv_full = gathered[0]
    attn_out_full = gathered[1]
    vectors = [vector_arg.astype(jnp.float32) for vector_arg in gathered[2:]]
    (
        gain_one,
        shift_one,
        qv_shift,
        attn_shift,
        gain_two,
        shift_two,
        hidden_shift,
        ff_shift,
        conv_shift,
        gain_three,
        shift_three,
    ) = vectors
    ff_in_part, ff_out_part, conv_part = (
        lax.all_gather(w_ff_in, "dp", axis=0, tiled=True),
        lax.all_gather(w_ff_out, "dp", axis=1, tiled=True),
        lax.all_gather(conv_weight, "dp", axis=0, tiled=True),
    )
    model_width = chars.shape[1]
    tok_rows = chars.shape[0]
    seq_count = segment_ids.shape[0]
    seq_len = segment_ids.shape[1]
    mp_rank = lax.axis_index("mp")
    hidden_part = ff_in_part.shape[1]
    channel_part = conv_part.shape[1]
    inputs = chars.astype(jnp.float32)
    normed_one = layer_norm(inputs, gain_one, shift_one).astype(jnp.bfloat16)
    qkv_shift = jnp.concatenate(
        [qv_shift[:model_width], jnp.zeros((model_width,), jnp.float32), qv_shift[model_width:]]
    )
    projected = (
        jnp.dot(normed_one, qkv_full, preferred_element_type=jnp.float32) + qkv_shift
    ).astype(jnp.bfloat16)
    per_seq = projected.reshape(seq_count, seq_len, 3, HEADS, HDIM)
    queries = per_seq[:, :, 0]
    key_rows = per_seq[:, :, 1]
    value_rows = per_seq[:, :, 2]
    merged, log_norm = lax.map(
        attend_forward, (queries, key_rows, value_rows, segment_ids, window_offsets)
    )
    heads_low = merged.reshape(tok_rows, model_width).astype(jnp.bfloat16)
    resid_one = (
        inputs + jnp.dot(heads_low, attn_out_full, preferred_element_type=jnp.float32) + attn_shift
    )
    normed_two = layer_norm(resid_one, gain_two, shift_two).astype(jnp.bfloat16)
    ff_in_use, ff_out_use, conv_use = (ff_in_part, ff_out_part, conv_part)
    ff_rows_in = lax.all_gather(normed_two, "mp", axis=0, tiled=True)
    hidden_bias = lax.dynamic_slice_in_dim(hidden_shift, mp_rank * hidden_part, hidden_part)
    hidden_pre = jnp.dot(ff_rows_in, ff_in_use, preferred_element_type=jnp.float32) + hidden_bias
    hidden_act = gelu_exact(hidden_pre).astype(jnp.bfloat16)
    ff_sum = lax.psum_scatter(
        jnp.dot(hidden_act, ff_out_use, preferred_element_type=jnp.float32).astype(jnp.bfloat16),
        "mp",
        scatter_dimension=0,
        tiled=True,
    ).astype(jnp.float32)
    resid_two = resid_one + ff_sum + ff_shift
    mol_rows = resid_two.astype(jnp.bfloat16).reshape(tok_rows // KER, KER * model_width)
    mol_group = lax.all_gather(mol_rows, "mp", axis=0, tiled=True)
    channel_bias = lax.dynamic_slice_in_dim(conv_shift, mp_rank * channel_part, channel_part)
    conv_pre = jnp.dot(mol_group, conv_use, preferred_element_type=jnp.float32) + channel_bias
    channel_act = gelu_exact(conv_pre).astype(jnp.bfloat16)
    conv_act = lax.all_to_all(channel_act, "mp", split_axis=0, concat_axis=1, tiled=True)
    act_float = conv_act.astype(jnp.float32)
    molecules = layer_norm(act_float, gain_three, shift_three)
    d_act, d_gain_three, d_shift_three = norm_backward(
        act_float, gain_three, shift_three, d_molecules.astype(jnp.float32)
    )
    d_act_low = d_act.astype(jnp.bfloat16)
    d_act_cols = lax.all_to_all(d_act_low, "mp", split_axis=1, concat_axis=0, tiled=True)
    d_conv_pre = gelu_backward(conv_pre, d_act_cols.astype(jnp.float32)).astype(jnp.bfloat16)
    d_conv_w = jnp.einsum("mk,mc->kc", mol_group, d_conv_pre, preferred_element_type=jnp.float32)
    d_conv_shift = lax.dynamic_update_slice_in_dim(
        jnp.zeros((model_width,), jnp.float32),
        jnp.sum(d_conv_pre.astype(jnp.float32), axis=0),
        mp_rank * channel_part,
        0,
    )
    d_mol = lax.psum_scatter(
        jnp.einsum("mc,kc->mk", d_conv_pre, conv_use, preferred_element_type=jnp.float32).astype(
            jnp.bfloat16
        ),
        "mp",
        scatter_dimension=0,
        tiled=True,
    ).astype(jnp.float32)
    d_resid_two = d_mol.reshape(tok_rows, model_width)
    d_ff_low = d_resid_two.astype(jnp.bfloat16)
    d_ff_shift = jnp.sum(d_ff_low.astype(jnp.float32), axis=0)
    d_ff_rows = lax.all_gather(d_ff_low, "mp", axis=0, tiled=True)
    d_hidden_act = jnp.einsum(
        "gc,fc->gf", d_ff_rows, ff_out_use, preferred_element_type=jnp.float32
    )
    d_ff_out_w = jnp.einsum("gf,gc->fc", hidden_act, d_ff_rows, preferred_element_type=jnp.float32)
    d_hidden = gelu_backward(hidden_pre, d_hidden_act).astype(jnp.bfloat16)
    d_hidden_sum = jnp.sum(d_hidden.astype(jnp.float32), axis=0)
    d_ff_in_w = jnp.einsum("gd,gf->df", ff_rows_in, d_hidden, preferred_element_type=jnp.float32)
    d_hidden_shift = lax.dynamic_update_slice_in_dim(
        jnp.zeros((hidden_shift.shape[0],), jnp.float32), d_hidden_sum, mp_rank * hidden_part, 0
    )
    d_normed_two = lax.psum_scatter(
        jnp.einsum("gf,df->gd", d_hidden, ff_in_use, preferred_element_type=jnp.float32).astype(
            jnp.bfloat16
        ),
        "mp",
        scatter_dimension=0,
        tiled=True,
    ).astype(jnp.float32)
    d_resid_from, d_gain_two, d_shift_two = norm_backward(
        resid_one, gain_two, shift_two, d_normed_two
    )
    d_resid_one = d_resid_two + d_resid_from
    d_attn_low = d_resid_one.astype(jnp.bfloat16)
    d_attn_shift = jnp.sum(d_attn_low.astype(jnp.float32), axis=0)
    d_attn_out_w = jnp.einsum(
        "te,tc->ec", heads_low, d_attn_low, preferred_element_type=jnp.float32
    )
    d_heads_low = jnp.einsum(
        "tc,ec->te", d_attn_low, attn_out_full, preferred_element_type=jnp.float32
    ).astype(jnp.bfloat16)
    d_heads_seq = d_heads_low.reshape(seq_count, seq_len, HEADS, HDIM)
    d_queries, d_keys, d_vals = lax.map(
        attend_backward,
        (queries, key_rows, value_rows, segment_ids, window_offsets, log_norm, d_heads_seq),
    )
    d_projected = jnp.concatenate(
        [
            d_queries.reshape(tok_rows, model_width),
            d_keys.reshape(tok_rows, model_width),
            d_vals.reshape(tok_rows, model_width),
        ],
        axis=1,
    ).astype(jnp.bfloat16)
    d_proj_sum = jnp.sum(d_projected.astype(jnp.float32), axis=0)
    d_qv_shift = jnp.concatenate([d_proj_sum[:model_width], d_proj_sum[2 * model_width :]])
    d_qkv_w = jnp.einsum("td,te->de", normed_one, d_projected, preferred_element_type=jnp.float32)
    d_normed_one = jnp.einsum(
        "te,de->td", d_projected, qkv_full, preferred_element_type=jnp.float32
    )
    d_inputs_from, d_gain_one, d_shift_one = norm_backward(
        inputs, gain_one, shift_one, d_normed_one
    )
    d_chars = d_resid_one + d_inputs_from
    d_ff_in_own, d_ff_out_own, d_conv_own = (
        lax.psum_scatter(
            d_ff_in_w.astype(jnp.bfloat16), "dp", scatter_dimension=0, tiled=True
        ).astype(jnp.float32),
        lax.psum_scatter(
            d_ff_out_w.astype(jnp.bfloat16), "dp", scatter_dimension=1, tiled=True
        ).astype(jnp.float32),
        lax.psum_scatter(
            d_conv_w.astype(jnp.bfloat16), "dp", scatter_dimension=0, tiled=True
        ).astype(jnp.float32),
    )
    owned = (
        lax.psum_scatter(d_qkv_w, ("dp", "mp"), scatter_dimension=0, tiled=True),
        lax.psum_scatter(d_attn_out_w, ("dp", "mp"), scatter_dimension=0, tiled=True),
        lax.psum_scatter(d_gain_one, ("dp", "mp"), scatter_dimension=0, tiled=True),
        lax.psum_scatter(d_shift_one, ("dp", "mp"), scatter_dimension=0, tiled=True),
        lax.psum_scatter(d_qv_shift, ("dp", "mp"), scatter_dimension=0, tiled=True),
        lax.psum_scatter(d_attn_shift, ("dp", "mp"), scatter_dimension=0, tiled=True),
        lax.psum_scatter(d_gain_two, ("dp", "mp"), scatter_dimension=0, tiled=True),
        lax.psum_scatter(d_shift_two, ("dp", "mp"), scatter_dimension=0, tiled=True),
        lax.psum_scatter(d_hidden_shift, ("dp", "mp"), scatter_dimension=0, tiled=True),
        lax.psum_scatter(d_ff_shift, ("dp", "mp"), scatter_dimension=0, tiled=True),
        lax.psum_scatter(d_conv_shift, ("dp", "mp"), scatter_dimension=0, tiled=True),
        lax.psum_scatter(d_gain_three, ("dp", "mp"), scatter_dimension=0, tiled=True),
        lax.psum_scatter(d_shift_three, ("dp", "mp"), scatter_dimension=0, tiled=True),
    )
    return (
        molecules,
        d_chars,
        owned[2],
        owned[3],
        owned[0],
        owned[4],
        owned[1],
        owned[5],
        owned[6],
        owned[7],
        d_ff_in_own,
        owned[8],
        d_ff_out_own,
        owned[9],
        d_conv_own,
        owned[10],
        owned[11],
        owned[12],
    )


HALF = 0.5
ERFC_P = 0.3
ERFC_Q = (
    0.16918934881687164,
    0.17069095373153687,
    0.1485210806131363,
    0.2141820192337036,
    -0.09282728284597397,
    0.5449684858322144,
    -0.5097734332084656,
    0.4843021035194397,
    -0.12925326824188232,
)
BF = jnp.bfloat16
F32 = jnp.float32
MESH_ID = pl.DeviceIdType.MESH
ALL = slice(None)
LINKS = ("z1", "z2", "z3", "x", "y", "c")
VMEM_CAP = 62 * 2**20
SLOT = 128


def nn(lhs, rhs):
    return lax.dot_general(lhs, rhs, (((1,), (0,)), ((), ())), preferred_element_type=F32)


def nt(lhs, rhs):
    return lax.dot_general(lhs, rhs, (((1,), (1,)), ((), ())), preferred_element_type=F32)


def tn(lhs, rhs):
    return lax.dot_general(lhs, rhs, (((0,), (0,)), ((), ())), preferred_element_type=F32)


def gelu_pair(v):
    size = jnp.abs(v)
    t = 1.0 / (1.0 + (ERFC_P * 0.7071067811865476) * size)
    q = ERFC_Q[-1]
    for coef in ERFC_Q[-2::-1]:
        q = q * t + coef
    bell = jnp.exp(-0.5 * (v * v))
    tail = (HALF * bell) * (q * t)
    phi = jnp.where(v >= 0, 1.0 - tail, tail)
    return v * phi, phi + v * (bell * 0.3989422804014327)


def norm_stats(v):
    mean = jnp.mean(v, axis=-1, keepdims=True)
    cen = v - mean
    r = lax.rsqrt(jnp.mean(cen * cen, axis=-1, keepdims=True) + layer_eps)
    return cen * r, r


def norm_grad(vhat, r, t):
    m1 = jnp.mean(t, axis=-1, keepdims=True)
    m2 = jnp.mean(t * vhat, axis=-1, keepdims=True)
    return r * (t - m1 - vhat * m2)


def head_masks(rows, scale):
    lane = lax.broadcasted_iota(jnp.int32, (rows, 128), 1)
    low = jnp.where(lane < HDIM, scale, 0.0).astype(BF)
    high = jnp.where(lane < HDIM, 0.0, scale).astype(BF)
    return low, high


def split_heads(pair, masks):
    return jnp.concatenate([pair * masks[0], pair * masks[1]], axis=0)


class Place:
    def __init__(self):
        dp = lax.axis_index("dp")
        self.x = lax.axis_index("mp")
        self.z, self.y, self.c = lax.div(dp, 4), lax.rem(lax.div(dp, 2), 2), lax.rem(dp, 2)
        z, y, c, x = self.z, self.y, self.c, self.x
        self.nx, self.ny, self.nc = 1 - x, 1 - y, 1 - c
        self.at = [c * 0 + k for k in range(3)]
        self.far_z = {1: z + 1 - 2 * lax.rem(z, 2), 2: lax.rem(z + 2, 4), 3: 3 - z}
        at = lambda zz, yy, cc, xx: (zz * 4 + yy * 2 + cc, xx)
        self.peer = {
            "z1": at(self.far_z[1], y, c, x),
            "z2": at(self.far_z[2], y, c, x),
            "z3": at(self.far_z[3], y, c, x),
            "x": at(z, y, c, 1 - x),
            "y": at(z, 1 - y, c, x),
            "c": at(z, y, 1 - c, x),
        }

    def barrier(self):
        sem = pltpu.get_barrier_semaphore()
        for peer in self.peer.values():
            pl.semaphore_signal(sem, inc=1, device_id=peer, device_id_type=MESH_ID)
        pl.semaphore_wait(sem, len(self.peer))


def rows_of(ref, xs):
    if isinstance(xs, slice):
        return xs
    half = ref.shape[-2] // 2
    return pl.ds(pl.multiple_of(xs * half, 8), half)


def block(ref, kind, zs, ys, cs, xs, cut):
    if kind == 0:
        return ref.at[(zs, ys, cs, xs) + cut]
    if kind == 1:
        return ref.at[(xs, zs, ys, cs) + cut]
    return ref.at[zs, ys, cs, rows_of(ref, xs), cut[1]]


class Sends:
    def __init__(self, place, send_sem, recv_sem):
        self.place, self.send_sem, self.recv_sem, self.made = place, send_sem, recv_sem, {}
        self.live = False

    def go(self, key, src, dst, link):
        if self.live:
            self.made[key].start()
            return
        i = len(self.made)
        self.made[key] = pltpu.make_async_remote_copy(
            src_ref=src,
            dst_ref=dst,
            send_sem=self.send_sem.at[i],
            recv_sem=self.recv_sem.at[i],
            device_id=self.place.peer[link],
            device_id_type=MESH_ID,
        )

    def got(self, key):
        if self.live:
            self.made[key].wait_recv()

    def sent(self):
        for copy in self.made.values():
            copy.wait_send()


def order(half):
    return ("x", "y") if half == 0 else ("y", "x")


def gather_stage(sends, stage, i, t, kind, own, full, cuts):
    p = sends.place
    z, y, c, x = p.z, p.y, p.c, p.x
    for h, cut in enumerate(cuts):
        if cut is None:
            continue
        a, b = order(h)
        if stage == 0:
            dst = block(full, kind, z, y, c, x, cut)
            for k in ("z1", "z2", "z3"):
                sends.go((i, h, k), own.at[cut], dst, k)
        elif stage == 1:
            for k in ("z1", "z2", "z3"):
                sends.got((i, h, k))
            v = block(full, kind, ALL, y, c, x, cut)
            sends.go((i, h, "a"), v, v, a)
            sends.go((i, h, "b1"), v, v, b)
            sends.go((i, h, "c1"), v, v, "c")
        elif stage == 2:
            sends.got((i, h, "a"))
            v = block(full, kind, ALL, y, c, p.nx, cut) if h == 0 else block(full, kind, ALL, p.ny, c, x, cut)
            sends.go((i, h, "b2"), v, v, b)
            sends.go((i, h, "c2"), v, v, "c")
        elif stage == 3:
            sends.got((i, h, "b1"))
            sends.got((i, h, "b2"))
            v = block(full, kind, ALL, p.ny, c, ALL, cut) if h == 0 else block(full, kind, ALL, ALL, c, p.nx, cut)
            sends.go((i, h, "c3"), v, v, "c")
        else:
            for k in ("c1", "c2", "c3"):
                sends.got((i, h, k))


def col_cuts(cols, parts):
    step = cols // (2 * parts)
    return [((ALL, slice(2 * step * i, 2 * step * i + step)), (ALL, slice(2 * step * i + step, 2 * step * (i + 1)))) for i in range(parts)]


def row_cuts(rows, parts):
    step = rows // (2 * parts)
    return [((slice(2 * step * i, 2 * step * i + step), ALL), (slice(2 * step * i + step, 2 * step * (i + 1)), ALL)) for i in range(parts)]


def gather_plan(shapes):
    plan = [(0, 0, ((ALL, ALL), None))]
    plan += [(1, 2, c) for c in col_cuts(shapes[1][1], 3)]
    plan += [(2, 2, c) for c in col_cuts(shapes[2][1], 1)]
    plan += [(3, 1, c) for c in col_cuts(shapes[3][1], 3)]
    plan += [(4, 1, c) for c in col_cuts(shapes[4][1], 3)]
    plan += [(5, 1, c) for c in row_cuts(shapes[5][0], 3)]
    return plan


def forward_kernel(dims, sizes, n_send, *refs):
    (off_ref, seg_ref, x_ref, dmol_ref, vec_own, qkv_own, wo_own, wi_own, wf_own, cv_own) = refs[:10]
    outs = refs[10:28]
    (mol_out, vec_out, ln3_out, dcp_out, qkv_o, wo_o, wi_o, wf_o, cv_o, ns_o, proj_o, prob_o, heads_o, r1_o, n2_o, act_o, gd_o, mi_o) = outs
    (vec_g, qkv_g, wo_g, wi_g, wf_g, cv_g, vec_f, vecs, pad, ns, proj, prob, heads, r1, n2, act, gd, r2, molin, local_sem, out_sem, send_sem, recv_sem) = refs[28:]
    tok, d, ff = dims
    win = WIN
    nw = tok // win + 1
    half_ff = ff // 2
    mols = tok // KER
    place = Place()
    owns = (vec_own, qkv_own, wo_own, wi_own, wf_own, cv_own)
    fulls = (vec_g, qkv_g, wo_g, wi_g, wf_g, cv_g)
    plan = gather_plan([o.shape for o in owns])
    kinds = (0, 2, 2, 1, 1, 1)
    place.barrier()
    sends = Sends(place, send_sem, recv_sem)
    local = []
    for i, (own, full, kind) in enumerate(zip(owns, fulls, kinds)):
        copy = pltpu.make_async_copy(own, block(full, kind, place.z, place.y, place.c, place.x, (ALL, ALL)), local_sem.at[i])
        copy.start()
        local.append(copy)

    def comm_stage(stage, i):
        t, kind, cuts = plan[i]
        if sends.live and stage == 1 and local[t] is not None:
            local[t].wait()
            local[t] = None
        gather_stage(sends, stage, i, t, kind, owns[t], fulls[t], cuts)

    for stage in range(5):
        for i in range(len(plan)):
            comm_stage(stage, i)
    sends.live = True
    ticks = []
    for tick in range(len(plan) + 4):
        steps = [(s, tick - s) for s in range(5) if 0 <= tick - s < len(plan)]
        ticks.append(functools.partial(lambda st: [comm_stage(s, i) for s, i in st], steps))
    done_tick = {i: i + 4 for i in range(len(plan))}
    state = {"tick": 0}

    def comm(upto):
        while state["tick"] <= upto and state["tick"] < len(ticks):
            ticks[state["tick"]]()
            state["tick"] += 1

    def need(t):
        comm(max(done_tick[i] for i in range(len(plan)) if plan[i][0] == t))

    out_copies = []

    def flush(src, dst):
        copy = pltpu.make_async_copy(src, dst, out_sem.at[len(out_copies)])
        copy.start()
        out_copies.append(copy)

    def unpack_vectors():
        nrow = vec_f.shape[0] // 16
        vec_f[...] = vec_g[...].reshape(vec_f.shape).astype(F32)
        for v, (width, count) in enumerate(sizes):
            col = lax.broadcasted_iota(jnp.int32, (SLOT, width), 1).astype(F32)
            row = lax.broadcasted_iota(jnp.int32, (SLOT, width), 0).astype(F32)
            owner = jnp.floor((col + 0.5) * (1.0 / count))
            pick = jnp.where(col - owner * count == row, 1.0, 0.0).astype(BF)
            spread = nn(vec_f[pl.ds(v, nrow, stride=16), :].astype(BF), pick)
            col2 = lax.broadcasted_iota(jnp.int32, (nrow, width), 1).astype(F32)
            row2 = lax.broadcasted_iota(jnp.int32, (nrow, width), 0).astype(F32)
            owner2 = jnp.floor((col2 + 0.5) * (1.0 / count))
            mine = jnp.where(row2 == owner2, spread, 0.0)
            vecs[v : v + 1, :width] = jnp.sum(mine, axis=0, keepdims=True)

    def vec(v, lo, hi):
        return vecs[v : v + 1, lo:hi]

    offset = off_ref[0]

    need(0)
    unpack_vectors()
    flush(vecs, vec_out)

    pad[0:win, :] = jnp.zeros((win, d), BF)
    pad[win + tok : 2 * win + tok, :] = jnp.zeros((win, d), BF)

    @pl.loop(0, tok // 128)
    def _(b):
        rows = pl.ds(pl.multiple_of(b * 128, 128), 128)
        vhat, _ = norm_stats(x_ref[rows, :].astype(F32))
        pad[pl.ds(pl.multiple_of(b * 128 + win, 128), 128), :] = (vhat * vec(0, 0, d) + vec(1, 0, d)).astype(BF)

    ri = lax.broadcasted_iota(jnp.int32, (win, 2 * win), 0)
    rj = lax.broadcasted_iota(jnp.int32, (win, 2 * win), 1)
    shift_in = jnp.where(rj == ri + (win - offset), 1.0, 0.0).astype(BF)
    shift_out = jnp.where(rj == ri + offset, 1.0, 0.0).astype(BF)

    @pl.loop(0, nw)
    def _(w):
        at = pl.multiple_of(w * win, win)
        ns[pl.ds(at, win), :] = nn(shift_in, pad[pl.ds(at, 2 * win), :]).astype(BF)

    flush(ns, ns_o)

    need(1)
    flush(qkv_g, qkv_o)
    wq = qkv_g.reshape(d, 3 * d)
    for blk3 in range(3):
        bias_row = None if blk3 == 1 else vec(2, (blk3 // 2) * d, (blk3 // 2) * d + d)

        @pl.loop(0, nw // 3)
        def _(b):
            rows = pl.ds(pl.multiple_of(b * 384, 128), 384)
            for n0 in range(0, d, 256):
                val = nn(ns[rows, :], wq[:, blk3 * d + n0 : blk3 * d + n0 + 256])
                if bias_row is not None:
                    val = val + bias_row[:, n0 : n0 + 256]
                proj[rows, blk3 * d + n0 : blk3 * d + n0 + 256] = val.astype(BF)

    flush(proj, proj_o)

    qmask = head_masks(win, HDIM**-0.5)
    vmask = head_masks(win, 1.0)
    seg_row = jnp.concatenate([seg_ref[0:1, :].astype(F32), jnp.full((1, win), -1.0, F32)], axis=1)
    seg_row = pltpu.roll(jnp.broadcast_to(seg_row, (8, tok + win)), offset, axis=1)
    segs = vec_f
    for w in range(nw):
        segs[w * 8 : w * 8 + 8, 0:win] = seg_row[:, w * win : (w + 1) * win]

    @pl.loop(0, nw)
    def _(w):
        rows = pl.ds(pl.multiple_of(w * win, win), win)
        seg_q = jnp.broadcast_to(segs[pl.ds(pl.multiple_of(w * 8, 8), 8), 0:win][0:1], (win, win))
        same = seg_q == seg_q.T
        same2 = jnp.concatenate([same, same], axis=1)
        for pr in range(HEADS // 2):
            lanes = slice(pr * 128, pr * 128 + 128)
            q2 = proj[rows, pr * 128 : pr * 128 + 128]
            k2 = proj[rows, d + pr * 128 : d + pr * 128 + 128]
            v2 = proj[rows, 2 * d + pr * 128 : 2 * d + pr * 128 + 128]
            s = jnp.where(same2, nt(k2, split_heads(q2, qmask)), -1e30)
            e = jnp.exp(s - jnp.max(s, axis=0, keepdims=True))
            pb = (e * (1.0 / jnp.sum(e, axis=0, keepdims=True))).astype(BF)
            prob[w, pr] = pb
            stacked = jnp.concatenate([pb[:, :win], pb[:, win:]], axis=0)
            pad[rows, lanes] = tn(stacked, split_heads(v2, vmask)).astype(BF)

    flush(prob, prob_o)

    need(2)
    flush(wo_g, wo_o)
    wo = wo_g.reshape(d, d)

    @pl.loop(0, tok // 128)
    def _(b):
        at = pl.multiple_of(b * 128, 128)
        hb = nn(shift_out, pad[pl.ds(at, 2 * win), :]).astype(BF)
        heads[pl.ds(at, 128), :] = hb

    @pl.loop(0, tok // 256)
    def _(b):
        rows = pl.ds(pl.multiple_of(b * 256, 256), 256)
        val = x_ref[rows, :].astype(F32) + nn(heads[rows, :], wo[...]) + vec(3, 0, d)
        r1[rows, :] = val
        vhat, _ = norm_stats(val)
        n2[rows, :] = (vhat * vec(4, 0, d) + vec(5, 0, d)).astype(BF)

    flush(heads, heads_o)
    flush(r1, r1_o)
    flush(n2, n2_o)

    need(3)
    flush(wi_g, wi_o)
    wi = wi_g.reshape(2, d, half_ff)
    for hx in range(2):

        @pl.loop(0, half_ff // 256)
        def _(j):
            cols = pl.ds(pl.multiple_of(j * 256, 256), 256)
            ocols = pl.ds(pl.multiple_of(hx * half_ff + j * 256, 256), 256)
            bias_row = vecs[6:7, ocols]
            for m in range(0, tok, 256):
                pre = nn(n2[m : m + 256, :], wi[hx, :, cols]) + bias_row
                g, dg = gelu_pair(pre)
                act[m : m + 256, ocols] = g.astype(BF)
                gd[m : m + 256, ocols] = dg.astype(BF)

    flush(act, act_o)
    flush(gd, gd_o)

    need(4)
    flush(wf_g, wf_o)
    wf = wf_g.reshape(2, d, half_ff)

    @pl.loop(0, tok // 256)
    def _(b):
        rows = pl.ds(pl.multiple_of(b * 256, 256), 256)
        for n0 in range(0, d, 256):
            cols = slice(n0, n0 + 256)
            val = nt(act[rows, 0:half_ff], wf[0, cols, :]) + nt(act[rows, half_ff:], wf[1, cols, :])
            val = r1[rows, cols] + val + vec(7, n0, n0 + 256)
            r2[n0 // 128, rows, :] = val[:, :128]
            r2[n0 // 128 + 1, rows, :] = val[:, 128:]

    for k in range(KER):
        for q in range(d // 128):
            molin[:, k * d + q * 128 : k * d + q * 128 + 128] = r2[q, pl.ds(k, mols, stride=KER), :].astype(BF)

    flush(molin, mi_o)
    need(5)
    flush(cv_g, cv_o)
    cv = cv_g.reshape(2, KER * d, d // 2)
    pre = jnp.concatenate([nn(molin[...], cv[0]), nn(molin[...], cv[1])], axis=1) + vec(8, 0, d)
    g, dg = gelu_pair(pre)
    vhat, r = norm_stats(g.astype(BF).astype(F32))
    mol_out[...] = vhat * vec(9, 0, d) + vec(10, 0, d)
    cot = dmol_ref[...].astype(F32)
    ln3_out[0:1, :] = jnp.sum(cot * vhat, axis=0, keepdims=True)
    ln3_out[1:2, :] = jnp.sum(cot, axis=0, keepdims=True)
    da = norm_grad(vhat, r, cot * vec(9, 0, d)).astype(BF).astype(F32)
    dcp_out[...] = (da * dg).astype(BF)
    sends.sent()
    for copy in out_copies:
        copy.wait()


def scatter_plan(shapes):
    plan = [(5, 1, c) for c in row_cuts(shapes[5][0], 3)]
    for wf_cut, wi_cut in zip(col_cuts(shapes[4][1], 3), col_cuts(shapes[3][1], 3)):
        plan += [(4, 1, wf_cut), (3, 1, wi_cut)]
    plan += [(2, 2, c) for c in col_cuts(shapes[2][1], 1)]
    plan += [(1, 2, c) for c in col_cuts(shapes[1][1], 3)]
    plan += [(0, 0, ((ALL, ALL), None))]
    return plan


def backward_kernel(dims, sizes, n_send, *refs):
    (off_ref, x_ref, dcp_ref, vecs, ln3_ref, qkv_i, wo_i, wi_i, wf_i, cv_i, ns_i, proj_i, prob_i, heads_i, r1_i, n2_i, act_i, gd_i, mi_i) = refs[:19]
    dch_out = refs[19]
    own_outs = refs[20:26]
    grads = refs[26:32]
    from_core = refs[32:38]
    from_b = refs[38:44]
    from_a = refs[44:50]
    from_z = refs[50:56]
    sums, res_sem, tile_sem, load_sem, out_sem, send_sem, recv_sem = refs[56:]
    tok, d, ff = dims
    win = WIN
    nw = tok // win + 1
    half_ff = ff // 2
    mols = tok // KER
    place = Place()
    z, y, c, x = place.z, place.y, place.c, place.x
    plan = scatter_plan([o.shape for o in own_outs])
    place.barrier()
    sends = Sends(place, send_sem, recv_sem)

    def add_blocks(dst_of, src_of):
        if not sends.live:
            return

        @pl.loop(0, 4)
        def _(zz):
            dst, src = dst_of(zz), src_of(zz)
            dst[...] = dst[...] + src[...]

    def comm_stage(stage, i):
        t, kind, cuts = plan[i]
        g, rc, rb, ra, rz, own = grads[t], from_core[t], from_b[t], from_a[t], from_z[t], own_outs[t]

        def core_blk(zs, ys, xs, cut):
            if kind == 2:
                return rc.at[zs, ys, rows_of(rc, xs), cut[1]]
            return rc.at[(zs, ys, xs) + cut] if kind == 0 else rc.at[(xs, zs, ys) + cut]

        for h, cut in enumerate(cuts):
            if cut is None:
                continue
            a, b = order(h)
            if stage == 0:
                sends.go((i, h, "c"), block(g, kind, ALL, ALL, place.nc, ALL, cut), core_blk(ALL, ALL, ALL, cut), "c")
            elif stage == 1:
                sends.got((i, h, "c"))
                for far in (1, 0):
                    for o in range(2):
                        ys, xs = (place.ny if far else y, place.at[o]) if h == 0 else (place.at[o], place.nx if far else x)
                        add_blocks(lambda zz: block(g, kind, zz, ys, c, xs, cut), lambda zz: core_blk(zz, ys, xs, cut))
                        if far:
                            sends.go((i, h, "b", o), block(g, kind, ALL, ys, c, xs, cut), rb.at[(place.at[o], ALL) + cut], b)
            elif stage == 2:
                sends.got((i, h, "b", 0))
                sends.got((i, h, "b", 1))
                near, other = (x, place.nx) if h == 0 else (y, place.ny)
                for far in (1, 0):
                    o = other if far else near
                    ys, xs = (y, o) if h == 0 else (o, x)
                    add_blocks(lambda zz: block(g, kind, zz, ys, c, xs, cut), lambda zz: rb.at[(o, zz) + cut])
                    if far:
                        sends.go((i, h, "a"), block(g, kind, ALL, ys, c, xs, cut), ra.at[(ALL,) + cut], a)
            elif stage == 3:
                sends.got((i, h, "a"))
                add_blocks(lambda zz: block(g, kind, zz, y, c, x, cut), lambda zz: ra.at[(zz,) + cut])
                for k in (1, 2, 3):
                    sends.go((i, h, "z", k), block(g, kind, place.far_z[k], y, c, x, cut), rz.at[(place.at[k - 1],) + cut], "z%d" % k)
            else:
                for k in (1, 2, 3):
                    sends.got((i, h, "z", k))
                if not sends.live:
                    continue
                total = block(g, kind, z, y, c, x, cut)[...].astype(F32)
                for k in range(3):
                    total = total + rz.at[(place.at[k],) + cut][...].astype(F32)
                own[cut] = total

    for stage in range(5):
        for i in range(len(plan)):
            comm_stage(stage, i)
    sends.live = True
    ticks = []
    for tick in range(len(plan) + 4):
        steps = [(s, tick - s) for s in range(5) if 0 <= tick - s < len(plan)]
        ticks.append(functools.partial(lambda st: [comm_stage(s, i) for s, i in st], steps))
    state = {"tick": 0, "load": 0}

    def comm(upto):
        while state["tick"] <= upto and state["tick"] < len(ticks):
            ticks[state["tick"]]()
            state["tick"] += 1

    def load(src, dst):
        copy = pltpu.make_async_copy(src, dst, load_sem.at[state["load"]])
        state["load"] += 1
        copy.start()
        return copy

    def vec(v, lo, hi):
        return vecs[v : v + 1, lo:hi]

    offset = off_ref[0]
    ri = lax.broadcasted_iota(jnp.int32, (win, 2 * win), 0)
    rj = lax.broadcasted_iota(jnp.int32, (win, 2 * win), 1)
    shift_in = jnp.where(rj == ri + (win - offset), 1.0, 0.0).astype(BF)
    shift_out = jnp.where(rj == ri + offset, 1.0, 0.0).astype(BF)
    sums[...] = jnp.zeros_like(sums)
    sums[9:10, 0:d] = ln3_ref[0:1, :]
    sums[10:11, 0:d] = ln3_ref[1:2, :]
    sums[8:9, 0:d] = jnp.sum(dcp_ref[...].astype(F32), axis=0, keepdims=True)
    g_vec, g_qkv, g_wo, g_wi, g_wf, g_cv = grads
    g_cv2 = g_cv.reshape(2, KER * d, d // 2)
    g_wi2 = g_wi.reshape(2, d, half_ff)
    g_wf2 = g_wf.reshape(2, d, half_ff)

    def whole(dres):
        def conv_part(cv, mi, spread):
            loads = [load(mi_i, mi), load(cv_i, cv)]
            cv2 = cv.reshape(2, KER * d, d // 2)
            loads[0].wait()

            @pl.loop(0, KER * d // 256)
            def _(b):
                rows = pl.ds(pl.multiple_of(b * 256, 256), 256)
                val = tn(mi[:, rows], dcp_ref[...]).astype(BF)
                g_cv2[0, rows, :] = val[:, : d // 2]
                g_cv2[1, rows, :] = val[:, d // 2 :]

            comm(2)
            loads[1].wait()
            for k in range(KER):
                for n0 in range(0, d, 256):
                    rows = slice(k * d + n0, k * d + n0 + 256)
                    val = nt(dcp_ref[:, : d // 2], cv2[0, rows, :]) + nt(dcp_ref[:, d // 2 :], cv2[1, rows, :])
                    spread[n0 // 128, pl.ds(k, mols, stride=KER), :] = val[:, :128]
                    spread[n0 // 128 + 1, pl.ds(k, mols, stride=KER), :] = val[:, 128:]
            for q in range(d // 128):
                dres[:, q * 128 : q * 128 + 128] = spread[q]

        pl.run_scoped(conv_part, pltpu.VMEM(cv_i.shape, BF), pltpu.VMEM(mi_i.shape, BF), pltpu.VMEM((d // 128, tok, 128), F32))

        def ff_part(dn2):
            def inner(act, gd, wf, wi, dff, dff_t, n2_t, dh, n2):
                n2_load = load(n2_i, n2)
                wi2, wf2 = wi_i.reshape(2, d, half_ff), wf_i.reshape(2, d, half_ff)

                def tile_copies(j):
                    slot, hx, jj = lax.rem(j, 2), lax.rem(j, 2), lax.div(j, 2)
                    cols = pl.ds(pl.multiple_of(hx * half_ff + jj * 256, 256), 256)
                    wcols = pl.ds(pl.multiple_of(jj * 256, 256), 256)
                    pairs = (
                        (act_i.at[:, cols], act),
                        (gd_i.at[:, cols], gd),
                        (wf_i.at[hx, :, :, :, :, wcols], wf),
                        (wi_i.at[hx, :, :, :, :, wcols], wi),
                    )
                    return [pltpu.make_async_copy(s, b.at[slot], tile_sem.at[slot, q]) for q, (s, b) in enumerate(pairs)]

                for copy in tile_copies(0):
                    copy.start()

                @pl.loop(0, tok // 256)
                def _(b):
                    rows = pl.ds(pl.multiple_of(b * 256, 256), 256)
                    val = dres[rows, :].astype(BF)
                    dff[rows, :] = val
                    sums[7:8, 0:d] += jnp.sum(val.astype(F32), axis=0, keepdims=True)
                    dff_t[:, rows] = val.T

                n2_load.wait()

                @pl.loop(0, tok // 256)
                def _(b):
                    rows = pl.ds(pl.multiple_of(b * 256, 256), 256)
                    n2_t[:, rows] = n2[rows, :].T

                dn2[...] = jnp.zeros_like(dn2)
                n_tiles = ff // 256
                for group in range(3):

                    @pl.loop(group * n_tiles // 3, (group + 1) * n_tiles // 3)
                    def _(j):
                        slot, hx, jj = lax.rem(j, 2), lax.rem(j, 2), lax.div(j, 2)
                        for copy in tile_copies(j):
                            copy.wait()

                        @pl.when(j + 1 < n_tiles)
                        def _():
                            for copy in tile_copies(j + 1):
                                copy.start()

                        wcols = pl.ds(pl.multiple_of(jj * 256, 256), 256)
                        wf_j = wf.at[slot].reshape(d, 256)
                        wi_j = wi.at[slot].reshape(d, 256)
                        total = jnp.zeros((1, 256), F32)
                        for m in range(0, tok, 256):
                            val = (nn(dff[m : m + 256, :], wf_j[...]) * gd[slot, m : m + 256, :].astype(F32)).astype(BF)
                            dh[m : m + 256, :] = val
                            total = total + jnp.sum(val.astype(F32), axis=0, keepdims=True)
                        sums[6:7, pl.ds(pl.multiple_of(hx * half_ff + jj * 256, 256), 256)] = total
                        for m in range(0, d, 256):
                            g_wf2[hx, m : m + 256, wcols] = nn(dff_t[m : m + 256, :], act[slot]).astype(BF)
                            g_wi2[hx, m : m + 256, wcols] = nn(n2_t[m : m + 256, :], dh[...]).astype(BF)
                        for m in range(0, tok, 256):
                            dn2[m : m + 256, :] += nt(dh[m : m + 256, :], wi_j[...])

                    comm(4 + 2 * group)

            pl.run_scoped(
                inner,
                pltpu.VMEM((2, tok, 256), BF),
                pltpu.VMEM((2, tok, 256), BF),
                pltpu.VMEM((2, 4, 2, 2, d // 16, 256), BF),
                pltpu.VMEM((2, 4, 2, 2, d // 16, 256), BF),
                pltpu.VMEM((tok, d), BF),
                pltpu.VMEM((d, tok), BF),
                pltpu.VMEM((d, tok), BF),
                pltpu.VMEM((tok, 256), BF),
                pltpu.VMEM((tok, d), BF),
            )

            def norm_part(r1):
                load(r1_i, r1).wait()

                @pl.loop(0, tok // 128)
                def _(b):
                    rows = pl.ds(pl.multiple_of(b * 128, 128), 128)
                    vhat, r = norm_stats(r1[rows, :])
                    cot = dn2[rows, :]
                    sums[4:5, 0:d] += jnp.sum(cot * vhat, axis=0, keepdims=True)
                    sums[5:6, 0:d] += jnp.sum(cot, axis=0, keepdims=True)
                    dres[rows, :] = dres[rows, :] + norm_grad(vhat, r, cot * vec(4, 0, d))

            pl.run_scoped(norm_part, pltpu.VMEM((tok, d), F32))

        pl.run_scoped(ff_part, pltpu.VMEM((tok, d), F32))

        def attn_part(proj, wqkv, ns, dpad):
            proj_load, qkv_load, ns_load = load(proj_i, proj), load(qkv_i, wqkv), load(ns_i, ns)

            def out_part(heads, wo, dattn):
                loads = [load(heads_i, heads), load(wo_i, wo)]
                wo2 = wo.reshape(d, d)
                g_wo2 = g_wo.reshape(d, d)

                @pl.loop(0, tok // 256)
                def _(b):
                    rows = pl.ds(pl.multiple_of(b * 256, 256), 256)
                    val = dres[rows, :].astype(BF)
                    dattn[rows, :] = val
                    sums[3:4, 0:d] += jnp.sum(val.astype(F32), axis=0, keepdims=True)

                for copy in loads:
                    copy.wait()

                @pl.loop(0, d // 256)
                def _(b):
                    rows = pl.ds(pl.multiple_of(b * 256, 256), 256)
                    g_wo2[rows, :] = tn(heads[:, rows], dattn[...]).astype(BF)

                comm(9)
                dpad[0:win, :] = jnp.zeros((win, d), BF)
                dpad[win + tok : 2 * win + tok, :] = jnp.zeros((win, d), BF)

                @pl.loop(0, tok // 256)
                def _(b):
                    at = pl.multiple_of(b * 256, 256)
                    dpad[pl.ds(at + win, 256), :] = nt(dattn[pl.ds(at, 256), :], wo2[...]).astype(BF)

            pl.run_scoped(out_part, pltpu.VMEM((tok, d), BF), pltpu.VMEM(wo_i.shape, BF), pltpu.VMEM((tok, d), BF))

            qmask = head_masks(win, HDIM**-0.5)
            vmask = head_masks(win, 1.0)

            def core_part(prob):
                def prob_copy(w):
                    return pltpu.make_async_copy(prob_i.at[w], prob.at[lax.rem(w, 2)], res_sem.at[lax.rem(w, 2)])

                prob_copy(0).start()
                proj_load.wait()

                @pl.loop(0, nw)
                def _(w):
                    prob_copy(w).wait()

                    @pl.when(w + 1 < nw)
                    def _():
                        prob_copy(w + 1).start()

                    at = pl.multiple_of(w * win, win)
                    rows = pl.ds(at, win)
                    dhw = nn(shift_in, dpad[pl.ds(at, 2 * win), :]).astype(BF)
                    for pr in range(HEADS // 2):
                        lq = slice(pr * 128, pr * 128 + 128)
                        lk = slice(d + pr * 128, d + pr * 128 + 128)
                        lv = slice(2 * d + pr * 128, 2 * d + pr * 128 + 128)
                        q2, k2, v2 = proj[rows, lq], proj[rows, lk], proj[rows, lv]
                        pb = prob[lax.rem(w, 2), pr]
                        dbd = split_heads(dhw[:, lq], vmask)
                        dp = nt(v2, dbd)
                        pf = pb.astype(F32)
                        ds = (pf * (dp - jnp.sum(pf * dp, axis=0, keepdims=True))).astype(BF)
                        stacked = jnp.concatenate([ds[:, :win], ds[:, win:]], axis=0)
                        dq = tn(stacked, split_heads(k2, qmask)).astype(BF)
                        dk = nn(ds, split_heads(q2, qmask)).astype(BF)
                        dv = nn(pb, dbd).astype(BF)
                        proj[rows, lq] = dq
                        proj[rows, lk] = dk
                        proj[rows, lv] = dv

            pl.run_scoped(core_part, pltpu.VMEM((2,) + prob_i.shape[1:], BF))

            g_qkv2 = g_qkv.reshape(d, 3 * d)
            wqkv2 = wqkv.reshape(d, 3 * d)

            def last_part(ns_t, hi, lo):
                ns_load.wait()

                @pl.loop(0, nw // 3)
                def _(b):
                    rows = pl.ds(pl.multiple_of(b * 384, 128), 384)
                    ns_t[:, rows] = ns[rows, :].T

                for n0 in range(0, 3 * d, 256):
                    part = proj[:, n0 : n0 + 256]
                    if n0 // d != 1:
                        at = n0 if n0 < d else n0 - d
                        sums[2:3, at : at + 256] = jnp.sum(part.astype(F32), axis=0, keepdims=True)

                    @pl.loop(0, d // 256)
                    def _(b):
                        rows = pl.ds(pl.multiple_of(b * 256, 256), 256)
                        g_qkv2[rows, n0 : n0 + 256] = nn(ns_t[rows, :], proj[:, n0 : n0 + 256]).astype(BF)

                comm(12)
                qkv_load.wait()

                @pl.loop(0, nw // 3)
                def _(b):
                    rows = pl.ds(pl.multiple_of(b * 384, 128), 384)
                    for n0 in range(0, d, 256):
                        val = nt(proj[rows, :], wqkv2[n0 : n0 + 256, :])
                        top = val.astype(BF)
                        hi[rows, n0 : n0 + 256] = top
                        lo[rows, n0 : n0 + 256] = (val - top.astype(F32)).astype(BF)

                @pl.loop(0, tok // 128)
                def _(b):
                    at = pl.multiple_of(b * 128, 128)
                    rows = pl.ds(at, 128)
                    both = pl.ds(at, 2 * win)
                    cot = nn(shift_out, hi[both, :]) + nn(shift_out, lo[both, :])
                    vhat, r = norm_stats(x_ref[rows, :].astype(F32))
                    sums[0:1, 0:d] += jnp.sum(cot * vhat, axis=0, keepdims=True)
                    sums[1:2, 0:d] += jnp.sum(cot, axis=0, keepdims=True)
                    dres[rows, :] = dres[rows, :] + norm_grad(vhat, r, cot * vec(0, 0, d))

            pl.run_scoped(last_part, pltpu.VMEM((d, nw * win), BF), pltpu.VMEM((nw * win, d), BF), pltpu.VMEM((nw * win, d), BF))

        pl.run_scoped(
            attn_part,
            pltpu.VMEM(proj_i.shape, BF),
            pltpu.VMEM(qkv_i.shape, BF),
            pltpu.VMEM(ns_i.shape, BF),
            pltpu.VMEM((tok + 2 * win, d), BF),
        )
        done = pltpu.make_async_copy(dres, dch_out, out_sem.at[0])
        done.start()

        g_vec2 = g_vec.reshape(-1, SLOT)
        nrow = g_vec2.shape[0] // 16
        g_vec[...] = jnp.zeros_like(g_vec)
        for v, (width, count) in enumerate(sizes):
            col = lax.broadcasted_iota(jnp.int32, (SLOT, width), 1).astype(F32)
            row = lax.broadcasted_iota(jnp.int32, (SLOT, width), 0).astype(F32)
            owner = jnp.floor((col + 0.5) * (1.0 / count))
            pick = jnp.where(col - owner * count == row, 1.0, 0.0).astype(BF)
            col2 = lax.broadcasted_iota(jnp.int32, (nrow, width), 1).astype(F32)
            row2 = lax.broadcasted_iota(jnp.int32, (nrow, width), 0).astype(F32)
            mine = jnp.where(row2 == jnp.floor((col2 + 0.5) * (1.0 / count)), sums[v : v + 1, :width], 0.0)
            top = mine.astype(BF)
            rest = (mine - top.astype(F32)).astype(BF)
            g_vec2[pl.ds(v, nrow, stride=16), :] = nt(top, pick) + nt(rest, pick)
        comm(len(ticks))
        sends.sent()
        done.wait()

    pl.run_scoped(whole, pltpu.VMEM((tok, d), F32))


def quick_mesh(mesh):
    return mesh.shape["dp"] == 16 and mesh.shape["mp"] == 2


def gathered_shape(shape, kind):
    if kind == 2:
        return (4, 2, 2, 2 * shape[0], shape[1])
    return ((4, 2, 2, 2) if kind == 0 else (2, 4, 2, 2)) + shape


def fast_shards(*args):
    (chars, seg, offs, l1g, l1b, wqkv, qvb, wo, aob, l2g, l2b, wi, fib, wf, fob, cv, cvb, l3g, l3b, dmol) = args
    tok, d = chars.shape
    mols = dmol.shape[0]
    vectors = (l1g, l1b, qvb, aob, l2g, l2b, fib, fob, cvb, l3g, l3b)
    sizes = tuple((v.shape[0] * 32, v.shape[0]) for v in vectors)
    ff = sizes[6][0]
    dims = (tok, d, ff)
    nw = tok // WIN + 1
    vec_own = jnp.stack([jnp.pad(v, (0, SLOT - v.shape[0])) for v in vectors] + [jnp.zeros((SLOT,), BF)] * 5)
    owns = (vec_own, wqkv, wo, wi, wf.T, cv)
    kinds = (0, 2, 2, 1, 1, 1)
    full = [gathered_shape(o.shape, k) for o, k in zip(owns, kinds)]
    plan = gather_plan([o.shape for o in owns])
    n_send = sum(9 * sum(cut is not None for cut in cuts) for _, _, cuts in plan)
    on_chip = pl.BlockSpec(memory_space=pltpu.VMEM)
    scalar = pl.BlockSpec(memory_space=pltpu.SMEM)
    any_mem = pl.BlockSpec(memory_space=pl.ANY)
    bf = lambda *s: jax.ShapeDtypeStruct(s, BF)
    f32 = lambda *s: jax.ShapeDtypeStruct(s, F32)
    prob_shape = (nw, HEADS // 2, WIN, 2 * WIN)
    saved = pl.pallas_call(
        functools.partial(forward_kernel, dims, sizes, n_send),
        out_shape=[
            f32(mols, d),
            f32(16, ff),
            f32(8, d),
            bf(mols, d),
            *[bf(*s) for s in full[1:]],
            bf(nw * WIN, d),
            bf(nw * WIN, 3 * d),
            bf(*prob_shape),
            bf(tok, d),
            f32(tok, d),
            bf(tok, d),
            bf(tok, ff),
            bf(tok, ff),
            bf(mols, KER * d),
        ],
        in_specs=[scalar] + [on_chip] * 9,
        out_specs=[on_chip, any_mem, on_chip, on_chip] + [any_mem] * 14,
        scratch_shapes=[
            *[pltpu.VMEM(s, BF) for s in full],
            pltpu.VMEM((512, SLOT), F32),
            pltpu.VMEM((16, ff), F32),
            pltpu.VMEM((tok + 2 * WIN, d), BF),
            pltpu.VMEM((nw * WIN, d), BF),
            pltpu.VMEM((nw * WIN, 3 * d), BF),
            pltpu.VMEM(prob_shape, BF),
            pltpu.VMEM((tok, d), BF),
            pltpu.VMEM((tok, d), F32),
            pltpu.VMEM((tok, d), BF),
            pltpu.VMEM((tok, ff), BF),
            pltpu.VMEM((tok, ff), BF),
            pltpu.VMEM((d // 128, tok, 128), F32),
            pltpu.VMEM((mols, KER * d), BF),
            pltpu.SemaphoreType.DMA((6,)),
            pltpu.SemaphoreType.DMA((16,)),
            pltpu.SemaphoreType.DMA((n_send,)),
            pltpu.SemaphoreType.DMA((n_send,)),
        ],
        compiler_params=pltpu.CompilerParams(collective_id=1, has_side_effects=True, vmem_limit_bytes=VMEM_CAP),
        name="gather_forward",
    )(offs, seg, chars, dmol, *owns)
    (mol, vecs, ln3, dcp, qkv_f, wo_f, wi_f, wf_f, cv_f, ns, proj, prob, heads, r1, n2, act, gd, mi) = saved

    own_shapes = [o.shape for o in owns]
    kind_core = lambda s, k: (4, 2, 2 * s[0], s[1]) if k == 2 else ((4, 2, 2) if k == 0 else (2, 4, 2)) + s
    types = [F32] + [BF] * 5
    plan = scatter_plan(own_shapes)
    n_back = sum(7 * sum(cut is not None for cut in cuts) for _, _, cuts in plan)
    back = pl.pallas_call(
        functools.partial(backward_kernel, dims, sizes, n_back),
        out_shape=[f32(tok, d)] + [f32(*s) for s in own_shapes],
        in_specs=[scalar] + [on_chip] * 4 + [any_mem] * 14,
        out_specs=[any_mem] + [on_chip] * 6,
        scratch_shapes=[
            *[pltpu.VMEM(s, t) for s, t in zip(full, types)],
            *[pltpu.VMEM(kind_core(s, k), t) for s, k, t in zip(own_shapes, kinds, types)],
            *[pltpu.VMEM((2, 4) + s, t) for s, t in zip(own_shapes, types)],
            *[pltpu.VMEM((4,) + s, t) for s, t in zip(own_shapes, types)],
            *[pltpu.VMEM((3,) + s, t) for s, t in zip(own_shapes, types)],
            pltpu.VMEM((16, ff), F32),
            pltpu.SemaphoreType.DMA((2,)),
            pltpu.SemaphoreType.DMA((2, 4)),
            pltpu.SemaphoreType.DMA((16,)),
            pltpu.SemaphoreType.DMA((1,)),
            pltpu.SemaphoreType.DMA((n_back,)),
            pltpu.SemaphoreType.DMA((n_back,)),
        ],
        compiler_params=pltpu.CompilerParams(collective_id=2, has_side_effects=True, vmem_limit_bytes=VMEM_CAP),
        name="backward_scatter",
    )(offs, chars, dcp, vecs, ln3, qkv_f, wo_f, wi_f, wf_f, cv_f, ns, proj, prob, heads, r1, n2, act, gd, mi)
    d_chars, d_vec, d_qkv, d_wo, d_wi, d_wf, d_cv = back
    dv = [d_vec[i, : v.shape[0]] for i, v in enumerate(vectors)]
    return (
        mol,
        d_chars,
        dv[0],
        dv[1],
        d_qkv,
        dv[2],
        d_wo,
        dv[3],
        dv[4],
        dv[5],
        d_wi,
        dv[6],
        d_wf.T,
        dv[7],
        d_cv,
        dv[8],
        dv[9],
        dv[10],
    )


def solution(mesh):
    placed = (
        P(("dp", "mp"), None),
        P(("dp", "mp"), None),
        P(("dp", "mp")),
        P(("dp", "mp")),
        P(("dp", "mp")),
        P(("dp", "mp"), None),
        P(("dp", "mp")),
        P(("dp", "mp"), None),
        P(("dp", "mp")),
        P(("dp", "mp")),
        P(("dp", "mp")),
        P("dp", "mp"),
        P(("dp", "mp")),
        P("mp", "dp"),
        P(("dp", "mp")),
        P("dp", "mp"),
        P(("dp", "mp")),
        P(("dp", "mp")),
        P(("dp", "mp")),
        P(("dp", "mp"), None),
    )
    return jax.shard_map(
        fast_shards if quick_mesh(mesh) else shards,
        mesh=mesh,
        in_specs=placed,
        out_specs=(
            P(("dp", "mp"), None),
            P(("dp", "mp"), None),
            P(("dp", "mp")),
            P(("dp", "mp")),
            P(("dp", "mp"), None),
            P(("dp", "mp")),
            P(("dp", "mp"), None),
            P(("dp", "mp")),
            P(("dp", "mp")),
            P(("dp", "mp")),
            P("dp", "mp"),
            P(("dp", "mp")),
            P("mp", "dp"),
            P(("dp", "mp")),
            P("dp", "mp"),
            P(("dp", "mp")),
            P(("dp", "mp")),
            P(("dp", "mp")),
        ),
        check_vma=False,
    )
```

```python
import functools

import jax
import jax.numpy as jnp
from jax import lax
from jax.experimental import pallas as pl
from jax.experimental.pallas import tpu as pltpu
from jax.sharding import PartitionSpec as P

HEADS = 12
HDIM = 64
KER = 4
WIN = 128


layer_eps = 1e-06


def layer_norm(row_values, gain_vec, shift_vec):
    centred = row_values - jnp.mean(row_values, axis=-1, keepdims=True)
    spread = jnp.mean(centred * centred, axis=-1, keepdims=True)
    return centred * lax.rsqrt(spread + layer_eps) * gain_vec + shift_vec


def gelu_exact(values):
    return jax.nn.gelu(values, approximate=False)


def norm_backward(row_values, gain_vec, shift_vec, grad_out):
    _, pullback = jax.vjp(layer_norm, row_values, gain_vec, shift_vec)
    return pullback(grad_out)


def gelu_backward(values, grad_out):
    _, pullback = jax.vjp(gelu_exact, values)
    return pullback(grad_out)[0]


def three_blocks(rows, fill_value):
    edge = jnp.full_like(rows[:1], fill_value)
    before = jnp.concatenate([edge, rows[:-1]], axis=0)
    after = jnp.concatenate([rows[1:], edge], axis=0)
    return jnp.concatenate([before, rows, after], axis=1)


def fold_blocks(band_grad):
    edge = jnp.zeros_like(band_grad[:1, :WIN])
    from_next = jnp.concatenate([band_grad[1:, :WIN], edge], axis=0)
    from_prev = jnp.concatenate([edge, band_grad[:-1, 2 * WIN :]], axis=0)
    return band_grad[:, WIN : 2 * WIN] + from_next + from_prev


def band_inputs(queries, key_rows, value_rows, seg_row, offset):
    seq_len = queries.shape[0]
    block_count = seq_len // WIN
    win_row = (jnp.arange(seq_len, dtype=jnp.int32) + offset) // WIN
    seg_blk = seg_row.reshape(block_count, WIN)
    win_blk = win_row.reshape(block_count, WIN)
    return (
        queries.reshape(block_count, WIN, HEADS, HDIM),
        three_blocks(key_rows.reshape(block_count, WIN, HEADS, HDIM), 0),
        three_blocks(value_rows.reshape(block_count, WIN, HEADS, HDIM), 0),
        seg_blk,
        win_blk,
        three_blocks(seg_blk, 0),
        three_blocks(win_blk, -1),
    )


def band_scores(query_blk, key_band, seg_blk, win_blk, seg_band, win_band):
    raw_scores = jnp.einsum(
        "bqhd,bkhd->bhqk", query_blk, key_band, preferred_element_type=jnp.float32
    ) * HDIM ** (-0.5)
    allowed = (seg_blk[:, :, None] == seg_band[:, None, :]) & (
        win_blk[:, :, None] == win_band[:, None, :]
    )
    return jnp.where(allowed[:, None], raw_scores, -1e30)


def attend_forward(seq_item):
    queries, key_rows, value_rows, seg_row, offset = seq_item
    seq_len = queries.shape[0]
    query_blk, key_band, val_band, seg_blk, win_blk, seg_band, win_band = band_inputs(
        queries, key_rows, value_rows, seg_row, offset
    )
    scores = band_scores(query_blk, key_band, seg_blk, win_blk, seg_band, win_band)
    row_peak = jnp.max(scores, axis=-1, keepdims=True)
    exp_scores = jnp.exp(scores - row_peak)
    row_total = jnp.sum(exp_scores, axis=-1, keepdims=True)
    prob_low = (exp_scores / row_total).astype(jnp.bfloat16)
    merged = jnp.einsum("bhqk,bkhd->bqhd", prob_low, val_band, preferred_element_type=jnp.float32)
    return (merged.reshape(seq_len, HEADS * HDIM), (row_peak + jnp.log(row_total))[..., 0])


def attend_backward(seq_item):
    queries, key_rows, value_rows, seg_row, offset, log_norm, d_heads = seq_item
    seq_len = queries.shape[0]
    block_count = seq_len // WIN
    score_scale = HDIM ** (-0.5)
    query_blk, key_band, val_band, seg_blk, win_blk, seg_band, win_band = band_inputs(
        queries, key_rows, value_rows, seg_row, offset
    )
    grad_blk = d_heads.reshape(block_count, WIN, HEADS, HDIM)
    scores = band_scores(query_blk, key_band, seg_blk, win_blk, seg_band, win_band)
    prob_blk = jnp.exp(scores - log_norm[..., None])
    d_probs = jnp.einsum("bqhd,bkhd->bhqk", grad_blk, val_band, preferred_element_type=jnp.float32)
    row_dot = jnp.sum(prob_blk * d_probs, axis=-1, keepdims=True)
    d_scores = (prob_blk * (d_probs - row_dot)).astype(jnp.bfloat16)
    d_query = (
        jnp.einsum("bhqk,bkhd->bqhd", d_scores, key_band, preferred_element_type=jnp.float32)
        * score_scale
    )
    d_key_band = (
        jnp.einsum("bhqk,bqhd->bkhd", d_scores, query_blk, preferred_element_type=jnp.float32)
        * score_scale
    )
    d_val_band = jnp.einsum(
        "bhqk,bqhd->bkhd",
        prob_blk.astype(jnp.bfloat16),
        grad_blk,
        preferred_element_type=jnp.float32,
    )
    d_keys = fold_blocks(d_key_band)
    d_vals = fold_blocks(d_val_band)
    return (
        d_query.reshape(seq_len, HEADS * HDIM),
        d_keys.reshape(seq_len, HEADS * HDIM),
        d_vals.reshape(seq_len, HEADS * HDIM),
    )


def shards(
    chars,
    segment_ids,
    window_offsets,
    ln1_gain,
    ln1_bias,
    w_qkv,
    qv_bias,
    w_attn_out,
    attn_out_bias,
    ln2_gain,
    ln2_bias,
    w_ff_in,
    ff_in_bias,
    w_ff_out,
    ff_out_bias,
    conv_weight,
    conv_bias,
    ln3_gain,
    ln3_bias,
    d_molecules,
):
    gathered = (
        lax.all_gather(w_qkv, ("dp", "mp"), axis=0, tiled=True),
        lax.all_gather(w_attn_out, ("dp", "mp"), axis=0, tiled=True),
        lax.all_gather(ln1_gain, ("dp", "mp"), axis=0, tiled=True),
        lax.all_gather(ln1_bias, ("dp", "mp"), axis=0, tiled=True),
        lax.all_gather(qv_bias, ("dp", "mp"), axis=0, tiled=True),
        lax.all_gather(attn_out_bias, ("dp", "mp"), axis=0, tiled=True),
        lax.all_gather(ln2_gain, ("dp", "mp"), axis=0, tiled=True),
        lax.all_gather(ln2_bias, ("dp", "mp"), axis=0, tiled=True),
        lax.all_gather(ff_in_bias, ("dp", "mp"), axis=0, tiled=True),
        lax.all_gather(ff_out_bias, ("dp", "mp"), axis=0, tiled=True),
        lax.all_gather(conv_bias, ("dp", "mp"), axis=0, tiled=True),
        lax.all_gather(ln3_gain, ("dp", "mp"), axis=0, tiled=True),
        lax.all_gather(ln3_bias, ("dp", "mp"), axis=0, tiled=True),
    )
    qkv_full = gathered[0]
    attn_out_full = gathered[1]
    vectors = [vector_arg.astype(jnp.float32) for vector_arg in gathered[2:]]
    (
        gain_one,
        shift_one,
        qv_shift,
        attn_shift,
        gain_two,
        shift_two,
        hidden_shift,
        ff_shift,
        conv_shift,
        gain_three,
        shift_three,
    ) = vectors
    ff_in_part, ff_out_part, conv_part = (
        lax.all_gather(w_ff_in, "dp", axis=0, tiled=True),
        lax.all_gather(w_ff_out, "dp", axis=1, tiled=True),
        lax.all_gather(conv_weight, "dp", axis=0, tiled=True),
    )
    model_width = chars.shape[1]
    tok_rows = chars.shape[0]
    seq_count = segment_ids.shape[0]
    seq_len = segment_ids.shape[1]
    mp_rank = lax.axis_index("mp")
    hidden_part = ff_in_part.shape[1]
    channel_part = conv_part.shape[1]
    inputs = chars.astype(jnp.float32)
    normed_one = layer_norm(inputs, gain_one, shift_one).astype(jnp.bfloat16)
    qkv_shift = jnp.concatenate(
        [qv_shift[:model_width], jnp.zeros((model_width,), jnp.float32), qv_shift[model_width:]]
    )
    projected = (
        jnp.dot(normed_one, qkv_full, preferred_element_type=jnp.float32) + qkv_shift
    ).astype(jnp.bfloat16)
    per_seq = projected.reshape(seq_count, seq_len, 3, HEADS, HDIM)
    queries = per_seq[:, :, 0]
    key_rows = per_seq[:, :, 1]
    value_rows = per_seq[:, :, 2]
    merged, log_norm = lax.map(
        attend_forward, (queries, key_rows, value_rows, segment_ids, window_offsets)
    )
    heads_low = merged.reshape(tok_rows, model_width).astype(jnp.bfloat16)
    resid_one = (
        inputs + jnp.dot(heads_low, attn_out_full, preferred_element_type=jnp.float32) + attn_shift
    )
    normed_two = layer_norm(resid_one, gain_two, shift_two).astype(jnp.bfloat16)
    ff_in_use, ff_out_use, conv_use = (ff_in_part, ff_out_part, conv_part)
    ff_rows_in = lax.all_gather(normed_two, "mp", axis=0, tiled=True)
    hidden_bias = lax.dynamic_slice_in_dim(hidden_shift, mp_rank * hidden_part, hidden_part)
    hidden_pre = jnp.dot(ff_rows_in, ff_in_use, preferred_element_type=jnp.float32) + hidden_bias
    hidden_act = gelu_exact(hidden_pre).astype(jnp.bfloat16)
    ff_sum = lax.psum_scatter(
        jnp.dot(hidden_act, ff_out_use, preferred_element_type=jnp.float32).astype(jnp.bfloat16),
        "mp",
        scatter_dimension=0,
        tiled=True,
    ).astype(jnp.float32)
    resid_two = resid_one + ff_sum + ff_shift
    mol_rows = resid_two.astype(jnp.bfloat16).reshape(tok_rows // KER, KER * model_width)
    mol_group = lax.all_gather(mol_rows, "mp", axis=0, tiled=True)
    channel_bias = lax.dynamic_slice_in_dim(conv_shift, mp_rank * channel_part, channel_part)
    conv_pre = jnp.dot(mol_group, conv_use, preferred_element_type=jnp.float32) + channel_bias
    channel_act = gelu_exact(conv_pre).astype(jnp.bfloat16)
    conv_act = lax.all_to_all(channel_act, "mp", split_axis=0, concat_axis=1, tiled=True)
    act_float = conv_act.astype(jnp.float32)
    molecules = layer_norm(act_float, gain_three, shift_three)
    d_act, d_gain_three, d_shift_three = norm_backward(
        act_float, gain_three, shift_three, d_molecules.astype(jnp.float32)
    )
    d_act_low = d_act.astype(jnp.bfloat16)
    d_act_cols = lax.all_to_all(d_act_low, "mp", split_axis=1, concat_axis=0, tiled=True)
    d_conv_pre = gelu_backward(conv_pre, d_act_cols.astype(jnp.float32)).astype(jnp.bfloat16)
    d_conv_w = jnp.einsum("mk,mc->kc", mol_group, d_conv_pre, preferred_element_type=jnp.float32)
    d_conv_shift = lax.dynamic_update_slice_in_dim(
        jnp.zeros((model_width,), jnp.float32),
        jnp.sum(d_conv_pre.astype(jnp.float32), axis=0),
        mp_rank * channel_part,
        0,
    )
    d_mol = lax.psum_scatter(
        jnp.einsum("mc,kc->mk", d_conv_pre, conv_use, preferred_element_type=jnp.float32).astype(
            jnp.bfloat16
        ),
        "mp",
        scatter_dimension=0,
        tiled=True,
    ).astype(jnp.float32)
    d_resid_two = d_mol.reshape(tok_rows, model_width)
    d_ff_low = d_resid_two.astype(jnp.bfloat16)
    d_ff_shift = jnp.sum(d_ff_low.astype(jnp.float32), axis=0)
    d_ff_rows = lax.all_gather(d_ff_low, "mp", axis=0, tiled=True)
    d_hidden_act = jnp.einsum(
        "gc,fc->gf", d_ff_rows, ff_out_use, preferred_element_type=jnp.float32
    )
    d_ff_out_w = jnp.einsum("gf,gc->fc", hidden_act, d_ff_rows, preferred_element_type=jnp.float32)
    d_hidden = gelu_backward(hidden_pre, d_hidden_act).astype(jnp.bfloat16)
    d_hidden_sum = jnp.sum(d_hidden.astype(jnp.float32), axis=0)
    d_ff_in_w = jnp.einsum("gd,gf->df", ff_rows_in, d_hidden, preferred_element_type=jnp.float32)
    d_hidden_shift = lax.dynamic_update_slice_in_dim(
        jnp.zeros((hidden_shift.shape[0],), jnp.float32), d_hidden_sum, mp_rank * hidden_part, 0
    )
    d_normed_two = lax.psum_scatter(
        jnp.einsum("gf,df->gd", d_hidden, ff_in_use, preferred_element_type=jnp.float32).astype(
            jnp.bfloat16
        ),
        "mp",
        scatter_dimension=0,
        tiled=True,
    ).astype(jnp.float32)
    d_resid_from, d_gain_two, d_shift_two = norm_backward(
        resid_one, gain_two, shift_two, d_normed_two
    )
    d_resid_one = d_resid_two + d_resid_from
    d_attn_low = d_resid_one.astype(jnp.bfloat16)
    d_attn_shift = jnp.sum(d_attn_low.astype(jnp.float32), axis=0)
    d_attn_out_w = jnp.einsum(
        "te,tc->ec", heads_low, d_attn_low, preferred_element_type=jnp.float32
    )
    d_heads_low = jnp.einsum(
        "tc,ec->te", d_attn_low, attn_out_full, preferred_element_type=jnp.float32
    ).astype(jnp.bfloat16)
    d_heads_seq = d_heads_low.reshape(seq_count, seq_len, HEADS, HDIM)
    d_queries, d_keys, d_vals = lax.map(
        attend_backward,
        (queries, key_rows, value_rows, segment_ids, window_offsets, log_norm, d_heads_seq),
    )
    d_projected = jnp.concatenate(
        [
            d_queries.reshape(tok_rows, model_width),
            d_keys.reshape(tok_rows, model_width),
            d_vals.reshape(tok_rows, model_width),
        ],
        axis=1,
    ).astype(jnp.bfloat16)
    d_proj_sum = jnp.sum(d_projected.astype(jnp.float32), axis=0)
    d_qv_shift = jnp.concatenate([d_proj_sum[:model_width], d_proj_sum[2 * model_width :]])
    d_qkv_w = jnp.einsum("td,te->de", normed_one, d_projected, preferred_element_type=jnp.float32)
    d_normed_one = jnp.einsum(
        "te,de->td", d_projected, qkv_full, preferred_element_type=jnp.float32
    )
    d_inputs_from, d_gain_one, d_shift_one = norm_backward(
        inputs, gain_one, shift_one, d_normed_one
    )
    d_chars = d_resid_one + d_inputs_from
    d_ff_in_own, d_ff_out_own, d_conv_own = (
        lax.psum_scatter(
            d_ff_in_w.astype(jnp.bfloat16), "dp", scatter_dimension=0, tiled=True
        ).astype(jnp.float32),
        lax.psum_scatter(
            d_ff_out_w.astype(jnp.bfloat16), "dp", scatter_dimension=1, tiled=True
        ).astype(jnp.float32),
        lax.psum_scatter(
            d_conv_w.astype(jnp.bfloat16), "dp", scatter_dimension=0, tiled=True
        ).astype(jnp.float32),
    )
    owned = (
        lax.psum_scatter(d_qkv_w, ("dp", "mp"), scatter_dimension=0, tiled=True),
        lax.psum_scatter(d_attn_out_w, ("dp", "mp"), scatter_dimension=0, tiled=True),
        lax.psum_scatter(d_gain_one, ("dp", "mp"), scatter_dimension=0, tiled=True),
        lax.psum_scatter(d_shift_one, ("dp", "mp"), scatter_dimension=0, tiled=True),
        lax.psum_scatter(d_qv_shift, ("dp", "mp"), scatter_dimension=0, tiled=True),
        lax.psum_scatter(d_attn_shift, ("dp", "mp"), scatter_dimension=0, tiled=True),
        lax.psum_scatter(d_gain_two, ("dp", "mp"), scatter_dimension=0, tiled=True),
        lax.psum_scatter(d_shift_two, ("dp", "mp"), scatter_dimension=0, tiled=True),
        lax.psum_scatter(d_hidden_shift, ("dp", "mp"), scatter_dimension=0, tiled=True),
        lax.psum_scatter(d_ff_shift, ("dp", "mp"), scatter_dimension=0, tiled=True),
        lax.psum_scatter(d_conv_shift, ("dp", "mp"), scatter_dimension=0, tiled=True),
        lax.psum_scatter(d_gain_three, ("dp", "mp"), scatter_dimension=0, tiled=True),
        lax.psum_scatter(d_shift_three, ("dp", "mp"), scatter_dimension=0, tiled=True),
    )
    return (
        molecules,
        d_chars,
        owned[2],
        owned[3],
        owned[0],
        owned[4],
        owned[1],
        owned[5],
        owned[6],
        owned[7],
        d_ff_in_own,
        owned[8],
        d_ff_out_own,
        owned[9],
        d_conv_own,
        owned[10],
        owned[11],
        owned[12],
    )


GATHER_TABLE = (
    ((0, 0), (0, 1), (1, 0), (0, 2), (2, 0), (1, 1), (0, 3), (3, 0), (1, 2), (0, 4), (4, 0),),
    ((2, 1), (1, 3), (0, 5),),
    ((2, 2), (1, 4), (0, 6),),
    (),
    ((0, 7),),
    ((3, 1),),
    ((1, 5), (0, 8),),
    ((4, 1), (1, 6), (0, 9), (2, 3), (3, 2), (4, 2), (1, 7), (1, 8), (0, 10), (2, 4), (3, 3), (2, 5), (2, 6), (1, 9), (1, 10), (0, 11), (4, 3), (2, 7), (0, 12),),
    ((2, 8), (0, 13),),
    ((3, 4), (3, 5), (1, 11), (0, 14),),
    ((3, 6), (1, 12), (0, 15),),
    ((4, 4), (4, 5), (2, 9), (1, 13), (0, 16),),
    ((4, 6),),
    ((2, 10), (1, 14), (0, 17),),
    ((3, 7), (3, 8),),
    ((1, 15), (0, 18),),
    ((2, 11),),
    ((4, 7), (4, 8), (1, 16), (0, 19),),
    ((2, 12),),
    ((3, 9), (1, 17), (0, 20),),
    ((1, 18), (0, 21),),
    ((4, 9), (2, 13),),
    ((3, 10), (1, 19), (0, 22),),
    ((2, 14), (1, 20),),
    ((4, 10), (2, 15),),
    ((3, 11), (1, 21),),
    ((2, 16), (1, 22),),
    ((4, 11), (3, 12),),
    ((2, 17),),
    ((4, 12), (2, 18),),
    ((3, 13),),
    ((2, 19),),
    ((4, 13), (3, 14),),
    ((2, 20),),
    ((4, 14), (3, 15),),
    (),
    ((4, 15), (3, 16), (2, 21), (4, 16), (2, 22),),
    ((3, 17), (3, 18),),
    ((3, 19),),
    ((4, 17), (4, 18), (3, 20), (3, 21),),
    ((4, 19), (3, 22),),
    ((4, 20), (4, 21), (4, 22),),
    (),
)
SCATTER_TABLE = (
    ((0, 0), (0, 1),),
    ((0, 2), (0, 3),),
    ((0, 4), (0, 5),),
    (),
    ((1, 0),),
    ((1, 1), (1, 2), (1, 3),),
    ((1, 4), (1, 5),),
    (),
    (),
    ((2, 0),),
    ((2, 1), (0, 6), (0, 7),),
    ((2, 2),),
    ((2, 3), (0, 8), (0, 9),),
    ((2, 4), (1, 6),),
    ((3, 0), (2, 5), (1, 7), (0, 10), (0, 11),),
    ((3, 1), (3, 2), (1, 8), (1, 9),),
    ((3, 3), (3, 4), (0, 12), (0, 13),),
    ((2, 6), (1, 10), (1, 11),),
    ((4, 0), (3, 5), (2, 7), (0, 14), (0, 15),),
    ((4, 1), (2, 8), (1, 12), (1, 13),),
    ((4, 2), (4, 3), (3, 6), (2, 9), (0, 16), (0, 17),),
    (),
    ((4, 4), (2, 10), (1, 14), (1, 15),),
    (),
    ((4, 5), (2, 11),),
    ((3, 7),),
    (),
    ((3, 8), (1, 16),),
    ((1, 17),),
    ((4, 6), (2, 12), (2, 13), (0, 18),),
    ((3, 9), (3, 10),),
    ((4, 7),),
    ((2, 14),),
    (),
    ((4, 8),),
    ((2, 15),),
    ((3, 11),),
    ((1, 18),),
    (),
    ((2, 16),),
    (),
    ((4, 9),),
    ((4, 10), (3, 12), (3, 13), (3, 14), (2, 17), (0, 19),),
    ((3, 15),),
    ((4, 11),),
    (),
    (),
    (),
    ((2, 18),),
    (),
    ((3, 16),),
    (),
    ((4, 12), (3, 17), (1, 19), (0, 20),),
    ((4, 13),),
    (),
    (),
    ((4, 14), (3, 18),),
    (),
    (),
    (),
    ((4, 15),),
    (),
    ((4, 16), (4, 17), (1, 20), (0, 21),),
    ((2, 19),),
    ((4, 18),),
    (),
    (),
    (),
    (),
    (),
    ((1, 21),),
    (),
    (),
    (),
    ((3, 19), (2, 20), (0, 22), (2, 21), (1, 22), (3, 20), (4, 19), (3, 21), (2, 22), (4, 20), (3, 22), (4, 21), (4, 22),),
)
HALF = 0.5
ERFC_P = 0.3
ERFC_Q = (
    0.16918934881687164,
    0.17069095373153687,
    0.1485210806131363,
    0.2141820192337036,
    -0.09282728284597397,
    0.5449684858322144,
    -0.5097734332084656,
    0.4843021035194397,
    -0.12925326824188232,
)
BF = jnp.bfloat16
F32 = jnp.float32
MESH_ID = pl.DeviceIdType.MESH
ALL = slice(None)
LINKS = ("z1", "z2", "z3", "x", "y", "c")
VMEM_CAP = 62 * 2**20
SLOT = 128


def nn(lhs, rhs):
    return lax.dot_general(lhs, rhs, (((1,), (0,)), ((), ())), preferred_element_type=F32)


def nt(lhs, rhs):
    return lax.dot_general(lhs, rhs, (((1,), (1,)), ((), ())), preferred_element_type=F32)


def tn(lhs, rhs):
    return lax.dot_general(lhs, rhs, (((0,), (0,)), ((), ())), preferred_element_type=F32)


def gelu_pair(v):
    size = jnp.abs(v)
    t = 1.0 / (1.0 + (ERFC_P * 0.7071067811865476) * size)
    q = ERFC_Q[-1]
    for coef in ERFC_Q[-2::-1]:
        q = q * t + coef
    bell = jnp.exp(-0.5 * (v * v))
    tail = (HALF * bell) * (q * t)
    phi = jnp.where(v >= 0, 1.0 - tail, tail)
    return v * phi, phi + v * (bell * 0.3989422804014327)


def norm_stats(v):
    mean = jnp.mean(v, axis=-1, keepdims=True)
    cen = v - mean
    r = lax.rsqrt(jnp.mean(cen * cen, axis=-1, keepdims=True) + layer_eps)
    return cen * r, r


def norm_grad(vhat, r, t):
    m1 = jnp.mean(t, axis=-1, keepdims=True)
    m2 = jnp.mean(t * vhat, axis=-1, keepdims=True)
    return r * (t - m1 - vhat * m2)


def head_masks(rows, scale):
    lane = lax.broadcasted_iota(jnp.int32, (rows, 128), 1)
    low = jnp.where(lane < HDIM, scale, 0.0).astype(BF)
    high = jnp.where(lane < HDIM, 0.0, scale).astype(BF)
    return low, high


def split_heads(pair, masks):
    return jnp.concatenate([pair * masks[0], pair * masks[1]], axis=0)


class Place:
    def __init__(self):
        dp = lax.axis_index("dp")
        self.x = lax.axis_index("mp")
        self.z, self.y, self.c = lax.div(dp, 4), lax.rem(lax.div(dp, 2), 2), lax.rem(dp, 2)
        z, y, c, x = self.z, self.y, self.c, self.x
        self.nx, self.ny, self.nc = 1 - x, 1 - y, 1 - c
        self.at = [c * 0 + k for k in range(3)]
        self.far_z = {1: z + 1 - 2 * lax.rem(z, 2), 2: lax.rem(z + 2, 4), 3: 3 - z}
        at = lambda zz, yy, cc, xx: (zz * 4 + yy * 2 + cc, xx)
        self.peer = {
            "z1": at(self.far_z[1], y, c, x),
            "z2": at(self.far_z[2], y, c, x),
            "z3": at(self.far_z[3], y, c, x),
            "x": at(z, y, c, 1 - x),
            "y": at(z, 1 - y, c, x),
            "c": at(z, y, 1 - c, x),
        }

    def barrier(self):
        sem = pltpu.get_barrier_semaphore()
        for peer in self.peer.values():
            pl.semaphore_signal(sem, inc=1, device_id=peer, device_id_type=MESH_ID)
        pl.semaphore_wait(sem, len(self.peer))


def rows_of(ref, xs):
    if isinstance(xs, slice):
        return xs
    half = ref.shape[-2] // 2
    return pl.ds(pl.multiple_of(xs * half, 8), half)


def block(ref, kind, zs, ys, cs, xs, cut):
    if kind == 0:
        return ref.at[(zs, ys, cs, xs) + cut]
    if kind == 1:
        return ref.at[(xs, zs, ys, cs) + cut]
    return ref.at[zs, ys, cs, rows_of(ref, xs), cut[1]]


class Sends:
    def __init__(self, place, send_sem, recv_sem):
        self.place, self.send_sem, self.recv_sem, self.made = place, send_sem, recv_sem, {}
        self.live = False

    def go(self, key, src, dst, link):
        if self.live:
            self.made[key].start()
            return
        i = len(self.made)
        self.made[key] = pltpu.make_async_remote_copy(
            src_ref=src,
            dst_ref=dst,
            send_sem=self.send_sem.at[i],
            recv_sem=self.recv_sem.at[i],
            device_id=self.place.peer[link],
            device_id_type=MESH_ID,
        )

    def got(self, key):
        if self.live:
            self.made[key].wait_recv()

    def sent(self):
        for copy in self.made.values():
            copy.wait_send()


def order(half):
    return ("x", "y") if half == 0 else ("y", "x")


def gather_stage(sends, stage, i, t, kind, own, full, cuts):
    p = sends.place
    z, y, c, x = p.z, p.y, p.c, p.x
    for h, cut in enumerate(cuts):
        if cut is None:
            continue
        a, b = order(h)
        if stage == 0:
            dst = block(full, kind, z, y, c, x, cut)
            for k in ("z1", "z2", "z3"):
                sends.go((i, h, k), own.at[cut], dst, k)
        elif stage == 1:
            for k in ("z1", "z2", "z3"):
                sends.got((i, h, k))
            v = block(full, kind, ALL, y, c, x, cut)
            sends.go((i, h, "a"), v, v, a)
            sends.go((i, h, "b1"), v, v, b)
            sends.go((i, h, "c1"), v, v, "c")
        elif stage == 2:
            sends.got((i, h, "a"))
            v = block(full, kind, ALL, y, c, p.nx, cut) if h == 0 else block(full, kind, ALL, p.ny, c, x, cut)
            sends.go((i, h, "b2"), v, v, b)
            sends.go((i, h, "c2"), v, v, "c")
        elif stage == 3:
            sends.got((i, h, "b1"))
            sends.got((i, h, "b2"))
            v = block(full, kind, ALL, p.ny, c, ALL, cut) if h == 0 else block(full, kind, ALL, ALL, c, p.nx, cut)
            sends.go((i, h, "c3"), v, v, "c")
        else:
            for k in ("c1", "c2", "c3"):
                sends.got((i, h, k))


def col_cuts(cols, parts):
    step = cols // (2 * parts)
    return [((ALL, slice(2 * step * i, 2 * step * i + step)), (ALL, slice(2 * step * i + step, 2 * step * (i + 1)))) for i in range(parts)]


def row_cuts(rows, parts):
    step = rows // (2 * parts)
    return [((slice(2 * step * i, 2 * step * i + step), ALL), (slice(2 * step * i + step, 2 * step * (i + 1)), ALL)) for i in range(parts)]


def gather_plan(shapes):
    plan = [(0, 0, ((ALL, ALL), None))]
    plan += [(1, 2, c) for c in col_cuts(shapes[1][1], 3)]
    plan += [(2, 2, c) for c in col_cuts(shapes[2][1], 1)]
    plan += [(3, 1, c) for c in col_cuts(shapes[3][1], 6)]
    plan += [(4, 1, c) for c in col_cuts(shapes[4][1], 6)]
    plan += [(5, 1, c) for c in row_cuts(shapes[5][0], 6)]
    return plan


class Ticks:
    def __init__(self, table, stage_fn):
        self.table, self.stage_fn, self.count = table, stage_fn, 0

    def run(self, k):
        for s, i in self.table[k]:
            self.stage_fn(s, i)

    def point(self):
        self.count += 1
        self.run(self.count - 1)

    def within(self, index, values):
        for value in values:
            if self.table[self.count]:
                pl.when(index == value)(functools.partial(self.run, self.count))
            self.count += 1


def forward_kernel(dims, sizes, n_send, *refs):
    (off_ref, seg_ref, x_ref, dmol_ref, vec_own, qkv_own, wo_own, wi_own, wf_own, cv_own) = refs[:10]
    outs = refs[10:28]
    (mol_out, vec_out, ln3_out, dcp_out, qkv_o, wo_o, wi_o, wf_o, cv_o, ns_o, proj_o, prob_o, heads_o, r1_o, n2_o, act_o, gd_o, mi_o) = outs
    (vec_g, qkv_g, wo_g, wi_g, wf_g, cv_g, vec_f, vecs, pad, ns, proj, prob, heads, r1, n2, act, gd, r2, molin, local_sem, out_sem, send_sem, recv_sem) = refs[28:]
    tok, d, ff = dims
    win = WIN
    nw = tok // win + 1
    half_ff = ff // 2
    mols = tok // KER
    place = Place()
    owns = (vec_own, qkv_own, wo_own, wi_own, wf_own, cv_own)
    fulls = (vec_g, qkv_g, wo_g, wi_g, wf_g, cv_g)
    plan = gather_plan([o.shape for o in owns])
    kinds = (0, 2, 2, 1, 1, 1)
    place.barrier()
    sends = Sends(place, send_sem, recv_sem)
    local = []
    for i, (own, full, kind) in enumerate(zip(owns, fulls, kinds)):
        copy = pltpu.make_async_copy(own, block(full, kind, place.z, place.y, place.c, place.x, (ALL, ALL)), local_sem.at[i])
        copy.start()
        local.append(copy)

    def comm_stage(stage, i):
        t, kind, cuts = plan[i]
        if sends.live and stage == 1 and (i == 0 or plan[i - 1][0] != t):
            local[t].wait()
        gather_stage(sends, stage, i, t, kind, owns[t], fulls[t], cuts)

    for stage in range(5):
        for i in range(len(plan)):
            comm_stage(stage, i)
    sends.live = True
    ticks = Ticks(GATHER_TABLE, comm_stage)

    out_copies = []

    def flush(src, dst):
        copy = pltpu.make_async_copy(src, dst, out_sem.at[len(out_copies)])
        copy.start()
        out_copies.append(copy)

    def unpack_vectors():
        nrow = vec_f.shape[0] // 16
        vec_f[...] = vec_g[...].reshape(vec_f.shape).astype(F32)
        for v, (width, count) in enumerate(sizes):
            col = lax.broadcasted_iota(jnp.int32, (SLOT, width), 1).astype(F32)
            row = lax.broadcasted_iota(jnp.int32, (SLOT, width), 0).astype(F32)
            owner = jnp.floor((col + 0.5) * (1.0 / count))
            pick = jnp.where(col - owner * count == row, 1.0, 0.0).astype(BF)
            spread = nn(vec_f[pl.ds(v, nrow, stride=16), :].astype(BF), pick)
            col2 = lax.broadcasted_iota(jnp.int32, (nrow, width), 1).astype(F32)
            row2 = lax.broadcasted_iota(jnp.int32, (nrow, width), 0).astype(F32)
            owner2 = jnp.floor((col2 + 0.5) * (1.0 / count))
            mine = jnp.where(row2 == owner2, spread, 0.0)
            vecs[v : v + 1, :width] = jnp.sum(mine, axis=0, keepdims=True)

    def vec(v, lo, hi):
        return vecs[v : v + 1, lo:hi]

    offset = off_ref[0]

    ticks.point()
    unpack_vectors()
    ticks.point()
    flush(vecs, vec_out)

    pad[0:win, :] = jnp.zeros((win, d), BF)
    pad[win + tok : 2 * win + tok, :] = jnp.zeros((win, d), BF)

    @pl.loop(0, tok // 128)
    def _(b):
        rows = pl.ds(pl.multiple_of(b * 128, 128), 128)
        vhat, _ = norm_stats(x_ref[rows, :].astype(F32))
        pad[pl.ds(pl.multiple_of(b * 128 + win, 128), 128), :] = (vhat * vec(0, 0, d) + vec(1, 0, d)).astype(BF)
        ticks.within(b, (1, 3, 5, 7))

    ri = lax.broadcasted_iota(jnp.int32, (win, 2 * win), 0)
    rj = lax.broadcasted_iota(jnp.int32, (win, 2 * win), 1)
    shift_in = jnp.where(rj == ri + (win - offset), 1.0, 0.0).astype(BF)
    shift_out = jnp.where(rj == ri + offset, 1.0, 0.0).astype(BF)

    @pl.loop(0, nw)
    def _(w):
        at = pl.multiple_of(w * win, win)
        ns[pl.ds(at, win), :] = nn(shift_in, pad[pl.ds(at, 2 * win), :]).astype(BF)
        ticks.within(w, (4,))

    flush(ns, ns_o)

    ticks.point()
    flush(qkv_g, qkv_o)
    wq = qkv_g.reshape(d, 3 * d)
    for blk3 in range(3):
        bias_row = None if blk3 == 1 else vec(2, (blk3 // 2) * d, (blk3 // 2) * d + d)

        @pl.loop(0, nw // 3)
        def _(b):
            rows = pl.ds(pl.multiple_of(b * 384, 128), 384)
            for n0 in range(0, d, 256):
                val = nn(ns[rows, :], wq[:, blk3 * d + n0 : blk3 * d + n0 + 256])
                if bias_row is not None:
                    val = val + bias_row[:, n0 : n0 + 256]
                proj[rows, blk3 * d + n0 : blk3 * d + n0 + 256] = val.astype(BF)

        ticks.point()

    flush(proj, proj_o)

    qmask = head_masks(win, HDIM**-0.5)
    vmask = head_masks(win, 1.0)
    seg_row = jnp.concatenate([seg_ref[0:1, :].astype(F32), jnp.full((1, win), -1.0, F32)], axis=1)
    seg_row = pltpu.roll(jnp.broadcast_to(seg_row, (8, tok + win)), offset, axis=1)
    segs = vec_f
    for w in range(nw):
        segs[w * 8 : w * 8 + 8, 0:win] = seg_row[:, w * win : (w + 1) * win]

    @pl.loop(0, nw)
    def _(w):
        rows = pl.ds(pl.multiple_of(w * win, win), win)
        seg_q = jnp.broadcast_to(segs[pl.ds(pl.multiple_of(w * 8, 8), 8), 0:win][0:1], (win, win))
        same = seg_q == seg_q.T
        same2 = jnp.concatenate([same, same], axis=1)
        for pr in range(HEADS // 2):
            lanes = slice(pr * 128, pr * 128 + 128)
            q2 = proj[rows, pr * 128 : pr * 128 + 128]
            k2 = proj[rows, d + pr * 128 : d + pr * 128 + 128]
            v2 = proj[rows, 2 * d + pr * 128 : 2 * d + pr * 128 + 128]
            s = jnp.where(same2, nt(k2, split_heads(q2, qmask)), -1e30)
            e = jnp.exp(s - jnp.max(s, axis=0, keepdims=True))
            pb = (e * (1.0 / jnp.sum(e, axis=0, keepdims=True))).astype(BF)
            prob[w, pr] = pb
            stacked = jnp.concatenate([pb[:, :win], pb[:, win:]], axis=0)
            pad[rows, lanes] = tn(stacked, split_heads(v2, vmask)).astype(BF)
        ticks.within(w, range(nw))

    flush(prob, prob_o)

    flush(wo_g, wo_o)
    wo = wo_g.reshape(d, d)

    @pl.loop(0, tok // 128)
    def _(b):
        at = pl.multiple_of(b * 128, 128)
        hb = nn(shift_out, pad[pl.ds(at, 2 * win), :]).astype(BF)
        heads[pl.ds(at, 128), :] = hb

    ticks.point()

    @pl.loop(0, tok // 256)
    def _(b):
        rows = pl.ds(pl.multiple_of(b * 256, 256), 256)
        val = x_ref[rows, :].astype(F32) + nn(heads[rows, :], wo[...]) + vec(3, 0, d)
        r1[rows, :] = val
        vhat, _ = norm_stats(val)
        n2[rows, :] = (vhat * vec(4, 0, d) + vec(5, 0, d)).astype(BF)
        ticks.within(b, (0, 1, 2))

    flush(heads, heads_o)
    flush(r1, r1_o)
    flush(n2, n2_o)

    wi = wi_g.reshape(2, d, half_ff)

    @pl.loop(0, half_ff // 256)
    def _(j):
        cols = pl.ds(pl.multiple_of(j * 256, 256), 256)
        base = ticks.count
        for hx in range(2):
            for q in range(half_ff // 256):
                if ticks.table[base + 2 * q + hx]:
                    pl.when(j == q)(functools.partial(ticks.run, base + 2 * q + hx))
            ocols = pl.ds(pl.multiple_of(hx * half_ff + j * 256, 256), 256)
            bias_row = vecs[6:7, ocols]
            for m in range(0, tok, 256):
                pre = nn(n2[m : m + 256, :], wi[hx, :, cols]) + bias_row
                g, dg = gelu_pair(pre)
                act[m : m + 256, ocols] = g.astype(BF)
                gd[m : m + 256, ocols] = dg.astype(BF)
        ticks.count = base + 2 * (half_ff // 256)

    flush(act, act_o)
    flush(gd, gd_o)

    ticks.point()
    flush(wi_g, wi_o)
    flush(wf_g, wf_o)
    wf = wf_g.reshape(2, d, half_ff)

    @pl.loop(0, tok // 256)
    def _(b):
        rows = pl.ds(pl.multiple_of(b * 256, 256), 256)
        for n0 in range(0, d, 256):
            cols = slice(n0, n0 + 256)
            val = nt(act[rows, 0:half_ff], wf[0, cols, :]) + nt(act[rows, half_ff:], wf[1, cols, :])
            val = r1[rows, cols] + val + vec(7, n0, n0 + 256)
            r2[n0 // 128, rows, :] = val[:, :128]
            r2[n0 // 128 + 1, rows, :] = val[:, 128:]
        ticks.within(b, range(4))

    for k in range(KER):
        for q in range(d // 128):
            molin[:, k * d + q * 128 : k * d + q * 128 + 128] = r2[q, pl.ds(k, mols, stride=KER), :].astype(BF)

    flush(molin, mi_o)
    ticks.point()
    flush(cv_g, cv_o)
    cv = cv_g.reshape(2, KER * d, d // 2)
    pre = jnp.concatenate([nn(molin[...], cv[0]), nn(molin[...], cv[1])], axis=1) + vec(8, 0, d)
    g, dg = gelu_pair(pre)
    vhat, r = norm_stats(g.astype(BF).astype(F32))
    mol_out[...] = vhat * vec(9, 0, d) + vec(10, 0, d)
    cot = dmol_ref[...].astype(F32)
    ln3_out[0:1, :] = jnp.sum(cot * vhat, axis=0, keepdims=True)
    ln3_out[1:2, :] = jnp.sum(cot, axis=0, keepdims=True)
    da = norm_grad(vhat, r, cot * vec(9, 0, d)).astype(BF).astype(F32)
    dcp_out[...] = (da * dg).astype(BF)
    sends.sent()
    for copy in out_copies:
        copy.wait()


def scatter_plan(shapes):
    plan = [(5, 1, c) for c in row_cuts(shapes[5][0], 6)]
    for wf_cut, wi_cut in zip(col_cuts(shapes[4][1], 6), col_cuts(shapes[3][1], 6)):
        plan += [(4, 1, wf_cut), (3, 1, wi_cut)]
    plan += [(2, 2, c) for c in col_cuts(shapes[2][1], 1)]
    plan += [(1, 2, c) for c in col_cuts(shapes[1][1], 3)]
    plan += [(0, 0, ((ALL, ALL), None))]
    return plan


def backward_kernel(dims, sizes, n_send, *refs):
    (off_ref, x_ref, dcp_ref, vecs, ln3_ref, qkv_i, wo_i, wi_i, wf_i, cv_i, ns_i, proj_i, prob_i, heads_i, r1_i, n2_i, act_i, gd_i, mi_i) = refs[:19]
    dch_out = refs[19]
    own_outs = refs[20:26]
    grads = refs[26:32]
    from_core = refs[32:38]
    from_b = refs[38:44]
    from_a = refs[44:50]
    from_z = refs[50:56]
    sums, res_sem, tile_sem, load_sem, out_sem, send_sem, recv_sem = refs[56:]
    tok, d, ff = dims
    win = WIN
    nw = tok // win + 1
    half_ff = ff // 2
    mols = tok // KER
    place = Place()
    z, y, c, x = place.z, place.y, place.c, place.x
    plan = scatter_plan([o.shape for o in own_outs])
    place.barrier()
    sends = Sends(place, send_sem, recv_sem)

    def add_blocks(dst_of, src_of):
        if not sends.live:
            return

        @pl.loop(0, 4)
        def _(zz):
            dst, src = dst_of(zz), src_of(zz)
            dst[...] = dst[...] + src[...]

    def comm_stage(stage, i):
        t, kind, cuts = plan[i]
        g, rc, rb, ra, rz, own = grads[t], from_core[t], from_b[t], from_a[t], from_z[t], own_outs[t]

        def core_blk(zs, ys, xs, cut):
            if kind == 2:
                return rc.at[zs, ys, rows_of(rc, xs), cut[1]]
            return rc.at[(zs, ys, xs) + cut] if kind == 0 else rc.at[(xs, zs, ys) + cut]

        for h, cut in enumerate(cuts):
            if cut is None:
                continue
            a, b = order(h)
            if stage == 0:
                sends.go((i, h, "c"), block(g, kind, ALL, ALL, place.nc, ALL, cut), core_blk(ALL, ALL, ALL, cut), "c")
            elif stage == 1:
                sends.got((i, h, "c"))
                for far in (1, 0):
                    for o in range(2):
                        ys, xs = (place.ny if far else y, place.at[o]) if h == 0 else (place.at[o], place.nx if far else x)
                        add_blocks(lambda zz: block(g, kind, zz, ys, c, xs, cut), lambda zz: core_blk(zz, ys, xs, cut))
                        if far:
                            sends.go((i, h, "b", o), block(g, kind, ALL, ys, c, xs, cut), rb.at[(place.at[o], ALL) + cut], b)
            elif stage == 2:
                sends.got((i, h, "b", 0))
                sends.got((i, h, "b", 1))
                near, other = (x, place.nx) if h == 0 else (y, place.ny)
                for far in (1, 0):
                    o = other if far else near
                    ys, xs = (y, o) if h == 0 else (o, x)
                    add_blocks(lambda zz: block(g, kind, zz, ys, c, xs, cut), lambda zz: rb.at[(o, zz) + cut])
                    if far:
                        sends.go((i, h, "a"), block(g, kind, ALL, ys, c, xs, cut), ra.at[(ALL,) + cut], a)
            elif stage == 3:
                sends.got((i, h, "a"))
                add_blocks(lambda zz: block(g, kind, zz, y, c, x, cut), lambda zz: ra.at[(zz,) + cut])
                for k in (1, 2, 3):
                    sends.go((i, h, "z", k), block(g, kind, place.far_z[k], y, c, x, cut), rz.at[(place.at[k - 1],) + cut], "z%d" % k)
            else:
                for k in (1, 2, 3):
                    sends.got((i, h, "z", k))
                if not sends.live:
                    continue
                total = block(g, kind, z, y, c, x, cut)[...].astype(F32)
                for k in range(3):
                    total = total + rz.at[(place.at[k],) + cut][...].astype(F32)
                if t != 1:
                    own[cut] = total
                    continue
                for q in range(0, cut[1].stop - cut[1].start, 128):
                    part, r = divmod(cut[1].start + q, d)
                    to = (r // 256) * d + part * 256 + r % 256
                    own[:, to : to + 128] = total[:, q : q + 128]

    for stage in range(5):
        for i in range(len(plan)):
            comm_stage(stage, i)
    sends.live = True
    ticks = Ticks(SCATTER_TABLE, comm_stage)
    state = {"load": 0}

    def load(src, dst):
        copy = pltpu.make_async_copy(src, dst, load_sem.at[state["load"]])
        state["load"] += 1
        copy.start()
        return copy

    def vec(v, lo, hi):
        return vecs[v : v + 1, lo:hi]

    offset = off_ref[0]
    ri = lax.broadcasted_iota(jnp.int32, (win, 2 * win), 0)
    rj = lax.broadcasted_iota(jnp.int32, (win, 2 * win), 1)
    shift_in = jnp.where(rj == ri + (win - offset), 1.0, 0.0).astype(BF)
    shift_out = jnp.where(rj == ri + offset, 1.0, 0.0).astype(BF)
    sums[...] = jnp.zeros_like(sums)
    sums[9:10, 0:d] = ln3_ref[0:1, :]
    sums[10:11, 0:d] = ln3_ref[1:2, :]
    sums[8:9, 0:d] = jnp.sum(dcp_ref[...].astype(F32), axis=0, keepdims=True)
    g_vec, g_qkv, g_wo, g_wi, g_wf, g_cv = grads
    g_cv2 = g_cv.reshape(2, KER * d, d // 2)
    g_wi2 = g_wi.reshape(2, d, half_ff)
    g_wf2 = g_wf.reshape(2, d, half_ff)

    def whole(dres):
        def conv_part(cv, mi, spread):
            loads = [load(mi_i, mi), load(cv_i, cv)]
            cv2 = cv.reshape(2, KER * d, d // 2)
            loads[0].wait()

            @pl.loop(0, KER * d // 256)
            def _(b):
                rows = pl.ds(pl.multiple_of(b * 256, 256), 256)
                val = tn(mi[:, rows], dcp_ref[...]).astype(BF)
                g_cv2[0, rows, :] = val[:, : d // 2]
                g_cv2[1, rows, :] = val[:, d // 2 :]

            ticks.point()
            loads[1].wait()
            for k in range(KER):
                for n0 in range(0, d, 256):
                    rows = slice(k * d + n0, k * d + n0 + 256)
                    val = nt(dcp_ref[:, : d // 2], cv2[0, rows, :]) + nt(dcp_ref[:, d // 2 :], cv2[1, rows, :])
                    spread[n0 // 128, pl.ds(k, mols, stride=KER), :] = val[:, :128]
                    spread[n0 // 128 + 1, pl.ds(k, mols, stride=KER), :] = val[:, 128:]
                ticks.point()
            for q in range(d // 128):
                dres[:, q * 128 : q * 128 + 128] = spread[q]

        pl.run_scoped(conv_part, pltpu.VMEM(cv_i.shape, BF), pltpu.VMEM(mi_i.shape, BF), pltpu.VMEM((d // 128, tok, 128), F32))
        ticks.point()

        def ff_part(dn2):
            def inner(act, gd, wf, wi, dff, dff_t, n2_t, dh, n2):
                n2_load = load(n2_i, n2)
                wi2, wf2 = wi_i.reshape(2, d, half_ff), wf_i.reshape(2, d, half_ff)

                def tile_copies(j):
                    slot, hx, jj = lax.rem(j, 2), lax.rem(j, 2), lax.div(j, 2)
                    cols = pl.ds(pl.multiple_of(hx * half_ff + jj * 256, 256), 256)
                    wcols = pl.ds(pl.multiple_of(jj * 256, 256), 256)
                    pairs = (
                        (act_i.at[:, cols], act),
                        (gd_i.at[:, cols], gd),
                        (wf_i.at[hx, :, :, :, :, wcols], wf),
                        (wi_i.at[hx, :, :, :, :, wcols], wi),
                    )
                    return [pltpu.make_async_copy(s, b.at[slot], tile_sem.at[slot, q]) for q, (s, b) in enumerate(pairs)]

                for copy in tile_copies(0):
                    copy.start()

                @pl.loop(0, tok // 256)
                def _(b):
                    rows = pl.ds(pl.multiple_of(b * 256, 256), 256)
                    val = dres[rows, :].astype(BF)
                    dff[rows, :] = val
                    sums[7:8, 0:d] += jnp.sum(val.astype(F32), axis=0, keepdims=True)
                    dff_t[:, rows] = val.T

                ticks.point()

                n2_load.wait()

                @pl.loop(0, tok // 256)
                def _(b):
                    rows = pl.ds(pl.multiple_of(b * 256, 256), 256)
                    n2_t[:, rows] = n2[rows, :].T

                ticks.point()

                dn2[...] = jnp.zeros_like(dn2)
                n_tiles = ff // 256
                ticks.point()
                if True:

                    @pl.loop(0, n_tiles)
                    def _(j):
                        slot, hx, jj = lax.rem(j, 2), lax.rem(j, 2), lax.div(j, 2)
                        for copy in tile_copies(j):
                            copy.wait()

                        @pl.when(j + 1 < n_tiles)
                        def _():
                            for copy in tile_copies(j + 1):
                                copy.start()

                        wcols = pl.ds(pl.multiple_of(jj * 256, 256), 256)
                        wf_j = wf.at[slot].reshape(d, 256)
                        wi_j = wi.at[slot].reshape(d, 256)
                        total = jnp.zeros((1, 256), F32)
                        for m in range(0, tok, 256):
                            val = (nn(dff[m : m + 256, :], wf_j[...]) * gd[slot, m : m + 256, :].astype(F32)).astype(BF)
                            dh[m : m + 256, :] = val
                            total = total + jnp.sum(val.astype(F32), axis=0, keepdims=True)
                        sums[6:7, pl.ds(pl.multiple_of(hx * half_ff + jj * 256, 256), 256)] = total
                        for m in range(0, d, 256):
                            g_wf2[hx, m : m + 256, wcols] = nn(dff_t[m : m + 256, :], act[slot]).astype(BF)
                            g_wi2[hx, m : m + 256, wcols] = nn(n2_t[m : m + 256, :], dh[...]).astype(BF)
                        for m in range(0, tok, 256):
                            dn2[m : m + 256, :] += nt(dh[m : m + 256, :], wi_j[...])
                        ticks.within(j, range(12))

            pl.run_scoped(
                inner,
                pltpu.VMEM((2, tok, 256), BF),
                pltpu.VMEM((2, tok, 256), BF),
                pltpu.VMEM((2, 4, 2, 2, d // 16, 256), BF),
                pltpu.VMEM((2, 4, 2, 2, d // 16, 256), BF),
                pltpu.VMEM((tok, d), BF),
                pltpu.VMEM((d, tok), BF),
                pltpu.VMEM((d, tok), BF),
                pltpu.VMEM((tok, 256), BF),
                pltpu.VMEM((tok, d), BF),
            )

            def norm_part(r1):
                load(r1_i, r1).wait()

                @pl.loop(0, tok // 128)
                def _(b):
                    rows = pl.ds(pl.multiple_of(b * 128, 128), 128)
                    vhat, r = norm_stats(r1[rows, :])
                    cot = dn2[rows, :]
                    sums[4:5, 0:d] += jnp.sum(cot * vhat, axis=0, keepdims=True)
                    sums[5:6, 0:d] += jnp.sum(cot, axis=0, keepdims=True)
                    dres[rows, :] = dres[rows, :] + norm_grad(vhat, r, cot * vec(4, 0, d))
                    ticks.within(b, range(8))

            pl.run_scoped(norm_part, pltpu.VMEM((tok, d), F32))

        pl.run_scoped(ff_part, pltpu.VMEM((tok, d), F32))

        def attn_part(proj, wqkv, ns_t, dpad):
            proj_load, qkv_load = load(proj_i, proj), load(qkv_i, wqkv)

            def turn_part(ns):
                load(ns_i, ns).wait()

                @pl.loop(0, nw // 3)
                def _(b):
                    rows = pl.ds(pl.multiple_of(b * 384, 128), 384)
                    ns_t[:, rows] = ns[rows, :].T

            pl.run_scoped(turn_part, pltpu.VMEM(ns_i.shape, BF))

            def out_part(heads, wo, dattn):
                loads = [load(heads_i, heads), load(wo_i, wo)]
                wo2 = wo.reshape(d, d)
                g_wo2 = g_wo.reshape(d, d)

                @pl.loop(0, tok // 256)
                def _(b):
                    rows = pl.ds(pl.multiple_of(b * 256, 256), 256)
                    val = dres[rows, :].astype(BF)
                    dattn[rows, :] = val
                    sums[3:4, 0:d] += jnp.sum(val.astype(F32), axis=0, keepdims=True)

                for copy in loads:
                    copy.wait()

                @pl.loop(0, d // 256)
                def _(b):
                    rows = pl.ds(pl.multiple_of(b * 256, 256), 256)
                    g_wo2[rows, :] = tn(heads[:, rows], dattn[...]).astype(BF)

                ticks.point()
                dpad[0:win, :] = jnp.zeros((win, d), BF)
                dpad[win + tok : 2 * win + tok, :] = jnp.zeros((win, d), BF)

                @pl.loop(0, tok // 256)
                def _(b):
                    at = pl.multiple_of(b * 256, 256)
                    dpad[pl.ds(at + win, 256), :] = nt(dattn[pl.ds(at, 256), :], wo2[...]).astype(BF)
                    ticks.within(b, (0, 1, 2))

            pl.run_scoped(out_part, pltpu.VMEM((tok, d), BF), pltpu.VMEM(wo_i.shape, BF), pltpu.VMEM((tok, d), BF))

            qmask = head_masks(win, HDIM**-0.5)
            vmask = head_masks(win, 1.0)

            g_qkv2 = g_qkv.reshape(d, 3 * d)
            wqkv2 = wqkv.reshape(d, 3 * d)

            def core_part(prob):
                def prob_copy(i):
                    g, w, slot = lax.div(i, nw), lax.rem(i, nw), lax.rem(i, 2)
                    return pltpu.make_async_copy(prob_i.at[w, pl.ds(2 * g, 2)], prob.at[slot], res_sem.at[slot])

                prob_copy(0).start()
                proj_load.wait()
                base = ticks.count

                @pl.loop(0, d // 256)
                def _(g):
                    @pl.loop(0, nw)
                    def _(w):
                        i = g * nw + w
                        prob_copy(i).wait()

                        @pl.when(i + 1 < nw * (d // 256))
                        def _():
                            prob_copy(i + 1).start()

                        at = pl.multiple_of(w * win, win)
                        rows = pl.ds(at, win)
                        lq, lk, lv = [pl.ds(pl.multiple_of(r * d + g * 256, 256), 256) for r in range(3)]
                        dhw = nn(shift_in, dpad[pl.ds(at, 2 * win), lq]).astype(BF)
                        q4, k4, v4 = proj[rows, lq], proj[rows, lk], proj[rows, lv]
                        new = [[], [], []]
                        for pr in range(2):
                            lanes = slice(pr * 128, pr * 128 + 128)
                            q2, k2, v2 = q4[:, lanes], k4[:, lanes], v4[:, lanes]
                            pb = prob[lax.rem(i, 2), pr]
                            dbd = split_heads(dhw[:, lanes], vmask)
                            dp = nt(v2, dbd)
                            pf = pb.astype(F32)
                            ds = (pf * (dp - jnp.sum(pf * dp, axis=0, keepdims=True))).astype(BF)
                            stacked = jnp.concatenate([ds[:, :win], ds[:, win:]], axis=0)
                            new[0].append(tn(stacked, split_heads(k2, qmask)).astype(BF))
                            new[1].append(nn(ds, split_heads(q2, qmask)).astype(BF))
                            new[2].append(nn(pb, dbd).astype(BF))
                        for lanes, parts in zip((lq, lk, lv), new):
                            proj[rows, lanes] = jnp.concatenate(parts, axis=1)
                        for q in range(3):
                            for ww in range(nw):
                                if ticks.table[base + q * (nw + 1) + ww]:
                                    pl.when(i == q * nw + ww)(functools.partial(ticks.run, base + q * (nw + 1) + ww))

                    for r in range(3):
                        cols = pl.ds(pl.multiple_of(r * d + g * 256, 256), 256)
                        to = pl.ds(pl.multiple_of(g * d + r * 256, 256), 256)
                        part = proj[:, cols]
                        if r != 1:
                            into = pl.ds(pl.multiple_of((r // 2) * d + g * 256, 256), 256)
                            sums[2:3, into] = jnp.sum(part.astype(F32), axis=0, keepdims=True)
                        for m in range(0, d, 256):
                            g_qkv2[m : m + 256, to] = nn(ns_t[m : m + 256, :], part).astype(BF)
                    for q in range(3):
                        pl.when(g == q)(functools.partial(ticks.run, base + q * (nw + 1) + nw))
                ticks.count = base + 3 * (nw + 1)

            pl.run_scoped(core_part, pltpu.VMEM((2, 2, win, 2 * win), BF))

            def last_part(hi, lo):
                qkv_load.wait()

                @pl.loop(0, nw // 3)
                def _(b):
                    rows = pl.ds(pl.multiple_of(b * 384, 128), 384)
                    for n0 in range(0, d, 256):
                        val = nt(proj[rows, :], wqkv2[n0 : n0 + 256, :])
                        top = val.astype(BF)
                        hi[rows, n0 : n0 + 256] = top
                        lo[rows, n0 : n0 + 256] = (val - top.astype(F32)).astype(BF)
                    ticks.within(b, range(3))

                @pl.loop(0, tok // 128)
                def _(b):
                    at = pl.multiple_of(b * 128, 128)
                    rows = pl.ds(at, 128)
                    both = pl.ds(at, 2 * win)
                    cot = nn(shift_out, hi[both, :]) + nn(shift_out, lo[both, :])
                    vhat, r = norm_stats(x_ref[rows, :].astype(F32))
                    sums[0:1, 0:d] += jnp.sum(cot * vhat, axis=0, keepdims=True)
                    sums[1:2, 0:d] += jnp.sum(cot, axis=0, keepdims=True)
                    dres[rows, :] = dres[rows, :] + norm_grad(vhat, r, cot * vec(0, 0, d))
                    ticks.within(b, range(8))

            pl.run_scoped(last_part, pltpu.VMEM((nw * win, d), BF), pltpu.VMEM((nw * win, d), BF))

        pl.run_scoped(
            attn_part,
            pltpu.VMEM(proj_i.shape, BF),
            pltpu.VMEM(qkv_i.shape, BF),
            pltpu.VMEM((d, nw * win), BF),
            pltpu.VMEM((tok + 2 * win, d), BF),
        )
        done = pltpu.make_async_copy(dres, dch_out, out_sem.at[0])
        done.start()

        g_vec2 = g_vec.reshape(-1, SLOT)
        nrow = g_vec2.shape[0] // 16
        g_vec[...] = jnp.zeros_like(g_vec)
        for v, (width, count) in enumerate(sizes):
            col = lax.broadcasted_iota(jnp.int32, (SLOT, width), 1).astype(F32)
            row = lax.broadcasted_iota(jnp.int32, (SLOT, width), 0).astype(F32)
            owner = jnp.floor((col + 0.5) * (1.0 / count))
            pick = jnp.where(col - owner * count == row, 1.0, 0.0).astype(BF)
            col2 = lax.broadcasted_iota(jnp.int32, (nrow, width), 1).astype(F32)
            row2 = lax.broadcasted_iota(jnp.int32, (nrow, width), 0).astype(F32)
            mine = jnp.where(row2 == jnp.floor((col2 + 0.5) * (1.0 / count)), sums[v : v + 1, :width], 0.0)
            top = mine.astype(BF)
            rest = (mine - top.astype(F32)).astype(BF)
            g_vec2[pl.ds(v, nrow, stride=16), :] = nt(top, pick) + nt(rest, pick)
        ticks.point()
        sends.sent()
        done.wait()

    pl.run_scoped(whole, pltpu.VMEM((tok, d), F32))


def quick_mesh(mesh):
    return mesh.shape["dp"] == 16 and mesh.shape["mp"] == 2


def gathered_shape(shape, kind):
    if kind == 2:
        return (4, 2, 2, 2 * shape[0], shape[1])
    return ((4, 2, 2, 2) if kind == 0 else (2, 4, 2, 2)) + shape


def place_kernel(widths, *refs):
    n = (len(refs) - 3 - len(widths)) // 3
    sources, vec_ref, outs, vec_outs = refs[:n], refs[n], refs[n + 1 : 2 * n + 1], refs[2 * n + 1 : 2 * n + 1 + len(widths)]
    held, in_sem, out_sem = refs[-n - 2 : -2], refs[-2], refs[-1]
    loads = [pltpu.make_async_copy(s, h, in_sem.at[i]) for i, (s, h) in enumerate(zip(sources, held))]
    stores = [pltpu.make_async_copy(h, o, out_sem.at[i]) for i, (h, o) in enumerate(zip(held, outs))]
    for copy in loads:
        copy.start()
    for v, (width, out) in enumerate(zip(widths, vec_outs)):
        out[...] = vec_ref[v, :width]
    for load, store in zip(loads, stores):
        load.wait()
        store.start()
    for copy in stores:
        copy.wait()


def fast_shards(*args):
    (chars, seg, offs, l1g, l1b, wqkv, qvb, wo, aob, l2g, l2b, wi, fib, wf, fob, cv, cvb, l3g, l3b, dmol) = args
    tok, d = chars.shape
    mols = dmol.shape[0]
    vectors = (l1g, l1b, qvb, aob, l2g, l2b, fib, fob, cvb, l3g, l3b)
    sizes = tuple((v.shape[0] * 32, v.shape[0]) for v in vectors)
    ff = sizes[6][0]
    dims = (tok, d, ff)
    nw = tok // WIN + 1
    vec_own = sum(jnp.pad(v[None], ((i, 15 - i), (0, SLOT - v.shape[0]))) for i, v in enumerate(vectors))
    owns = (vec_own, wqkv, wo, wi, wf.T, cv)
    kinds = (0, 2, 2, 1, 1, 1)
    full = [gathered_shape(o.shape, k) for o, k in zip(owns, kinds)]
    plan = gather_plan([o.shape for o in owns])
    n_send = sum(9 * sum(cut is not None for cut in cuts) for _, _, cuts in plan)
    on_chip = pl.BlockSpec(memory_space=pltpu.VMEM)
    scalar = pl.BlockSpec(memory_space=pltpu.SMEM)
    any_mem = pl.BlockSpec(memory_space=pl.ANY)
    bf = lambda *s: jax.ShapeDtypeStruct(s, BF)
    f32 = lambda *s: jax.ShapeDtypeStruct(s, F32)
    prob_shape = (nw, HEADS // 2, WIN, 2 * WIN)
    saved = pl.pallas_call(
        functools.partial(forward_kernel, dims, sizes, n_send),
        out_shape=[
            f32(mols, d),
            f32(16, ff),
            f32(8, d),
            bf(mols, d),
            *[bf(*s) for s in full[1:]],
            bf(nw * WIN, d),
            bf(nw * WIN, 3 * d),
            bf(*prob_shape),
            bf(tok, d),
            f32(tok, d),
            bf(tok, d),
            bf(tok, ff),
            bf(tok, ff),
            bf(mols, KER * d),
        ],
        in_specs=[scalar] + [on_chip] * 9,
        out_specs=[on_chip, any_mem, on_chip, on_chip] + [any_mem] * 14,
        scratch_shapes=[
            *[pltpu.VMEM(s, BF) for s in full],
            pltpu.VMEM((512, SLOT), F32),
            pltpu.VMEM((16, ff), F32),
            pltpu.VMEM((tok + 2 * WIN, d), BF),
            pltpu.VMEM((nw * WIN, d), BF),
            pltpu.VMEM((nw * WIN, 3 * d), BF),
            pltpu.VMEM(prob_shape, BF),
            pltpu.VMEM((tok, d), BF),
            pltpu.VMEM((tok, d), F32),
            pltpu.VMEM((tok, d), BF),
            pltpu.VMEM((tok, ff), BF),
            pltpu.VMEM((tok, ff), BF),
            pltpu.VMEM((d // 128, tok, 128), F32),
            pltpu.VMEM((mols, KER * d), BF),
            pltpu.SemaphoreType.DMA((6,)),
            pltpu.SemaphoreType.DMA((16,)),
            pltpu.SemaphoreType.DMA((n_send,)),
            pltpu.SemaphoreType.DMA((n_send,)),
        ],
        compiler_params=pltpu.CompilerParams(collective_id=1, has_side_effects=True, vmem_limit_bytes=VMEM_CAP),
        name="gather_forward",
    )(offs, seg, chars, dmol, *owns)
    (mol, vecs, ln3, dcp, qkv_f, wo_f, wi_f, wf_f, cv_f, ns, proj, prob, heads, r1, n2, act, gd, mi) = saved

    own_shapes = [o.shape for o in owns]
    kind_core = lambda s, k: (4, 2, 2 * s[0], s[1]) if k == 2 else ((4, 2, 2) if k == 0 else (2, 4, 2)) + s
    types = [F32] + [BF] * 5
    plan = scatter_plan(own_shapes)
    n_back = sum(7 * sum(cut is not None for cut in piece[2]) for piece in plan if piece is not None)
    back = pl.pallas_call(
        functools.partial(backward_kernel, dims, sizes, n_back),
        out_shape=[f32(tok, d)] + [f32(*s) for s in own_shapes],
        in_specs=[scalar] + [on_chip] * 4 + [any_mem] * 14,
        out_specs=[any_mem] + [on_chip] * 6,
        scratch_shapes=[
            *[pltpu.VMEM(s, t) for s, t in zip(full, types)],
            *[pltpu.VMEM(kind_core(s, k), t) for s, k, t in zip(own_shapes, kinds, types)],
            *[pltpu.VMEM((2, 4) + s, t) for s, t in zip(own_shapes, types)],
            *[pltpu.VMEM((4,) + s, t) for s, t in zip(own_shapes, types)],
            *[pltpu.VMEM((3,) + s, t) for s, t in zip(own_shapes, types)],
            pltpu.VMEM((16, ff), F32),
            pltpu.SemaphoreType.DMA((2,)),
            pltpu.SemaphoreType.DMA((2, 4)),
            pltpu.SemaphoreType.DMA((16,)),
            pltpu.SemaphoreType.DMA((1,)),
            pltpu.SemaphoreType.DMA((n_back,)),
            pltpu.SemaphoreType.DMA((n_back,)),
        ],
        compiler_params=pltpu.CompilerParams(collective_id=2, has_side_effects=True, vmem_limit_bytes=VMEM_CAP),
        name="backward_scatter",
    )(offs, chars, dcp, vecs, ln3, qkv_f, wo_f, wi_f, wf_f, cv_f, ns, proj, prob, heads, r1, n2, act, gd, mi)
    d_chars, d_vec, d_qkv, d_wo, d_wi, d_wf, d_cv = back
    large = (d_wo, d_qkv, d_wi, d_wf, d_cv, mol, d_chars)
    done = pl.pallas_call(
        functools.partial(place_kernel, tuple(v.shape[0] for v in vectors)),
        out_shape=[f32(*a.shape) for a in large] + [f32(v.shape[0]) for v in vectors],
        in_specs=[any_mem] * len(large) + [on_chip],
        out_specs=[any_mem] * len(large) + [on_chip] * len(vectors),
        scratch_shapes=[
            *[pltpu.VMEM(a.shape, F32) for a in large],
            pltpu.SemaphoreType.DMA((len(large),)),
            pltpu.SemaphoreType.DMA((len(large),)),
        ],
        compiler_params=pltpu.CompilerParams(vmem_limit_bytes=VMEM_CAP),
        name="place",
    )(*large, d_vec)
    d_wo, d_qkv, d_wi, d_wf, d_cv, mol, d_chars = done[: len(large)]
    dv = done[len(large) :]
    return (
        mol,
        d_chars,
        dv[0],
        dv[1],
        d_qkv,
        dv[2],
        d_wo,
        dv[3],
        dv[4],
        dv[5],
        d_wi,
        dv[6],
        d_wf.T,
        dv[7],
        d_cv,
        dv[8],
        dv[9],
        dv[10],
    )


def solution(mesh):
    placed = (
        P(("dp", "mp"), None),
        P(("dp", "mp"), None),
        P(("dp", "mp")),
        P(("dp", "mp")),
        P(("dp", "mp")),
        P(("dp", "mp"), None),
        P(("dp", "mp")),
        P(("dp", "mp"), None),
        P(("dp", "mp")),
        P(("dp", "mp")),
        P(("dp", "mp")),
        P("dp", "mp"),
        P(("dp", "mp")),
        P("mp", "dp"),
        P(("dp", "mp")),
        P("dp", "mp"),
        P(("dp", "mp")),
        P(("dp", "mp")),
        P(("dp", "mp")),
        P(("dp", "mp"), None),
    )
    return jax.shard_map(
        fast_shards if quick_mesh(mesh) else shards,
        mesh=mesh,
        in_specs=placed,
        out_specs=(
            P(("dp", "mp"), None),
            P(("dp", "mp"), None),
            P(("dp", "mp")),
            P(("dp", "mp")),
            P(("dp", "mp"), None),
            P(("dp", "mp")),
            P(("dp", "mp"), None),
            P(("dp", "mp")),
            P(("dp", "mp")),
            P(("dp", "mp")),
            P("dp", "mp"),
            P(("dp", "mp")),
            P("mp", "dp"),
            P(("dp", "mp")),
            P("dp", "mp"),
            P(("dp", "mp")),
            P(("dp", "mp")),
            P(("dp", "mp")),
        ),
        check_vma=False,
    )
```

```python
import functools

import jax
import jax.numpy as jnp
from jax import lax
from jax.experimental import pallas as pl
from jax.experimental.pallas import tpu as pltpu
from jax.sharding import PartitionSpec as P

HEADS = 12
HDIM = 64
KER = 4
WIN = 128


layer_eps = 1e-06


def layer_norm(row_values, gain_vec, shift_vec):
    centred = row_values - jnp.mean(row_values, axis=-1, keepdims=True)
    spread = jnp.mean(centred * centred, axis=-1, keepdims=True)
    return centred * lax.rsqrt(spread + layer_eps) * gain_vec + shift_vec


def gelu_exact(values):
    return jax.nn.gelu(values, approximate=False)


def norm_backward(row_values, gain_vec, shift_vec, grad_out):
    _, pullback = jax.vjp(layer_norm, row_values, gain_vec, shift_vec)
    return pullback(grad_out)


def gelu_backward(values, grad_out):
    _, pullback = jax.vjp(gelu_exact, values)
    return pullback(grad_out)[0]


def three_blocks(rows, fill_value):
    edge = jnp.full_like(rows[:1], fill_value)
    before = jnp.concatenate([edge, rows[:-1]], axis=0)
    after = jnp.concatenate([rows[1:], edge], axis=0)
    return jnp.concatenate([before, rows, after], axis=1)


def fold_blocks(band_grad):
    edge = jnp.zeros_like(band_grad[:1, :WIN])
    from_next = jnp.concatenate([band_grad[1:, :WIN], edge], axis=0)
    from_prev = jnp.concatenate([edge, band_grad[:-1, 2 * WIN :]], axis=0)
    return band_grad[:, WIN : 2 * WIN] + from_next + from_prev


def band_inputs(queries, key_rows, value_rows, seg_row, offset):
    seq_len = queries.shape[0]
    block_count = seq_len // WIN
    win_row = (jnp.arange(seq_len, dtype=jnp.int32) + offset) // WIN
    seg_blk = seg_row.reshape(block_count, WIN)
    win_blk = win_row.reshape(block_count, WIN)
    return (
        queries.reshape(block_count, WIN, HEADS, HDIM),
        three_blocks(key_rows.reshape(block_count, WIN, HEADS, HDIM), 0),
        three_blocks(value_rows.reshape(block_count, WIN, HEADS, HDIM), 0),
        seg_blk,
        win_blk,
        three_blocks(seg_blk, 0),
        three_blocks(win_blk, -1),
    )


def band_scores(query_blk, key_band, seg_blk, win_blk, seg_band, win_band):
    raw_scores = jnp.einsum(
        "bqhd,bkhd->bhqk", query_blk, key_band, preferred_element_type=jnp.float32
    ) * HDIM ** (-0.5)
    allowed = (seg_blk[:, :, None] == seg_band[:, None, :]) & (
        win_blk[:, :, None] == win_band[:, None, :]
    )
    return jnp.where(allowed[:, None], raw_scores, -1e30)


def attend_forward(seq_item):
    queries, key_rows, value_rows, seg_row, offset = seq_item
    seq_len = queries.shape[0]
    query_blk, key_band, val_band, seg_blk, win_blk, seg_band, win_band = band_inputs(
        queries, key_rows, value_rows, seg_row, offset
    )
    scores = band_scores(query_blk, key_band, seg_blk, win_blk, seg_band, win_band)
    row_peak = jnp.max(scores, axis=-1, keepdims=True)
    exp_scores = jnp.exp(scores - row_peak)
    row_total = jnp.sum(exp_scores, axis=-1, keepdims=True)
    prob_low = (exp_scores / row_total).astype(jnp.bfloat16)
    merged = jnp.einsum("bhqk,bkhd->bqhd", prob_low, val_band, preferred_element_type=jnp.float32)
    return (merged.reshape(seq_len, HEADS * HDIM), (row_peak + jnp.log(row_total))[..., 0])


def attend_backward(seq_item):
    queries, key_rows, value_rows, seg_row, offset, log_norm, d_heads = seq_item
    seq_len = queries.shape[0]
    block_count = seq_len // WIN
    score_scale = HDIM ** (-0.5)
    query_blk, key_band, val_band, seg_blk, win_blk, seg_band, win_band = band_inputs(
        queries, key_rows, value_rows, seg_row, offset
    )
    grad_blk = d_heads.reshape(block_count, WIN, HEADS, HDIM)
    scores = band_scores(query_blk, key_band, seg_blk, win_blk, seg_band, win_band)
    prob_blk = jnp.exp(scores - log_norm[..., None])
    d_probs = jnp.einsum("bqhd,bkhd->bhqk", grad_blk, val_band, preferred_element_type=jnp.float32)
    row_dot = jnp.sum(prob_blk * d_probs, axis=-1, keepdims=True)
    d_scores = (prob_blk * (d_probs - row_dot)).astype(jnp.bfloat16)
    d_query = (
        jnp.einsum("bhqk,bkhd->bqhd", d_scores, key_band, preferred_element_type=jnp.float32)
        * score_scale
    )
    d_key_band = (
        jnp.einsum("bhqk,bqhd->bkhd", d_scores, query_blk, preferred_element_type=jnp.float32)
        * score_scale
    )
    d_val_band = jnp.einsum(
        "bhqk,bqhd->bkhd",
        prob_blk.astype(jnp.bfloat16),
        grad_blk,
        preferred_element_type=jnp.float32,
    )
    d_keys = fold_blocks(d_key_band)
    d_vals = fold_blocks(d_val_band)
    return (
        d_query.reshape(seq_len, HEADS * HDIM),
        d_keys.reshape(seq_len, HEADS * HDIM),
        d_vals.reshape(seq_len, HEADS * HDIM),
    )


def shards(
    chars,
    segment_ids,
    window_offsets,
    ln1_gain,
    ln1_bias,
    w_qkv,
    qv_bias,
    w_attn_out,
    attn_out_bias,
    ln2_gain,
    ln2_bias,
    w_ff_in,
    ff_in_bias,
    w_ff_out,
    ff_out_bias,
    conv_weight,
    conv_bias,
    ln3_gain,
    ln3_bias,
    d_molecules,
):
    gathered = (
        lax.all_gather(w_qkv, ("dp", "mp"), axis=0, tiled=True),
        lax.all_gather(w_attn_out, ("dp", "mp"), axis=0, tiled=True),
        lax.all_gather(ln1_gain, ("dp", "mp"), axis=0, tiled=True),
        lax.all_gather(ln1_bias, ("dp", "mp"), axis=0, tiled=True),
        lax.all_gather(qv_bias, ("dp", "mp"), axis=0, tiled=True),
        lax.all_gather(attn_out_bias, ("dp", "mp"), axis=0, tiled=True),
        lax.all_gather(ln2_gain, ("dp", "mp"), axis=0, tiled=True),
        lax.all_gather(ln2_bias, ("dp", "mp"), axis=0, tiled=True),
        lax.all_gather(ff_in_bias, ("dp", "mp"), axis=0, tiled=True),
        lax.all_gather(ff_out_bias, ("dp", "mp"), axis=0, tiled=True),
        lax.all_gather(conv_bias, ("dp", "mp"), axis=0, tiled=True),
        lax.all_gather(ln3_gain, ("dp", "mp"), axis=0, tiled=True),
        lax.all_gather(ln3_bias, ("dp", "mp"), axis=0, tiled=True),
    )
    qkv_full = gathered[0]
    attn_out_full = gathered[1]
    vectors = [vector_arg.astype(jnp.float32) for vector_arg in gathered[2:]]
    (
        gain_one,
        shift_one,
        qv_shift,
        attn_shift,
        gain_two,
        shift_two,
        hidden_shift,
        ff_shift,
        conv_shift,
        gain_three,
        shift_three,
    ) = vectors
    ff_in_part, ff_out_part, conv_part = (
        lax.all_gather(w_ff_in, "dp", axis=0, tiled=True),
        lax.all_gather(w_ff_out, "dp", axis=1, tiled=True),
        lax.all_gather(conv_weight, "dp", axis=0, tiled=True),
    )
    model_width = chars.shape[1]
    tok_rows = chars.shape[0]
    seq_count = segment_ids.shape[0]
    seq_len = segment_ids.shape[1]
    mp_rank = lax.axis_index("mp")
    hidden_part = ff_in_part.shape[1]
    channel_part = conv_part.shape[1]
    inputs = chars.astype(jnp.float32)
    normed_one = layer_norm(inputs, gain_one, shift_one).astype(jnp.bfloat16)
    qkv_shift = jnp.concatenate(
        [qv_shift[:model_width], jnp.zeros((model_width,), jnp.float32), qv_shift[model_width:]]
    )
    projected = (
        jnp.dot(normed_one, qkv_full, preferred_element_type=jnp.float32) + qkv_shift
    ).astype(jnp.bfloat16)
    per_seq = projected.reshape(seq_count, seq_len, 3, HEADS, HDIM)
    queries = per_seq[:, :, 0]
    key_rows = per_seq[:, :, 1]
    value_rows = per_seq[:, :, 2]
    merged, log_norm = lax.map(
        attend_forward, (queries, key_rows, value_rows, segment_ids, window_offsets)
    )
    heads_low = merged.reshape(tok_rows, model_width).astype(jnp.bfloat16)
    resid_one = (
        inputs + jnp.dot(heads_low, attn_out_full, preferred_element_type=jnp.float32) + attn_shift
    )
    normed_two = layer_norm(resid_one, gain_two, shift_two).astype(jnp.bfloat16)
    ff_in_use, ff_out_use, conv_use = (ff_in_part, ff_out_part, conv_part)
    ff_rows_in = lax.all_gather(normed_two, "mp", axis=0, tiled=True)
    hidden_bias = lax.dynamic_slice_in_dim(hidden_shift, mp_rank * hidden_part, hidden_part)
    hidden_pre = jnp.dot(ff_rows_in, ff_in_use, preferred_element_type=jnp.float32) + hidden_bias
    hidden_act = gelu_exact(hidden_pre).astype(jnp.bfloat16)
    ff_sum = lax.psum_scatter(
        jnp.dot(hidden_act, ff_out_use, preferred_element_type=jnp.float32).astype(jnp.bfloat16),
        "mp",
        scatter_dimension=0,
        tiled=True,
    ).astype(jnp.float32)
    resid_two = resid_one + ff_sum + ff_shift
    mol_rows = resid_two.astype(jnp.bfloat16).reshape(tok_rows // KER, KER * model_width)
    mol_group = lax.all_gather(mol_rows, "mp", axis=0, tiled=True)
    channel_bias = lax.dynamic_slice_in_dim(conv_shift, mp_rank * channel_part, channel_part)
    conv_pre = jnp.dot(mol_group, conv_use, preferred_element_type=jnp.float32) + channel_bias
    channel_act = gelu_exact(conv_pre).astype(jnp.bfloat16)
    conv_act = lax.all_to_all(channel_act, "mp", split_axis=0, concat_axis=1, tiled=True)
    act_float = conv_act.astype(jnp.float32)
    molecules = layer_norm(act_float, gain_three, shift_three)
    d_act, d_gain_three, d_shift_three = norm_backward(
        act_float, gain_three, shift_three, d_molecules.astype(jnp.float32)
    )
    d_act_low = d_act.astype(jnp.bfloat16)
    d_act_cols = lax.all_to_all(d_act_low, "mp", split_axis=1, concat_axis=0, tiled=True)
    d_conv_pre = gelu_backward(conv_pre, d_act_cols.astype(jnp.float32)).astype(jnp.bfloat16)
    d_conv_w = jnp.einsum("mk,mc->kc", mol_group, d_conv_pre, preferred_element_type=jnp.float32)
    d_conv_shift = lax.dynamic_update_slice_in_dim(
        jnp.zeros((model_width,), jnp.float32),
        jnp.sum(d_conv_pre.astype(jnp.float32), axis=0),
        mp_rank * channel_part,
        0,
    )
    d_mol = lax.psum_scatter(
        jnp.einsum("mc,kc->mk", d_conv_pre, conv_use, preferred_element_type=jnp.float32).astype(
            jnp.bfloat16
        ),
        "mp",
        scatter_dimension=0,
        tiled=True,
    ).astype(jnp.float32)
    d_resid_two = d_mol.reshape(tok_rows, model_width)
    d_ff_low = d_resid_two.astype(jnp.bfloat16)
    d_ff_shift = jnp.sum(d_ff_low.astype(jnp.float32), axis=0)
    d_ff_rows = lax.all_gather(d_ff_low, "mp", axis=0, tiled=True)
    d_hidden_act = jnp.einsum(
        "gc,fc->gf", d_ff_rows, ff_out_use, preferred_element_type=jnp.float32
    )
    d_ff_out_w = jnp.einsum("gf,gc->fc", hidden_act, d_ff_rows, preferred_element_type=jnp.float32)
    d_hidden = gelu_backward(hidden_pre, d_hidden_act).astype(jnp.bfloat16)
    d_hidden_sum = jnp.sum(d_hidden.astype(jnp.float32), axis=0)
    d_ff_in_w = jnp.einsum("gd,gf->df", ff_rows_in, d_hidden, preferred_element_type=jnp.float32)
    d_hidden_shift = lax.dynamic_update_slice_in_dim(
        jnp.zeros((hidden_shift.shape[0],), jnp.float32), d_hidden_sum, mp_rank * hidden_part, 0
    )
    d_normed_two = lax.psum_scatter(
        jnp.einsum("gf,df->gd", d_hidden, ff_in_use, preferred_element_type=jnp.float32).astype(
            jnp.bfloat16
        ),
        "mp",
        scatter_dimension=0,
        tiled=True,
    ).astype(jnp.float32)
    d_resid_from, d_gain_two, d_shift_two = norm_backward(
        resid_one, gain_two, shift_two, d_normed_two
    )
    d_resid_one = d_resid_two + d_resid_from
    d_attn_low = d_resid_one.astype(jnp.bfloat16)
    d_attn_shift = jnp.sum(d_attn_low.astype(jnp.float32), axis=0)
    d_attn_out_w = jnp.einsum(
        "te,tc->ec", heads_low, d_attn_low, preferred_element_type=jnp.float32
    )
    d_heads_low = jnp.einsum(
        "tc,ec->te", d_attn_low, attn_out_full, preferred_element_type=jnp.float32
    ).astype(jnp.bfloat16)
    d_heads_seq = d_heads_low.reshape(seq_count, seq_len, HEADS, HDIM)
    d_queries, d_keys, d_vals = lax.map(
        attend_backward,
        (queries, key_rows, value_rows, segment_ids, window_offsets, log_norm, d_heads_seq),
    )
    d_projected = jnp.concatenate(
        [
            d_queries.reshape(tok_rows, model_width),
            d_keys.reshape(tok_rows, model_width),
            d_vals.reshape(tok_rows, model_width),
        ],
        axis=1,
    ).astype(jnp.bfloat16)
    d_proj_sum = jnp.sum(d_projected.astype(jnp.float32), axis=0)
    d_qv_shift = jnp.concatenate([d_proj_sum[:model_width], d_proj_sum[2 * model_width :]])
    d_qkv_w = jnp.einsum("td,te->de", normed_one, d_projected, preferred_element_type=jnp.float32)
    d_normed_one = jnp.einsum(
        "te,de->td", d_projected, qkv_full, preferred_element_type=jnp.float32
    )
    d_inputs_from, d_gain_one, d_shift_one = norm_backward(
        inputs, gain_one, shift_one, d_normed_one
    )
    d_chars = d_resid_one + d_inputs_from
    d_ff_in_own, d_ff_out_own, d_conv_own = (
        lax.psum_scatter(
            d_ff_in_w.astype(jnp.bfloat16), "dp", scatter_dimension=0, tiled=True
        ).astype(jnp.float32),
        lax.psum_scatter(
            d_ff_out_w.astype(jnp.bfloat16), "dp", scatter_dimension=1, tiled=True
        ).astype(jnp.float32),
        lax.psum_scatter(
            d_conv_w.astype(jnp.bfloat16), "dp", scatter_dimension=0, tiled=True
        ).astype(jnp.float32),
    )
    owned = (
        lax.psum_scatter(d_qkv_w, ("dp", "mp"), scatter_dimension=0, tiled=True),
        lax.psum_scatter(d_attn_out_w, ("dp", "mp"), scatter_dimension=0, tiled=True),
        lax.psum_scatter(d_gain_one, ("dp", "mp"), scatter_dimension=0, tiled=True),
        lax.psum_scatter(d_shift_one, ("dp", "mp"), scatter_dimension=0, tiled=True),
        lax.psum_scatter(d_qv_shift, ("dp", "mp"), scatter_dimension=0, tiled=True),
        lax.psum_scatter(d_attn_shift, ("dp", "mp"), scatter_dimension=0, tiled=True),
        lax.psum_scatter(d_gain_two, ("dp", "mp"), scatter_dimension=0, tiled=True),
        lax.psum_scatter(d_shift_two, ("dp", "mp"), scatter_dimension=0, tiled=True),
        lax.psum_scatter(d_hidden_shift, ("dp", "mp"), scatter_dimension=0, tiled=True),
        lax.psum_scatter(d_ff_shift, ("dp", "mp"), scatter_dimension=0, tiled=True),
        lax.psum_scatter(d_conv_shift, ("dp", "mp"), scatter_dimension=0, tiled=True),
        lax.psum_scatter(d_gain_three, ("dp", "mp"), scatter_dimension=0, tiled=True),
        lax.psum_scatter(d_shift_three, ("dp", "mp"), scatter_dimension=0, tiled=True),
    )
    return (
        molecules,
        d_chars,
        owned[2],
        owned[3],
        owned[0],
        owned[4],
        owned[1],
        owned[5],
        owned[6],
        owned[7],
        d_ff_in_own,
        owned[8],
        d_ff_out_own,
        owned[9],
        d_conv_own,
        owned[10],
        owned[11],
        owned[12],
    )


NEAR_FIRST = (False, True, False, False, False, False, True, True, False, False, False, False, False, False, True, False, False, False, True, True, True, False)
GATHER_TABLE = (
    ((0, 0), (0, 1), (1, 0), (0, 2), (2, 0), (0, 3), (3, 0), (1, 1), (1, 2), (4, 0), (2, 2),),
    ((1, 3), (0, 4),),
    (),
    ((2, 1),),
    ((3, 2), (0, 5),),
    (),
    ((0, 6),),
    ((2, 3), (1, 4), (1, 5), (0, 7), (3, 1), (4, 2), (0, 8), (4, 1), (1, 6), (5, 2), (0, 9), (3, 3), (4, 3), (0, 10),),
    ((2, 4), (0, 11),),
    ((2, 5), (1, 7), (2, 7), (1, 8), (2, 8), (1, 9),),
    ((2, 6), (1, 10),),
    ((3, 4), (1, 11), (0, 12),),
    ((3, 5), (3, 7),),
    ((4, 4), (0, 13),),
    (),
    ((4, 5), (3, 8), (2, 9), (0, 14),),
    ((3, 6), (1, 12),),
    ((0, 15),),
    ((4, 6), (2, 10), (1, 13),),
    ((0, 16),),
    ((2, 11), (1, 14), (0, 17),),
    ((4, 7), (4, 8), (0, 18),),
    ((3, 9), (1, 16),),
    ((5, 7), (5, 8), (2, 12), (1, 15), (2, 15), (1, 17),),
    ((4, 9), (3, 10), (0, 19),),
    ((3, 11), (2, 13), (1, 18), (0, 20),),
    ((4, 10), (2, 14), (3, 15), (0, 21),),
    ((4, 11), (0, 22),),
    ((3, 12), (2, 16),),
    (),
    ((4, 12), (2, 17), (1, 19), (2, 19),),
    ((3, 13), (1, 22),),
    ((2, 18), (1, 20), (2, 20),),
    ((4, 13), (3, 14), (3, 19),),
    ((4, 15), (3, 16), (1, 21), (2, 21),),
    ((4, 14), (3, 17), (3, 20),),
    ((5, 15), (4, 16),),
    ((4, 17), (3, 21), (2, 22),),
    ((3, 18),),
    ((4, 19),),
    ((4, 18), (4, 20),),
    ((5, 19), (4, 21), (3, 22),),
    ((5, 20),),
    ((5, 21), (4, 22),),
    (),
)
SCATTER_TABLE = (
    ((0, 0), (0, 1),),
    ((0, 2), (0, 3),),
    ((0, 4),),
    ((0, 5),),
    (),
    (),
    (),
    ((1, 0), (1, 1), (1, 2),),
    ((1, 3), (1, 4), (1, 5),),
    (),
    (),
    ((0, 6), (0, 7),),
    ((2, 0),),
    ((2, 1), (0, 8), (0, 9),),
    ((2, 2), (1, 6), (1, 7),),
    ((2, 3), (2, 4), (0, 10), (0, 11),),
    ((2, 5), (1, 8), (1, 9),),
    ((3, 0), (3, 1), (0, 12), (0, 13),),
    ((3, 2), (1, 10), (1, 11),),
    ((2, 6), (2, 7), (0, 14), (0, 15),),
    ((3, 3), (3, 4), (1, 12), (1, 13),),
    ((4, 0), (4, 1), (3, 5), (2, 8), (0, 16), (0, 17),),
    ((1, 14), (1, 15),),
    ((4, 2), (2, 9),),
    (),
    ((2, 10),),
    ((4, 3),),
    ((1, 16),),
    ((2, 11), (1, 17),),
    ((4, 4), (3, 6), (3, 7),),
    ((4, 5), (0, 18),),
    ((2, 12),),
    (),
    ((3, 8), (2, 13),),
    ((4, 6), (2, 14), (1, 18),),
    ((4, 7), (3, 9), (2, 15),),
    ((4, 8), (3, 10), (2, 16), (0, 19),),
    ((3, 11),),
    ((3, 12), (2, 17),),
    ((4, 9), (3, 13), (3, 14), (1, 19),),
    ((4, 10), (4, 11), (3, 15), (2, 18), (0, 20),),
    ((4, 12), (3, 16), (3, 17),),
    ((4, 13),),
    ((4, 14), (2, 19), (1, 20),),
    ((4, 15), (3, 18), (0, 21),),
    ((4, 16),),
    ((4, 17),),
    ((3, 19),),
    (),
    (),
    ((1, 21),),
    (),
    ((2, 20),),
    (),
    (),
    ((4, 18),),
    ((0, 22), (4, 19), (2, 21), (3, 20), (1, 22), (3, 21), (2, 22), (4, 20), (3, 22), (4, 21), (4, 22),),
)
HALF = 0.5
ERFC_P = 0.3
ERFC_Q = (
    0.16918934881687164,
    0.17069095373153687,
    0.1485210806131363,
    0.2141820192337036,
    -0.09282728284597397,
    0.5449684858322144,
    -0.5097734332084656,
    0.4843021035194397,
    -0.12925326824188232,
)
BF = jnp.bfloat16
F32 = jnp.float32
MESH_ID = pl.DeviceIdType.MESH
ALL = slice(None)
LINKS = ("z1", "z2", "z3", "x", "y", "c")
VMEM_CAP = 62 * 2**20
SLOT = 128
KINDS = (0, 2, 2, 1, 1, 1)
FF_ROWS = 512


def nn(lhs, rhs):
    return lax.dot_general(lhs, rhs, (((1,), (0,)), ((), ())), preferred_element_type=F32)


def nt(lhs, rhs):
    return lax.dot_general(lhs, rhs, (((1,), (1,)), ((), ())), preferred_element_type=F32)


def tn(lhs, rhs):
    return lax.dot_general(lhs, rhs, (((0,), (0,)), ((), ())), preferred_element_type=F32)


def gelu_pair(v):
    size = jnp.abs(v)
    t = 1.0 / (1.0 + (ERFC_P * 0.7071067811865476) * size)
    q = ERFC_Q[-1]
    for coef in ERFC_Q[-2::-1]:
        q = q * t + coef
    bell = jnp.exp(-0.5 * (v * v))
    tail = (HALF * bell) * (q * t)
    phi = jnp.where(v >= 0, 1.0 - tail, tail)
    return v * phi, phi + v * (bell * 0.3989422804014327)


def norm_stats(v):
    mean = jnp.mean(v, axis=-1, keepdims=True)
    cen = v - mean
    r = lax.rsqrt(jnp.mean(cen * cen, axis=-1, keepdims=True) + layer_eps)
    return cen * r, r


def norm_grad(vhat, r, t):
    m1 = jnp.mean(t, axis=-1, keepdims=True)
    m2 = jnp.mean(t * vhat, axis=-1, keepdims=True)
    return r * (t - m1 - vhat * m2)


def head_masks(rows, scale):
    lane = lax.broadcasted_iota(jnp.int32, (rows, 128), 1)
    low = jnp.where(lane < HDIM, scale, 0.0).astype(BF)
    high = jnp.where(lane < HDIM, 0.0, scale).astype(BF)
    return low, high


def split_heads(pair, masks):
    return jnp.concatenate([pair * masks[0], pair * masks[1]], axis=0)


def vector_masks(width, count, nrow):
    col = lax.broadcasted_iota(jnp.int32, (SLOT, width), 1).astype(F32)
    row = lax.broadcasted_iota(jnp.int32, (SLOT, width), 0).astype(F32)
    pick = jnp.where(col - jnp.floor((col + 0.5) * (1.0 / count)) * count == row, 1.0, 0.0).astype(BF)
    col = lax.broadcasted_iota(jnp.int32, (nrow, width), 1).astype(F32)
    row = lax.broadcasted_iota(jnp.int32, (nrow, width), 0).astype(F32)
    return pick, jnp.floor((col + 0.5) * (1.0 / count)) == row


class Place:
    def __init__(self):
        dp = lax.axis_index("dp")
        self.x = lax.axis_index("mp")
        self.z, self.y, self.c = lax.div(dp, 4), lax.rem(lax.div(dp, 2), 2), lax.rem(dp, 2)
        z, y, c, x = self.z, self.y, self.c, self.x
        self.nx, self.ny, self.nc = 1 - x, 1 - y, 1 - c
        self.at = [c * 0 + k for k in range(3)]
        self.far_z = {1: z + 1 - 2 * lax.rem(z, 2), 2: lax.rem(z + 2, 4), 3: 3 - z}
        at = lambda zz, yy, cc, xx: (zz * 4 + yy * 2 + cc, xx)
        self.peer = {
            "z1": at(self.far_z[1], y, c, x),
            "z2": at(self.far_z[2], y, c, x),
            "z3": at(self.far_z[3], y, c, x),
            "x": at(z, y, c, 1 - x),
            "y": at(z, 1 - y, c, x),
            "c": at(z, y, 1 - c, x),
        }

    def barrier(self):
        sem = pltpu.get_barrier_semaphore()
        for peer in self.peer.values():
            pl.semaphore_signal(sem, inc=1, device_id=peer, device_id_type=MESH_ID)
        pl.semaphore_wait(sem, len(self.peer))


def rows_of(ref, xs):
    if isinstance(xs, slice):
        return xs
    half = ref.shape[-2] // 2
    return pl.ds(pl.multiple_of(xs * half, 8), half)


def block(ref, kind, zs, ys, cs, xs, cut):
    if kind == 0:
        return ref.at[(zs, ys, cs, xs) + cut]
    if kind == 1:
        return ref.at[(xs, zs, ys, cs) + cut]
    return ref.at[zs, ys, cs, rows_of(ref, xs), cut[1]]


class Sends:
    STEPS = ("z", "a", "b", "c", "w")

    def __init__(self, place, send_sem, recv_sem):
        self.place, self.send_sem, self.recv_sem = place, send_sem, recv_sem
        self.copies, self.waits = {}, {}
        self.live = False

    def copy(self, t, i, step, src, dst, link):
        out = self.STEPS.index("a" if step == "w" else step)
        return pltpu.make_async_remote_copy(
            src_ref=src,
            dst_ref=dst,
            send_sem=self.send_sem.at[4 * t + out],
            recv_sem=self.recv_sem.at[5 * i + self.STEPS.index(step)],
            device_id=self.place.peer[link],
            device_id_type=MESH_ID,
        )

    def go(self, t, i, step, part, src, dst, link):
        if self.live:
            self.copies[i, step, part].start()
        else:
            self.copies[i, step, part] = self.copy(t, i, step, src, dst, link)

    def got(self, t, i, step, all_of):
        if self.live:
            self.waits[i, step].wait_recv()
        else:
            self.waits[i, step] = self.copy(t, i, step, all_of, all_of, "c")

    def sent(self, t, sizes):
        for step, view in sizes.items():
            self.copy(t, 0, step, view, view, "c").wait_send()


def union(cuts):
    if cuts[1] is None:
        return cuts[0]
    return tuple(p if p == q else slice(p.start, q.stop) for p, q in zip(*cuts))


def order(half):
    return ("x", "y") if half == 0 else ("y", "x")


def gather_stage(sends, stage, i, t, kind, own, full, cuts, near_first):
    p = sends.place
    z, y, c, x = p.z, p.y, p.c, p.x
    whole = union(cuts)
    three = block(full, kind, slice(0, 3), y, c, x, whole)
    size = {
        "z": three,
        "w": three,
        "a": block(full, kind, z if near_first else ALL, y, c, x, whole),
        "b": block(full, kind, ALL, y, c, ALL, whole),
        "c": block(full, kind, ALL, ALL, c, ALL, whole),
    }
    waits = ((), ("a",), ("z",), ("w",), ("b",), ("c",)) if near_first else ((), ("z",), ("a",), ("b",), ("c",))
    if stage >= len(waits):
        return
    for step in waits[stage]:
        sends.got(t, i, step, size[step])
    for h, cut in enumerate(cuts):
        if cut is None:
            continue
        a, b = order(h)
        mine = block(full, kind, z, y, c, x, cut)
        line = block(full, kind, ALL, y, c, x, cut)
        if h == 0:
            next_one, next_line = block(full, kind, z, y, c, p.nx, cut), block(full, kind, ALL, y, c, p.nx, cut)
            far = block(full, kind, ALL, p.ny, c, ALL, cut)
        else:
            next_one, next_line = block(full, kind, z, p.ny, c, x, cut), block(full, kind, ALL, p.ny, c, x, cut)
            far = block(full, kind, ALL, ALL, c, p.nx, cut)
        own_z = [("z", k, own.at[cut], mine, k) for k in ("z1", "z2", "z3")]
        line_b, line_c = ("b", 1, line, line, b), ("c", 1, line, line, "c")
        next_bc = [("b", 2, next_line, next_line, b), ("c", 2, next_line, next_line, "c")]
        far_c = [("c", 3, far, far, "c")]
        if near_first:
            next_z = [("w", k, next_one, next_one, k) for k in ("z1", "z2", "z3")]
            steps = ([("a", 1, own.at[cut], mine, a)] + own_z, next_z, [line_b, line_c], next_bc, far_c, [])
        else:
            steps = (own_z, [("a", 1, line, line, a), line_b, line_c], next_bc, far_c, [])
        for step, part, src, dst, link in steps[stage]:
            sends.go(t, i, step, (h, part), src, dst, link)


def col_cuts(cols, parts):
    step = cols // (2 * parts)
    return [((ALL, slice(2 * step * i, 2 * step * i + step)), (ALL, slice(2 * step * i + step, 2 * step * (i + 1)))) for i in range(parts)]


def row_cuts(rows, parts):
    step = rows // (2 * parts)
    return [((slice(2 * step * i, 2 * step * i + step), ALL), (slice(2 * step * i + step, 2 * step * (i + 1)), ALL)) for i in range(parts)]


def block_cuts(rows, cols, col_parts, row_parts):
    step, width = rows // (2 * row_parts), cols // col_parts
    cuts = []
    for q in range(col_parts):
        lanes = slice(q * width, q * width + width)
        for r in range(row_parts):
            low = 2 * step * r
            cuts.append(((slice(low, low + step), lanes), (slice(low + step, low + 2 * step), lanes)))
    return cuts


def gather_plan(shapes):
    plan = [(0, 0, ((ALL, ALL), None))]
    plan += [(1, 2, c) for c in col_cuts(shapes[1][1], 3)]
    plan += [(2, 2, c) for c in col_cuts(shapes[2][1], 1)]
    plan += [(3, 1, c) for c in col_cuts(shapes[3][1], 6)]
    plan += [(4, 1, c) for c in col_cuts(shapes[4][1], 6)]
    plan += [(5, 1, c) for c in block_cuts(shapes[5][0], shapes[5][1], 3, 2)]
    return [piece + (near,) for piece, near in zip(plan, (False,) + NEAR_FIRST)]


class Ticks:
    def __init__(self, table, stage_fn):
        self.table, self.stage_fn, self.count = table, stage_fn, 0

    def run(self, k):
        for s, i in self.table[k]:
            self.stage_fn(s, i)

    def point(self):
        self.count += 1
        self.run(self.count - 1)

    def within(self, index, values):
        for value in values:
            if self.table[self.count]:
                pl.when(index == value)(functools.partial(self.run, self.count))
            self.count += 1


def forward_kernel(dims, sizes, *refs):
    (off_ref, seg_ref, x_ref, dmol_ref, vec_own, qkv_own, wo_own, wi_own, wf_own, cv_own) = refs[:10]
    outs = refs[10:28]
    (mol_out, vec_out, ln3_out, dcp_out, qkv_o, wo_o, wi_o, wf_o, cv_o, nst_o, proj_o, prob_o, headst_o, r1_o, n2t_o, act_o, gd_o, mit_o) = outs
    (vec_g, qkv_g, wo_g, wi_g, wf_g, cv_g, vec_f, vecs, pad, ns, proj, prob, heads, r1, n2, act, gd, r2, molin, local_sem, out_sem, send_sem, recv_sem) = refs[28:]
    tok, d, ff = dims
    win = WIN
    nw = tok // win + 1
    half_ff = ff // 2
    mols = tok // KER
    place = Place()
    owns = (vec_own, qkv_own, wo_own, wi_own, wf_own, cv_own)
    fulls = (vec_g, qkv_g, wo_g, wi_g, wf_g, cv_g)
    plan = gather_plan([o.shape for o in owns])
    kinds = KINDS
    place.barrier()
    sends = Sends(place, send_sem, recv_sem)
    local = []
    for i, (own, full, kind) in enumerate(zip(owns, fulls, kinds)):
        copy = pltpu.make_async_copy(own, block(full, kind, place.z, place.y, place.c, place.x, (ALL, ALL)), local_sem.at[i])
        copy.start()
        local.append(copy)

    def comm_stage(stage, i):
        t, kind, cuts, near_first = plan[i]
        if sends.live and stage == (2 if near_first else 1) and (i == 0 or plan[i - 1][0] != t):
            local[t].wait()
        gather_stage(sends, stage, i, t, kind, owns[t], fulls[t], cuts, near_first)

    for stage in range(6):
        for i in range(len(plan)):
            comm_stage(stage, i)
    sends.live = True
    ticks = Ticks(GATHER_TABLE, comm_stage)

    out_copies = []

    def flush(src, dst):
        copy = pltpu.make_async_copy(src, dst, out_sem.at[len(out_copies)])
        copy.start()
        out_copies.append(copy)
        return copy

    def unpack_vectors():
        nrow = vec_f.shape[0] // 16
        vec_f[...] = vec_g[...].reshape(vec_f.shape).astype(F32)
        for width, count in sorted(set(sizes)):
            pick, mine = vector_masks(width, count, nrow)
            for v in [i for i, s in enumerate(sizes) if s == (width, count)]:
                spread = nn(vec_f[pl.ds(v, nrow, stride=16), :].astype(BF), pick)
                vecs[v : v + 1, :width] = jnp.sum(jnp.where(mine, spread, 0.0), axis=0, keepdims=True)

    def vec(v, lo, hi):
        return vecs[v : v + 1, lo:hi]

    offset = off_ref[0]

    ticks.point()
    unpack_vectors()
    ticks.point()
    flush(vecs, vec_out)

    pad[0:win, :] = jnp.zeros((win, d), BF)
    pad[win + tok : 2 * win + tok, :] = jnp.zeros((win, d), BF)

    @pl.loop(0, tok // 128)
    def _(b):
        rows = pl.ds(pl.multiple_of(b * 128, 128), 128)
        vhat, _ = norm_stats(x_ref[rows, :].astype(F32))
        pad[pl.ds(pl.multiple_of(b * 128 + win, 128), 128), :] = (vhat * vec(0, 0, d) + vec(1, 0, d)).astype(BF)
        ticks.within(b, (1, 3, 5, 7))

    ri = lax.broadcasted_iota(jnp.int32, (win, 2 * win), 0)
    rj = lax.broadcasted_iota(jnp.int32, (win, 2 * win), 1)
    shift_in = jnp.where(rj == ri + (win - offset), 1.0, 0.0).astype(BF)
    shift_out = jnp.where(rj == ri + offset, 1.0, 0.0).astype(BF)

    @pl.loop(0, nw)
    def _(w):
        at = pl.multiple_of(w * win, win)
        ns[pl.ds(at, win), :] = nn(shift_in, pad[pl.ds(at, 2 * win), :]).astype(BF)
        ticks.within(w, (4,))

    ns_t = act.at[0:d, 0 : nw * win]

    @pl.loop(0, nw // 3)
    def _(b):
        rows = pl.ds(pl.multiple_of(b * 384, 128), 384)
        ns_t[:, rows] = ns[rows, :].T

    ns_t_copy = flush(ns_t, nst_o)

    ticks.point()
    flush(qkv_g, qkv_o)
    wq = qkv_g.reshape(d, 3 * d)
    for blk3 in range(3):
        bias_row = None if blk3 == 1 else vec(2, (blk3 // 2) * d, (blk3 // 2) * d + d)

        @pl.loop(0, nw // 3)
        def _(b):
            rows = pl.ds(pl.multiple_of(b * 384, 128), 384)
            for n0 in range(0, d, 256):
                val = nn(ns[rows, :], wq[:, blk3 * d + n0 : blk3 * d + n0 + 256])
                if bias_row is not None:
                    val = val + bias_row[:, n0 : n0 + 256]
                proj[rows, blk3 * d + n0 : blk3 * d + n0 + 256] = val.astype(BF)

        ticks.point()

    proj_copy = flush(proj, proj_o)

    qmask = head_masks(win, HDIM**-0.5)
    vmask = head_masks(win, 1.0)
    seg_row = jnp.concatenate([seg_ref[0:1, :].astype(F32), jnp.full((1, win), -1.0, F32)], axis=1)
    seg_row = pltpu.roll(jnp.broadcast_to(seg_row, (8, tok + win)), offset, axis=1)
    segs = vec_f
    for w in range(nw):
        segs[w * 8 : w * 8 + 8, 0:win] = seg_row[:, w * win : (w + 1) * win]

    @pl.loop(0, nw)
    def _(w):
        rows = pl.ds(pl.multiple_of(w * win, win), win)
        seg_q = jnp.broadcast_to(segs[pl.ds(pl.multiple_of(w * 8, 8), 8), 0:win][0:1], (win, win))
        same = seg_q == seg_q.T
        same2 = jnp.concatenate([same, same], axis=1)
        for pr in range(HEADS // 2):
            lanes = slice(pr * 128, pr * 128 + 128)
            q2 = proj[rows, pr * 128 : pr * 128 + 128]
            k2 = proj[rows, d + pr * 128 : d + pr * 128 + 128]
            v2 = proj[rows, 2 * d + pr * 128 : 2 * d + pr * 128 + 128]
            s = jnp.where(same2, nt(k2, split_heads(q2, qmask)), -1e30)
            e = jnp.exp(s - jnp.max(s, axis=0, keepdims=True))
            pb = (e * (1.0 / jnp.sum(e, axis=0, keepdims=True))).astype(BF)
            prob[w, pr] = pb
            stacked = jnp.concatenate([pb[:, :win], pb[:, win:]], axis=0)
            pad[rows, lanes] = tn(stacked, split_heads(v2, vmask)).astype(BF)
        ticks.within(w, range(nw))

    prob_copy = flush(prob, prob_o)

    flush(wo_g, wo_o)
    wo = wo_g.reshape(d, d)
    proj_copy.wait()
    heads_t = proj.at[0:d, 0:tok]
    n2_t = proj.at[0:d, tok : 2 * tok]

    @pl.loop(0, tok // 128)
    def _(b):
        at = pl.multiple_of(b * 128, 128)
        hb = nn(shift_out, pad[pl.ds(at, 2 * win), :]).astype(BF)
        heads[pl.ds(at, 128), :] = hb
        heads_t[:, pl.ds(at, 128)] = hb.T

    ticks.point()

    @pl.loop(0, tok // 256)
    def _(b):
        rows = pl.ds(pl.multiple_of(b * 256, 256), 256)
        val = x_ref[rows, :].astype(F32) + nn(heads[rows, :], wo[...]) + vec(3, 0, d)
        r1[rows, :] = val
        vhat, _ = norm_stats(val)
        low = (vhat * vec(4, 0, d) + vec(5, 0, d)).astype(BF)
        n2[rows, :] = low
        n2_t[:, rows] = low.T
        ticks.within(b, (0, 1, 2))

    flush(heads_t, headst_o)
    flush(r1, r1_o)
    flush(n2_t, n2t_o)
    ns_t_copy.wait()

    wi = wi_g.reshape(2, d, half_ff)

    @pl.loop(0, half_ff // 256)
    def _(j):
        cols = pl.ds(pl.multiple_of(j * 256, 256), 256)
        base = ticks.count
        for hx in range(2):
            for q in range(half_ff // 256):
                if ticks.table[base + 2 * q + hx]:
                    pl.when(j == q)(functools.partial(ticks.run, base + 2 * q + hx))
            ocols = pl.ds(pl.multiple_of(hx * half_ff + j * 256, 256), 256)
            bias_row = vecs[6:7, ocols]
            for m in range(0, tok, 256):
                pre = nn(n2[m : m + 256, :], wi[hx, :, cols]) + bias_row
                g, dg = gelu_pair(pre)
                act[m : m + 256, ocols] = g.astype(BF)
                gd[m : m + 256, ocols] = dg.astype(BF)
        ticks.count = base + 2 * (half_ff // 256)

    flush(act, act_o)
    flush(gd, gd_o)

    ticks.point()
    flush(wi_g, wi_o)
    flush(wf_g, wf_o)
    wf = wf_g.reshape(2, d, half_ff)

    @pl.loop(0, tok // 256)
    def _(b):
        rows = pl.ds(pl.multiple_of(b * 256, 256), 256)
        for n0 in range(0, d, 256):
            cols = slice(n0, n0 + 256)
            val = nt(act[rows, 0:half_ff], wf[0, cols, :]) + nt(act[rows, half_ff:], wf[1, cols, :])
            val = r1[rows, cols] + val + vec(7, n0, n0 + 256)
            r2[n0 // 128, rows, :] = val[:, :128]
            r2[n0 // 128 + 1, rows, :] = val[:, 128:]
        ticks.within(b, range(4))

    for k in range(KER):
        for q in range(d // 128):
            molin[:, k * d + q * 128 : k * d + q * 128 + 128] = r2[q, pl.ds(k, mols, stride=KER), :].astype(BF)

    prob_copy.wait()
    for k in range(KER):
        for q in range(d // 128):
            prob[k, q] = molin[:, k * d + q * 128 : k * d + q * 128 + 128].T
    flush(prob.at[0:KER], mit_o)
    cv = cv_g.reshape(2, KER * d, d // 2)
    parts = {}
    for q in range(3):
        ticks.point()
        for hx in range(2):
            at = hx * (d // 2) + q * 128
            pre = nn(molin[...], cv[hx, :, q * 128 : q * 128 + 128]) + vec(8, at, at + 128)
            parts[at] = gelu_pair(pre)
    flush(cv_g, cv_o)
    g = jnp.concatenate([parts[at][0] for at in range(0, d, 128)], axis=1)
    dg = jnp.concatenate([parts[at][1] for at in range(0, d, 128)], axis=1)
    vhat, r = norm_stats(g.astype(BF).astype(F32))
    mol_out[...] = vhat * vec(9, 0, d) + vec(10, 0, d)
    cot = dmol_ref[...].astype(F32)
    ln3_out[0:1, :] = jnp.sum(cot * vhat, axis=0, keepdims=True)
    ln3_out[1:2, :] = jnp.sum(cot, axis=0, keepdims=True)
    da = norm_grad(vhat, r, cot * vec(9, 0, d)).astype(BF).astype(F32)
    dcp_out[...] = (da * dg).astype(BF)
    for t, (full, kind) in enumerate(zip(fulls, kinds)):
        pick = functools.partial(block, full, kind, cut=(ALL, ALL))
        z, y, c, x = place.z, place.y, place.c, place.x
        sends.sent(t, {"z": pick(slice(0, 3), y, c, x), "a": pick(ALL, y, c, x), "b": pick(ALL, y, c, ALL), "c": pick(ALL, ALL, c, ALL)})
    for copy in out_copies:
        if not any(copy is early for early in (ns_t_copy, proj_copy, prob_copy)):
            copy.wait()


def scatter_plan(shapes):
    plan = [(5, 1, c) for c in row_cuts(shapes[5][0], 6)]
    for wf_cut, wi_cut in zip(col_cuts(shapes[4][1], 6), col_cuts(shapes[3][1], 6)):
        plan += [(4, 1, wf_cut), (3, 1, wi_cut)]
    plan += [(2, 2, c) for c in col_cuts(shapes[2][1], 1)]
    plan += [(1, 2, c) for c in col_cuts(shapes[1][1], 3)]
    plan += [(0, 0, ((ALL, ALL), None))]
    return plan


def backward_kernel(dims, sizes, *refs):
    (off_ref, x_ref, dcp_ref, vecs, ln3_ref, qkv_i, wo_i, wi_i, wf_i, cv_i, nst_i, proj_i, prob_i, headst_i, r1_i, n2t_i, act_i, gd_i, mit_i) = refs[:19]
    dch_out = refs[19]
    own_outs = refs[20:26]
    grads = refs[26:32]
    from_core = refs[32:38]
    from_b = refs[38:44]
    from_a = refs[44:50]
    from_z = refs[50:56]
    sums, res_sem, tile_sem, load_sem, out_sem, send_sem, recv_sem = refs[56:]
    tok, d, ff = dims
    win = WIN
    nw = tok // win + 1
    half_ff = ff // 2
    mols = tok // KER
    place = Place()
    z, y, c, x = place.z, place.y, place.c, place.x
    plan = scatter_plan([o.shape for o in own_outs])
    place.barrier()
    sends = Sends(place, send_sem, recv_sem)

    def add_blocks(dst_of, src_of):
        if not sends.live:
            return

        @pl.loop(0, 4)
        def _(zz):
            dst, src = dst_of(zz), src_of(zz)
            dst[...] = dst[...] + src[...]

    def comm_stage(stage, i):
        t, kind, cuts = plan[i]
        g, rc, rb, ra, rz, own = grads[t], from_core[t], from_b[t], from_a[t], from_z[t], own_outs[t]

        def core_blk(zs, ys, xs, cut):
            if kind == 2:
                return rc.at[zs, ys, rows_of(rc, xs), cut[1]]
            return rc.at[(zs, ys, xs) + cut] if kind == 0 else rc.at[(xs, zs, ys) + cut]

        whole = union(cuts)
        waits = {
            1: ("c", core_blk(ALL, ALL, ALL, whole)),
            2: ("b", rb.at[(ALL, ALL) + whole]),
            3: ("a", ra.at[(ALL,) + whole]),
            4: ("z", rz.at[(ALL,) + whole]),
        }
        if stage > 0:
            sends.got(t, i, *waits[stage])
        for h, cut in enumerate(cuts):
            if cut is None:
                continue
            a, b = order(h)
            if stage == 0:
                sends.go(t, i, "c", h, block(g, kind, ALL, ALL, place.nc, ALL, cut), core_blk(ALL, ALL, ALL, cut), "c")
            elif stage == 1:
                for far in (1, 0):
                    for o in range(2):
                        ys, xs = (place.ny if far else y, place.at[o]) if h == 0 else (place.at[o], place.nx if far else x)
                        add_blocks(lambda zz: block(g, kind, zz, ys, c, xs, cut), lambda zz: core_blk(zz, ys, xs, cut))
                        if far:
                            sends.go(t, i, "b", (h, o), block(g, kind, ALL, ys, c, xs, cut), rb.at[(place.at[o], ALL) + cut], b)
            elif stage == 2:
                near, other = (x, place.nx) if h == 0 else (y, place.ny)
                for far in (1, 0):
                    o = other if far else near
                    ys, xs = (y, o) if h == 0 else (o, x)
                    add_blocks(lambda zz: block(g, kind, zz, ys, c, xs, cut), lambda zz: rb.at[(o, zz) + cut])
                    if far:
                        sends.go(t, i, "a", h, block(g, kind, ALL, ys, c, xs, cut), ra.at[(ALL,) + cut], a)
            elif stage == 3:
                add_blocks(lambda zz: block(g, kind, zz, y, c, x, cut), lambda zz: ra.at[(zz,) + cut])
                for q in (1, 2, 3):
                    sends.go(t, i, "z", (h, q), block(g, kind, place.far_z[q], y, c, x, cut), rz.at[(place.at[q - 1],) + cut], "z%d" % q)
            elif sends.live:
                total = block(g, kind, z, y, c, x, cut)[...].astype(F32)
                for q in range(3):
                    total = total + rz.at[(place.at[q],) + cut][...].astype(F32)
                if t != 1:
                    own[cut] = total
                    continue
                for q in range(0, cut[1].stop - cut[1].start, 128):
                    part, r = divmod(cut[1].start + q, d)
                    to = (r // 256) * d + part * 256 + r % 256
                    own[:, to : to + 128] = total[:, q : q + 128]

    for stage in range(5):
        for i in range(len(plan)):
            comm_stage(stage, i)
    sends.live = True
    ticks = Ticks(SCATTER_TABLE, comm_stage)
    state = {"load": 0}

    def load(src, dst):
        copy = pltpu.make_async_copy(src, dst, load_sem.at[state["load"]])
        state["load"] += 1
        copy.start()
        return copy

    def vec(v, lo, hi):
        return vecs[v : v + 1, lo:hi]

    offset = off_ref[0]
    ri = lax.broadcasted_iota(jnp.int32, (win, 2 * win), 0)
    rj = lax.broadcasted_iota(jnp.int32, (win, 2 * win), 1)
    shift_in = jnp.where(rj == ri + (win - offset), 1.0, 0.0).astype(BF)
    shift_out = jnp.where(rj == ri + offset, 1.0, 0.0).astype(BF)
    sums[...] = jnp.zeros_like(sums)
    sums[9:10, 0:d] = ln3_ref[0:1, :]
    sums[10:11, 0:d] = ln3_ref[1:2, :]
    sums[8:9, 0:d] = jnp.sum(dcp_ref[...].astype(F32), axis=0, keepdims=True)
    g_vec, g_qkv, g_wo, g_wi, g_wf, g_cv = grads
    g_cv2 = g_cv.reshape(2, KER * d, d // 2)
    g_wi2 = g_wi.reshape(2, d, half_ff)
    g_wf2 = g_wf.reshape(2, d, half_ff)

    def rows_of_dres(dres, rows):
        return jnp.concatenate([dres[q, rows, :] for q in range(d // 128)], axis=1)

    def set_dres(dres, rows, val):
        for q in range(d // 128):
            dres[q, rows, :] = val[:, q * 128 : q * 128 + 128]

    def whole(dres, dpad):
        def conv_part(cv, mi):
            loads = [load(mit_i, mi), load(cv_i, cv)]
            cv2 = cv.reshape(2, KER * d, d // 2)
            loads[0].wait()
            for kk in range(KER):
                val = nn(mi[kk].reshape(d, mols), dcp_ref[...]).astype(BF)
                g_cv2[0, kk * d : kk * d + d, :] = val[:, : d // 2]
                g_cv2[1, kk * d : kk * d + d, :] = val[:, d // 2 :]

            ticks.point()
            loads[1].wait()
            for kk in range(KER):
                for n0 in range(0, d, 256):
                    rows = slice(kk * d + n0, kk * d + n0 + 256)
                    val = nt(dcp_ref[:, : d // 2], cv2[0, rows, :]) + nt(dcp_ref[:, d // 2 :], cv2[1, rows, :])
                    dres[n0 // 128, pl.ds(kk, mols, stride=KER), :] = val[:, :128]
                    dres[n0 // 128 + 1, pl.ds(kk, mols, stride=KER), :] = val[:, 128:]
                ticks.point()

        pl.run_scoped(conv_part, pltpu.VMEM(cv_i.shape, BF), pltpu.VMEM(mit_i.shape, BF))

        def ff_part(dn2, r1):
            r1_load = load(r1_i, r1)

            def inner(act, gd, wf, wi, dff, dff_t, n2_t, dh):
                n2_load = load(n2t_i, n2_t)

                def tile_copies(j):
                    slot, hx, jj = lax.rem(j, 2), lax.rem(j, 2), lax.div(j, 2)
                    cols = pl.ds(pl.multiple_of(hx * half_ff + jj * 256, 256), 256)
                    wcols = pl.ds(pl.multiple_of(jj * 256, 256), 256)
                    pairs = (
                        (act_i.at[:, cols], act),
                        (gd_i.at[:, cols], gd),
                        (wf_i.at[hx, :, :, :, :, wcols], wf),
                        (wi_i.at[hx, :, :, :, :, wcols], wi),
                    )
                    return [pltpu.make_async_copy(s, b.at[slot], tile_sem.at[slot, q]) for q, (s, b) in enumerate(pairs)]

                for copy in tile_copies(0):
                    copy.start()
                ticks.point()

                @pl.loop(0, tok // 256)
                def _(b):
                    rows = pl.ds(pl.multiple_of(b * 256, 256), 256)
                    val = rows_of_dres(dres, rows).astype(BF)
                    dff[rows, :] = val
                    sums[7:8, 0:d] += jnp.sum(val.astype(F32), axis=0, keepdims=True)
                    dff_t[:, rows] = val.T
                    ticks.within(b, range(4))

                n2_load.wait()
                n_tiles = ff // 256

                @pl.loop(0, n_tiles)
                def _(j):
                    slot, hx, jj = lax.rem(j, 2), lax.rem(j, 2), lax.div(j, 2)
                    for copy in tile_copies(j):
                        copy.wait()

                    @pl.when(j + 1 < n_tiles)
                    def _():
                        for copy in tile_copies(j + 1):
                            copy.start()

                    wcols = pl.ds(pl.multiple_of(jj * 256, 256), 256)
                    wf_j = wf.at[slot].reshape(d, 256)
                    wi_j = wi.at[slot].reshape(d, 256)
                    total = jnp.zeros((1, 256), F32)
                    for m in range(0, tok, FF_ROWS):
                        val = (nn(dff[m : m + FF_ROWS, :], wf_j[...]) * gd[slot, m : m + FF_ROWS, :].astype(F32)).astype(BF)
                        dh[m : m + FF_ROWS, :] = val
                        total = total + jnp.sum(val.astype(F32), axis=0, keepdims=True)
                    sums[6:7, pl.ds(pl.multiple_of(hx * half_ff + jj * 256, 256), 256)] = total
                    g_wf2[hx, :, wcols] = nn(dff_t[...], act[slot]).astype(BF)
                    g_wi2[hx, :, wcols] = nn(n2_t[...], dh[...]).astype(BF)

                    @pl.when(j == 0)
                    def _():
                        dn2[...] = nt(dh[...], wi_j[...])

                    @pl.when(j > 0)
                    def _():
                        dn2[...] += nt(dh[...], wi_j[...])

                    ticks.within(j, range(12))

            pl.run_scoped(
                inner,
                pltpu.VMEM((2, tok, 256), BF),
                pltpu.VMEM((2, tok, 256), BF),
                pltpu.VMEM((2, 4, 2, 2, d // 16, 256), BF),
                pltpu.VMEM((2, 4, 2, 2, d // 16, 256), BF),
                pltpu.VMEM((tok, d), BF),
                pltpu.VMEM((d, tok), BF),
                pltpu.VMEM((d, tok), BF),
                pltpu.VMEM((tok, 256), BF),
            )

            def out_part(heads_t, wo, dattn):
                loads = [load(headst_i, heads_t), load(wo_i, wo)]
                wo2 = wo.reshape(d, d)
                g_wo2 = g_wo.reshape(d, d)
                r1_load.wait()

                @pl.loop(0, tok // 128)
                def _(b):
                    rows = pl.ds(pl.multiple_of(b * 128, 128), 128)
                    vhat, r = norm_stats(r1[rows, :])
                    cot = dn2[rows, :]
                    sums[4:5, 0:d] += jnp.sum(cot * vhat, axis=0, keepdims=True)
                    sums[5:6, 0:d] += jnp.sum(cot, axis=0, keepdims=True)
                    val = rows_of_dres(dres, rows) + norm_grad(vhat, r, cot * vec(4, 0, d))
                    set_dres(dres, rows, val)
                    low = val.astype(BF)
                    dattn[rows, :] = low
                    sums[3:4, 0:d] += jnp.sum(low.astype(F32), axis=0, keepdims=True)
                    ticks.within(b, range(8))

                for copy in loads:
                    copy.wait()
                g_wo2[...] = nn(heads_t[...], dattn[...]).astype(BF)
                ticks.point()
                dpad[0:win, :] = jnp.zeros((win, d), BF)
                dpad[win + tok : 2 * win + tok, :] = jnp.zeros((win, d), BF)

                @pl.loop(0, tok // 512)
                def _(b):
                    at = pl.multiple_of(b * 512, 256)
                    dpad[pl.ds(at + win, 512), :] = nt(dattn[pl.ds(at, 512), :], wo2[...]).astype(BF)
                    ticks.within(b, (0, 1))

            pl.run_scoped(out_part, pltpu.VMEM((d, tok), BF), pltpu.VMEM(wo_i.shape, BF), pltpu.VMEM((tok, d), BF))

        pl.run_scoped(ff_part, pltpu.VMEM((tok, d), F32), pltpu.VMEM((tok, d), F32))

        def attn_part(proj, wqkv, ns_t, lo):
            proj_loads = [load(proj_i.at[pl.ds(b * 384, 384)], proj.at[pl.ds(b * 384, 384)]) for b in range(nw // 3)]
            ns_load, qkv_load = load(nst_i, ns_t), load(qkv_i, wqkv)
            qmask = head_masks(win, HDIM**-0.5)
            vmask = head_masks(win, 1.0)
            g_qkv2 = g_qkv.reshape(d, 3 * d)
            wqkv2 = wqkv.reshape(d, 3 * d)

            def core_part(prob):
                n3 = nw // 3

                def prob_copy(i):
                    g, b, slot = lax.div(i, n3), lax.rem(i, n3), lax.rem(i, 2)
                    return pltpu.make_async_copy(prob_i.at[pl.ds(3 * b, 3), pl.ds(2 * g, 2)], prob.at[slot], res_sem.at[slot])

                prob_copy(0).start()
                ns_load.wait()
                base = ticks.count

                @pl.loop(0, d // 256)
                def _(g):
                    lq, lk, lv = [pl.ds(pl.multiple_of(r * d + g * 256, 256), 256) for r in range(3)]

                    @pl.loop(0, n3)
                    def _(b):
                        i = g * n3 + b
                        for q in range(n3):
                            pl.when(i == q)(proj_loads[q].wait)
                        prob_copy(i).wait()

                        @pl.when(i + 1 < n3 * (d // 256))
                        def _():
                            prob_copy(i + 1).start()

                        for u in range(3):
                            at = pl.multiple_of(b * (3 * win) + u * win, win)
                            rows = pl.ds(at, win)
                            dhw = nn(shift_in, dpad[pl.ds(at, 2 * win), lq]).astype(BF)
                            q4, k4, v4 = proj[rows, lq], proj[rows, lk], proj[rows, lv]
                            new = [[], [], []]
                            for pr in range(2):
                                lanes = slice(pr * 128, pr * 128 + 128)
                                q2, k2, v2 = q4[:, lanes], k4[:, lanes], v4[:, lanes]
                                pb = prob[lax.rem(i, 2), u, pr]
                                dbd = split_heads(dhw[:, lanes], vmask)
                                dp = nt(v2, dbd)
                                pf = pb.astype(F32)
                                ds = (pf * (dp - jnp.sum(pf * dp, axis=0, keepdims=True))).astype(BF)
                                stacked = jnp.concatenate([ds[:, :win], ds[:, win:]], axis=0)
                                new[0].append(tn(stacked, split_heads(k2, qmask)).astype(BF))
                                new[1].append(nn(ds, split_heads(q2, qmask)).astype(BF))
                                new[2].append(nn(pb, dbd).astype(BF))
                            for lanes, parts in zip((lq, lk, lv), new):
                                proj[rows, lanes] = jnp.concatenate(parts, axis=1)
                        for q in range(3):
                            for bb in range(n3):
                                if ticks.table[base + q * (n3 + 1) + bb]:
                                    pl.when(i == q * n3 + bb)(functools.partial(ticks.run, base + q * (n3 + 1) + bb))

                    for r, cols in enumerate((lq, lk, lv)):
                        to = pl.ds(pl.multiple_of(g * d + r * 256, 256), 256)
                        part = proj[:, cols]
                        if r != 1:
                            into = pl.ds(pl.multiple_of((r // 2) * d + g * 256, 256), 256)
                            sums[2:3, into] = jnp.sum(part.astype(F32), axis=0, keepdims=True)
                        g_qkv2[:, to] = nn(ns_t[...], part).astype(BF)
                    for q in range(3):
                        pl.when(g == q)(functools.partial(ticks.run, base + q * (n3 + 1) + n3))

                ticks.count = base + 3 * (n3 + 1)

            pl.run_scoped(core_part, pltpu.VMEM((2, 3, 2, win, 2 * win), BF))
            qkv_load.wait()

            @pl.loop(0, nw // 3)
            def _(b):
                rows = pl.ds(pl.multiple_of(b * 384, 128), 384)
                for n0 in range(0, d, 256):
                    val = nt(proj[rows, :], wqkv2[n0 : n0 + 256, :])
                    top = val.astype(BF)
                    dpad[rows, n0 : n0 + 256] = top
                    lo[rows, n0 : n0 + 256] = (val - top.astype(F32)).astype(BF)
                ticks.within(b, range(3))

            @pl.loop(0, tok // 128)
            def _(b):
                at = pl.multiple_of(b * 128, 128)
                rows = pl.ds(at, 128)
                both = pl.ds(at, 2 * win)
                cot = nn(shift_out, dpad[both, :]) + nn(shift_out, lo[both, :])
                vhat, r = norm_stats(x_ref[rows, :].astype(F32))
                sums[0:1, 0:d] += jnp.sum(cot * vhat, axis=0, keepdims=True)
                sums[1:2, 0:d] += jnp.sum(cot, axis=0, keepdims=True)
                set_dres(dres, rows, rows_of_dres(dres, rows) + norm_grad(vhat, r, cot * vec(0, 0, d)))
                ticks.within(b, range(8))

        pl.run_scoped(
            attn_part,
            pltpu.VMEM(proj_i.shape, BF),
            pltpu.VMEM(qkv_i.shape, BF),
            pltpu.VMEM(nst_i.shape, BF),
            pltpu.VMEM((nw * win, d), BF),
        )
        done = pltpu.make_async_copy(dres, dch_out, out_sem.at[0])
        done.start()

        g_vec2 = g_vec.reshape(-1, SLOT)
        nrow = g_vec2.shape[0] // 16
        g_vec[...] = jnp.zeros_like(g_vec)
        for width, count in sorted(set(sizes)):
            pick, mine = vector_masks(width, count, nrow)
            for v in [i for i, s in enumerate(sizes) if s == (width, count)]:
                spread = jnp.where(mine, sums[v : v + 1, :width], 0.0)
                top = spread.astype(BF)
                rest = (spread - top.astype(F32)).astype(BF)
                g_vec2[pl.ds(v, nrow, stride=16), :] = nt(top, pick) + nt(rest, pick)
        ticks.point()
        for t, g in enumerate(grads):
            pick = functools.partial(block, g, KINDS[t], cut=(ALL, ALL))
            sends.sent(t, {"z": pick(slice(0, 3), y, c, x), "a": pick(ALL, y, c, x), "b": pick(ALL, y, c, ALL), "c": pick(ALL, ALL, c, ALL)})
        done.wait()

    pl.run_scoped(whole, pltpu.VMEM((d // 128, tok, 128), F32), pltpu.VMEM((tok + 2 * win, d), BF))


def quick_mesh(mesh):
    return mesh.shape["dp"] == 16 and mesh.shape["mp"] == 2


def gathered_shape(shape, kind):
    if kind == 2:
        return (4, 2, 2, 2 * shape[0], shape[1])
    return ((4, 2, 2, 2) if kind == 0 else (2, 4, 2, 2)) + shape


def place_kernel(widths, *refs):
    n = (len(refs) - 3 - len(widths)) // 3
    sources, vec_ref, outs, vec_outs = refs[:n], refs[n], refs[n + 1 : 2 * n + 1], refs[2 * n + 1 : 2 * n + 1 + len(widths)]
    held, in_sem, out_sem = refs[-n - 2 : -2], refs[-2], refs[-1]
    loads = [pltpu.make_async_copy(s, h, in_sem.at[i]) for i, (s, h) in enumerate(zip(sources, held))]
    stores = [[pltpu.make_async_copy(h, o, out_sem.at[i])] for i, (h, o) in enumerate(zip(held[:-1], outs))]
    parts = held[-1].shape[0]
    stores.append([pltpu.make_async_copy(held[-1].at[q], outs[-1].at[:, q * SLOT : q * SLOT + SLOT], out_sem.at[n - 1 + q]) for q in range(parts)])
    for copy in loads:
        copy.start()
    for v, (width, out) in enumerate(zip(widths, vec_outs)):
        out[...] = vec_ref[v, :width]
    for load, store in zip(loads, stores):
        load.wait()
        for copy in store:
            copy.start()
    for store in stores:
        for copy in store:
            copy.wait()


def fast_shards(*args):
    (chars, seg, offs, l1g, l1b, wqkv, qvb, wo, aob, l2g, l2b, wi, fib, wf, fob, cv, cvb, l3g, l3b, dmol) = args
    tok, d = chars.shape
    mols = dmol.shape[0]
    vectors = (l1g, l1b, qvb, aob, l2g, l2b, fib, fob, cvb, l3g, l3b)
    sizes = tuple((v.shape[0] * 32, v.shape[0]) for v in vectors)
    ff = sizes[6][0]
    dims = (tok, d, ff)
    nw = tok // WIN + 1
    vec_own = sum(jnp.pad(v[None], ((i, 15 - i), (0, SLOT - v.shape[0]))) for i, v in enumerate(vectors))
    owns = (vec_own, wqkv, wo, wi, wf.T, cv)
    kinds = KINDS
    full = [gathered_shape(o.shape, k) for o, k in zip(owns, kinds)]
    plan = gather_plan([o.shape for o in owns])
    n_wait = 5 * len(plan)
    on_chip = pl.BlockSpec(memory_space=pltpu.VMEM)
    scalar = pl.BlockSpec(memory_space=pltpu.SMEM)
    any_mem = pl.BlockSpec(memory_space=pl.ANY)
    bf = lambda *s: jax.ShapeDtypeStruct(s, BF)
    f32 = lambda *s: jax.ShapeDtypeStruct(s, F32)
    prob_shape = (nw, HEADS // 2, WIN, 2 * WIN)
    saved = pl.pallas_call(
        functools.partial(forward_kernel, dims, sizes),
        out_shape=[
            f32(mols, d),
            f32(16, ff),
            f32(8, d),
            bf(mols, d),
            *[bf(*s) for s in full[1:]],
            bf(d, nw * WIN),
            bf(nw * WIN, 3 * d),
            bf(*prob_shape),
            bf(d, tok),
            f32(tok, d),
            bf(d, tok),
            bf(tok, ff),
            bf(tok, ff),
            bf(KER, d // SLOT, SLOT, mols),
        ],
        in_specs=[scalar] + [on_chip] * 9,
        out_specs=[on_chip, any_mem, on_chip, on_chip] + [any_mem] * 14,
        scratch_shapes=[
            *[pltpu.VMEM(s, BF) for s in full],
            pltpu.VMEM((512, SLOT), F32),
            pltpu.VMEM((16, ff), F32),
            pltpu.VMEM((tok + 2 * WIN, d), BF),
            pltpu.VMEM((nw * WIN, d), BF),
            pltpu.VMEM((nw * WIN, 3 * d), BF),
            pltpu.VMEM(prob_shape, BF),
            pltpu.VMEM((tok, d), BF),
            pltpu.VMEM((tok, d), F32),
            pltpu.VMEM((tok, d), BF),
            pltpu.VMEM((tok, ff), BF),
            pltpu.VMEM((tok, ff), BF),
            pltpu.VMEM((d // 128, tok, 128), F32),
            pltpu.VMEM((mols, KER * d), BF),
            pltpu.SemaphoreType.DMA((6,)),
            pltpu.SemaphoreType.DMA((16,)),
            pltpu.SemaphoreType.DMA((24,)),
            pltpu.SemaphoreType.DMA((n_wait,)),
        ],
        compiler_params=pltpu.CompilerParams(collective_id=1, has_side_effects=True, vmem_limit_bytes=VMEM_CAP),
        name="gather_forward",
    )(offs, seg, chars, dmol, *owns)
    (mol, vecs, ln3, dcp, qkv_f, wo_f, wi_f, wf_f, cv_f, ns, proj, prob, heads, r1, n2, act, gd, mi) = saved

    own_shapes = [o.shape for o in owns]
    kind_core = lambda s, k: (4, 2, 2 * s[0], s[1]) if k == 2 else ((4, 2, 2) if k == 0 else (2, 4, 2)) + s
    types = [F32] + [BF] * 5
    plan = scatter_plan(own_shapes)
    n_back = 5 * len(plan)
    back = pl.pallas_call(
        functools.partial(backward_kernel, dims, sizes),
        out_shape=[f32(d // SLOT, tok, SLOT)] + [f32(*s) for s in own_shapes],
        in_specs=[scalar] + [on_chip] * 4 + [any_mem] * 14,
        out_specs=[any_mem] + [on_chip] * 6,
        scratch_shapes=[
            *[pltpu.VMEM(s, t) for s, t in zip(full, types)],
            *[pltpu.VMEM(kind_core(s, k), t) for s, k, t in zip(own_shapes, kinds, types)],
            *[pltpu.VMEM((2, 4) + s, t) for s, t in zip(own_shapes, types)],
            *[pltpu.VMEM((4,) + s, t) for s, t in zip(own_shapes, types)],
            *[pltpu.VMEM((3,) + s, t) for s, t in zip(own_shapes, types)],
            pltpu.VMEM((16, ff), F32),
            pltpu.SemaphoreType.DMA((2,)),
            pltpu.SemaphoreType.DMA((2, 4)),
            pltpu.SemaphoreType.DMA((16,)),
            pltpu.SemaphoreType.DMA((1,)),
            pltpu.SemaphoreType.DMA((24,)),
            pltpu.SemaphoreType.DMA((n_back,)),
        ],
        compiler_params=pltpu.CompilerParams(collective_id=2, has_side_effects=True, vmem_limit_bytes=VMEM_CAP),
        name="backward_scatter",
    )(offs, chars, dcp, vecs, ln3, qkv_f, wo_f, wi_f, wf_f, cv_f, ns, proj, prob, heads, r1, n2, act, gd, mi)
    d_chars, d_vec, d_qkv, d_wo, d_wi, d_wf, d_cv = back
    large = (d_wo, d_qkv, d_wi, d_wf, d_cv, mol, d_chars)
    done = pl.pallas_call(
        functools.partial(place_kernel, tuple(v.shape[0] for v in vectors)),
        out_shape=[f32(*a.shape) for a in large[:-1]] + [f32(tok, d)] + [f32(v.shape[0]) for v in vectors],
        in_specs=[any_mem] * len(large) + [on_chip],
        out_specs=[any_mem] * len(large) + [on_chip] * len(vectors),
        scratch_shapes=[
            *[pltpu.VMEM(a.shape, F32) for a in large],
            pltpu.SemaphoreType.DMA((len(large),)),
            pltpu.SemaphoreType.DMA((len(large) + d // SLOT,)),
        ],
        compiler_params=pltpu.CompilerParams(vmem_limit_bytes=VMEM_CAP),
        name="place",
    )(*large, d_vec)
    d_wo, d_qkv, d_wi, d_wf, d_cv, mol, d_chars = done[: len(large)]
    dv = done[len(large) :]
    return (
        mol,
        d_chars,
        dv[0],
        dv[1],
        d_qkv,
        dv[2],
        d_wo,
        dv[3],
        dv[4],
        dv[5],
        d_wi,
        dv[6],
        d_wf.T,
        dv[7],
        d_cv,
        dv[8],
        dv[9],
        dv[10],
    )


def solution(mesh):
    placed = (
        P(("dp", "mp"), None),
        P(("dp", "mp"), None),
        P(("dp", "mp")),
        P(("dp", "mp")),
        P(("dp", "mp")),
        P(("dp", "mp"), None),
        P(("dp", "mp")),
        P(("dp", "mp"), None),
        P(("dp", "mp")),
        P(("dp", "mp")),
        P(("dp", "mp")),
        P("dp", "mp"),
        P(("dp", "mp")),
        P("mp", "dp"),
        P(("dp", "mp")),
        P("dp", "mp"),
        P(("dp", "mp")),
        P(("dp", "mp")),
        P(("dp", "mp")),
        P(("dp", "mp"), None),
    )
    return jax.shard_map(
        fast_shards if quick_mesh(mesh) else shards,
        mesh=mesh,
        in_specs=placed,
        out_specs=(
            P(("dp", "mp"), None),
            P(("dp", "mp"), None),
            P(("dp", "mp")),
            P(("dp", "mp")),
            P(("dp", "mp"), None),
            P(("dp", "mp")),
            P(("dp", "mp"), None),
            P(("dp", "mp")),
            P(("dp", "mp")),
            P(("dp", "mp")),
            P("dp", "mp"),
            P(("dp", "mp")),
            P("mp", "dp"),
            P(("dp", "mp")),
            P("dp", "mp"),
            P(("dp", "mp")),
            P(("dp", "mp")),
            P(("dp", "mp")),
        ),
        check_vma=False,
    )
```

```python
import functools

import jax
import jax.numpy as jnp
from jax import lax
from jax.experimental import pallas as pl
from jax.experimental.pallas import tpu as pltpu
from jax.sharding import PartitionSpec as P

HEADS = 12
HDIM = 64
KER = 4
WIN = 128


layer_eps = 1e-06


def layer_norm(row_values, gain_vec, shift_vec):
    centred = row_values - jnp.mean(row_values, axis=-1, keepdims=True)
    spread = jnp.mean(centred * centred, axis=-1, keepdims=True)
    return centred * lax.rsqrt(spread + layer_eps) * gain_vec + shift_vec


def gelu_exact(values):
    return jax.nn.gelu(values, approximate=False)


def norm_backward(row_values, gain_vec, shift_vec, grad_out):
    _, pullback = jax.vjp(layer_norm, row_values, gain_vec, shift_vec)
    return pullback(grad_out)


def gelu_backward(values, grad_out):
    _, pullback = jax.vjp(gelu_exact, values)
    return pullback(grad_out)[0]


def three_blocks(rows, fill_value):
    edge = jnp.full_like(rows[:1], fill_value)
    before = jnp.concatenate([edge, rows[:-1]], axis=0)
    after = jnp.concatenate([rows[1:], edge], axis=0)
    return jnp.concatenate([before, rows, after], axis=1)


def fold_blocks(band_grad):
    edge = jnp.zeros_like(band_grad[:1, :WIN])
    from_next = jnp.concatenate([band_grad[1:, :WIN], edge], axis=0)
    from_prev = jnp.concatenate([edge, band_grad[:-1, 2 * WIN :]], axis=0)
    return band_grad[:, WIN : 2 * WIN] + from_next + from_prev


def band_inputs(queries, key_rows, value_rows, seg_row, offset):
    seq_len = queries.shape[0]
    block_count = seq_len // WIN
    win_row = (jnp.arange(seq_len, dtype=jnp.int32) + offset) // WIN
    seg_blk = seg_row.reshape(block_count, WIN)
    win_blk = win_row.reshape(block_count, WIN)
    return (
        queries.reshape(block_count, WIN, HEADS, HDIM),
        three_blocks(key_rows.reshape(block_count, WIN, HEADS, HDIM), 0),
        three_blocks(value_rows.reshape(block_count, WIN, HEADS, HDIM), 0),
        seg_blk,
        win_blk,
        three_blocks(seg_blk, 0),
        three_blocks(win_blk, -1),
    )


def band_scores(query_blk, key_band, seg_blk, win_blk, seg_band, win_band):
    raw_scores = jnp.einsum(
        "bqhd,bkhd->bhqk", query_blk, key_band, preferred_element_type=jnp.float32
    ) * HDIM ** (-0.5)
    allowed = (seg_blk[:, :, None] == seg_band[:, None, :]) & (
        win_blk[:, :, None] == win_band[:, None, :]
    )
    return jnp.where(allowed[:, None], raw_scores, -1e30)


def attend_forward(seq_item):
    queries, key_rows, value_rows, seg_row, offset = seq_item
    seq_len = queries.shape[0]
    query_blk, key_band, val_band, seg_blk, win_blk, seg_band, win_band = band_inputs(
        queries, key_rows, value_rows, seg_row, offset
    )
    scores = band_scores(query_blk, key_band, seg_blk, win_blk, seg_band, win_band)
    row_peak = jnp.max(scores, axis=-1, keepdims=True)
    exp_scores = jnp.exp(scores - row_peak)
    row_total = jnp.sum(exp_scores, axis=-1, keepdims=True)
    prob_low = (exp_scores / row_total).astype(jnp.bfloat16)
    merged = jnp.einsum("bhqk,bkhd->bqhd", prob_low, val_band, preferred_element_type=jnp.float32)
    return (merged.reshape(seq_len, HEADS * HDIM), (row_peak + jnp.log(row_total))[..., 0])


def attend_backward(seq_item):
    queries, key_rows, value_rows, seg_row, offset, log_norm, d_heads = seq_item
    seq_len = queries.shape[0]
    block_count = seq_len // WIN
    score_scale = HDIM ** (-0.5)
    query_blk, key_band, val_band, seg_blk, win_blk, seg_band, win_band = band_inputs(
        queries, key_rows, value_rows, seg_row, offset
    )
    grad_blk = d_heads.reshape(block_count, WIN, HEADS, HDIM)
    scores = band_scores(query_blk, key_band, seg_blk, win_blk, seg_band, win_band)
    prob_blk = jnp.exp(scores - log_norm[..., None])
    d_probs = jnp.einsum("bqhd,bkhd->bhqk", grad_blk, val_band, preferred_element_type=jnp.float32)
    row_dot = jnp.sum(prob_blk * d_probs, axis=-1, keepdims=True)
    d_scores = (prob_blk * (d_probs - row_dot)).astype(jnp.bfloat16)
    d_query = (
        jnp.einsum("bhqk,bkhd->bqhd", d_scores, key_band, preferred_element_type=jnp.float32)
        * score_scale
    )
    d_key_band = (
        jnp.einsum("bhqk,bqhd->bkhd", d_scores, query_blk, preferred_element_type=jnp.float32)
        * score_scale
    )
    d_val_band = jnp.einsum(
        "bhqk,bqhd->bkhd",
        prob_blk.astype(jnp.bfloat16),
        grad_blk,
        preferred_element_type=jnp.float32,
    )
    d_keys = fold_blocks(d_key_band)
    d_vals = fold_blocks(d_val_band)
    return (
        d_query.reshape(seq_len, HEADS * HDIM),
        d_keys.reshape(seq_len, HEADS * HDIM),
        d_vals.reshape(seq_len, HEADS * HDIM),
    )


def shards(
    chars,
    segment_ids,
    window_offsets,
    ln1_gain,
    ln1_bias,
    w_qkv,
    qv_bias,
    w_attn_out,
    attn_out_bias,
    ln2_gain,
    ln2_bias,
    w_ff_in,
    ff_in_bias,
    w_ff_out,
    ff_out_bias,
    conv_weight,
    conv_bias,
    ln3_gain,
    ln3_bias,
    d_molecules,
):
    gathered = (
        lax.all_gather(w_qkv, ("dp", "mp"), axis=0, tiled=True),
        lax.all_gather(w_attn_out, ("dp", "mp"), axis=0, tiled=True),
        lax.all_gather(ln1_gain, ("dp", "mp"), axis=0, tiled=True),
        lax.all_gather(ln1_bias, ("dp", "mp"), axis=0, tiled=True),
        lax.all_gather(qv_bias, ("dp", "mp"), axis=0, tiled=True),
        lax.all_gather(attn_out_bias, ("dp", "mp"), axis=0, tiled=True),
        lax.all_gather(ln2_gain, ("dp", "mp"), axis=0, tiled=True),
        lax.all_gather(ln2_bias, ("dp", "mp"), axis=0, tiled=True),
        lax.all_gather(ff_in_bias, ("dp", "mp"), axis=0, tiled=True),
        lax.all_gather(ff_out_bias, ("dp", "mp"), axis=0, tiled=True),
        lax.all_gather(conv_bias, ("dp", "mp"), axis=0, tiled=True),
        lax.all_gather(ln3_gain, ("dp", "mp"), axis=0, tiled=True),
        lax.all_gather(ln3_bias, ("dp", "mp"), axis=0, tiled=True),
    )
    qkv_full = gathered[0]
    attn_out_full = gathered[1]
    vectors = [vector_arg.astype(jnp.float32) for vector_arg in gathered[2:]]
    (
        gain_one,
        shift_one,
        qv_shift,
        attn_shift,
        gain_two,
        shift_two,
        hidden_shift,
        ff_shift,
        conv_shift,
        gain_three,
        shift_three,
    ) = vectors
    ff_in_part, ff_out_part, conv_part = (
        lax.all_gather(w_ff_in, "dp", axis=0, tiled=True),
        lax.all_gather(w_ff_out, "dp", axis=1, tiled=True),
        lax.all_gather(conv_weight, "dp", axis=0, tiled=True),
    )
    model_width = chars.shape[1]
    tok_rows = chars.shape[0]
    seq_count = segment_ids.shape[0]
    seq_len = segment_ids.shape[1]
    mp_rank = lax.axis_index("mp")
    hidden_part = ff_in_part.shape[1]
    channel_part = conv_part.shape[1]
    inputs = chars.astype(jnp.float32)
    normed_one = layer_norm(inputs, gain_one, shift_one).astype(jnp.bfloat16)
    qkv_shift = jnp.concatenate(
        [qv_shift[:model_width], jnp.zeros((model_width,), jnp.float32), qv_shift[model_width:]]
    )
    projected = (
        jnp.dot(normed_one, qkv_full, preferred_element_type=jnp.float32) + qkv_shift
    ).astype(jnp.bfloat16)
    per_seq = projected.reshape(seq_count, seq_len, 3, HEADS, HDIM)
    queries = per_seq[:, :, 0]
    key_rows = per_seq[:, :, 1]
    value_rows = per_seq[:, :, 2]
    merged, log_norm = lax.map(
        attend_forward, (queries, key_rows, value_rows, segment_ids, window_offsets)
    )
    heads_low = merged.reshape(tok_rows, model_width).astype(jnp.bfloat16)
    resid_one = (
        inputs + jnp.dot(heads_low, attn_out_full, preferred_element_type=jnp.float32) + attn_shift
    )
    normed_two = layer_norm(resid_one, gain_two, shift_two).astype(jnp.bfloat16)
    ff_in_use, ff_out_use, conv_use = (ff_in_part, ff_out_part, conv_part)
    ff_rows_in = lax.all_gather(normed_two, "mp", axis=0, tiled=True)
    hidden_bias = lax.dynamic_slice_in_dim(hidden_shift, mp_rank * hidden_part, hidden_part)
    hidden_pre = jnp.dot(ff_rows_in, ff_in_use, preferred_element_type=jnp.float32) + hidden_bias
    hidden_act = gelu_exact(hidden_pre).astype(jnp.bfloat16)
    ff_sum = lax.psum_scatter(
        jnp.dot(hidden_act, ff_out_use, preferred_element_type=jnp.float32).astype(jnp.bfloat16),
        "mp",
        scatter_dimension=0,
        tiled=True,
    ).astype(jnp.float32)
    resid_two = resid_one + ff_sum + ff_shift
    mol_rows = resid_two.astype(jnp.bfloat16).reshape(tok_rows // KER, KER * model_width)
    mol_group = lax.all_gather(mol_rows, "mp", axis=0, tiled=True)
    channel_bias = lax.dynamic_slice_in_dim(conv_shift, mp_rank * channel_part, channel_part)
    conv_pre = jnp.dot(mol_group, conv_use, preferred_element_type=jnp.float32) + channel_bias
    channel_act = gelu_exact(conv_pre).astype(jnp.bfloat16)
    conv_act = lax.all_to_all(channel_act, "mp", split_axis=0, concat_axis=1, tiled=True)
    act_float = conv_act.astype(jnp.float32)
    molecules = layer_norm(act_float, gain_three, shift_three)
    d_act, d_gain_three, d_shift_three = norm_backward(
        act_float, gain_three, shift_three, d_molecules.astype(jnp.float32)
    )
    d_act_low = d_act.astype(jnp.bfloat16)
    d_act_cols = lax.all_to_all(d_act_low, "mp", split_axis=1, concat_axis=0, tiled=True)
    d_conv_pre = gelu_backward(conv_pre, d_act_cols.astype(jnp.float32)).astype(jnp.bfloat16)
    d_conv_w = jnp.einsum("mk,mc->kc", mol_group, d_conv_pre, preferred_element_type=jnp.float32)
    d_conv_shift = lax.dynamic_update_slice_in_dim(
        jnp.zeros((model_width,), jnp.float32),
        jnp.sum(d_conv_pre.astype(jnp.float32), axis=0),
        mp_rank * channel_part,
        0,
    )
    d_mol = lax.psum_scatter(
        jnp.einsum("mc,kc->mk", d_conv_pre, conv_use, preferred_element_type=jnp.float32).astype(
            jnp.bfloat16
        ),
        "mp",
        scatter_dimension=0,
        tiled=True,
    ).astype(jnp.float32)
    d_resid_two = d_mol.reshape(tok_rows, model_width)
    d_ff_low = d_resid_two.astype(jnp.bfloat16)
    d_ff_shift = jnp.sum(d_ff_low.astype(jnp.float32), axis=0)
    d_ff_rows = lax.all_gather(d_ff_low, "mp", axis=0, tiled=True)
    d_hidden_act = jnp.einsum(
        "gc,fc->gf", d_ff_rows, ff_out_use, preferred_element_type=jnp.float32
    )
    d_ff_out_w = jnp.einsum("gf,gc->fc", hidden_act, d_ff_rows, preferred_element_type=jnp.float32)
    d_hidden = gelu_backward(hidden_pre, d_hidden_act).astype(jnp.bfloat16)
    d_hidden_sum = jnp.sum(d_hidden.astype(jnp.float32), axis=0)
    d_ff_in_w = jnp.einsum("gd,gf->df", ff_rows_in, d_hidden, preferred_element_type=jnp.float32)
    d_hidden_shift = lax.dynamic_update_slice_in_dim(
        jnp.zeros((hidden_shift.shape[0],), jnp.float32), d_hidden_sum, mp_rank * hidden_part, 0
    )
    d_normed_two = lax.psum_scatter(
        jnp.einsum("gf,df->gd", d_hidden, ff_in_use, preferred_element_type=jnp.float32).astype(
            jnp.bfloat16
        ),
        "mp",
        scatter_dimension=0,
        tiled=True,
    ).astype(jnp.float32)
    d_resid_from, d_gain_two, d_shift_two = norm_backward(
        resid_one, gain_two, shift_two, d_normed_two
    )
    d_resid_one = d_resid_two + d_resid_from
    d_attn_low = d_resid_one.astype(jnp.bfloat16)
    d_attn_shift = jnp.sum(d_attn_low.astype(jnp.float32), axis=0)
    d_attn_out_w = jnp.einsum(
        "te,tc->ec", heads_low, d_attn_low, preferred_element_type=jnp.float32
    )
    d_heads_low = jnp.einsum(
        "tc,ec->te", d_attn_low, attn_out_full, preferred_element_type=jnp.float32
    ).astype(jnp.bfloat16)
    d_heads_seq = d_heads_low.reshape(seq_count, seq_len, HEADS, HDIM)
    d_queries, d_keys, d_vals = lax.map(
        attend_backward,
        (queries, key_rows, value_rows, segment_ids, window_offsets, log_norm, d_heads_seq),
    )
    d_projected = jnp.concatenate(
        [
            d_queries.reshape(tok_rows, model_width),
            d_keys.reshape(tok_rows, model_width),
            d_vals.reshape(tok_rows, model_width),
        ],
        axis=1,
    ).astype(jnp.bfloat16)
    d_proj_sum = jnp.sum(d_projected.astype(jnp.float32), axis=0)
    d_qv_shift = jnp.concatenate([d_proj_sum[:model_width], d_proj_sum[2 * model_width :]])
    d_qkv_w = jnp.einsum("td,te->de", normed_one, d_projected, preferred_element_type=jnp.float32)
    d_normed_one = jnp.einsum(
        "te,de->td", d_projected, qkv_full, preferred_element_type=jnp.float32
    )
    d_inputs_from, d_gain_one, d_shift_one = norm_backward(
        inputs, gain_one, shift_one, d_normed_one
    )
    d_chars = d_resid_one + d_inputs_from
    d_ff_in_own, d_ff_out_own, d_conv_own = (
        lax.psum_scatter(
            d_ff_in_w.astype(jnp.bfloat16), "dp", scatter_dimension=0, tiled=True
        ).astype(jnp.float32),
        lax.psum_scatter(
            d_ff_out_w.astype(jnp.bfloat16), "dp", scatter_dimension=1, tiled=True
        ).astype(jnp.float32),
        lax.psum_scatter(
            d_conv_w.astype(jnp.bfloat16), "dp", scatter_dimension=0, tiled=True
        ).astype(jnp.float32),
    )
    owned = (
        lax.psum_scatter(d_qkv_w, ("dp", "mp"), scatter_dimension=0, tiled=True),
        lax.psum_scatter(d_attn_out_w, ("dp", "mp"), scatter_dimension=0, tiled=True),
        lax.psum_scatter(d_gain_one, ("dp", "mp"), scatter_dimension=0, tiled=True),
        lax.psum_scatter(d_shift_one, ("dp", "mp"), scatter_dimension=0, tiled=True),
        lax.psum_scatter(d_qv_shift, ("dp", "mp"), scatter_dimension=0, tiled=True),
        lax.psum_scatter(d_attn_shift, ("dp", "mp"), scatter_dimension=0, tiled=True),
        lax.psum_scatter(d_gain_two, ("dp", "mp"), scatter_dimension=0, tiled=True),
        lax.psum_scatter(d_shift_two, ("dp", "mp"), scatter_dimension=0, tiled=True),
        lax.psum_scatter(d_hidden_shift, ("dp", "mp"), scatter_dimension=0, tiled=True),
        lax.psum_scatter(d_ff_shift, ("dp", "mp"), scatter_dimension=0, tiled=True),
        lax.psum_scatter(d_conv_shift, ("dp", "mp"), scatter_dimension=0, tiled=True),
        lax.psum_scatter(d_gain_three, ("dp", "mp"), scatter_dimension=0, tiled=True),
        lax.psum_scatter(d_shift_three, ("dp", "mp"), scatter_dimension=0, tiled=True),
    )
    return (
        molecules,
        d_chars,
        owned[2],
        owned[3],
        owned[0],
        owned[4],
        owned[1],
        owned[5],
        owned[6],
        owned[7],
        d_ff_in_own,
        owned[8],
        d_ff_out_own,
        owned[9],
        d_conv_own,
        owned[10],
        owned[11],
        owned[12],
    )


NEAR_FIRST = (False, True, False, False, False, False, True, True, False, False, False, False, False, False, True, False, False, False, True, True, True, False)
GATHER_TABLE = (
    ((0, 0), (0, 1), (1, 0), (0, 2), (2, 0), (0, 3), (3, 0), (1, 1), (1, 2), (4, 0), (2, 2),),
    ((1, 3), (0, 4),),
    (),
    ((2, 1),),
    ((3, 2), (0, 5),),
    (),
    ((0, 6),),
    ((2, 3), (1, 4), (1, 5), (0, 7), (3, 1), (4, 2), (0, 8), (4, 1), (1, 6), (5, 2), (0, 9), (3, 3), (4, 3), (0, 10),),
    ((2, 4), (0, 11),),
    ((2, 5), (1, 7), (2, 7), (1, 8), (2, 8), (1, 9),),
    ((2, 6), (1, 10),),
    ((3, 4), (1, 11), (0, 12),),
    ((3, 5), (3, 7),),
    ((4, 4), (0, 13),),
    (),
    ((4, 5), (3, 8), (2, 9), (0, 14),),
    ((3, 6), (1, 12),),
    ((0, 15),),
    ((4, 6), (2, 10), (1, 13),),
    ((0, 16),),
    ((2, 11), (1, 14), (0, 17),),
    ((4, 7), (4, 8), (0, 18),),
    ((3, 9), (1, 16),),
    ((5, 7), (5, 8), (2, 12), (1, 15), (2, 15), (1, 17),),
    ((4, 9), (3, 10), (0, 19),),
    ((3, 11), (2, 13), (1, 18), (0, 20),),
    ((4, 10), (2, 14), (3, 15), (0, 21),),
    ((4, 11), (0, 22),),
    ((3, 12), (2, 16),),
    (),
    ((4, 12), (2, 17), (1, 19), (2, 19),),
    ((3, 13), (1, 22),),
    ((2, 18), (1, 20), (2, 20),),
    ((4, 13), (3, 14), (3, 19),),
    ((4, 15), (3, 16), (1, 21), (2, 21),),
    ((4, 14), (3, 17), (3, 20),),
    ((5, 15), (4, 16),),
    ((4, 17), (3, 21), (2, 22),),
    ((3, 18),),
    ((4, 19),),
    ((4, 18), (4, 20),),
    ((5, 19), (4, 21), (3, 22),),
    ((5, 20),),
    ((5, 21), (4, 22),),
    (),
)
SCATTER_TABLE = (
    ((0, 0), (0, 1),),
    ((0, 2), (0, 3),),
    ((0, 4),),
    ((0, 5),),
    (),
    (),
    (),
    ((1, 0), (1, 1), (1, 2),),
    ((1, 3), (1, 4), (1, 5),),
    (),
    (),
    ((0, 6), (0, 7),),
    ((2, 0),),
    ((2, 1), (0, 8), (0, 9),),
    ((2, 2), (1, 6), (1, 7),),
    ((2, 3), (2, 4), (0, 10), (0, 11),),
    ((2, 5), (1, 8), (1, 9),),
    ((3, 0), (3, 1), (0, 12), (0, 13),),
    ((3, 2), (1, 10), (1, 11),),
    ((2, 6), (2, 7), (0, 14), (0, 15),),
    ((3, 3), (3, 4), (1, 12), (1, 13),),
    ((4, 0), (4, 1), (3, 5), (2, 8), (0, 16), (0, 17),),
    ((1, 14), (1, 15),),
    ((4, 2), (2, 9),),
    (),
    ((2, 10),),
    ((4, 3),),
    ((1, 16),),
    ((2, 11), (1, 17),),
    ((4, 4), (3, 6), (3, 7),),
    ((4, 5), (0, 18),),
    ((2, 12),),
    (),
    ((3, 8), (2, 13),),
    ((4, 6), (2, 14), (1, 18),),
    ((4, 7), (3, 9), (2, 15),),
    ((4, 8), (3, 10), (2, 16), (0, 19),),
    ((3, 11),),
    ((3, 12), (2, 17),),
    ((4, 9), (3, 13), (3, 14), (1, 19),),
    ((4, 10), (4, 11), (3, 15), (2, 18), (0, 20),),
    ((4, 12), (3, 16), (3, 17),),
    ((4, 13),),
    ((4, 14), (2, 19), (1, 20),),
    ((4, 15), (3, 18), (0, 21),),
    ((4, 16),),
    ((4, 17),),
    ((3, 19),),
    (),
    (),
    ((1, 21),),
    (),
    ((2, 20),),
    (),
    (),
    ((4, 18),),
    ((0, 22), (4, 19), (2, 21), (3, 20), (1, 22), (3, 21), (2, 22), (4, 20), (3, 22), (4, 21), (4, 22),),
)
HALF = 0.5
ERFC_P = 0.3
ERFC_Q = (
    0.16918934881687164,
    0.17069095373153687,
    0.1485210806131363,
    0.2141820192337036,
    -0.09282728284597397,
    0.5449684858322144,
    -0.5097734332084656,
    0.4843021035194397,
    -0.12925326824188232,
)
BF = jnp.bfloat16
F32 = jnp.float32
MESH_ID = pl.DeviceIdType.MESH
ALL = slice(None)
LINKS = ("z1", "z2", "z3", "x", "y", "c")
VMEM_CAP = 63 * 2**20
SLOT = 128
KINDS = (0, 2, 2, 1, 1, 1)
FF_ROWS = 512


def nn(lhs, rhs):
    return lax.dot_general(lhs, rhs, (((1,), (0,)), ((), ())), preferred_element_type=F32)


def nt(lhs, rhs):
    return lax.dot_general(lhs, rhs, (((1,), (1,)), ((), ())), preferred_element_type=F32)


def tn(lhs, rhs):
    return lax.dot_general(lhs, rhs, (((0,), (0,)), ((), ())), preferred_element_type=F32)


def gelu_pair(v):
    size = jnp.abs(v)
    t = 1.0 / (1.0 + (ERFC_P * 0.7071067811865476) * size)
    q = ERFC_Q[-1]
    for coef in ERFC_Q[-2::-1]:
        q = q * t + coef
    bell = jnp.exp(-0.5 * (v * v))
    tail = (HALF * bell) * (q * t)
    phi = jnp.where(v >= 0, 1.0 - tail, tail)
    return v * phi, phi + v * (bell * 0.3989422804014327)


def norm_stats(v):
    mean = jnp.mean(v, axis=-1, keepdims=True)
    cen = v - mean
    r = lax.rsqrt(jnp.mean(cen * cen, axis=-1, keepdims=True) + layer_eps)
    return cen * r, r


def norm_grad(vhat, r, t):
    m1 = jnp.mean(t, axis=-1, keepdims=True)
    m2 = jnp.mean(t * vhat, axis=-1, keepdims=True)
    return r * (t - m1 - vhat * m2)


def head_masks(rows, scale):
    lane = lax.broadcasted_iota(jnp.int32, (rows, 128), 1)
    low = jnp.where(lane < HDIM, scale, 0.0).astype(BF)
    high = jnp.where(lane < HDIM, 0.0, scale).astype(BF)
    return low, high


def split_heads(pair, masks):
    return jnp.concatenate([pair * masks[0], pair * masks[1]], axis=0)


def vector_masks(width, count, nrow):
    col = lax.broadcasted_iota(jnp.int32, (SLOT, width), 1).astype(F32)
    row = lax.broadcasted_iota(jnp.int32, (SLOT, width), 0).astype(F32)
    pick = jnp.where(col - jnp.floor((col + 0.5) * (1.0 / count)) * count == row, 1.0, 0.0).astype(BF)
    col = lax.broadcasted_iota(jnp.int32, (nrow, width), 1).astype(F32)
    row = lax.broadcasted_iota(jnp.int32, (nrow, width), 0).astype(F32)
    return pick, jnp.floor((col + 0.5) * (1.0 / count)) == row


class Place:
    def __init__(self):
        dp = lax.axis_index("dp")
        self.x = lax.axis_index("mp")
        self.z, self.y, self.c = lax.div(dp, 4), lax.rem(lax.div(dp, 2), 2), lax.rem(dp, 2)
        z, y, c, x = self.z, self.y, self.c, self.x
        self.nx, self.ny, self.nc = 1 - x, 1 - y, 1 - c
        self.at = [c * 0 + k for k in range(3)]
        self.far_z = {1: z + 1 - 2 * lax.rem(z, 2), 2: lax.rem(z + 2, 4), 3: 3 - z}
        at = lambda zz, yy, cc, xx: (zz * 4 + yy * 2 + cc, xx)
        self.peer = {
            "z1": at(self.far_z[1], y, c, x),
            "z2": at(self.far_z[2], y, c, x),
            "z3": at(self.far_z[3], y, c, x),
            "x": at(z, y, c, 1 - x),
            "y": at(z, 1 - y, c, x),
            "c": at(z, y, 1 - c, x),
        }

    def barrier(self):
        sem = pltpu.get_barrier_semaphore()
        for peer in self.peer.values():
            pl.semaphore_signal(sem, inc=1, device_id=peer, device_id_type=MESH_ID)
        pl.semaphore_wait(sem, len(self.peer))


def rows_of(ref, xs):
    if isinstance(xs, slice):
        return xs
    half = ref.shape[-2] // 2
    return pl.ds(pl.multiple_of(xs * half, 8), half)


def block(ref, kind, zs, ys, cs, xs, cut):
    if kind == 0:
        return ref.at[(zs, ys, cs, xs) + cut]
    if kind == 1:
        return ref.at[(xs, zs, ys, cs) + cut]
    return ref.at[zs, ys, cs, rows_of(ref, xs), cut[1]]


class Sends:
    STEPS = ("z", "a", "b", "c", "w")

    def __init__(self, place, send_sem, recv_sem):
        self.place, self.send_sem, self.recv_sem = place, send_sem, recv_sem
        self.copies, self.waits = {}, {}
        self.live = False

    def copy(self, t, i, step, src, dst, link):
        out = self.STEPS.index("a" if step == "w" else step)
        return pltpu.make_async_remote_copy(
            src_ref=src,
            dst_ref=dst,
            send_sem=self.send_sem.at[4 * t + out],
            recv_sem=self.recv_sem.at[5 * i + self.STEPS.index(step)],
            device_id=self.place.peer[link],
            device_id_type=MESH_ID,
        )

    def go(self, t, i, step, part, src, dst, link):
        if self.live:
            self.copies[i, step, part].start()
        else:
            self.copies[i, step, part] = self.copy(t, i, step, src, dst, link)

    def got(self, t, i, step, all_of):
        if self.live:
            self.waits[i, step].wait_recv()
        else:
            self.waits[i, step] = self.copy(t, i, step, all_of, all_of, "c")

    def sent(self, t, sizes):
        for step, view in sizes.items():
            self.copy(t, 0, step, view, view, "c").wait_send()


def union(cuts):
    if cuts[1] is None:
        return cuts[0]
    return tuple(p if p == q else slice(p.start, q.stop) for p, q in zip(*cuts))


def order(half):
    return ("x", "y") if half == 0 else ("y", "x")


def gather_stage(sends, stage, i, t, kind, own, full, cuts, near_first):
    p = sends.place
    z, y, c, x = p.z, p.y, p.c, p.x
    whole = union(cuts)
    three = block(full, kind, slice(0, 3), y, c, x, whole)
    size = {
        "z": three,
        "w": three,
        "a": block(full, kind, z if near_first else ALL, y, c, x, whole),
        "b": block(full, kind, ALL, y, c, ALL, whole),
        "c": block(full, kind, ALL, ALL, c, ALL, whole),
    }
    waits = ((), ("a",), ("z",), ("w",), ("b",), ("c",)) if near_first else ((), ("z",), ("a",), ("b",), ("c",))
    if stage >= len(waits):
        return
    for step in waits[stage]:
        sends.got(t, i, step, size[step])
    for h, cut in enumerate(cuts):
        if cut is None:
            continue
        a, b = order(h)
        mine = block(full, kind, z, y, c, x, cut)
        line = block(full, kind, ALL, y, c, x, cut)
        if h == 0:
            next_one, next_line = block(full, kind, z, y, c, p.nx, cut), block(full, kind, ALL, y, c, p.nx, cut)
            far = block(full, kind, ALL, p.ny, c, ALL, cut)
        else:
            next_one, next_line = block(full, kind, z, p.ny, c, x, cut), block(full, kind, ALL, p.ny, c, x, cut)
            far = block(full, kind, ALL, ALL, c, p.nx, cut)
        own_z = [("z", k, own.at[cut], mine, k) for k in ("z1", "z2", "z3")]
        line_b, line_c = ("b", 1, line, line, b), ("c", 1, line, line, "c")
        next_bc = [("b", 2, next_line, next_line, b), ("c", 2, next_line, next_line, "c")]
        far_c = [("c", 3, far, far, "c")]
        if near_first:
            next_z = [("w", k, next_one, next_one, k) for k in ("z1", "z2", "z3")]
            steps = ([("a", 1, own.at[cut], mine, a)] + own_z, next_z, [line_b, line_c], next_bc, far_c, [])
        else:
            steps = (own_z, [("a", 1, line, line, a), line_b, line_c], next_bc, far_c, [])
        for step, part, src, dst, link in steps[stage]:
            sends.go(t, i, step, (h, part), src, dst, link)


def col_cuts(cols, parts):
    step = cols // (2 * parts)
    return [((ALL, slice(2 * step * i, 2 * step * i + step)), (ALL, slice(2 * step * i + step, 2 * step * (i + 1)))) for i in range(parts)]


def row_cuts(rows, parts):
    step = rows // (2 * parts)
    return [((slice(2 * step * i, 2 * step * i + step), ALL), (slice(2 * step * i + step, 2 * step * (i + 1)), ALL)) for i in range(parts)]


def block_cuts(rows, cols, col_parts, row_parts):
    step, width = rows // (2 * row_parts), cols // col_parts
    cuts = []
    for q in range(col_parts):
        lanes = slice(q * width, q * width + width)
        for r in range(row_parts):
            low = 2 * step * r
            cuts.append(((slice(low, low + step), lanes), (slice(low + step, low + 2 * step), lanes)))
    return cuts


def gather_plan(shapes):
    plan = [(0, 0, ((ALL, ALL), None))]
    plan += [(1, 2, c) for c in col_cuts(shapes[1][1], 3)]
    plan += [(2, 2, c) for c in col_cuts(shapes[2][1], 1)]
    plan += [(3, 1, c) for c in col_cuts(shapes[3][1], 6)]
    plan += [(4, 1, c) for c in col_cuts(shapes[4][1], 6)]
    plan += [(5, 1, c) for c in block_cuts(shapes[5][0], shapes[5][1], 3, 2)]
    return [piece + (near,) for piece, near in zip(plan, (False,) + NEAR_FIRST)]


class Ticks:
    def __init__(self, table, stage_fn):
        self.table, self.stage_fn, self.count = table, stage_fn, 0

    def run(self, k):
        for s, i in self.table[k]:
            self.stage_fn(s, i)

    def point(self):
        self.count += 1
        self.run(self.count - 1)

    def within(self, index, values):
        for value in values:
            if self.table[self.count]:
                pl.when(index == value)(functools.partial(self.run, self.count))
            self.count += 1


def forward_kernel(dims, sizes, *refs):
    (off_ref, seg_ref, x_ref, dmol_ref, vec_own, qkv_own, wo_own, wi_own, wf_own, cv_own) = refs[:10]
    outs = refs[10:28]
    (mol_out, vec_out, ln3_out, dcp_out, qkv_o, wo_o, wi_o, wf_o, cv_o, nst_o, proj_o, prob_o, headst_o, r1_o, n2t_o, act_o, gd_o, mit_o) = outs
    (vec_g, qkv_g, wo_g, wi_g, wf_g, cv_g, vec_f, vecs, pad, ns, proj, prob, heads, r1, n2, act, gd, r2, molin, local_sem, out_sem, send_sem, recv_sem) = refs[28:]
    tok, d, ff = dims
    win = WIN
    nw = tok // win + 1
    half_ff = ff // 2
    mols = tok // KER
    place = Place()
    owns = (vec_own, qkv_own, wo_own, wi_own, wf_own, cv_own)
    fulls = (vec_g, qkv_g, wo_g, wi_g, wf_g, cv_g)
    plan = gather_plan([o.shape for o in owns])
    kinds = KINDS
    place.barrier()
    sends = Sends(place, send_sem, recv_sem)
    local = []
    for i, (own, full, kind) in enumerate(zip(owns, fulls, kinds)):
        copy = pltpu.make_async_copy(own, block(full, kind, place.z, place.y, place.c, place.x, (ALL, ALL)), local_sem.at[i])
        copy.start()
        local.append(copy)

    def comm_stage(stage, i):
        t, kind, cuts, near_first = plan[i]
        if sends.live and stage == (2 if near_first else 1) and (i == 0 or plan[i - 1][0] != t):
            local[t].wait()
        gather_stage(sends, stage, i, t, kind, owns[t], fulls[t], cuts, near_first)

    for stage in range(6):
        for i in range(len(plan)):
            comm_stage(stage, i)
    sends.live = True
    ticks = Ticks(GATHER_TABLE, comm_stage)

    out_copies = []

    def flush(src, dst):
        copy = pltpu.make_async_copy(src, dst, out_sem.at[len(out_copies)])
        copy.start()
        out_copies.append(copy)
        return copy

    def unpack_vectors():
        nrow = vec_f.shape[0] // 16
        vec_f[...] = vec_g[...].reshape(vec_f.shape).astype(F32)
        for width, count in sorted(set(sizes)):
            pick, mine = vector_masks(width, count, nrow)
            for v in [i for i, s in enumerate(sizes) if s == (width, count)]:
                spread = nn(vec_f[pl.ds(v, nrow, stride=16), :].astype(BF), pick)
                vecs[v : v + 1, :width] = jnp.sum(jnp.where(mine, spread, 0.0), axis=0, keepdims=True)

    def vec(v, lo, hi):
        return vecs[v : v + 1, lo:hi]

    offset = off_ref[0]

    ticks.point()
    unpack_vectors()
    ticks.point()
    flush(vecs, vec_out)

    pad[0:win, :] = jnp.zeros((win, d), BF)
    pad[win + tok : 2 * win + tok, :] = jnp.zeros((win, d), BF)

    @pl.loop(0, tok // 128)
    def _(b):
        rows = pl.ds(pl.multiple_of(b * 128, 128), 128)
        vhat, _ = norm_stats(x_ref[rows, :].astype(F32))
        pad[pl.ds(pl.multiple_of(b * 128 + win, 128), 128), :] = (vhat * vec(0, 0, d) + vec(1, 0, d)).astype(BF)
        ticks.within(b, (1, 3, 5, 7))

    ri = lax.broadcasted_iota(jnp.int32, (win, 2 * win), 0)
    rj = lax.broadcasted_iota(jnp.int32, (win, 2 * win), 1)
    shift_in = jnp.where(rj == ri + (win - offset), 1.0, 0.0).astype(BF)
    shift_out = jnp.where(rj == ri + offset, 1.0, 0.0).astype(BF)

    @pl.loop(0, nw)
    def _(w):
        at = pl.multiple_of(w * win, win)
        ns[pl.ds(at, win), :] = nn(shift_in, pad[pl.ds(at, 2 * win), :]).astype(BF)
        ticks.within(w, (4,))

    ns_t = act.at[0:d, 0 : nw * win]

    @pl.loop(0, nw // 3)
    def _(b):
        rows = pl.ds(pl.multiple_of(b * 384, 128), 384)
        ns_t[:, rows] = ns[rows, :].T

    ns_t_copy = flush(ns_t, nst_o)

    ticks.point()
    flush(qkv_g, qkv_o)
    wq = qkv_g.reshape(d, 3 * d)
    for blk3 in range(3):
        bias_row = None if blk3 == 1 else vec(2, (blk3 // 2) * d, (blk3 // 2) * d + d)

        @pl.loop(0, nw // 3)
        def _(b):
            rows = pl.ds(pl.multiple_of(b * 384, 128), 384)
            for n0 in range(0, d, 256):
                val = nn(ns[rows, :], wq[:, blk3 * d + n0 : blk3 * d + n0 + 256])
                if bias_row is not None:
                    val = val + bias_row[:, n0 : n0 + 256]
                proj[rows, blk3 * d + n0 : blk3 * d + n0 + 256] = val.astype(BF)

        ticks.point()

    proj_copy = flush(proj, proj_o)

    qmask = head_masks(win, HDIM**-0.5)
    vmask = head_masks(win, 1.0)
    seg_row = jnp.concatenate([seg_ref[0:1, :].astype(F32), jnp.full((1, win), -1.0, F32)], axis=1)
    seg_row = pltpu.roll(jnp.broadcast_to(seg_row, (8, tok + win)), offset, axis=1)
    segs = vec_f
    for w in range(nw):
        segs[w * 8 : w * 8 + 8, 0:win] = seg_row[:, w * win : (w + 1) * win]

    @pl.loop(0, nw)
    def _(w):
        rows = pl.ds(pl.multiple_of(w * win, win), win)
        seg_q = jnp.broadcast_to(segs[pl.ds(pl.multiple_of(w * 8, 8), 8), 0:win][0:1], (win, win))
        same = seg_q == seg_q.T
        same2 = jnp.concatenate([same, same], axis=1)
        for pr in range(HEADS // 2):
            lanes = slice(pr * 128, pr * 128 + 128)
            q2 = proj[rows, pr * 128 : pr * 128 + 128]
            k2 = proj[rows, d + pr * 128 : d + pr * 128 + 128]
            v2 = proj[rows, 2 * d + pr * 128 : 2 * d + pr * 128 + 128]
            s = jnp.where(same2, nt(k2, split_heads(q2, qmask)), -1e30)
            e = jnp.exp(s - jnp.max(s, axis=0, keepdims=True))
            pb = (e * (1.0 / jnp.sum(e, axis=0, keepdims=True))).astype(BF)
            prob[w, pr] = pb
            stacked = jnp.concatenate([pb[:, :win], pb[:, win:]], axis=0)
            pad[rows, lanes] = tn(stacked, split_heads(v2, vmask)).astype(BF)
        ticks.within(w, range(nw))

    prob_copy = flush(prob, prob_o)

    flush(wo_g, wo_o)
    wo = wo_g.reshape(d, d)
    proj_copy.wait()
    heads_t = proj.at[0:d, 0:tok]
    n2_t = proj.at[0:d, tok : 2 * tok]

    @pl.loop(0, tok // 128)
    def _(b):
        at = pl.multiple_of(b * 128, 128)
        hb = nn(shift_out, pad[pl.ds(at, 2 * win), :]).astype(BF)
        heads[pl.ds(at, 128), :] = hb
        heads_t[:, pl.ds(at, 128)] = hb.T

    ticks.point()

    @pl.loop(0, tok // 256)
    def _(b):
        rows = pl.ds(pl.multiple_of(b * 256, 256), 256)
        val = x_ref[rows, :].astype(F32) + nn(heads[rows, :], wo[...]) + vec(3, 0, d)
        r1[rows, :] = val
        vhat, _ = norm_stats(val)
        low = (vhat * vec(4, 0, d) + vec(5, 0, d)).astype(BF)
        n2[rows, :] = low
        n2_t[:, rows] = low.T
        ticks.within(b, (0, 1, 2))

    flush(heads_t, headst_o)
    flush(r1, r1_o)
    flush(n2_t, n2t_o)
    ns_t_copy.wait()

    wi = wi_g.reshape(2, d, half_ff)

    @pl.loop(0, half_ff // 256)
    def _(j):
        cols = pl.ds(pl.multiple_of(j * 256, 256), 256)
        base = ticks.count
        for hx in range(2):
            for q in range(half_ff // 256):
                if ticks.table[base + 2 * q + hx]:
                    pl.when(j == q)(functools.partial(ticks.run, base + 2 * q + hx))
            ocols = pl.ds(pl.multiple_of(hx * half_ff + j * 256, 256), 256)
            bias_row = vecs[6:7, ocols]
            for m in range(0, tok, 256):
                pre = nn(n2[m : m + 256, :], wi[hx, :, cols]) + bias_row
                g, dg = gelu_pair(pre)
                act[m : m + 256, ocols] = g.astype(BF)
                gd[m : m + 256, ocols] = dg.astype(BF)
        ticks.count = base + 2 * (half_ff // 256)

    flush(act, act_o)
    flush(gd, gd_o)

    ticks.point()
    flush(wi_g, wi_o)
    flush(wf_g, wf_o)
    wf = wf_g.reshape(2, d, half_ff)

    @pl.loop(0, tok // 256)
    def _(b):
        rows = pl.ds(pl.multiple_of(b * 256, 256), 256)
        for n0 in range(0, d, 256):
            cols = slice(n0, n0 + 256)
            val = nt(act[rows, 0:half_ff], wf[0, cols, :]) + nt(act[rows, half_ff:], wf[1, cols, :])
            val = r1[rows, cols] + val + vec(7, n0, n0 + 256)
            r2[n0 // 128, rows, :] = val[:, :128]
            r2[n0 // 128 + 1, rows, :] = val[:, 128:]
        ticks.within(b, range(4))

    for k in range(KER):
        for q in range(d // 128):
            molin[:, k * d + q * 128 : k * d + q * 128 + 128] = r2[q, pl.ds(k, mols, stride=KER), :].astype(BF)

    prob_copy.wait()
    for k in range(KER):
        for q in range(d // 128):
            prob[k, q] = molin[:, k * d + q * 128 : k * d + q * 128 + 128].T
    flush(prob.at[0:KER], mit_o)
    cv = cv_g.reshape(2, KER * d, d // 2)
    parts = {}
    for q in range(3):
        ticks.point()
        for hx in range(2):
            at = hx * (d // 2) + q * 128
            pre = nn(molin[...], cv[hx, :, q * 128 : q * 128 + 128]) + vec(8, at, at + 128)
            parts[at] = gelu_pair(pre)
    flush(cv_g, cv_o)
    g = jnp.concatenate([parts[at][0] for at in range(0, d, 128)], axis=1)
    dg = jnp.concatenate([parts[at][1] for at in range(0, d, 128)], axis=1)
    vhat, r = norm_stats(g.astype(BF).astype(F32))
    mol_out[...] = vhat * vec(9, 0, d) + vec(10, 0, d)
    cot = dmol_ref[...].astype(F32)
    ln3_out[0:1, :] = jnp.sum(cot * vhat, axis=0, keepdims=True)
    ln3_out[1:2, :] = jnp.sum(cot, axis=0, keepdims=True)
    da = norm_grad(vhat, r, cot * vec(9, 0, d)).astype(BF).astype(F32)
    dcp_out[...] = (da * dg).astype(BF)
    for t, (full, kind) in enumerate(zip(fulls, kinds)):
        pick = functools.partial(block, full, kind, cut=(ALL, ALL))
        z, y, c, x = place.z, place.y, place.c, place.x
        sends.sent(t, {"z": pick(slice(0, 3), y, c, x), "a": pick(ALL, y, c, x), "b": pick(ALL, y, c, ALL), "c": pick(ALL, ALL, c, ALL)})
    for copy in out_copies:
        if not any(copy is early for early in (ns_t_copy, proj_copy, prob_copy)):
            copy.wait()


def scatter_plan(shapes):
    plan = [(5, 1, c) for c in row_cuts(shapes[5][0], 6)]
    for wf_cut, wi_cut in zip(col_cuts(shapes[4][1], 6), col_cuts(shapes[3][1], 6)):
        plan += [(4, 1, wf_cut), (3, 1, wi_cut)]
    plan += [(2, 2, c) for c in col_cuts(shapes[2][1], 1)]
    plan += [(1, 2, c) for c in col_cuts(shapes[1][1], 3)]
    plan += [(0, 0, ((ALL, ALL), None))]
    return plan


def backward_kernel(dims, sizes, *refs):
    (off_ref, x_i, dcp_ref, vecs, ln3_ref, qkv_i, wo_i, wi_i, wf_i, cv_i, nst_i, proj_i, prob_i, headst_i, r1_i, n2t_i, act_i, gd_i, mit_i) = refs[:19]
    dch_out = refs[19]
    own_outs = refs[20:26]
    grads = refs[26:32]
    from_core = refs[32:38]
    from_b = refs[38:44]
    from_a = refs[44:50]
    from_z = refs[50:56]
    sums, res_sem, tile_sem, load_sem, out_sem, send_sem, recv_sem = refs[56:]
    tok, d, ff = dims
    win = WIN
    nw = tok // win + 1
    half_ff = ff // 2
    mols = tok // KER
    place = Place()
    z, y, c, x = place.z, place.y, place.c, place.x
    plan = scatter_plan([o.shape for o in own_outs])
    place.barrier()
    sends = Sends(place, send_sem, recv_sem)

    def add_blocks(dst_of, src_of):
        if not sends.live:
            return

        dst, src = dst_of(ALL), src_of(ALL)
        dst[...] = dst[...] + src[...]

    def comm_stage(stage, i):
        t, kind, cuts = plan[i]
        g, rc, rb, ra, rz, own = grads[t], from_core[t], from_b[t], from_a[t], from_z[t], own_outs[t]

        def core_blk(zs, ys, xs, cut):
            if kind == 2:
                return rc.at[zs, ys, rows_of(rc, xs), cut[1]]
            return rc.at[(zs, ys, xs) + cut] if kind == 0 else rc.at[(xs, zs, ys) + cut]

        whole = union(cuts)
        waits = {
            1: ("c", core_blk(ALL, ALL, ALL, whole)),
            2: ("b", rb.at[(ALL, ALL) + whole]),
            3: ("a", ra.at[(ALL,) + whole]),
            4: ("z", rz.at[(ALL,) + whole]),
        }
        if stage > 0:
            sends.got(t, i, *waits[stage])
        for h, cut in enumerate(cuts):
            if cut is None:
                continue
            a, b = order(h)
            if stage == 0:
                sends.go(t, i, "c", h, block(g, kind, ALL, ALL, place.nc, ALL, cut), core_blk(ALL, ALL, ALL, cut), "c")
            elif stage == 1:
                for far in (1, 0):
                    for o in range(2):
                        ys, xs = (place.ny if far else y, place.at[o]) if h == 0 else (place.at[o], place.nx if far else x)
                        add_blocks(lambda zz: block(g, kind, zz, ys, c, xs, cut), lambda zz: core_blk(zz, ys, xs, cut))
                        if far:
                            sends.go(t, i, "b", (h, o), block(g, kind, ALL, ys, c, xs, cut), rb.at[(place.at[o], ALL) + cut], b)
            elif stage == 2:
                near, other = (x, place.nx) if h == 0 else (y, place.ny)
                for far in (1, 0):
                    o = other if far else near
                    ys, xs = (y, o) if h == 0 else (o, x)
                    add_blocks(lambda zz: block(g, kind, zz, ys, c, xs, cut), lambda zz: rb.at[(o, zz) + cut])
                    if far:
                        sends.go(t, i, "a", h, block(g, kind, ALL, ys, c, xs, cut), ra.at[(ALL,) + cut], a)
            elif stage == 3:
                add_blocks(lambda zz: block(g, kind, zz, y, c, x, cut), lambda zz: ra.at[(zz,) + cut])
                for q in (1, 2, 3):
                    sends.go(t, i, "z", (h, q), block(g, kind, place.far_z[q], y, c, x, cut), rz.at[(place.at[q - 1],) + cut], "z%d" % q)
            elif sends.live:
                total = block(g, kind, z, y, c, x, cut)[...].astype(F32)
                for q in range(3):
                    total = total + rz.at[(place.at[q],) + cut][...].astype(F32)
                if t != 1:
                    own[cut] = total
                    continue
                for q in range(0, cut[1].stop - cut[1].start, 128):
                    part, r = divmod(cut[1].start + q, d)
                    to = (r // 256) * d + part * 256 + r % 256
                    own[:, to : to + 128] = total[:, q : q + 128]

    for stage in range(5):
        for i in range(len(plan)):
            comm_stage(stage, i)
    sends.live = True
    ticks = Ticks(SCATTER_TABLE, comm_stage)
    state = {"load": 0}

    def load(src, dst):
        copy = pltpu.make_async_copy(src, dst, load_sem.at[state["load"]])
        state["load"] += 1
        copy.start()
        return copy

    def vec(v, lo, hi):
        return vecs[v : v + 1, lo:hi]

    offset = off_ref[0]
    ri = lax.broadcasted_iota(jnp.int32, (win, 2 * win), 0)
    rj = lax.broadcasted_iota(jnp.int32, (win, 2 * win), 1)
    shift_in = jnp.where(rj == ri + (win - offset), 1.0, 0.0).astype(BF)
    shift_out = jnp.where(rj == ri + offset, 1.0, 0.0).astype(BF)
    sums[...] = jnp.zeros_like(sums)
    sums[9:10, 0:d] = ln3_ref[0:1, :]
    sums[10:11, 0:d] = ln3_ref[1:2, :]
    sums[8:9, 0:d] = jnp.sum(dcp_ref[...].astype(F32), axis=0, keepdims=True)
    g_vec, g_qkv, g_wo, g_wi, g_wf, g_cv = grads
    g_cv2 = g_cv.reshape(2, KER * d, d // 2)
    g_wi2 = g_wi.reshape(2, d, half_ff)
    g_wf2 = g_wf.reshape(2, d, half_ff)

    def rows_of_dres(dres, rows):
        return jnp.concatenate([dres[q, rows, :] for q in range(d // 128)], axis=1)

    def set_dres(dres, rows, val):
        for q in range(d // 128):
            dres[q, rows, :] = val[:, q * 128 : q * 128 + 128]

    def whole(dres, dpad):
        def conv_part(cv, mi):
            loads = [load(mit_i, mi), load(cv_i, cv)]
            cv2 = cv.reshape(2, KER * d, d // 2)
            loads[0].wait()
            for kk in range(KER):
                val = nn(mi[kk].reshape(d, mols), dcp_ref[...]).astype(BF)
                g_cv2[0, kk * d : kk * d + d, :] = val[:, : d // 2]
                g_cv2[1, kk * d : kk * d + d, :] = val[:, d // 2 :]

            ticks.point()
            loads[1].wait()
            for kk in range(KER):
                for n0 in range(0, d, 256):
                    rows = slice(kk * d + n0, kk * d + n0 + 256)
                    val = nt(dcp_ref[:, : d // 2], cv2[0, rows, :]) + nt(dcp_ref[:, d // 2 :], cv2[1, rows, :])
                    dres[n0 // 128, pl.ds(kk, mols, stride=KER), :] = val[:, :128]
                    dres[n0 // 128 + 1, pl.ds(kk, mols, stride=KER), :] = val[:, 128:]
                ticks.point()

        pl.run_scoped(conv_part, pltpu.VMEM(cv_i.shape, BF), pltpu.VMEM(mit_i.shape, BF))

        def attn_part(proj, ns_t, dn1, loads, wqkv):
            proj_loads, ns_load = loads[:-1], loads[-1]
            qkv_load = load(qkv_i, wqkv)
            qmask = head_masks(win, HDIM**-0.5)
            vmask = head_masks(win, 1.0)
            g_qkv2 = g_qkv.reshape(d, 3 * d)
            wqkv2 = wqkv.reshape(d, 3 * d)

            def core_part(prob):
                n3 = nw // 3

                def prob_copy(i):
                    g, b, slot = lax.div(i, n3), lax.rem(i, n3), lax.rem(i, 2)
                    return pltpu.make_async_copy(prob_i.at[pl.ds(3 * b, 3), pl.ds(2 * g, 2)], prob.at[slot], res_sem.at[slot])

                prob_copy(0).start()
                ns_load.wait()
                base = ticks.count

                @pl.loop(0, d // 256)
                def _(g):
                    lq, lk, lv = [pl.ds(pl.multiple_of(r * d + g * 256, 256), 256) for r in range(3)]

                    @pl.loop(0, n3)
                    def _(b):
                        i = g * n3 + b
                        for q in range(n3):
                            pl.when(i == q)(proj_loads[q].wait)
                        prob_copy(i).wait()

                        @pl.when(i + 1 < n3 * (d // 256))
                        def _():
                            prob_copy(i + 1).start()

                        for u in range(3):
                            at = pl.multiple_of(b * (3 * win) + u * win, win)
                            rows = pl.ds(at, win)
                            dhw = nn(shift_in, dpad[pl.ds(at, 2 * win), lq]).astype(BF)
                            q4, k4, v4 = proj[rows, lq], proj[rows, lk], proj[rows, lv]
                            new = [[], [], []]
                            for pr in range(2):
                                lanes = slice(pr * 128, pr * 128 + 128)
                                q2, k2, v2 = q4[:, lanes], k4[:, lanes], v4[:, lanes]
                                pb = prob[lax.rem(i, 2), u, pr]
                                dbd = split_heads(dhw[:, lanes], vmask)
                                dp = nt(v2, dbd)
                                pf = pb.astype(F32)
                                ds = (pf * (dp - jnp.sum(pf * dp, axis=0, keepdims=True))).astype(BF)
                                stacked = jnp.concatenate([ds[:, :win], ds[:, win:]], axis=0)
                                new[0].append(tn(stacked, split_heads(k2, qmask)).astype(BF))
                                new[1].append(nn(ds, split_heads(q2, qmask)).astype(BF))
                                new[2].append(nn(pb, dbd).astype(BF))
                            for lanes, parts in zip((lq, lk, lv), new):
                                proj[rows, lanes] = jnp.concatenate(parts, axis=1)
                        for q in range(3):
                            for bb in range(n3):
                                if ticks.table[base + q * (n3 + 1) + bb]:
                                    pl.when(i == q * n3 + bb)(functools.partial(ticks.run, base + q * (n3 + 1) + bb))

                    for r, cols in enumerate((lq, lk, lv)):
                        to = pl.ds(pl.multiple_of(g * d + r * 256, 256), 256)
                        part = proj[:, cols]
                        if r != 1:
                            into = pl.ds(pl.multiple_of((r // 2) * d + g * 256, 256), 256)
                            sums[2:3, into] = jnp.sum(part.astype(F32), axis=0, keepdims=True)
                        g_qkv2[:, to] = nn(ns_t[...], part).astype(BF)
                    for q in range(3):
                        pl.when(g == q)(functools.partial(ticks.run, base + q * (n3 + 1) + n3))

                ticks.count = base + 3 * (n3 + 1)

            pl.run_scoped(core_part, pltpu.VMEM((2, 3, 2, win, 2 * win), BF))
            x_rows = dpad.at[0:tok]
            x_load = load(x_i, x_rows)
            qkv_load.wait()

            @pl.loop(0, nw // 3)
            def _(b):
                rows = pl.ds(pl.multiple_of(b * 384, 128), 384)
                for n0 in range(0, d, 256):
                    dn1[rows, n0 : n0 + 256] = nt(proj[rows, :], wqkv2[n0 : n0 + 256, :])
                ticks.within(b, range(3))

            x_load.wait()

            @pl.loop(0, tok // 128)
            def _(b):
                at = pl.multiple_of(b * 128, 128)
                rows = pl.ds(at, 128)
                both = pl.ds(at, 2 * win)
                high = dn1[both, :].astype(BF)
                cot = nn(shift_out, high) + nn(shift_out, (dn1[both, :] - high.astype(F32)).astype(BF))
                vhat, r = norm_stats(x_rows[rows, :].astype(F32))
                sums[0:1, 0:d] += jnp.sum(cot * vhat, axis=0, keepdims=True)
                sums[1:2, 0:d] += jnp.sum(cot, axis=0, keepdims=True)
                set_dres(dres, rows, rows_of_dres(dres, rows) + norm_grad(vhat, r, cot * vec(0, 0, d)))
                ticks.within(b, range(8))

        def ff_part(dn2_rows, r1):
            dn2 = dn2_rows.at[0:tok]
            r1_load = pltpu.make_async_copy(r1_i, r1, out_sem.at[1])
            def inner(act, gd, wf, wi, dff, dff_t, n2_t, dh):
                n2_load = load(n2t_i, n2_t)

                def tile_copies(j):
                    slot, hx, jj = lax.rem(j, 2), lax.rem(j, 2), lax.div(j, 2)
                    cols = pl.ds(pl.multiple_of(hx * half_ff + jj * 256, 256), 256)
                    wcols = pl.ds(pl.multiple_of(jj * 256, 256), 256)
                    pairs = (
                        (act_i.at[:, cols], act),
                        (gd_i.at[:, cols], gd),
                        (wf_i.at[hx, :, :, :, :, wcols], wf),
                        (wi_i.at[hx, :, :, :, :, wcols], wi),
                    )
                    return [pltpu.make_async_copy(s, b.at[slot], tile_sem.at[slot, q]) for q, (s, b) in enumerate(pairs)]

                for copy in tile_copies(0):
                    copy.start()
                r1_load.start()
                ticks.point()

                @pl.loop(0, tok // 256)
                def _(b):
                    rows = pl.ds(pl.multiple_of(b * 256, 256), 256)
                    val = rows_of_dres(dres, rows).astype(BF)
                    dff[rows, :] = val
                    sums[7:8, 0:d] += jnp.sum(val.astype(F32), axis=0, keepdims=True)
                    dff_t[:, rows] = val.T
                    ticks.within(b, range(4))

                n2_load.wait()
                n_tiles = ff // 256

                @pl.loop(0, n_tiles)
                def _(j):
                    slot, hx, jj = lax.rem(j, 2), lax.rem(j, 2), lax.div(j, 2)
                    for copy in tile_copies(j):
                        copy.wait()

                    @pl.when(j + 1 < n_tiles)
                    def _():
                        for copy in tile_copies(j + 1):
                            copy.start()

                    wcols = pl.ds(pl.multiple_of(jj * 256, 256), 256)
                    wf_j = wf.at[slot].reshape(d, 256)
                    wi_j = wi.at[slot].reshape(d, 256)
                    total = jnp.zeros((1, 256), F32)
                    for m in range(0, tok, FF_ROWS):
                        val = (nn(dff[m : m + FF_ROWS, :], wf_j[...]) * gd[slot, m : m + FF_ROWS, :].astype(F32)).astype(BF)
                        dh[m : m + FF_ROWS, :] = val
                        total = total + jnp.sum(val.astype(F32), axis=0, keepdims=True)
                    sums[6:7, pl.ds(pl.multiple_of(hx * half_ff + jj * 256, 256), 256)] = total
                    g_wf2[hx, :, wcols] = nn(dff_t[...], act[slot]).astype(BF)
                    g_wi2[hx, :, wcols] = nn(n2_t[...], dh[...]).astype(BF)

                    @pl.when(j == 0)
                    def _():
                        dn2[...] = nt(dh[...], wi_j[...])

                    @pl.when(j > 0)
                    def _():
                        dn2[...] += nt(dh[...], wi_j[...])

                    ticks.within(j, range(12))

            pl.run_scoped(
                inner,
                pltpu.VMEM((2, tok, 256), BF),
                pltpu.VMEM((2, tok, 256), BF),
                pltpu.VMEM((2, 4, 2, 2, d // 16, 256), BF),
                pltpu.VMEM((2, 4, 2, 2, d // 16, 256), BF),
                pltpu.VMEM((tok, d), BF),
                pltpu.VMEM((d, tok), BF),
                pltpu.VMEM((d, tok), BF),
                pltpu.VMEM((tok, 256), BF),
            )

            def out_part(heads_t, wo, dattn):
                loads = [load(headst_i, heads_t), load(wo_i, wo)]
                wo2 = wo.reshape(d, d)
                g_wo2 = g_wo.reshape(d, d)
                r1_load.wait()

                @pl.loop(0, tok // 128)
                def _(b):
                    rows = pl.ds(pl.multiple_of(b * 128, 128), 128)
                    vhat, r = norm_stats(r1[rows, :])
                    cot = dn2[rows, :]
                    sums[4:5, 0:d] += jnp.sum(cot * vhat, axis=0, keepdims=True)
                    sums[5:6, 0:d] += jnp.sum(cot, axis=0, keepdims=True)
                    val = rows_of_dres(dres, rows) + norm_grad(vhat, r, cot * vec(4, 0, d))
                    set_dres(dres, rows, val)
                    low = val.astype(BF)
                    dattn[rows, :] = low
                    sums[3:4, 0:d] += jnp.sum(low.astype(F32), axis=0, keepdims=True)
                    ticks.within(b, range(8))

                for copy in loads:
                    copy.wait()
                g_wo2[...] = nn(heads_t[...], dattn[...]).astype(BF)
                ticks.point()
                dpad[0:win, :] = jnp.zeros((win, d), BF)
                dpad[win + tok : 2 * win + tok, :] = jnp.zeros((win, d), BF)

                @pl.loop(0, tok // 512)
                def _(b):
                    at = pl.multiple_of(b * 512, 256)
                    dpad[pl.ds(at + win, 512), :] = nt(dattn[pl.ds(at, 512), :], wo2[...]).astype(BF)
                    ticks.within(b, (0, 1))

            def rest(proj, ns_t):
                loads = [load(proj_i.at[pl.ds(b * 384, 384)], proj.at[pl.ds(b * 384, 384)]) for b in range(nw // 3)]
                loads.append(load(nst_i, ns_t))
                pl.run_scoped(out_part, pltpu.VMEM((d, tok), BF), pltpu.VMEM(wo_i.shape, BF), pltpu.VMEM((tok, d), BF))
                pl.run_scoped(functools.partial(attn_part, proj, ns_t, dn2_rows, loads), pltpu.VMEM(qkv_i.shape, BF))

            pl.run_scoped(rest, pltpu.VMEM(proj_i.shape, BF), pltpu.VMEM(nst_i.shape, BF))

        pl.run_scoped(ff_part, pltpu.VMEM((nw * win, d), F32), pltpu.VMEM((tok, d), F32))
        done = pltpu.make_async_copy(dres, dch_out, out_sem.at[0])
        done.start()

        g_vec2 = g_vec.reshape(-1, SLOT)
        nrow = g_vec2.shape[0] // 16
        g_vec[...] = jnp.zeros_like(g_vec)
        for width, count in sorted(set(sizes)):
            pick, mine = vector_masks(width, count, nrow)
            for v in [i for i, s in enumerate(sizes) if s == (width, count)]:
                spread = jnp.where(mine, sums[v : v + 1, :width], 0.0)
                top = spread.astype(BF)
                rest = (spread - top.astype(F32)).astype(BF)
                g_vec2[pl.ds(v, nrow, stride=16), :] = nt(top, pick) + nt(rest, pick)
        ticks.point()
        for t, g in enumerate(grads):
            pick = functools.partial(block, g, KINDS[t], cut=(ALL, ALL))
            sends.sent(t, {"z": pick(slice(0, 3), y, c, x), "a": pick(ALL, y, c, x), "b": pick(ALL, y, c, ALL), "c": pick(ALL, ALL, c, ALL)})
        done.wait()

    pl.run_scoped(whole, pltpu.VMEM((d // 128, tok, 128), F32), pltpu.VMEM((tok + 2 * win, d), BF))


def quick_mesh(mesh):
    return mesh.shape["dp"] == 16 and mesh.shape["mp"] == 2


def gathered_shape(shape, kind):
    if kind == 2:
        return (4, 2, 2, 2 * shape[0], shape[1])
    return ((4, 2, 2, 2) if kind == 0 else (2, 4, 2, 2)) + shape


def place_kernel(widths, *refs):
    n = (len(refs) - 3 - len(widths)) // 3
    sources, vec_ref, outs, vec_outs = refs[:n], refs[n], refs[n + 1 : 2 * n + 1], refs[2 * n + 1 : 2 * n + 1 + len(widths)]
    held, in_sem, out_sem = refs[-n - 2 : -2], refs[-2], refs[-1]
    parts = held[-1].shape[0]
    pairs = [(sources[-1].at[q], held[-1].at[q], outs[-1].at[:, q * SLOT : q * SLOT + SLOT]) for q in range(parts)]
    pairs += list(zip(sources[:-1], held[:-1], outs[:-1]))
    loads = [pltpu.make_async_copy(s, h, in_sem.at[i]) for i, (s, h, _) in enumerate(pairs)]
    stores = [pltpu.make_async_copy(h, o, out_sem.at[i]) for i, (_, h, o) in enumerate(pairs)]
    for copy in loads:
        copy.start()
    for v, (width, out) in enumerate(zip(widths, vec_outs)):
        out[...] = vec_ref[v, :width]
    for load, store in zip(loads, stores):
        load.wait()
        store.start()
    for copy in stores:
        copy.wait()


def fast_shards(*args):
    (chars, seg, offs, l1g, l1b, wqkv, qvb, wo, aob, l2g, l2b, wi, fib, wf, fob, cv, cvb, l3g, l3b, dmol) = args
    tok, d = chars.shape
    mols = dmol.shape[0]
    vectors = (l1g, l1b, qvb, aob, l2g, l2b, fib, fob, cvb, l3g, l3b)
    sizes = tuple((v.shape[0] * 32, v.shape[0]) for v in vectors)
    ff = sizes[6][0]
    dims = (tok, d, ff)
    nw = tok // WIN + 1
    vec_own = sum(jnp.pad(v[None], ((i, 15 - i), (0, SLOT - v.shape[0]))) for i, v in enumerate(vectors))
    owns = (vec_own, wqkv, wo, wi, wf.T, cv)
    kinds = KINDS
    full = [gathered_shape(o.shape, k) for o, k in zip(owns, kinds)]
    plan = gather_plan([o.shape for o in owns])
    n_wait = 5 * len(plan)
    on_chip = pl.BlockSpec(memory_space=pltpu.VMEM)
    scalar = pl.BlockSpec(memory_space=pltpu.SMEM)
    any_mem = pl.BlockSpec(memory_space=pl.ANY)
    bf = lambda *s: jax.ShapeDtypeStruct(s, BF)
    f32 = lambda *s: jax.ShapeDtypeStruct(s, F32)
    prob_shape = (nw, HEADS // 2, WIN, 2 * WIN)
    saved = pl.pallas_call(
        functools.partial(forward_kernel, dims, sizes),
        out_shape=[
            f32(mols, d),
            f32(16, ff),
            f32(8, d),
            bf(mols, d),
            *[bf(*s) for s in full[1:]],
            bf(d, nw * WIN),
            bf(nw * WIN, 3 * d),
            bf(*prob_shape),
            bf(d, tok),
            f32(tok, d),
            bf(d, tok),
            bf(tok, ff),
            bf(tok, ff),
            bf(KER, d // SLOT, SLOT, mols),
        ],
        in_specs=[scalar] + [on_chip] * 9,
        out_specs=[on_chip, any_mem, on_chip, on_chip] + [any_mem] * 14,
        scratch_shapes=[
            *[pltpu.VMEM(s, BF) for s in full],
            pltpu.VMEM((512, SLOT), F32),
            pltpu.VMEM((16, ff), F32),
            pltpu.VMEM((tok + 2 * WIN, d), BF),
            pltpu.VMEM((nw * WIN, d), BF),
            pltpu.VMEM((nw * WIN, 3 * d), BF),
            pltpu.VMEM(prob_shape, BF),
            pltpu.VMEM((tok, d), BF),
            pltpu.VMEM((tok, d), F32),
            pltpu.VMEM((tok, d), BF),
            pltpu.VMEM((tok, ff), BF),
            pltpu.VMEM((tok, ff), BF),
            pltpu.VMEM((d // 128, tok, 128), F32),
            pltpu.VMEM((mols, KER * d), BF),
            pltpu.SemaphoreType.DMA((6,)),
            pltpu.SemaphoreType.DMA((16,)),
            pltpu.SemaphoreType.DMA((24,)),
            pltpu.SemaphoreType.DMA((n_wait,)),
        ],
        compiler_params=pltpu.CompilerParams(collective_id=1, has_side_effects=True, vmem_limit_bytes=VMEM_CAP),
        name="gather_forward",
    )(offs, seg, chars, dmol, *owns)
    (mol, vecs, ln3, dcp, qkv_f, wo_f, wi_f, wf_f, cv_f, ns, proj, prob, heads, r1, n2, act, gd, mi) = saved

    own_shapes = [o.shape for o in owns]
    kind_core = lambda s, k: (4, 2, 2 * s[0], s[1]) if k == 2 else ((4, 2, 2) if k == 0 else (2, 4, 2)) + s
    types = [F32] + [BF] * 5
    plan = scatter_plan(own_shapes)
    n_back = 5 * len(plan)
    back = pl.pallas_call(
        functools.partial(backward_kernel, dims, sizes),
        out_shape=[f32(d // SLOT, tok, SLOT)] + [f32(*s) for s in own_shapes],
        in_specs=[scalar, any_mem] + [on_chip] * 3 + [any_mem] * 14,
        out_specs=[any_mem] + [on_chip] * 6,
        scratch_shapes=[
            *[pltpu.VMEM(s, t) for s, t in zip(full, types)],
            *[pltpu.VMEM(kind_core(s, k), t) for s, k, t in zip(own_shapes, kinds, types)],
            *[pltpu.VMEM((2, 4) + s, t) for s, t in zip(own_shapes, types)],
            *[pltpu.VMEM((4,) + s, t) for s, t in zip(own_shapes, types)],
            *[pltpu.VMEM((3,) + s, t) for s, t in zip(own_shapes, types)],
            pltpu.VMEM((16, ff), F32),
            pltpu.SemaphoreType.DMA((2,)),
            pltpu.SemaphoreType.DMA((2, 4)),
            pltpu.SemaphoreType.DMA((16,)),
            pltpu.SemaphoreType.DMA((2,)),
            pltpu.SemaphoreType.DMA((24,)),
            pltpu.SemaphoreType.DMA((n_back,)),
        ],
        compiler_params=pltpu.CompilerParams(collective_id=2, has_side_effects=True, vmem_limit_bytes=VMEM_CAP),
        name="backward_scatter",
    )(offs, chars, dcp, vecs, ln3, qkv_f, wo_f, wi_f, wf_f, cv_f, ns, proj, prob, heads, r1, n2, act, gd, mi)
    d_chars, d_vec, d_qkv, d_wo, d_wi, d_wf, d_cv = back
    large = (d_wo, d_qkv, d_wi, d_wf, d_cv, mol, d_chars)
    done = pl.pallas_call(
        functools.partial(place_kernel, tuple(v.shape[0] for v in vectors)),
        out_shape=[f32(*a.shape) for a in large[:-1]] + [f32(tok, d)] + [f32(v.shape[0]) for v in vectors],
        in_specs=[any_mem] * len(large) + [on_chip],
        out_specs=[any_mem] * len(large) + [on_chip] * len(vectors),
        scratch_shapes=[
            *[pltpu.VMEM(a.shape, F32) for a in large],
            pltpu.SemaphoreType.DMA((len(large) - 1 + d // SLOT,)),
            pltpu.SemaphoreType.DMA((len(large) - 1 + d // SLOT,)),
        ],
        compiler_params=pltpu.CompilerParams(vmem_limit_bytes=VMEM_CAP),
        name="place",
    )(*large, d_vec)
    d_wo, d_qkv, d_wi, d_wf, d_cv, mol, d_chars = done[: len(large)]
    dv = done[len(large) :]
    return (
        mol,
        d_chars,
        dv[0],
        dv[1],
        d_qkv,
        dv[2],
        d_wo,
        dv[3],
        dv[4],
        dv[5],
        d_wi,
        dv[6],
        d_wf.T,
        dv[7],
        d_cv,
        dv[8],
        dv[9],
        dv[10],
    )


def solution(mesh):
    placed = (
        P(("dp", "mp"), None),
        P(("dp", "mp"), None),
        P(("dp", "mp")),
        P(("dp", "mp")),
        P(("dp", "mp")),
        P(("dp", "mp"), None),
        P(("dp", "mp")),
        P(("dp", "mp"), None),
        P(("dp", "mp")),
        P(("dp", "mp")),
        P(("dp", "mp")),
        P("dp", "mp"),
        P(("dp", "mp")),
        P("mp", "dp"),
        P(("dp", "mp")),
        P("dp", "mp"),
        P(("dp", "mp")),
        P(("dp", "mp")),
        P(("dp", "mp")),
        P(("dp", "mp"), None),
    )
    return jax.shard_map(
        fast_shards if quick_mesh(mesh) else shards,
        mesh=mesh,
        in_specs=placed,
        out_specs=(
            P(("dp", "mp"), None),
            P(("dp", "mp"), None),
            P(("dp", "mp")),
            P(("dp", "mp")),
            P(("dp", "mp"), None),
            P(("dp", "mp")),
            P(("dp", "mp"), None),
            P(("dp", "mp")),
            P(("dp", "mp")),
            P(("dp", "mp")),
            P("dp", "mp"),
            P(("dp", "mp")),
            P("mp", "dp"),
            P(("dp", "mp")),
            P("dp", "mp"),
            P(("dp", "mp")),
            P(("dp", "mp")),
            P(("dp", "mp")),
        ),
        check_vma=False,
    )
```

```python
import functools

import jax
import jax.numpy as jnp
from jax import lax
from jax.experimental import pallas as pl
from jax.experimental.pallas import tpu as pltpu
from jax.sharding import PartitionSpec as P

HEADS = 12
HDIM = 64
KER = 4
WIN = 128


layer_eps = 1e-06


def layer_norm(row_values, gain_vec, shift_vec):
    centred = row_values - jnp.mean(row_values, axis=-1, keepdims=True)
    spread = jnp.mean(centred * centred, axis=-1, keepdims=True)
    return centred * lax.rsqrt(spread + layer_eps) * gain_vec + shift_vec


def gelu_exact(values):
    return jax.nn.gelu(values, approximate=False)


def norm_backward(row_values, gain_vec, shift_vec, grad_out):
    _, pullback = jax.vjp(layer_norm, row_values, gain_vec, shift_vec)
    return pullback(grad_out)


def gelu_backward(values, grad_out):
    _, pullback = jax.vjp(gelu_exact, values)
    return pullback(grad_out)[0]


def three_blocks(rows, fill_value):
    edge = jnp.full_like(rows[:1], fill_value)
    before = jnp.concatenate([edge, rows[:-1]], axis=0)
    after = jnp.concatenate([rows[1:], edge], axis=0)
    return jnp.concatenate([before, rows, after], axis=1)


def fold_blocks(band_grad):
    edge = jnp.zeros_like(band_grad[:1, :WIN])
    from_next = jnp.concatenate([band_grad[1:, :WIN], edge], axis=0)
    from_prev = jnp.concatenate([edge, band_grad[:-1, 2 * WIN :]], axis=0)
    return band_grad[:, WIN : 2 * WIN] + from_next + from_prev


def band_inputs(queries, key_rows, value_rows, seg_row, offset):
    seq_len = queries.shape[0]
    block_count = seq_len // WIN
    win_row = (jnp.arange(seq_len, dtype=jnp.int32) + offset) // WIN
    seg_blk = seg_row.reshape(block_count, WIN)
    win_blk = win_row.reshape(block_count, WIN)
    return (
        queries.reshape(block_count, WIN, HEADS, HDIM),
        three_blocks(key_rows.reshape(block_count, WIN, HEADS, HDIM), 0),
        three_blocks(value_rows.reshape(block_count, WIN, HEADS, HDIM), 0),
        seg_blk,
        win_blk,
        three_blocks(seg_blk, 0),
        three_blocks(win_blk, -1),
    )


def band_scores(query_blk, key_band, seg_blk, win_blk, seg_band, win_band):
    raw_scores = jnp.einsum(
        "bqhd,bkhd->bhqk", query_blk, key_band, preferred_element_type=jnp.float32
    ) * HDIM ** (-0.5)
    allowed = (seg_blk[:, :, None] == seg_band[:, None, :]) & (
        win_blk[:, :, None] == win_band[:, None, :]
    )
    return jnp.where(allowed[:, None], raw_scores, -1e30)


def attend_forward(seq_item):
    queries, key_rows, value_rows, seg_row, offset = seq_item
    seq_len = queries.shape[0]
    query_blk, key_band, val_band, seg_blk, win_blk, seg_band, win_band = band_inputs(
        queries, key_rows, value_rows, seg_row, offset
    )
    scores = band_scores(query_blk, key_band, seg_blk, win_blk, seg_band, win_band)
    row_peak = jnp.max(scores, axis=-1, keepdims=True)
    exp_scores = jnp.exp(scores - row_peak)
    row_total = jnp.sum(exp_scores, axis=-1, keepdims=True)
    prob_low = (exp_scores / row_total).astype(jnp.bfloat16)
    merged = jnp.einsum("bhqk,bkhd->bqhd", prob_low, val_band, preferred_element_type=jnp.float32)
    return (merged.reshape(seq_len, HEADS * HDIM), (row_peak + jnp.log(row_total))[..., 0])


def attend_backward(seq_item):
    queries, key_rows, value_rows, seg_row, offset, log_norm, d_heads = seq_item
    seq_len = queries.shape[0]
    block_count = seq_len // WIN
    score_scale = HDIM ** (-0.5)
    query_blk, key_band, val_band, seg_blk, win_blk, seg_band, win_band = band_inputs(
        queries, key_rows, value_rows, seg_row, offset
    )
    grad_blk = d_heads.reshape(block_count, WIN, HEADS, HDIM)
    scores = band_scores(query_blk, key_band, seg_blk, win_blk, seg_band, win_band)
    prob_blk = jnp.exp(scores - log_norm[..., None])
    d_probs = jnp.einsum("bqhd,bkhd->bhqk", grad_blk, val_band, preferred_element_type=jnp.float32)
    row_dot = jnp.sum(prob_blk * d_probs, axis=-1, keepdims=True)
    d_scores = (prob_blk * (d_probs - row_dot)).astype(jnp.bfloat16)
    d_query = (
        jnp.einsum("bhqk,bkhd->bqhd", d_scores, key_band, preferred_element_type=jnp.float32)
        * score_scale
    )
    d_key_band = (
        jnp.einsum("bhqk,bqhd->bkhd", d_scores, query_blk, preferred_element_type=jnp.float32)
        * score_scale
    )
    d_val_band = jnp.einsum(
        "bhqk,bqhd->bkhd",
        prob_blk.astype(jnp.bfloat16),
        grad_blk,
        preferred_element_type=jnp.float32,
    )
    d_keys = fold_blocks(d_key_band)
    d_vals = fold_blocks(d_val_band)
    return (
        d_query.reshape(seq_len, HEADS * HDIM),
        d_keys.reshape(seq_len, HEADS * HDIM),
        d_vals.reshape(seq_len, HEADS * HDIM),
    )


def shards(
    chars,
    segment_ids,
    window_offsets,
    ln1_gain,
    ln1_bias,
    w_qkv,
    qv_bias,
    w_attn_out,
    attn_out_bias,
    ln2_gain,
    ln2_bias,
    w_ff_in,
    ff_in_bias,
    w_ff_out,
    ff_out_bias,
    conv_weight,
    conv_bias,
    ln3_gain,
    ln3_bias,
    d_molecules,
):
    gathered = (
        lax.all_gather(w_qkv, ("dp", "mp"), axis=0, tiled=True),
        lax.all_gather(w_attn_out, ("dp", "mp"), axis=0, tiled=True),
        lax.all_gather(ln1_gain, ("dp", "mp"), axis=0, tiled=True),
        lax.all_gather(ln1_bias, ("dp", "mp"), axis=0, tiled=True),
        lax.all_gather(qv_bias, ("dp", "mp"), axis=0, tiled=True),
        lax.all_gather(attn_out_bias, ("dp", "mp"), axis=0, tiled=True),
        lax.all_gather(ln2_gain, ("dp", "mp"), axis=0, tiled=True),
        lax.all_gather(ln2_bias, ("dp", "mp"), axis=0, tiled=True),
        lax.all_gather(ff_in_bias, ("dp", "mp"), axis=0, tiled=True),
        lax.all_gather(ff_out_bias, ("dp", "mp"), axis=0, tiled=True),
        lax.all_gather(conv_bias, ("dp", "mp"), axis=0, tiled=True),
        lax.all_gather(ln3_gain, ("dp", "mp"), axis=0, tiled=True),
        lax.all_gather(ln3_bias, ("dp", "mp"), axis=0, tiled=True),
    )
    qkv_full = gathered[0]
    attn_out_full = gathered[1]
    vectors = [vector_arg.astype(jnp.float32) for vector_arg in gathered[2:]]
    (
        gain_one,
        shift_one,
        qv_shift,
        attn_shift,
        gain_two,
        shift_two,
        hidden_shift,
        ff_shift,
        conv_shift,
        gain_three,
        shift_three,
    ) = vectors
    ff_in_part, ff_out_part, conv_part = (
        lax.all_gather(w_ff_in, "dp", axis=0, tiled=True),
        lax.all_gather(w_ff_out, "dp", axis=1, tiled=True),
        lax.all_gather(conv_weight, "dp", axis=0, tiled=True),
    )
    model_width = chars.shape[1]
    tok_rows = chars.shape[0]
    seq_count = segment_ids.shape[0]
    seq_len = segment_ids.shape[1]
    mp_rank = lax.axis_index("mp")
    hidden_part = ff_in_part.shape[1]
    channel_part = conv_part.shape[1]
    inputs = chars.astype(jnp.float32)
    normed_one = layer_norm(inputs, gain_one, shift_one).astype(jnp.bfloat16)
    qkv_shift = jnp.concatenate(
        [qv_shift[:model_width], jnp.zeros((model_width,), jnp.float32), qv_shift[model_width:]]
    )
    projected = (
        jnp.dot(normed_one, qkv_full, preferred_element_type=jnp.float32) + qkv_shift
    ).astype(jnp.bfloat16)
    per_seq = projected.reshape(seq_count, seq_len, 3, HEADS, HDIM)
    queries = per_seq[:, :, 0]
    key_rows = per_seq[:, :, 1]
    value_rows = per_seq[:, :, 2]
    merged, log_norm = lax.map(
        attend_forward, (queries, key_rows, value_rows, segment_ids, window_offsets)
    )
    heads_low = merged.reshape(tok_rows, model_width).astype(jnp.bfloat16)
    resid_one = (
        inputs + jnp.dot(heads_low, attn_out_full, preferred_element_type=jnp.float32) + attn_shift
    )
    normed_two = layer_norm(resid_one, gain_two, shift_two).astype(jnp.bfloat16)
    ff_in_use, ff_out_use, conv_use = (ff_in_part, ff_out_part, conv_part)
    ff_rows_in = lax.all_gather(normed_two, "mp", axis=0, tiled=True)
    hidden_bias = lax.dynamic_slice_in_dim(hidden_shift, mp_rank * hidden_part, hidden_part)
    hidden_pre = jnp.dot(ff_rows_in, ff_in_use, preferred_element_type=jnp.float32) + hidden_bias
    hidden_act = gelu_exact(hidden_pre).astype(jnp.bfloat16)
    ff_sum = lax.psum_scatter(
        jnp.dot(hidden_act, ff_out_use, preferred_element_type=jnp.float32).astype(jnp.bfloat16),
        "mp",
        scatter_dimension=0,
        tiled=True,
    ).astype(jnp.float32)
    resid_two = resid_one + ff_sum + ff_shift
    mol_rows = resid_two.astype(jnp.bfloat16).reshape(tok_rows // KER, KER * model_width)
    mol_group = lax.all_gather(mol_rows, "mp", axis=0, tiled=True)
    channel_bias = lax.dynamic_slice_in_dim(conv_shift, mp_rank * channel_part, channel_part)
    conv_pre = jnp.dot(mol_group, conv_use, preferred_element_type=jnp.float32) + channel_bias
    channel_act = gelu_exact(conv_pre).astype(jnp.bfloat16)
    conv_act = lax.all_to_all(channel_act, "mp", split_axis=0, concat_axis=1, tiled=True)
    act_float = conv_act.astype(jnp.float32)
    molecules = layer_norm(act_float, gain_three, shift_three)
    d_act, d_gain_three, d_shift_three = norm_backward(
        act_float, gain_three, shift_three, d_molecules.astype(jnp.float32)
    )
    d_act_low = d_act.astype(jnp.bfloat16)
    d_act_cols = lax.all_to_all(d_act_low, "mp", split_axis=1, concat_axis=0, tiled=True)
    d_conv_pre = gelu_backward(conv_pre, d_act_cols.astype(jnp.float32)).astype(jnp.bfloat16)
    d_conv_w = jnp.einsum("mk,mc->kc", mol_group, d_conv_pre, preferred_element_type=jnp.float32)
    d_conv_shift = lax.dynamic_update_slice_in_dim(
        jnp.zeros((model_width,), jnp.float32),
        jnp.sum(d_conv_pre.astype(jnp.float32), axis=0),
        mp_rank * channel_part,
        0,
    )
    d_mol = lax.psum_scatter(
        jnp.einsum("mc,kc->mk", d_conv_pre, conv_use, preferred_element_type=jnp.float32).astype(
            jnp.bfloat16
        ),
        "mp",
        scatter_dimension=0,
        tiled=True,
    ).astype(jnp.float32)
    d_resid_two = d_mol.reshape(tok_rows, model_width)
    d_ff_low = d_resid_two.astype(jnp.bfloat16)
    d_ff_shift = jnp.sum(d_ff_low.astype(jnp.float32), axis=0)
    d_ff_rows = lax.all_gather(d_ff_low, "mp", axis=0, tiled=True)
    d_hidden_act = jnp.einsum(
        "gc,fc->gf", d_ff_rows, ff_out_use, preferred_element_type=jnp.float32
    )
    d_ff_out_w = jnp.einsum("gf,gc->fc", hidden_act, d_ff_rows, preferred_element_type=jnp.float32)
    d_hidden = gelu_backward(hidden_pre, d_hidden_act).astype(jnp.bfloat16)
    d_hidden_sum = jnp.sum(d_hidden.astype(jnp.float32), axis=0)
    d_ff_in_w = jnp.einsum("gd,gf->df", ff_rows_in, d_hidden, preferred_element_type=jnp.float32)
    d_hidden_shift = lax.dynamic_update_slice_in_dim(
        jnp.zeros((hidden_shift.shape[0],), jnp.float32), d_hidden_sum, mp_rank * hidden_part, 0
    )
    d_normed_two = lax.psum_scatter(
        jnp.einsum("gf,df->gd", d_hidden, ff_in_use, preferred_element_type=jnp.float32).astype(
            jnp.bfloat16
        ),
        "mp",
        scatter_dimension=0,
        tiled=True,
    ).astype(jnp.float32)
    d_resid_from, d_gain_two, d_shift_two = norm_backward(
        resid_one, gain_two, shift_two, d_normed_two
    )
    d_resid_one = d_resid_two + d_resid_from
    d_attn_low = d_resid_one.astype(jnp.bfloat16)
    d_attn_shift = jnp.sum(d_attn_low.astype(jnp.float32), axis=0)
    d_attn_out_w = jnp.einsum(
        "te,tc->ec", heads_low, d_attn_low, preferred_element_type=jnp.float32
    )
    d_heads_low = jnp.einsum(
        "tc,ec->te", d_attn_low, attn_out_full, preferred_element_type=jnp.float32
    ).astype(jnp.bfloat16)
    d_heads_seq = d_heads_low.reshape(seq_count, seq_len, HEADS, HDIM)
    d_queries, d_keys, d_vals = lax.map(
        attend_backward,
        (queries, key_rows, value_rows, segment_ids, window_offsets, log_norm, d_heads_seq),
    )
    d_projected = jnp.concatenate(
        [
            d_queries.reshape(tok_rows, model_width),
            d_keys.reshape(tok_rows, model_width),
            d_vals.reshape(tok_rows, model_width),
        ],
        axis=1,
    ).astype(jnp.bfloat16)
    d_proj_sum = jnp.sum(d_projected.astype(jnp.float32), axis=0)
    d_qv_shift = jnp.concatenate([d_proj_sum[:model_width], d_proj_sum[2 * model_width :]])
    d_qkv_w = jnp.einsum("td,te->de", normed_one, d_projected, preferred_element_type=jnp.float32)
    d_normed_one = jnp.einsum(
        "te,de->td", d_projected, qkv_full, preferred_element_type=jnp.float32
    )
    d_inputs_from, d_gain_one, d_shift_one = norm_backward(
        inputs, gain_one, shift_one, d_normed_one
    )
    d_chars = d_resid_one + d_inputs_from
    d_ff_in_own, d_ff_out_own, d_conv_own = (
        lax.psum_scatter(
            d_ff_in_w.astype(jnp.bfloat16), "dp", scatter_dimension=0, tiled=True
        ).astype(jnp.float32),
        lax.psum_scatter(
            d_ff_out_w.astype(jnp.bfloat16), "dp", scatter_dimension=1, tiled=True
        ).astype(jnp.float32),
        lax.psum_scatter(
            d_conv_w.astype(jnp.bfloat16), "dp", scatter_dimension=0, tiled=True
        ).astype(jnp.float32),
    )
    owned = (
        lax.psum_scatter(d_qkv_w, ("dp", "mp"), scatter_dimension=0, tiled=True),
        lax.psum_scatter(d_attn_out_w, ("dp", "mp"), scatter_dimension=0, tiled=True),
        lax.psum_scatter(d_gain_one, ("dp", "mp"), scatter_dimension=0, tiled=True),
        lax.psum_scatter(d_shift_one, ("dp", "mp"), scatter_dimension=0, tiled=True),
        lax.psum_scatter(d_qv_shift, ("dp", "mp"), scatter_dimension=0, tiled=True),
        lax.psum_scatter(d_attn_shift, ("dp", "mp"), scatter_dimension=0, tiled=True),
        lax.psum_scatter(d_gain_two, ("dp", "mp"), scatter_dimension=0, tiled=True),
        lax.psum_scatter(d_shift_two, ("dp", "mp"), scatter_dimension=0, tiled=True),
        lax.psum_scatter(d_hidden_shift, ("dp", "mp"), scatter_dimension=0, tiled=True),
        lax.psum_scatter(d_ff_shift, ("dp", "mp"), scatter_dimension=0, tiled=True),
        lax.psum_scatter(d_conv_shift, ("dp", "mp"), scatter_dimension=0, tiled=True),
        lax.psum_scatter(d_gain_three, ("dp", "mp"), scatter_dimension=0, tiled=True),
        lax.psum_scatter(d_shift_three, ("dp", "mp"), scatter_dimension=0, tiled=True),
    )
    return (
        molecules,
        d_chars,
        owned[2],
        owned[3],
        owned[0],
        owned[4],
        owned[1],
        owned[5],
        owned[6],
        owned[7],
        d_ff_in_own,
        owned[8],
        d_ff_out_own,
        owned[9],
        d_conv_own,
        owned[10],
        owned[11],
        owned[12],
    )


NEAR_FIRST = (False, True, False, False, False, False, True, True, False, False, False, False, False, False, True, False, False, False, True, True, True, False)
GATHER_TABLE = (
    ((0, 0), (0, 1), (1, 0), (0, 2), (2, 0), (0, 3), (3, 0), (1, 1), (1, 2), (4, 0), (2, 2),),
    ((1, 3), (0, 4),),
    (),
    ((2, 1),),
    ((3, 2), (0, 5),),
    (),
    ((0, 6),),
    ((2, 3), (1, 4), (1, 5), (0, 7), (3, 1), (4, 2), (0, 8), (4, 1), (1, 6), (5, 2), (0, 9), (3, 3), (4, 3), (0, 10),),
    ((2, 4), (0, 11),),
    ((2, 5), (1, 7), (2, 7), (1, 8), (2, 8), (1, 9),),
    ((2, 6), (1, 10),),
    ((3, 4), (1, 11), (0, 12),),
    ((3, 5), (3, 7),),
    ((4, 4), (0, 13),),
    (),
    ((4, 5), (3, 8), (2, 9), (0, 14),),
    ((3, 6), (1, 12),),
    ((0, 15),),
    ((4, 6), (2, 10), (1, 13),),
    ((0, 16),),
    ((2, 11), (1, 14), (0, 17),),
    ((4, 7), (4, 8), (0, 18),),
    ((3, 9), (1, 16),),
    ((5, 7), (5, 8), (2, 12), (1, 15), (2, 15), (1, 17),),
    ((4, 9), (3, 10), (0, 19),),
    ((3, 11), (2, 13), (1, 18), (0, 20),),
    ((4, 10), (2, 14), (3, 15), (0, 21),),
    ((4, 11), (0, 22),),
    ((3, 12), (2, 16),),
    (),
    ((4, 12), (2, 17), (1, 19), (2, 19),),
    ((3, 13), (1, 22),),
    ((2, 18), (1, 20), (2, 20),),
    ((4, 13), (3, 14), (3, 19),),
    ((4, 15), (3, 16), (1, 21), (2, 21),),
    ((4, 14), (3, 17), (3, 20),),
    ((5, 15), (4, 16),),
    ((4, 17), (3, 21), (2, 22),),
    ((3, 18),),
    ((4, 19),),
    ((4, 18), (4, 20),),
    ((5, 19), (4, 21), (3, 22),),
    ((5, 20),),
    ((5, 21), (4, 22),),
    (),
)
SCATTER_TABLE = (
    ((0, 0), (0, 1), (0, 2), (0, 3), (0, 4), (0, 5),),
    (),
    (),
    (),
    (),
    (),
    (),
    ((1, 0), (1, 1), (1, 2),),
    ((1, 3), (1, 4),),
    ((1, 5),),
    (),
    ((0, 6), (0, 7),),
    ((2, 0),),
    ((2, 1), (0, 8), (0, 9),),
    ((2, 2), (1, 6), (1, 7),),
    ((2, 3), (0, 10), (0, 11),),
    ((2, 4), (1, 8), (1, 9),),
    ((3, 0), (2, 5), (0, 12), (0, 13),),
    ((3, 1), (3, 2), (1, 10), (1, 11),),
    ((2, 6), (0, 14), (0, 15),),
    ((3, 3), (2, 7), (1, 12), (1, 13),),
    ((4, 0), (3, 4), (0, 16), (0, 17),),
    ((4, 1), (2, 8), (1, 14),),
    ((1, 15),),
    ((4, 2), (2, 9),),
    ((3, 5),),
    (),
    ((4, 3), (1, 16),),
    ((2, 10), (1, 17),),
    (),
    ((4, 4), (3, 6), (2, 11), (0, 18),),
    ((3, 7),),
    (),
    ((4, 5), (2, 12),),
    ((3, 8), (2, 13), (1, 18),),
    ((4, 6), (2, 14),),
    ((4, 7), (3, 9), (2, 15), (0, 19),),
    ((4, 8), (2, 16),),
    ((3, 10),),
    ((3, 11), (2, 17), (1, 19),),
    ((4, 9), (3, 12), (3, 13), (0, 20),),
    ((2, 18),),
    ((4, 10), (4, 11), (3, 14), (3, 15), (3, 16),),
    ((3, 17), (1, 20),),
    ((4, 12), (4, 13), (2, 19), (0, 21),),
    ((3, 18),),
    ((4, 14),),
    ((4, 15),),
    (),
    (),
    (),
    ((1, 21),),
    ((4, 16), (2, 20),),
    (),
    (),
    (),
    ((4, 17), (3, 19), (0, 22),),
    (),
    (),
    (),
    (),
    (),
    (),
    (),
    (),
    ((4, 18), (1, 22), (2, 21), (3, 20), (4, 19), (2, 22), (3, 21), (4, 20), (3, 22), (4, 22), (4, 21),),
)
HALF = 0.5
ERFC_P = 0.3
ERFC_Q = (
    0.16918934881687164,
    0.17069095373153687,
    0.1485210806131363,
    0.2141820192337036,
    -0.09282728284597397,
    0.5449684858322144,
    -0.5097734332084656,
    0.4843021035194397,
    -0.12925326824188232,
)
BF = jnp.bfloat16
F32 = jnp.float32
MESH_ID = pl.DeviceIdType.MESH
ALL = slice(None)
LINKS = ("z1", "z2", "z3", "x", "y", "c")
VMEM_CAP = 63 * 2**20
SLOT = 128
KINDS = (0, 2, 2, 1, 1, 1)
FF_ROWS = 512


def nn(lhs, rhs):
    return lax.dot_general(lhs, rhs, (((1,), (0,)), ((), ())), preferred_element_type=F32)


def nt(lhs, rhs):
    return lax.dot_general(lhs, rhs, (((1,), (1,)), ((), ())), preferred_element_type=F32)


def tn(lhs, rhs):
    return lax.dot_general(lhs, rhs, (((0,), (0,)), ((), ())), preferred_element_type=F32)


def gelu_pair(v):
    size = jnp.abs(v)
    t = 1.0 / (1.0 + (ERFC_P * 0.7071067811865476) * size)
    q = ERFC_Q[-1]
    for coef in ERFC_Q[-2::-1]:
        q = q * t + coef
    bell = jnp.exp(-0.5 * (v * v))
    tail = (HALF * bell) * (q * t)
    phi = jnp.where(v >= 0, 1.0 - tail, tail)
    return v * phi, phi + v * (bell * 0.3989422804014327)


def norm_stats(v):
    mean = jnp.mean(v, axis=-1, keepdims=True)
    cen = v - mean
    r = lax.rsqrt(jnp.mean(cen * cen, axis=-1, keepdims=True) + layer_eps)
    return cen * r, r


def norm_grad(vhat, r, t):
    m1 = jnp.mean(t, axis=-1, keepdims=True)
    m2 = jnp.mean(t * vhat, axis=-1, keepdims=True)
    return r * (t - m1 - vhat * m2)


def head_masks(rows, scale):
    lane = lax.broadcasted_iota(jnp.int32, (rows, 128), 1)
    low = jnp.where(lane < HDIM, scale, 0.0).astype(BF)
    high = jnp.where(lane < HDIM, 0.0, scale).astype(BF)
    return low, high


def split_heads(pair, masks):
    return jnp.concatenate([pair * masks[0], pair * masks[1]], axis=0)


def vector_masks(width, count, nrow):
    col = lax.broadcasted_iota(jnp.int32, (SLOT, width), 1).astype(F32)
    row = lax.broadcasted_iota(jnp.int32, (SLOT, width), 0).astype(F32)
    pick = jnp.where(col - jnp.floor((col + 0.5) * (1.0 / count)) * count == row, 1.0, 0.0).astype(BF)
    col = lax.broadcasted_iota(jnp.int32, (nrow, width), 1).astype(F32)
    row = lax.broadcasted_iota(jnp.int32, (nrow, width), 0).astype(F32)
    return pick, jnp.floor((col + 0.5) * (1.0 / count)) == row


class Place:
    def __init__(self):
        dp = lax.axis_index("dp")
        self.x = lax.axis_index("mp")
        self.z, self.y, self.c = lax.div(dp, 4), lax.rem(lax.div(dp, 2), 2), lax.rem(dp, 2)
        z, y, c, x = self.z, self.y, self.c, self.x
        self.nx, self.ny, self.nc = 1 - x, 1 - y, 1 - c
        self.at = [c * 0 + k for k in range(3)]
        self.far_z = {1: z + 1 - 2 * lax.rem(z, 2), 2: lax.rem(z + 2, 4), 3: 3 - z}
        at = lambda zz, yy, cc, xx: (zz * 4 + yy * 2 + cc, xx)
        self.peer = {
            "z1": at(self.far_z[1], y, c, x),
            "z2": at(self.far_z[2], y, c, x),
            "z3": at(self.far_z[3], y, c, x),
            "x": at(z, y, c, 1 - x),
            "y": at(z, 1 - y, c, x),
            "c": at(z, y, 1 - c, x),
            "d": at(z, 1 - y, c, 1 - x),
        }

    def barrier(self):
        sem = pltpu.get_barrier_semaphore()
        for peer in self.peer.values():
            pl.semaphore_signal(sem, inc=1, device_id=peer, device_id_type=MESH_ID)
        pl.semaphore_wait(sem, len(self.peer))


def rows_of(ref, xs):
    if isinstance(xs, slice):
        return xs
    half = ref.shape[-2] // 2
    return pl.ds(pl.multiple_of(xs * half, 8), half)


def block(ref, kind, zs, ys, cs, xs, cut):
    if kind == 0:
        return ref.at[(zs, ys, cs, xs) + cut]
    if kind == 1:
        return ref.at[(xs, zs, ys, cs) + cut]
    return ref.at[zs, ys, cs, rows_of(ref, xs), cut[1]]


class Sends:
    STEPS = ("z", "a", "b", "c", "w")

    def __init__(self, place, send_sem, recv_sem):
        self.place, self.send_sem, self.recv_sem = place, send_sem, recv_sem
        self.copies, self.waits = {}, {}
        self.live = False

    def copy(self, t, i, step, src, dst, link):
        out = self.STEPS.index("a" if step == "w" else step)
        return pltpu.make_async_remote_copy(
            src_ref=src,
            dst_ref=dst,
            send_sem=self.send_sem.at[4 * t + out],
            recv_sem=self.recv_sem.at[5 * i + self.STEPS.index(step)],
            device_id=self.place.peer[link],
            device_id_type=MESH_ID,
        )

    def go(self, t, i, step, part, src, dst, link):
        if self.live:
            self.copies[i, step, part].start()
        else:
            self.copies[i, step, part] = self.copy(t, i, step, src, dst, link)

    def got(self, t, i, step, all_of):
        if self.live:
            self.waits[i, step].wait_recv()
        else:
            self.waits[i, step] = self.copy(t, i, step, all_of, all_of, "c")

    def sent(self, t, sizes):
        for step, view in sizes.items():
            self.copy(t, 0, step, view, view, "c").wait_send()


def union(cuts):
    if cuts[1] is None:
        return cuts[0]
    return tuple(p if p == q else slice(p.start, q.stop) for p, q in zip(*cuts))


def order(half):
    return ("x", "y") if half == 0 else ("y", "x")


def gather_stage(sends, stage, i, t, kind, own, full, cuts, near_first):
    p = sends.place
    z, y, c, x = p.z, p.y, p.c, p.x
    whole = union(cuts)
    three = block(full, kind, slice(0, 3), y, c, x, whole)
    size = {
        "z": three,
        "w": three,
        "a": block(full, kind, z if near_first else ALL, y, c, x, whole),
        "b": block(full, kind, ALL, y, c, ALL, whole),
        "c": block(full, kind, ALL, ALL, c, ALL, whole),
    }
    waits = ((), ("a",), ("z",), ("w",), ("b",), ("c",)) if near_first else ((), ("z",), ("a",), ("b",), ("c",))
    if stage >= len(waits):
        return
    for step in waits[stage]:
        sends.got(t, i, step, size[step])
    for h, cut in enumerate(cuts):
        if cut is None:
            continue
        a, b = order(h)
        mine = block(full, kind, z, y, c, x, cut)
        line = block(full, kind, ALL, y, c, x, cut)
        if h == 0:
            next_one, next_line = block(full, kind, z, y, c, p.nx, cut), block(full, kind, ALL, y, c, p.nx, cut)
            far = block(full, kind, ALL, p.ny, c, ALL, cut)
        else:
            next_one, next_line = block(full, kind, z, p.ny, c, x, cut), block(full, kind, ALL, p.ny, c, x, cut)
            far = block(full, kind, ALL, ALL, c, p.nx, cut)
        own_z = [("z", k, own.at[cut], mine, k) for k in ("z1", "z2", "z3")]
        line_b, line_c = ("b", 1, line, line, b), ("c", 1, line, line, "c")
        next_bc = [("b", 2, next_line, next_line, b), ("c", 2, next_line, next_line, "c")]
        far_c = [("c", 3, far, far, "c")]
        if near_first:
            next_z = [("w", k, next_one, next_one, k) for k in ("z1", "z2", "z3")]
            steps = ([("a", 1, own.at[cut], mine, a)] + own_z, next_z, [line_b, line_c], next_bc, far_c, [])
        else:
            steps = (own_z, [("a", 1, line, line, a), line_b, line_c], next_bc, far_c, [])
        for step, part, src, dst, link in steps[stage]:
            sends.go(t, i, step, (h, part), src, dst, link)


def col_cuts(cols, parts):
    step = cols // (2 * parts)
    return [((ALL, slice(2 * step * i, 2 * step * i + step)), (ALL, slice(2 * step * i + step, 2 * step * (i + 1)))) for i in range(parts)]


def row_cuts(rows, parts):
    step = rows // (2 * parts)
    return [((slice(2 * step * i, 2 * step * i + step), ALL), (slice(2 * step * i + step, 2 * step * (i + 1)), ALL)) for i in range(parts)]


def block_cuts(rows, cols, col_parts, row_parts):
    step, width = rows // (2 * row_parts), cols // col_parts
    cuts = []
    for q in range(col_parts):
        lanes = slice(q * width, q * width + width)
        for r in range(row_parts):
            low = 2 * step * r
            cuts.append(((slice(low, low + step), lanes), (slice(low + step, low + 2 * step), lanes)))
    return cuts


def gather_plan(shapes):
    plan = [(0, 0, ((ALL, ALL), None))]
    plan += [(1, 2, c) for c in col_cuts(shapes[1][1], 3)]
    plan += [(2, 2, c) for c in col_cuts(shapes[2][1], 1)]
    plan += [(3, 1, c) for c in col_cuts(shapes[3][1], 6)]
    plan += [(4, 1, c) for c in col_cuts(shapes[4][1], 6)]
    plan += [(5, 1, c) for c in block_cuts(shapes[5][0], shapes[5][1], 3, 2)]
    return [piece + (near,) for piece, near in zip(plan, (False,) + NEAR_FIRST)]


class Ticks:
    def __init__(self, table, stage_fn):
        self.table, self.stage_fn, self.count = table, stage_fn, 0

    def run(self, k):
        for s, i in self.table[k]:
            self.stage_fn(s, i)

    def point(self):
        self.count += 1
        self.run(self.count - 1)

    def within(self, index, values):
        for value in values:
            if self.table[self.count]:
                pl.when(index == value)(functools.partial(self.run, self.count))
            self.count += 1


def forward_kernel(dims, sizes, *refs):
    (off_ref, seg_ref, x_i, dmol_i, vec_own, qkv_own, wo_own, wi_own, wf_own, cv_own) = refs[:10]
    outs = refs[10:28]
    (mol_out, vec_out, ln3_out, dcp_out, qkv_o, wo_o, wi_o, wf_o, cv_o, nst_o, proj_o, prob_o, headst_o, r1_o, n2t_o, act_o, gd_o, mit_o) = outs
    (vec_g, qkv_g, wo_g, wi_g, wf_g, cv_g, vec_f, vecs, pad, ns, proj, prob, heads, r1, n2, act, gd, r2, molin, x_ref, dmol_ref, local_sem, out_sem, send_sem, recv_sem) = refs[28:]
    tok, d, ff = dims
    win = WIN
    nw = tok // win + 1
    half_ff = ff // 2
    mols = tok // KER
    x_load = pltpu.make_async_copy(x_i, x_ref, local_sem.at[6])
    dmol_load = pltpu.make_async_copy(dmol_i, dmol_ref, local_sem.at[7])
    x_load.start()
    dmol_load.start()
    place = Place()
    owns = (vec_own, qkv_own, wo_own, wi_own, wf_own, cv_own)
    fulls = (vec_g, qkv_g, wo_g, wi_g, wf_g, cv_g)
    plan = gather_plan([o.shape for o in owns])
    kinds = KINDS
    place.barrier()
    sends = Sends(place, send_sem, recv_sem)
    local = []
    for i, (own, full, kind) in enumerate(zip(owns, fulls, kinds)):
        copy = pltpu.make_async_copy(own, block(full, kind, place.z, place.y, place.c, place.x, (ALL, ALL)), local_sem.at[i])
        copy.start()
        local.append(copy)

    def comm_stage(stage, i):
        t, kind, cuts, near_first = plan[i]
        if sends.live and stage == (2 if near_first else 1) and (i == 0 or plan[i - 1][0] != t):
            local[t].wait()
        gather_stage(sends, stage, i, t, kind, owns[t], fulls[t], cuts, near_first)

    for stage in range(6):
        for i in range(len(plan)):
            comm_stage(stage, i)
    sends.live = True
    ticks = Ticks(GATHER_TABLE, comm_stage)

    out_copies = []

    def flush(src, dst):
        copy = pltpu.make_async_copy(src, dst, out_sem.at[len(out_copies)])
        copy.start()
        out_copies.append(copy)
        return copy

    def unpack_vectors():
        nrow = vec_f.shape[0] // 16
        vec_f[...] = vec_g[...].reshape(vec_f.shape).astype(F32)
        for width, count in sorted(set(sizes)):
            pick, mine = vector_masks(width, count, nrow)
            for v in [i for i, s in enumerate(sizes) if s == (width, count)]:
                spread = nn(vec_f[pl.ds(v, nrow, stride=16), :].astype(BF), pick)
                vecs[v : v + 1, :width] = jnp.sum(jnp.where(mine, spread, 0.0), axis=0, keepdims=True)

    def vec(v, lo, hi):
        return vecs[v : v + 1, lo:hi]

    offset = off_ref[0]

    ticks.point()
    unpack_vectors()
    ticks.point()
    flush(vecs, vec_out)

    x_load.wait()
    pad[0:win, :] = jnp.zeros((win, d), BF)
    pad[win + tok : 2 * win + tok, :] = jnp.zeros((win, d), BF)

    @pl.loop(0, tok // 128)
    def _(b):
        rows = pl.ds(pl.multiple_of(b * 128, 128), 128)
        vhat, _ = norm_stats(x_ref[rows, :].astype(F32))
        pad[pl.ds(pl.multiple_of(b * 128 + win, 128), 128), :] = (vhat * vec(0, 0, d) + vec(1, 0, d)).astype(BF)
        ticks.within(b, (1, 3, 5, 7))

    ri = lax.broadcasted_iota(jnp.int32, (win, 2 * win), 0)
    rj = lax.broadcasted_iota(jnp.int32, (win, 2 * win), 1)
    shift_in = jnp.where(rj == ri + (win - offset), 1.0, 0.0).astype(BF)
    shift_out = jnp.where(rj == ri + offset, 1.0, 0.0).astype(BF)

    @pl.loop(0, nw)
    def _(w):
        at = pl.multiple_of(w * win, win)
        ns[pl.ds(at, win), :] = nn(shift_in, pad[pl.ds(at, 2 * win), :]).astype(BF)
        ticks.within(w, (4,))

    ns_t = act.at[0:d, 0 : nw * win]

    @pl.loop(0, nw // 3)
    def _(b):
        rows = pl.ds(pl.multiple_of(b * 384, 128), 384)
        ns_t[:, rows] = ns[rows, :].T

    ns_t_copy = flush(ns_t, nst_o)

    ticks.point()
    flush(qkv_g, qkv_o)
    wq = qkv_g.reshape(d, 3 * d)
    for blk3 in range(3):
        bias_row = None if blk3 == 1 else vec(2, (blk3 // 2) * d, (blk3 // 2) * d + d)

        @pl.loop(0, nw // 3)
        def _(b):
            rows = pl.ds(pl.multiple_of(b * 384, 128), 384)
            for n0 in range(0, d, 256):
                val = nn(ns[rows, :], wq[:, blk3 * d + n0 : blk3 * d + n0 + 256])
                if bias_row is not None:
                    val = val + bias_row[:, n0 : n0 + 256]
                proj[rows, blk3 * d + n0 : blk3 * d + n0 + 256] = val.astype(BF)

        ticks.point()

    proj_copy = flush(proj, proj_o)

    qmask = head_masks(win, HDIM**-0.5)
    vmask = head_masks(win, 1.0)
    seg_row = jnp.concatenate([seg_ref[0:1, :].astype(F32), jnp.full((1, win), -1.0, F32)], axis=1)
    seg_row = pltpu.roll(jnp.broadcast_to(seg_row, (8, tok + win)), offset, axis=1)
    segs = vec_f
    for w in range(nw):
        segs[w * 8 : w * 8 + 8, 0:win] = seg_row[:, w * win : (w + 1) * win]

    @pl.loop(0, nw)
    def _(w):
        rows = pl.ds(pl.multiple_of(w * win, win), win)
        seg_q = jnp.broadcast_to(segs[pl.ds(pl.multiple_of(w * 8, 8), 8), 0:win][0:1], (win, win))
        same = seg_q == seg_q.T
        same2 = jnp.concatenate([same, same], axis=1)
        for pr in range(HEADS // 2):
            lanes = slice(pr * 128, pr * 128 + 128)
            q2 = proj[rows, pr * 128 : pr * 128 + 128]
            k2 = proj[rows, d + pr * 128 : d + pr * 128 + 128]
            v2 = proj[rows, 2 * d + pr * 128 : 2 * d + pr * 128 + 128]
            s = jnp.where(same2, nt(k2, split_heads(q2, qmask)), -1e30)
            e = jnp.exp(s - jnp.max(s, axis=0, keepdims=True))
            pb = (e * (1.0 / jnp.sum(e, axis=0, keepdims=True))).astype(BF)
            prob[w, pr] = pb
            stacked = jnp.concatenate([pb[:, :win], pb[:, win:]], axis=0)
            pad[rows, lanes] = tn(stacked, split_heads(v2, vmask)).astype(BF)
        ticks.within(w, range(nw))

    prob_copy = flush(prob, prob_o)

    flush(wo_g, wo_o)
    wo = wo_g.reshape(d, d)
    proj_copy.wait()
    heads_t = proj.at[0:d, 0:tok]
    n2_t = proj.at[0:d, tok : 2 * tok]

    @pl.loop(0, tok // 128)
    def _(b):
        at = pl.multiple_of(b * 128, 128)
        hb = nn(shift_out, pad[pl.ds(at, 2 * win), :]).astype(BF)
        heads[pl.ds(at, 128), :] = hb
        heads_t[:, pl.ds(at, 128)] = hb.T

    ticks.point()

    @pl.loop(0, tok // 256)
    def _(b):
        rows = pl.ds(pl.multiple_of(b * 256, 256), 256)
        val = x_ref[rows, :].astype(F32) + nn(heads[rows, :], wo[...]) + vec(3, 0, d)
        r1[rows, :] = val
        vhat, _ = norm_stats(val)
        low = (vhat * vec(4, 0, d) + vec(5, 0, d)).astype(BF)
        n2[rows, :] = low
        n2_t[:, rows] = low.T
        ticks.within(b, (0, 1, 2))

    flush(heads_t, headst_o)
    flush(r1, r1_o)
    flush(n2_t, n2t_o)
    ns_t_copy.wait()

    wi = wi_g.reshape(2, d, half_ff)

    @pl.loop(0, half_ff // 256)
    def _(j):
        cols = pl.ds(pl.multiple_of(j * 256, 256), 256)
        base = ticks.count
        for hx in range(2):
            for q in range(half_ff // 256):
                if ticks.table[base + 2 * q + hx]:
                    pl.when(j == q)(functools.partial(ticks.run, base + 2 * q + hx))
            ocols = pl.ds(pl.multiple_of(hx * half_ff + j * 256, 256), 256)
            bias_row = vecs[6:7, ocols]
            for m in range(0, tok, 256):
                pre = nn(n2[m : m + 256, :], wi[hx, :, cols]) + bias_row
                g, dg = gelu_pair(pre)
                act[m : m + 256, ocols] = g.astype(BF)
                gd[m : m + 256, ocols] = dg.astype(BF)
        ticks.count = base + 2 * (half_ff // 256)

    flush(act, act_o)
    flush(gd, gd_o)

    ticks.point()
    flush(wi_g, wi_o)
    flush(wf_g, wf_o)
    wf = wf_g.reshape(2, d, half_ff)

    @pl.loop(0, tok // 256)
    def _(b):
        rows = pl.ds(pl.multiple_of(b * 256, 256), 256)
        for n0 in range(0, d, 256):
            cols = slice(n0, n0 + 256)
            val = nt(act[rows, 0:half_ff], wf[0, cols, :]) + nt(act[rows, half_ff:], wf[1, cols, :])
            val = r1[rows, cols] + val + vec(7, n0, n0 + 256)
            r2[n0 // 128, rows, :] = val[:, :128]
            r2[n0 // 128 + 1, rows, :] = val[:, 128:]
        ticks.within(b, range(4))

    for k in range(KER):
        for q in range(d // 128):
            molin[:, k * d + q * 128 : k * d + q * 128 + 128] = r2[q, pl.ds(k, mols, stride=KER), :].astype(BF)

    prob_copy.wait()
    for k in range(KER):
        for q in range(d // 128):
            prob[k, q] = molin[:, k * d + q * 128 : k * d + q * 128 + 128].T
    flush(prob.at[0:KER], mit_o)
    cv = cv_g.reshape(2, KER * d, d // 2)
    parts = {}
    for q in range(3):
        ticks.point()
        for hx in range(2):
            at = hx * (d // 2) + q * 128
            pre = nn(molin[...], cv[hx, :, q * 128 : q * 128 + 128]) + vec(8, at, at + 128)
            parts[at] = gelu_pair(pre)
        flush(cv_g.at[:, :, :, :, :, q * 128 : q * 128 + 128], cv_o.at[:, :, :, :, :, q * 128 : q * 128 + 128])
    dmol_load.wait()
    g = jnp.concatenate([parts[at][0] for at in range(0, d, 128)], axis=1)
    dg = jnp.concatenate([parts[at][1] for at in range(0, d, 128)], axis=1)
    vhat, r = norm_stats(g.astype(BF).astype(F32))
    mol_out[...] = vhat * vec(9, 0, d) + vec(10, 0, d)
    cot = dmol_ref[...].astype(F32)
    ln3_out[0:1, :] = jnp.sum(cot * vhat, axis=0, keepdims=True)
    ln3_out[1:2, :] = jnp.sum(cot, axis=0, keepdims=True)
    da = norm_grad(vhat, r, cot * vec(9, 0, d)).astype(BF).astype(F32)
    dcp_out[...] = (da * dg).astype(BF)
    for t, (full, kind) in enumerate(zip(fulls, kinds)):
        pick = functools.partial(block, full, kind, cut=(ALL, ALL))
        z, y, c, x = place.z, place.y, place.c, place.x
        sends.sent(t, {"z": pick(slice(0, 3), y, c, x), "a": pick(ALL, y, c, x), "b": pick(ALL, y, c, ALL), "c": pick(ALL, ALL, c, ALL)})
    for copy in out_copies:
        if not any(copy is early for early in (ns_t_copy, proj_copy, prob_copy)):
            copy.wait()


def scatter_plan(shapes):
    plan = [(5, 1, c) for c in row_cuts(shapes[5][0], 6)]
    for wf_cut, wi_cut in zip(col_cuts(shapes[4][1], 6), col_cuts(shapes[3][1], 6)):
        plan += [(4, 1, wf_cut), (3, 1, wi_cut)]
    plan += [(2, 2, c) for c in col_cuts(shapes[2][1], 1)]
    plan += [(1, 2, c) for c in col_cuts(shapes[1][1], 3)]
    plan += [(0, 0, ((ALL, ALL), None))]
    return plan


def backward_kernel(dims, sizes, *refs):
    (off_ref, x_i, dcp_ref, vecs, ln3_ref, qkv_i, wo_i, wi_i, wf_i, cv_i, nst_i, proj_i, prob_i, headst_i, r1_i, n2t_i, act_i, gd_i, mit_i) = refs[:19]
    dch_out = refs[19]
    own_dst = refs[20:26]
    grads = refs[26:32]
    from_core = refs[32:38]
    from_b = refs[38:44]
    from_a = refs[44:50]
    from_z = refs[50:56]
    own_outs = refs[56:62]
    sums, res_sem, tile_sem, load_sem, out_sem, own_sem, send_sem, recv_sem = refs[62:]
    tok, d, ff = dims
    win = WIN
    nw = tok // win + 1
    half_ff = ff // 2
    mols = tok // KER
    place = Place()
    z, y, c, x = place.z, place.y, place.c, place.x
    plan = scatter_plan([o.shape for o in own_outs])
    place.barrier()
    sends = Sends(place, send_sem, recv_sem)

    def add_blocks(dst_of, src_of):
        if not sends.live:
            return

        dst, src = dst_of(ALL), src_of(ALL)
        dst[...] = dst[...] + src[...]

    def vector_stage(stage, i, kind, g, rc, rb, ra, rz, own):
        both, mine = (ALL, ALL), block(g, kind, ALL, y, c, x, (ALL, ALL))
        if stage == 0:
            sends.go(0, i, "c", 0, block(g, kind, ALL, ALL, place.nc, ALL, both), rc, "c")
        elif stage == 1:
            sends.got(0, i, "c", rc)
            for q in range(2):
                add_blocks(lambda zz: block(g, kind, zz, ALL, c, place.at[q], both), lambda zz: rc.at[zz, :, place.at[q]])
            sends.go(0, i, "b", 0, block(g, kind, ALL, y, c, place.nx, both), rb.at[place.at[0]], "x")
            sends.go(0, i, "b", 1, block(g, kind, ALL, place.ny, c, x, both), rb.at[place.at[1]], "y")
            sends.go(0, i, "a", 0, block(g, kind, ALL, place.ny, c, place.nx, both), ra, "d")
        elif stage == 2:
            sends.got(0, i, "b", rb)
            sends.got(0, i, "a", ra)
            if sends.live:
                mine[...] = (mine[...] + rb[0]) + (rb[1] + ra[...])
            for q in (1, 2, 3):
                sends.go(0, i, "z", q, block(g, kind, place.far_z[q], y, c, x, both), rz.at[place.at[q - 1]], "z%d" % q)
        elif stage == 3:
            sends.got(0, i, "z", rz)
            if sends.live:
                own[...] = (block(g, kind, z, y, c, x, both)[...] + rz[0]) + (rz[1] + rz[2])

    own_copies = [pltpu.make_async_copy(o, p, own_sem.at[q]) for q, (o, p) in enumerate(zip(own_outs, own_dst))]
    last_piece = {plan[i][0]: i for row in SCATTER_TABLE for step, i in row if step == (3 if plan[i][0] == 0 else 4)}

    def comm_stage(stage, i):
        work_stage(stage, i)
        t = plan[i][0]
        if sends.live and last_piece[t] == i and stage == (3 if t == 0 else 4):
            own_copies[t].start()

    def work_stage(stage, i):
        t, kind, cuts = plan[i]
        g, rc, rb, ra, rz, own = grads[t], from_core[t], from_b[t], from_a[t], from_z[t], own_outs[t]

        def core_blk(zs, ys, xs, cut):
            if kind == 2:
                return rc.at[zs, ys, rows_of(rc, xs), cut[1]]
            return rc.at[(zs, ys, xs) + cut] if kind == 0 else rc.at[(xs, zs, ys) + cut]

        if t == 0:
            vector_stage(stage, i, kind, g, rc, rb, ra, rz, own)
            return
        whole = union(cuts)
        waits = {
            1: ("c", core_blk(ALL, ALL, ALL, whole)),
            2: ("b", rb.at[(ALL, ALL) + whole]),
            3: ("a", ra.at[(ALL,) + whole]),
            4: ("z", rz.at[(ALL,) + whole]),
        }
        if stage > 0:
            sends.got(t, i, *waits[stage])
        for h, cut in enumerate(cuts):
            if cut is None:
                continue
            a, b = order(h)
            if stage == 0:
                sends.go(t, i, "c", h, block(g, kind, ALL, ALL, place.nc, ALL, cut), core_blk(ALL, ALL, ALL, cut), "c")
            elif stage == 1:
                for far in (1, 0):
                    for o in range(2):
                        ys, xs = (place.ny if far else y, place.at[o]) if h == 0 else (place.at[o], place.nx if far else x)
                        add_blocks(lambda zz: block(g, kind, zz, ys, c, xs, cut), lambda zz: core_blk(zz, ys, xs, cut))
                        if far:
                            sends.go(t, i, "b", (h, o), block(g, kind, ALL, ys, c, xs, cut), rb.at[(place.at[o], ALL) + cut], b)
            elif stage == 2:
                near, other = (x, place.nx) if h == 0 else (y, place.ny)
                for far in (1, 0):
                    o = other if far else near
                    ys, xs = (y, o) if h == 0 else (o, x)
                    add_blocks(lambda zz: block(g, kind, zz, ys, c, xs, cut), lambda zz: rb.at[(o, zz) + cut])
                    if far:
                        sends.go(t, i, "a", h, block(g, kind, ALL, ys, c, xs, cut), ra.at[(ALL,) + cut], a)
            elif stage == 3:
                add_blocks(lambda zz: block(g, kind, zz, y, c, x, cut), lambda zz: ra.at[(zz,) + cut])
                for q in (1, 2, 3):
                    sends.go(t, i, "z", (h, q), block(g, kind, place.far_z[q], y, c, x, cut), rz.at[(place.at[q - 1],) + cut], "z%d" % q)
            elif sends.live:
                total = block(g, kind, z, y, c, x, cut)[...].astype(F32)
                for q in range(3):
                    total = total + rz.at[(place.at[q],) + cut][...].astype(F32)
                if t != 1:
                    own[cut] = total
                    continue
                for q in range(0, cut[1].stop - cut[1].start, 128):
                    part, r = divmod(cut[1].start + q, d)
                    to = (r // 256) * d + part * 256 + r % 256
                    own[:, to : to + 128] = total[:, q : q + 128]

    for stage in range(5):
        for i in range(len(plan)):
            comm_stage(stage, i)
    sends.live = True
    ticks = Ticks(SCATTER_TABLE, comm_stage)
    state = {"load": 0}

    def load(src, dst):
        copy = pltpu.make_async_copy(src, dst, load_sem.at[state["load"]])
        state["load"] += 1
        copy.start()
        return copy

    def vec(v, lo, hi):
        return vecs[v : v + 1, lo:hi]

    offset = off_ref[0]
    ri = lax.broadcasted_iota(jnp.int32, (win, 2 * win), 0)
    rj = lax.broadcasted_iota(jnp.int32, (win, 2 * win), 1)
    shift_in = jnp.where(rj == ri + (win - offset), 1.0, 0.0).astype(BF)
    shift_out = jnp.where(rj == ri + offset, 1.0, 0.0).astype(BF)
    sums[...] = jnp.zeros_like(sums)
    sums[9:10, 0:d] = ln3_ref[0:1, :]
    sums[10:11, 0:d] = ln3_ref[1:2, :]
    sums[8:9, 0:d] = jnp.sum(dcp_ref[...].astype(F32), axis=0, keepdims=True)
    g_vec, g_qkv, g_wo, g_wi, g_wf, g_cv = grads
    g_cv2 = g_cv.reshape(2, KER * d, d // 2)
    g_wi2 = g_wi.reshape(2, d, half_ff)
    g_wf2 = g_wf.reshape(2, d, half_ff)

    def rows_of_dres(dres, rows):
        return jnp.concatenate([dres[q, rows, :] for q in range(d // 128)], axis=1)

    def set_dres(dres, rows, val):
        for q in range(d // 128):
            dres[q, rows, :] = val[:, q * 128 : q * 128 + 128]

    def whole(dres, dpad):
        def conv_part(cv, mi):
            loads = [load(mit_i, mi), load(cv_i, cv)]
            cv2 = cv.reshape(2, KER * d, d // 2)
            loads[0].wait()
            for kk in range(KER):
                val = nn(mi[kk].reshape(d, mols), dcp_ref[...]).astype(BF)
                g_cv2[0, kk * d : kk * d + d, :] = val[:, : d // 2]
                g_cv2[1, kk * d : kk * d + d, :] = val[:, d // 2 :]

            ticks.point()
            loads[1].wait()
            for kk in range(KER):
                for n0 in range(0, d, 256):
                    rows = slice(kk * d + n0, kk * d + n0 + 256)
                    val = nt(dcp_ref[:, : d // 2], cv2[0, rows, :]) + nt(dcp_ref[:, d // 2 :], cv2[1, rows, :])
                    dres[n0 // 128, pl.ds(kk, mols, stride=KER), :] = val[:, :128]
                    dres[n0 // 128 + 1, pl.ds(kk, mols, stride=KER), :] = val[:, 128:]
                ticks.point()

        pl.run_scoped(conv_part, pltpu.VMEM(cv_i.shape, BF), pltpu.VMEM(mit_i.shape, BF))

        def pack_vectors():
            g_vec2 = g_vec.reshape(-1, SLOT)
            nrow = g_vec2.shape[0] // 16
            g_vec[...] = jnp.zeros_like(g_vec)
            for width, count in sorted(set(sizes)):
                pick, mine = vector_masks(width, count, nrow)
                for v in [i for i, s in enumerate(sizes) if s == (width, count)]:
                    spread = jnp.where(mine, sums[v : v + 1, :width], 0.0)
                    top = spread.astype(BF)
                    rest = (spread - top.astype(F32)).astype(BF)
                    g_vec2[pl.ds(v, nrow, stride=16), :] = nt(top, pick) + nt(rest, pick)

        def attn_part(proj, ns_t, dn1, loads, wqkv):
            proj_loads, ns_load = loads[:-1], loads[-1]
            qkv_load = load(qkv_i, wqkv)
            qmask = head_masks(win, HDIM**-0.5)
            vmask = head_masks(win, 1.0)
            g_qkv2 = g_qkv.reshape(d, 3 * d)
            wqkv2 = wqkv.reshape(d, 3 * d)

            def core_part(prob):
                n3 = nw // 3

                def prob_copy(i):
                    g, b, slot = lax.div(i, n3), lax.rem(i, n3), lax.rem(i, 2)
                    return pltpu.make_async_copy(prob_i.at[pl.ds(3 * b, 3), pl.ds(2 * g, 2)], prob.at[slot], res_sem.at[slot])

                prob_copy(0).start()
                ns_load.wait()
                base = ticks.count

                @pl.loop(0, d // 256)
                def _(g):
                    lq, lk, lv = [pl.ds(pl.multiple_of(r * d + g * 256, 256), 256) for r in range(3)]

                    @pl.loop(0, n3)
                    def _(b):
                        i = g * n3 + b
                        for q in range(n3):
                            pl.when(i == q)(proj_loads[q].wait)
                        prob_copy(i).wait()

                        @pl.when(i + 1 < n3 * (d // 256))
                        def _():
                            prob_copy(i + 1).start()

                        for u in range(3):
                            at = pl.multiple_of(b * (3 * win) + u * win, win)
                            rows = pl.ds(at, win)
                            dhw = nn(shift_in, dpad[pl.ds(at, 2 * win), lq]).astype(BF)
                            q4, k4, v4 = proj[rows, lq], proj[rows, lk], proj[rows, lv]
                            new = [[], [], []]
                            for pr in range(2):
                                lanes = slice(pr * 128, pr * 128 + 128)
                                q2, k2, v2 = q4[:, lanes], k4[:, lanes], v4[:, lanes]
                                pb = prob[lax.rem(i, 2), u, pr]
                                dbd = split_heads(dhw[:, lanes], vmask)
                                dp = nt(v2, dbd)
                                pf = pb.astype(F32)
                                ds = (pf * (dp - jnp.sum(pf * dp, axis=0, keepdims=True))).astype(BF)
                                stacked = jnp.concatenate([ds[:, :win], ds[:, win:]], axis=0)
                                new[0].append(tn(stacked, split_heads(k2, qmask)).astype(BF))
                                new[1].append(nn(ds, split_heads(q2, qmask)).astype(BF))
                                new[2].append(nn(pb, dbd).astype(BF))
                            for lanes, parts in zip((lq, lk, lv), new):
                                proj[rows, lanes] = jnp.concatenate(parts, axis=1)
                        for q in range(3):
                            for bb in range(n3):
                                if ticks.table[base + q * (n3 + 1) + bb]:
                                    pl.when(i == q * n3 + bb)(functools.partial(ticks.run, base + q * (n3 + 1) + bb))

                    for r, cols in enumerate((lq, lk, lv)):
                        to = pl.ds(pl.multiple_of(g * d + r * 256, 256), 256)
                        part = proj[:, cols]
                        if r != 1:
                            into = pl.ds(pl.multiple_of((r // 2) * d + g * 256, 256), 256)
                            sums[2:3, into] = jnp.sum(part.astype(F32), axis=0, keepdims=True)
                        g_qkv2[:, to] = nn(ns_t[...], part).astype(BF)
                    for q in range(3):
                        pl.when(g == q)(functools.partial(ticks.run, base + q * (n3 + 1) + n3))

                ticks.count = base + 3 * (n3 + 1)

            pl.run_scoped(core_part, pltpu.VMEM((2, 3, 2, win, 2 * win), BF))
            x_rows = dpad.at[0:tok]
            x_load = load(x_i, x_rows)
            qkv_load.wait()

            @pl.loop(0, nw // 3)
            def _(b):
                rows = pl.ds(pl.multiple_of(b * 384, 128), 384)
                for n0 in range(0, d, 256):
                    dn1[rows, n0 : n0 + 256] = nt(proj[rows, :], wqkv2[n0 : n0 + 256, :])
                ticks.within(b, range(3))

            x_load.wait()

            @pl.loop(0, tok // 128)
            def _(b):
                at = pl.multiple_of(b * 128, 128)
                rows = pl.ds(at, 128)
                both = pl.ds(at, 2 * win)
                high = dn1[both, :].astype(BF)
                cot = nn(shift_out, high) + nn(shift_out, (dn1[both, :] - high.astype(F32)).astype(BF))
                vhat, _ = norm_stats(x_rows[rows, :].astype(F32))
                sums[0:1, 0:d] += jnp.sum(cot * vhat, axis=0, keepdims=True)
                sums[1:2, 0:d] += jnp.sum(cot, axis=0, keepdims=True)
                dn1[rows, :] = cot
                ticks.within(b, range(8))

            pack_vectors()
            ticks.point()

            @pl.loop(0, tok // 128)
            def _(b):
                rows = pl.ds(pl.multiple_of(b * 128, 128), 128)
                vhat, r = norm_stats(x_rows[rows, :].astype(F32))
                set_dres(dres, rows, rows_of_dres(dres, rows) + norm_grad(vhat, r, dn1[rows, :] * vec(0, 0, d)))
                ticks.within(b, range(8))

        def ff_part(dn2_rows, r1):
            dn2 = dn2_rows.at[0:tok]
            r1_load = pltpu.make_async_copy(r1_i, r1, out_sem.at[1])
            def inner(act, gd, wf, wi, dff, dff_t, n2_t, dh):
                n2_load = load(n2t_i, n2_t)

                def tile_copies(j):
                    slot, hx, jj = lax.rem(j, 2), lax.rem(j, 2), lax.div(j, 2)
                    cols = pl.ds(pl.multiple_of(hx * half_ff + jj * 256, 256), 256)
                    wcols = pl.ds(pl.multiple_of(jj * 256, 256), 256)
                    pairs = (
                        (act_i.at[:, cols], act),
                        (gd_i.at[:, cols], gd),
                        (wf_i.at[hx, :, :, :, :, wcols], wf),
                        (wi_i.at[hx, :, :, :, :, wcols], wi),
                    )
                    return [pltpu.make_async_copy(s, b.at[slot], tile_sem.at[slot, q]) for q, (s, b) in enumerate(pairs)]

                for copy in tile_copies(0):
                    copy.start()
                r1_load.start()
                ticks.point()

                @pl.loop(0, tok // 256)
                def _(b):
                    rows = pl.ds(pl.multiple_of(b * 256, 256), 256)
                    val = rows_of_dres(dres, rows).astype(BF)
                    dff[rows, :] = val
                    sums[7:8, 0:d] += jnp.sum(val.astype(F32), axis=0, keepdims=True)
                    dff_t[:, rows] = val.T
                    ticks.within(b, range(4))

                n2_load.wait()
                n_tiles = ff // 256

                @pl.loop(0, n_tiles)
                def _(j):
                    slot, hx, jj = lax.rem(j, 2), lax.rem(j, 2), lax.div(j, 2)
                    for copy in tile_copies(j):
                        copy.wait()

                    @pl.when(j + 1 < n_tiles)
                    def _():
                        for copy in tile_copies(j + 1):
                            copy.start()

                    wcols = pl.ds(pl.multiple_of(jj * 256, 256), 256)
                    wf_j = wf.at[slot].reshape(d, 256)
                    wi_j = wi.at[slot].reshape(d, 256)
                    total = jnp.zeros((1, 256), F32)
                    for m in range(0, tok, FF_ROWS):
                        val = (nn(dff[m : m + FF_ROWS, :], wf_j[...]) * gd[slot, m : m + FF_ROWS, :].astype(F32)).astype(BF)
                        dh[m : m + FF_ROWS, :] = val
                        total = total + jnp.sum(val.astype(F32), axis=0, keepdims=True)
                    sums[6:7, pl.ds(pl.multiple_of(hx * half_ff + jj * 256, 256), 256)] = total
                    g_wf2[hx, :, wcols] = nn(dff_t[...], act[slot]).astype(BF)
                    g_wi2[hx, :, wcols] = nn(n2_t[...], dh[...]).astype(BF)

                    @pl.when(j == 0)
                    def _():
                        dn2[...] = nt(dh[...], wi_j[...])

                    @pl.when(j > 0)
                    def _():
                        dn2[...] += nt(dh[...], wi_j[...])

                    ticks.within(j, range(12))

            pl.run_scoped(
                inner,
                pltpu.VMEM((2, tok, 256), BF),
                pltpu.VMEM((2, tok, 256), BF),
                pltpu.VMEM((2, 4, 2, 2, d // 16, 256), BF),
                pltpu.VMEM((2, 4, 2, 2, d // 16, 256), BF),
                pltpu.VMEM((tok, d), BF),
                pltpu.VMEM((d, tok), BF),
                pltpu.VMEM((d, tok), BF),
                pltpu.VMEM((tok, 256), BF),
            )

            def out_part(heads_t, wo, dattn):
                loads = [load(headst_i, heads_t), load(wo_i, wo)]
                wo2 = wo.reshape(d, d)
                g_wo2 = g_wo.reshape(d, d)
                r1_load.wait()

                @pl.loop(0, tok // 128)
                def _(b):
                    rows = pl.ds(pl.multiple_of(b * 128, 128), 128)
                    vhat, r = norm_stats(r1[rows, :])
                    cot = dn2[rows, :]
                    sums[4:5, 0:d] += jnp.sum(cot * vhat, axis=0, keepdims=True)
                    sums[5:6, 0:d] += jnp.sum(cot, axis=0, keepdims=True)
                    val = rows_of_dres(dres, rows) + norm_grad(vhat, r, cot * vec(4, 0, d))
                    set_dres(dres, rows, val)
                    low = val.astype(BF)
                    dattn[rows, :] = low
                    sums[3:4, 0:d] += jnp.sum(low.astype(F32), axis=0, keepdims=True)
                    ticks.within(b, range(8))

                for copy in loads:
                    copy.wait()
                g_wo2[...] = nn(heads_t[...], dattn[...]).astype(BF)
                ticks.point()
                dpad[0:win, :] = jnp.zeros((win, d), BF)
                dpad[win + tok : 2 * win + tok, :] = jnp.zeros((win, d), BF)

                @pl.loop(0, tok // 512)
                def _(b):
                    at = pl.multiple_of(b * 512, 256)
                    dpad[pl.ds(at + win, 512), :] = nt(dattn[pl.ds(at, 512), :], wo2[...]).astype(BF)
                    ticks.within(b, (0, 1))

            def rest(proj, ns_t):
                loads = [load(proj_i.at[pl.ds(b * 384, 384)], proj.at[pl.ds(b * 384, 384)]) for b in range(nw // 3)]
                loads.append(load(nst_i, ns_t))
                pl.run_scoped(out_part, pltpu.VMEM((d, tok), BF), pltpu.VMEM(wo_i.shape, BF), pltpu.VMEM((tok, d), BF))
                pl.run_scoped(functools.partial(attn_part, proj, ns_t, dn2_rows, loads), pltpu.VMEM(qkv_i.shape, BF))

            pl.run_scoped(rest, pltpu.VMEM(proj_i.shape, BF), pltpu.VMEM(nst_i.shape, BF))

        pl.run_scoped(ff_part, pltpu.VMEM((nw * win, d), F32), pltpu.VMEM((tok, d), F32))
        done = pltpu.make_async_copy(dres, dch_out, out_sem.at[0])
        done.start()

        ticks.point()
        for t, g in enumerate(grads):
            pick = functools.partial(block, g, KINDS[t], cut=(ALL, ALL))
            sends.sent(t, {"z": pick(slice(0, 3), y, c, x), "a": pick(ALL, y, c, x), "b": pick(ALL, y, c, ALL), "c": pick(ALL, ALL, c, ALL)})
        done.wait()
        for copy in own_copies:
            copy.wait()

    pl.run_scoped(whole, pltpu.VMEM((d // 128, tok, 128), F32), pltpu.VMEM((tok + 2 * win, d), BF))


def quick_mesh(mesh):
    return mesh.shape["dp"] == 16 and mesh.shape["mp"] == 2


def gathered_shape(shape, kind):
    if kind == 2:
        return (4, 2, 2, 2 * shape[0], shape[1])
    return ((4, 2, 2, 2) if kind == 0 else (2, 4, 2, 2)) + shape


def place_kernel(widths, *refs):
    n = (len(refs) - 3 - 2 * len(widths)) // 3
    sources, vec_ref, outs, vec_outs = refs[:n], refs[n], refs[n + 1 : 2 * n + 1], refs[2 * n + 1 : 2 * n + 1 + len(widths)]
    rest = refs[2 * n + 1 + len(widths) :]
    held, rows, in_sem, out_sem = rest[:n], rest[n : n + len(widths)], rest[-2], rest[-1]
    parts = held[-1].shape[0]
    pairs = [(sources[-1].at[q], held[-1].at[q], outs[-1].at[:, q * SLOT : q * SLOT + SLOT]) for q in range(parts)]
    pairs += list(zip(sources[:-1], held[:-1], outs[:-1]))
    loads = [pltpu.make_async_copy(s, h, in_sem.at[i]) for i, (s, h, _) in enumerate(pairs)]
    stores = [pltpu.make_async_copy(h, o, out_sem.at[i]) for i, (_, h, o) in enumerate(pairs)]
    for copy in loads:
        copy.start()
    for v, width in enumerate(widths):
        rows[v][...] = vec_ref[v, :width]
        stores.append(pltpu.make_async_copy(rows[v], vec_outs[v], out_sem.at[len(pairs) + v]))
        stores[-1].start()
    for load, store in zip(loads, stores):
        load.wait()
        store.start()
    for copy in stores:
        copy.wait()


def fast_shards(*args):
    (chars, seg, offs, l1g, l1b, wqkv, qvb, wo, aob, l2g, l2b, wi, fib, wf, fob, cv, cvb, l3g, l3b, dmol) = args
    tok, d = chars.shape
    mols = dmol.shape[0]
    vectors = (l1g, l1b, qvb, aob, l2g, l2b, fib, fob, cvb, l3g, l3b)
    sizes = tuple((v.shape[0] * 32, v.shape[0]) for v in vectors)
    ff = sizes[6][0]
    dims = (tok, d, ff)
    nw = tok // WIN + 1
    vec_own = sum(jnp.pad(v[None], ((i, 15 - i), (0, SLOT - v.shape[0]))) for i, v in enumerate(vectors))
    owns = (vec_own, wqkv, wo, wi, wf.T, cv)
    kinds = KINDS
    full = [gathered_shape(o.shape, k) for o, k in zip(owns, kinds)]
    plan = gather_plan([o.shape for o in owns])
    n_wait = 5 * len(plan)
    on_chip = pl.BlockSpec(memory_space=pltpu.VMEM)
    scalar = pl.BlockSpec(memory_space=pltpu.SMEM)
    any_mem = pl.BlockSpec(memory_space=pl.ANY)
    bf = lambda *s: jax.ShapeDtypeStruct(s, BF)
    f32 = lambda *s: jax.ShapeDtypeStruct(s, F32)
    prob_shape = (nw, HEADS // 2, WIN, 2 * WIN)
    saved = pl.pallas_call(
        functools.partial(forward_kernel, dims, sizes),
        out_shape=[
            f32(mols, d),
            f32(16, ff),
            f32(8, d),
            bf(mols, d),
            *[bf(*s) for s in full[1:]],
            bf(d, nw * WIN),
            bf(nw * WIN, 3 * d),
            bf(*prob_shape),
            bf(d, tok),
            f32(tok, d),
            bf(d, tok),
            bf(tok, ff),
            bf(tok, ff),
            bf(KER, d // SLOT, SLOT, mols),
        ],
        in_specs=[scalar, on_chip, any_mem, any_mem] + [on_chip] * 6,
        out_specs=[on_chip, any_mem, on_chip, on_chip] + [any_mem] * 14,
        scratch_shapes=[
            *[pltpu.VMEM(s, BF) for s in full],
            pltpu.VMEM((512, SLOT), F32),
            pltpu.VMEM((16, ff), F32),
            pltpu.VMEM((tok + 2 * WIN, d), BF),
            pltpu.VMEM((nw * WIN, d), BF),
            pltpu.VMEM((nw * WIN, 3 * d), BF),
            pltpu.VMEM(prob_shape, BF),
            pltpu.VMEM((tok, d), BF),
            pltpu.VMEM((tok, d), F32),
            pltpu.VMEM((tok, d), BF),
            pltpu.VMEM((tok, ff), BF),
            pltpu.VMEM((tok, ff), BF),
            pltpu.VMEM((d // 128, tok, 128), F32),
            pltpu.VMEM((mols, KER * d), BF),
            pltpu.VMEM((tok, d), BF),
            pltpu.VMEM((mols, d), BF),
            pltpu.SemaphoreType.DMA((8,)),
            pltpu.SemaphoreType.DMA((20,)),
            pltpu.SemaphoreType.DMA((24,)),
            pltpu.SemaphoreType.DMA((n_wait,)),
        ],
        compiler_params=pltpu.CompilerParams(collective_id=1, has_side_effects=True, vmem_limit_bytes=VMEM_CAP),
        name="gather_forward",
    )(offs, seg, chars, dmol, *owns)
    (mol, vecs, ln3, dcp, qkv_f, wo_f, wi_f, wf_f, cv_f, ns, proj, prob, heads, r1, n2, act, gd, mi) = saved

    own_shapes = [o.shape for o in owns]
    kind_core = lambda s, k: (4, 2, 2 * s[0], s[1]) if k == 2 else ((4, 2, 2) if k == 0 else (2, 4, 2)) + s
    types = [F32] + [BF] * 5
    plan = scatter_plan(own_shapes)
    n_back = 5 * len(plan)
    back = pl.pallas_call(
        functools.partial(backward_kernel, dims, sizes),
        out_shape=[f32(d // SLOT, tok, SLOT)] + [f32(*s) for s in own_shapes],
        in_specs=[scalar, any_mem] + [on_chip] * 3 + [any_mem] * 14,
        out_specs=[any_mem] * 7,
        scratch_shapes=[
            *[pltpu.VMEM(s, t) for s, t in zip(full, types)],
            *[pltpu.VMEM(kind_core(s, k), t) for s, k, t in zip(own_shapes, kinds, types)],
            *[pltpu.VMEM((2, 4) + s, t) for s, t in zip(own_shapes, types)],
            *[pltpu.VMEM((4,) + s, t) for s, t in zip(own_shapes, types)],
            *[pltpu.VMEM((3,) + s, t) for s, t in zip(own_shapes, types)],
            *[pltpu.VMEM(s, F32) for s in own_shapes],
            pltpu.VMEM((16, ff), F32),
            pltpu.SemaphoreType.DMA((2,)),
            pltpu.SemaphoreType.DMA((2, 4)),
            pltpu.SemaphoreType.DMA((16,)),
            pltpu.SemaphoreType.DMA((2,)),
            pltpu.SemaphoreType.DMA((6,)),
            pltpu.SemaphoreType.DMA((24,)),
            pltpu.SemaphoreType.DMA((n_back,)),
        ],
        compiler_params=pltpu.CompilerParams(collective_id=2, has_side_effects=True, vmem_limit_bytes=VMEM_CAP),
        name="backward_scatter",
    )(offs, chars, dcp, vecs, ln3, qkv_f, wo_f, wi_f, wf_f, cv_f, ns, proj, prob, heads, r1, n2, act, gd, mi)
    d_chars, d_vec, d_qkv, d_wo, d_wi, d_wf, d_cv = back
    large = (d_wo, d_qkv, d_wi, d_wf, d_cv, mol, d_chars)
    done = pl.pallas_call(
        functools.partial(place_kernel, tuple(v.shape[0] for v in vectors)),
        out_shape=[f32(*a.shape) for a in large[:-1]] + [f32(tok, d)] + [f32(v.shape[0]) for v in vectors],
        in_specs=[any_mem] * len(large) + [on_chip],
        out_specs=[any_mem] * (len(large) + len(vectors)),
        scratch_shapes=[
            *[pltpu.VMEM(a.shape, F32) for a in large],
            *[pltpu.VMEM(v.shape, F32) for v in vectors],
            pltpu.SemaphoreType.DMA((len(large) - 1 + d // SLOT,)),
            pltpu.SemaphoreType.DMA((len(large) - 1 + d // SLOT + len(vectors),)),
        ],
        compiler_params=pltpu.CompilerParams(vmem_limit_bytes=VMEM_CAP),
        name="place",
    )(*large, d_vec)
    d_wo, d_qkv, d_wi, d_wf, d_cv, mol, d_chars = done[: len(large)]
    dv = done[len(large) :]
    return (
        mol,
        d_chars,
        dv[0],
        dv[1],
        d_qkv,
        dv[2],
        d_wo,
        dv[3],
        dv[4],
        dv[5],
        d_wi,
        dv[6],
        d_wf.T,
        dv[7],
        d_cv,
        dv[8],
        dv[9],
        dv[10],
    )


def solution(mesh):
    placed = (
        P(("dp", "mp"), None),
        P(("dp", "mp"), None),
        P(("dp", "mp")),
        P(("dp", "mp")),
        P(("dp", "mp")),
        P(("dp", "mp"), None),
        P(("dp", "mp")),
        P(("dp", "mp"), None),
        P(("dp", "mp")),
        P(("dp", "mp")),
        P(("dp", "mp")),
        P("dp", "mp"),
        P(("dp", "mp")),
        P("mp", "dp"),
        P(("dp", "mp")),
        P("dp", "mp"),
        P(("dp", "mp")),
        P(("dp", "mp")),
        P(("dp", "mp")),
        P(("dp", "mp"), None),
    )
    return jax.shard_map(
        fast_shards if quick_mesh(mesh) else shards,
        mesh=mesh,
        in_specs=placed,
        out_specs=(
            P(("dp", "mp"), None),
            P(("dp", "mp"), None),
            P(("dp", "mp")),
            P(("dp", "mp")),
            P(("dp", "mp"), None),
            P(("dp", "mp")),
            P(("dp", "mp"), None),
            P(("dp", "mp")),
            P(("dp", "mp")),
            P(("dp", "mp")),
            P("dp", "mp"),
            P(("dp", "mp")),
            P("mp", "dp"),
            P(("dp", "mp")),
            P("dp", "mp"),
            P(("dp", "mp")),
            P(("dp", "mp")),
            P(("dp", "mp")),
        ),
        check_vma=False,
    )
```

```python
import functools

import jax
import jax.numpy as jnp
from jax import lax
from jax.experimental import pallas as pl
from jax.experimental.pallas import tpu as pltpu
from jax.sharding import PartitionSpec as P

HEADS = 12
HDIM = 64
KER = 4
WIN = 128


layer_eps = 1e-06


def layer_norm(row_values, gain_vec, shift_vec):
    centred = row_values - jnp.mean(row_values, axis=-1, keepdims=True)
    spread = jnp.mean(centred * centred, axis=-1, keepdims=True)
    return centred * lax.rsqrt(spread + layer_eps) * gain_vec + shift_vec


def gelu_exact(values):
    return jax.nn.gelu(values, approximate=False)


def norm_backward(row_values, gain_vec, shift_vec, grad_out):
    _, pullback = jax.vjp(layer_norm, row_values, gain_vec, shift_vec)
    return pullback(grad_out)


def gelu_backward(values, grad_out):
    _, pullback = jax.vjp(gelu_exact, values)
    return pullback(grad_out)[0]


def three_blocks(rows, fill_value):
    edge = jnp.full_like(rows[:1], fill_value)
    before = jnp.concatenate([edge, rows[:-1]], axis=0)
    after = jnp.concatenate([rows[1:], edge], axis=0)
    return jnp.concatenate([before, rows, after], axis=1)


def fold_blocks(band_grad):
    edge = jnp.zeros_like(band_grad[:1, :WIN])
    from_next = jnp.concatenate([band_grad[1:, :WIN], edge], axis=0)
    from_prev = jnp.concatenate([edge, band_grad[:-1, 2 * WIN :]], axis=0)
    return band_grad[:, WIN : 2 * WIN] + from_next + from_prev


def band_inputs(queries, key_rows, value_rows, seg_row, offset):
    seq_len = queries.shape[0]
    block_count = seq_len // WIN
    win_row = (jnp.arange(seq_len, dtype=jnp.int32) + offset) // WIN
    seg_blk = seg_row.reshape(block_count, WIN)
    win_blk = win_row.reshape(block_count, WIN)
    return (
        queries.reshape(block_count, WIN, HEADS, HDIM),
        three_blocks(key_rows.reshape(block_count, WIN, HEADS, HDIM), 0),
        three_blocks(value_rows.reshape(block_count, WIN, HEADS, HDIM), 0),
        seg_blk,
        win_blk,
        three_blocks(seg_blk, 0),
        three_blocks(win_blk, -1),
    )


def band_scores(query_blk, key_band, seg_blk, win_blk, seg_band, win_band):
    raw_scores = jnp.einsum(
        "bqhd,bkhd->bhqk", query_blk, key_band, preferred_element_type=jnp.float32
    ) * HDIM ** (-0.5)
    allowed = (seg_blk[:, :, None] == seg_band[:, None, :]) & (
        win_blk[:, :, None] == win_band[:, None, :]
    )
    return jnp.where(allowed[:, None], raw_scores, -1e30)


def attend_forward(seq_item):
    queries, key_rows, value_rows, seg_row, offset = seq_item
    seq_len = queries.shape[0]
    query_blk, key_band, val_band, seg_blk, win_blk, seg_band, win_band = band_inputs(
        queries, key_rows, value_rows, seg_row, offset
    )
    scores = band_scores(query_blk, key_band, seg_blk, win_blk, seg_band, win_band)
    row_peak = jnp.max(scores, axis=-1, keepdims=True)
    exp_scores = jnp.exp(scores - row_peak)
    row_total = jnp.sum(exp_scores, axis=-1, keepdims=True)
    prob_low = (exp_scores / row_total).astype(jnp.bfloat16)
    merged = jnp.einsum("bhqk,bkhd->bqhd", prob_low, val_band, preferred_element_type=jnp.float32)
    return (merged.reshape(seq_len, HEADS * HDIM), (row_peak + jnp.log(row_total))[..., 0])


def attend_backward(seq_item):
    queries, key_rows, value_rows, seg_row, offset, log_norm, d_heads = seq_item
    seq_len = queries.shape[0]
    block_count = seq_len // WIN
    score_scale = HDIM ** (-0.5)
    query_blk, key_band, val_band, seg_blk, win_blk, seg_band, win_band = band_inputs(
        queries, key_rows, value_rows, seg_row, offset
    )
    grad_blk = d_heads.reshape(block_count, WIN, HEADS, HDIM)
    scores = band_scores(query_blk, key_band, seg_blk, win_blk, seg_band, win_band)
    prob_blk = jnp.exp(scores - log_norm[..., None])
    d_probs = jnp.einsum("bqhd,bkhd->bhqk", grad_blk, val_band, preferred_element_type=jnp.float32)
    row_dot = jnp.sum(prob_blk * d_probs, axis=-1, keepdims=True)
    d_scores = (prob_blk * (d_probs - row_dot)).astype(jnp.bfloat16)
    d_query = (
        jnp.einsum("bhqk,bkhd->bqhd", d_scores, key_band, preferred_element_type=jnp.float32)
        * score_scale
    )
    d_key_band = (
        jnp.einsum("bhqk,bqhd->bkhd", d_scores, query_blk, preferred_element_type=jnp.float32)
        * score_scale
    )
    d_val_band = jnp.einsum(
        "bhqk,bqhd->bkhd",
        prob_blk.astype(jnp.bfloat16),
        grad_blk,
        preferred_element_type=jnp.float32,
    )
    d_keys = fold_blocks(d_key_band)
    d_vals = fold_blocks(d_val_band)
    return (
        d_query.reshape(seq_len, HEADS * HDIM),
        d_keys.reshape(seq_len, HEADS * HDIM),
        d_vals.reshape(seq_len, HEADS * HDIM),
    )


def shards(
    chars,
    segment_ids,
    window_offsets,
    ln1_gain,
    ln1_bias,
    w_qkv,
    qv_bias,
    w_attn_out,
    attn_out_bias,
    ln2_gain,
    ln2_bias,
    w_ff_in,
    ff_in_bias,
    w_ff_out,
    ff_out_bias,
    conv_weight,
    conv_bias,
    ln3_gain,
    ln3_bias,
    d_molecules,
):
    gathered = (
        lax.all_gather(w_qkv, ("dp", "mp"), axis=0, tiled=True),
        lax.all_gather(w_attn_out, ("dp", "mp"), axis=0, tiled=True),
        lax.all_gather(ln1_gain, ("dp", "mp"), axis=0, tiled=True),
        lax.all_gather(ln1_bias, ("dp", "mp"), axis=0, tiled=True),
        lax.all_gather(qv_bias, ("dp", "mp"), axis=0, tiled=True),
        lax.all_gather(attn_out_bias, ("dp", "mp"), axis=0, tiled=True),
        lax.all_gather(ln2_gain, ("dp", "mp"), axis=0, tiled=True),
        lax.all_gather(ln2_bias, ("dp", "mp"), axis=0, tiled=True),
        lax.all_gather(ff_in_bias, ("dp", "mp"), axis=0, tiled=True),
        lax.all_gather(ff_out_bias, ("dp", "mp"), axis=0, tiled=True),
        lax.all_gather(conv_bias, ("dp", "mp"), axis=0, tiled=True),
        lax.all_gather(ln3_gain, ("dp", "mp"), axis=0, tiled=True),
        lax.all_gather(ln3_bias, ("dp", "mp"), axis=0, tiled=True),
    )
    qkv_full = gathered[0]
    attn_out_full = gathered[1]
    vectors = [vector_arg.astype(jnp.float32) for vector_arg in gathered[2:]]
    (
        gain_one,
        shift_one,
        qv_shift,
        attn_shift,
        gain_two,
        shift_two,
        hidden_shift,
        ff_shift,
        conv_shift,
        gain_three,
        shift_three,
    ) = vectors
    ff_in_part, ff_out_part, conv_part = (
        lax.all_gather(w_ff_in, "dp", axis=0, tiled=True),
        lax.all_gather(w_ff_out, "dp", axis=1, tiled=True),
        lax.all_gather(conv_weight, "dp", axis=0, tiled=True),
    )
    model_width = chars.shape[1]
    tok_rows = chars.shape[0]
    seq_count = segment_ids.shape[0]
    seq_len = segment_ids.shape[1]
    mp_rank = lax.axis_index("mp")
    hidden_part = ff_in_part.shape[1]
    channel_part = conv_part.shape[1]
    inputs = chars.astype(jnp.float32)
    normed_one = layer_norm(inputs, gain_one, shift_one).astype(jnp.bfloat16)
    qkv_shift = jnp.concatenate(
        [qv_shift[:model_width], jnp.zeros((model_width,), jnp.float32), qv_shift[model_width:]]
    )
    projected = (
        jnp.dot(normed_one, qkv_full, preferred_element_type=jnp.float32) + qkv_shift
    ).astype(jnp.bfloat16)
    per_seq = projected.reshape(seq_count, seq_len, 3, HEADS, HDIM)
    queries = per_seq[:, :, 0]
    key_rows = per_seq[:, :, 1]
    value_rows = per_seq[:, :, 2]
    merged, log_norm = lax.map(
        attend_forward, (queries, key_rows, value_rows, segment_ids, window_offsets)
    )
    heads_low = merged.reshape(tok_rows, model_width).astype(jnp.bfloat16)
    resid_one = (
        inputs + jnp.dot(heads_low, attn_out_full, preferred_element_type=jnp.float32) + attn_shift
    )
    normed_two = layer_norm(resid_one, gain_two, shift_two).astype(jnp.bfloat16)
    ff_in_use, ff_out_use, conv_use = (ff_in_part, ff_out_part, conv_part)
    ff_rows_in = lax.all_gather(normed_two, "mp", axis=0, tiled=True)
    hidden_bias = lax.dynamic_slice_in_dim(hidden_shift, mp_rank * hidden_part, hidden_part)
    hidden_pre = jnp.dot(ff_rows_in, ff_in_use, preferred_element_type=jnp.float32) + hidden_bias
    hidden_act = gelu_exact(hidden_pre).astype(jnp.bfloat16)
    ff_sum = lax.psum_scatter(
        jnp.dot(hidden_act, ff_out_use, preferred_element_type=jnp.float32).astype(jnp.bfloat16),
        "mp",
        scatter_dimension=0,
        tiled=True,
    ).astype(jnp.float32)
    resid_two = resid_one + ff_sum + ff_shift
    mol_rows = resid_two.astype(jnp.bfloat16).reshape(tok_rows // KER, KER * model_width)
    mol_group = lax.all_gather(mol_rows, "mp", axis=0, tiled=True)
    channel_bias = lax.dynamic_slice_in_dim(conv_shift, mp_rank * channel_part, channel_part)
    conv_pre = jnp.dot(mol_group, conv_use, preferred_element_type=jnp.float32) + channel_bias
    channel_act = gelu_exact(conv_pre).astype(jnp.bfloat16)
    conv_act = lax.all_to_all(channel_act, "mp", split_axis=0, concat_axis=1, tiled=True)
    act_float = conv_act.astype(jnp.float32)
    molecules = layer_norm(act_float, gain_three, shift_three)
    d_act, d_gain_three, d_shift_three = norm_backward(
        act_float, gain_three, shift_three, d_molecules.astype(jnp.float32)
    )
    d_act_low = d_act.astype(jnp.bfloat16)
    d_act_cols = lax.all_to_all(d_act_low, "mp", split_axis=1, concat_axis=0, tiled=True)
    d_conv_pre = gelu_backward(conv_pre, d_act_cols.astype(jnp.float32)).astype(jnp.bfloat16)
    d_conv_w = jnp.einsum("mk,mc->kc", mol_group, d_conv_pre, preferred_element_type=jnp.float32)
    d_conv_shift = lax.dynamic_update_slice_in_dim(
        jnp.zeros((model_width,), jnp.float32),
        jnp.sum(d_conv_pre.astype(jnp.float32), axis=0),
        mp_rank * channel_part,
        0,
    )
    d_mol = lax.psum_scatter(
        jnp.einsum("mc,kc->mk", d_conv_pre, conv_use, preferred_element_type=jnp.float32).astype(
            jnp.bfloat16
        ),
        "mp",
        scatter_dimension=0,
        tiled=True,
    ).astype(jnp.float32)
    d_resid_two = d_mol.reshape(tok_rows, model_width)
    d_ff_low = d_resid_two.astype(jnp.bfloat16)
    d_ff_shift = jnp.sum(d_ff_low.astype(jnp.float32), axis=0)
    d_ff_rows = lax.all_gather(d_ff_low, "mp", axis=0, tiled=True)
    d_hidden_act = jnp.einsum(
        "gc,fc->gf", d_ff_rows, ff_out_use, preferred_element_type=jnp.float32
    )
    d_ff_out_w = jnp.einsum("gf,gc->fc", hidden_act, d_ff_rows, preferred_element_type=jnp.float32)
    d_hidden = gelu_backward(hidden_pre, d_hidden_act).astype(jnp.bfloat16)
    d_hidden_sum = jnp.sum(d_hidden.astype(jnp.float32), axis=0)
    d_ff_in_w = jnp.einsum("gd,gf->df", ff_rows_in, d_hidden, preferred_element_type=jnp.float32)
    d_hidden_shift = lax.dynamic_update_slice_in_dim(
        jnp.zeros((hidden_shift.shape[0],), jnp.float32), d_hidden_sum, mp_rank * hidden_part, 0
    )
    d_normed_two = lax.psum_scatter(
        jnp.einsum("gf,df->gd", d_hidden, ff_in_use, preferred_element_type=jnp.float32).astype(
            jnp.bfloat16
        ),
        "mp",
        scatter_dimension=0,
        tiled=True,
    ).astype(jnp.float32)
    d_resid_from, d_gain_two, d_shift_two = norm_backward(
        resid_one, gain_two, shift_two, d_normed_two
    )
    d_resid_one = d_resid_two + d_resid_from
    d_attn_low = d_resid_one.astype(jnp.bfloat16)
    d_attn_shift = jnp.sum(d_attn_low.astype(jnp.float32), axis=0)
    d_attn_out_w = jnp.einsum(
        "te,tc->ec", heads_low, d_attn_low, preferred_element_type=jnp.float32
    )
    d_heads_low = jnp.einsum(
        "tc,ec->te", d_attn_low, attn_out_full, preferred_element_type=jnp.float32
    ).astype(jnp.bfloat16)
    d_heads_seq = d_heads_low.reshape(seq_count, seq_len, HEADS, HDIM)
    d_queries, d_keys, d_vals = lax.map(
        attend_backward,
        (queries, key_rows, value_rows, segment_ids, window_offsets, log_norm, d_heads_seq),
    )
    d_projected = jnp.concatenate(
        [
            d_queries.reshape(tok_rows, model_width),
            d_keys.reshape(tok_rows, model_width),
            d_vals.reshape(tok_rows, model_width),
        ],
        axis=1,
    ).astype(jnp.bfloat16)
    d_proj_sum = jnp.sum(d_projected.astype(jnp.float32), axis=0)
    d_qv_shift = jnp.concatenate([d_proj_sum[:model_width], d_proj_sum[2 * model_width :]])
    d_qkv_w = jnp.einsum("td,te->de", normed_one, d_projected, preferred_element_type=jnp.float32)
    d_normed_one = jnp.einsum(
        "te,de->td", d_projected, qkv_full, preferred_element_type=jnp.float32
    )
    d_inputs_from, d_gain_one, d_shift_one = norm_backward(
        inputs, gain_one, shift_one, d_normed_one
    )
    d_chars = d_resid_one + d_inputs_from
    d_ff_in_own, d_ff_out_own, d_conv_own = (
        lax.psum_scatter(
            d_ff_in_w.astype(jnp.bfloat16), "dp", scatter_dimension=0, tiled=True
        ).astype(jnp.float32),
        lax.psum_scatter(
            d_ff_out_w.astype(jnp.bfloat16), "dp", scatter_dimension=1, tiled=True
        ).astype(jnp.float32),
        lax.psum_scatter(
            d_conv_w.astype(jnp.bfloat16), "dp", scatter_dimension=0, tiled=True
        ).astype(jnp.float32),
    )
    owned = (
        lax.psum_scatter(d_qkv_w, ("dp", "mp"), scatter_dimension=0, tiled=True),
        lax.psum_scatter(d_attn_out_w, ("dp", "mp"), scatter_dimension=0, tiled=True),
        lax.psum_scatter(d_gain_one, ("dp", "mp"), scatter_dimension=0, tiled=True),
        lax.psum_scatter(d_shift_one, ("dp", "mp"), scatter_dimension=0, tiled=True),
        lax.psum_scatter(d_qv_shift, ("dp", "mp"), scatter_dimension=0, tiled=True),
        lax.psum_scatter(d_attn_shift, ("dp", "mp"), scatter_dimension=0, tiled=True),
        lax.psum_scatter(d_gain_two, ("dp", "mp"), scatter_dimension=0, tiled=True),
        lax.psum_scatter(d_shift_two, ("dp", "mp"), scatter_dimension=0, tiled=True),
        lax.psum_scatter(d_hidden_shift, ("dp", "mp"), scatter_dimension=0, tiled=True),
        lax.psum_scatter(d_ff_shift, ("dp", "mp"), scatter_dimension=0, tiled=True),
        lax.psum_scatter(d_conv_shift, ("dp", "mp"), scatter_dimension=0, tiled=True),
        lax.psum_scatter(d_gain_three, ("dp", "mp"), scatter_dimension=0, tiled=True),
        lax.psum_scatter(d_shift_three, ("dp", "mp"), scatter_dimension=0, tiled=True),
    )
    return (
        molecules,
        d_chars,
        owned[2],
        owned[3],
        owned[0],
        owned[4],
        owned[1],
        owned[5],
        owned[6],
        owned[7],
        d_ff_in_own,
        owned[8],
        d_ff_out_own,
        owned[9],
        d_conv_own,
        owned[10],
        owned[11],
        owned[12],
    )


NEAR_FIRST = (False, True, False, False, False, False, True, True, False, False, False, False, False, False, True, False, False, False, True, True, True, False)
GATHER_TABLE = (
    ((0, 0), (0, 1), (1, 0), (0, 2), (2, 0), (0, 3), (3, 0), (1, 1), (1, 2), (4, 0), (2, 2),),
    ((1, 3), (0, 4),),
    (),
    ((2, 1),),
    ((3, 2), (0, 5),),
    (),
    ((0, 6),),
    ((2, 3), (1, 4), (1, 5), (0, 7), (3, 1), (4, 2), (0, 8), (4, 1), (1, 6), (5, 2), (0, 9), (3, 3), (4, 3), (0, 10),),
    ((2, 4), (0, 11),),
    ((2, 5), (1, 7), (2, 7), (1, 8), (2, 8), (1, 9),),
    ((2, 6), (1, 10),),
    ((3, 4), (1, 11), (0, 12),),
    ((3, 5), (3, 7),),
    ((4, 4), (0, 13),),
    (),
    ((4, 5), (3, 8), (2, 9), (0, 14),),
    ((3, 6), (1, 12),),
    ((0, 15),),
    ((4, 6), (2, 10), (1, 13),),
    ((0, 16),),
    ((2, 11), (1, 14), (0, 17),),
    ((4, 7), (4, 8), (0, 18),),
    ((3, 9), (1, 16),),
    ((5, 7), (5, 8), (2, 12), (1, 15), (2, 15), (1, 17),),
    ((4, 9), (3, 10), (0, 19),),
    ((3, 11), (2, 13), (1, 18), (0, 20),),
    ((4, 10), (2, 14), (3, 15), (0, 21),),
    ((4, 11), (0, 22),),
    ((3, 12), (2, 16),),
    (),
    ((4, 12), (2, 17), (1, 19), (2, 19),),
    ((3, 13), (1, 22),),
    ((2, 18), (1, 20), (2, 20),),
    ((4, 13), (3, 14), (3, 19),),
    ((4, 15), (3, 16), (1, 21), (2, 21),),
    ((4, 14), (3, 17), (3, 20),),
    ((5, 15), (4, 16),),
    ((4, 17), (3, 21), (2, 22),),
    ((3, 18),),
    ((4, 19),),
    ((4, 18), (4, 20),),
    ((5, 19), (4, 21), (3, 22),),
    ((5, 20),),
    ((5, 21), (4, 22),),
    (),
)
SCATTER_TABLE = (
    ((0, 0), (0, 1), (0, 2), (0, 3), (0, 4), (0, 5),),
    (),
    (),
    (),
    (),
    (),
    (),
    ((1, 0), (1, 1), (1, 2),),
    ((1, 3), (1, 4),),
    ((1, 5),),
    (),
    ((0, 6), (0, 7),),
    ((2, 0),),
    ((2, 1), (0, 8), (0, 9),),
    ((2, 2), (1, 6), (1, 7),),
    ((2, 3), (0, 10), (0, 11),),
    ((2, 4), (1, 8), (1, 9),),
    ((3, 0), (2, 5), (0, 12), (0, 13),),
    ((3, 1), (3, 2), (1, 10), (1, 11),),
    ((2, 6), (0, 14), (0, 15),),
    ((3, 3), (2, 7), (1, 12), (1, 13),),
    ((4, 0), (3, 4), (0, 16), (0, 17),),
    ((4, 1), (2, 8), (1, 14),),
    ((1, 15),),
    ((4, 2), (2, 9),),
    ((3, 5),),
    (),
    ((4, 3), (1, 16),),
    ((2, 10), (1, 17),),
    (),
    ((4, 4), (3, 6), (2, 11), (0, 18),),
    ((3, 7),),
    (),
    ((4, 5), (2, 12),),
    ((3, 8), (2, 13), (1, 18),),
    ((4, 6), (2, 14),),
    ((4, 7), (3, 9), (2, 15), (0, 19),),
    ((4, 8), (2, 16),),
    ((3, 10),),
    ((3, 11), (2, 17), (1, 19),),
    ((4, 9), (3, 12), (3, 13), (0, 20),),
    ((2, 18),),
    ((4, 10), (4, 11), (3, 14), (3, 15), (3, 16),),
    ((3, 17), (1, 20),),
    ((4, 12), (4, 13), (2, 19), (0, 21),),
    ((3, 18),),
    ((4, 14),),
    ((4, 15),),
    (),
    (),
    (),
    ((1, 21),),
    ((4, 16), (2, 20),),
    (),
    (),
    (),
    ((4, 17), (3, 19), (0, 22),),
    (),
    (),
    (),
    (),
    (),
    (),
    (),
    (),
    ((4, 18), (1, 22), (2, 21), (3, 20), (4, 19), (2, 22), (3, 21), (4, 20), (3, 22), (4, 22), (4, 21),),
)
HALF = 0.5
ERFC_P = 0.3
ERFC_Q = (
    0.16918934881687164,
    0.17069095373153687,
    0.1485210806131363,
    0.2141820192337036,
    -0.09282728284597397,
    0.5449684858322144,
    -0.5097734332084656,
    0.4843021035194397,
    -0.12925326824188232,
)
BF = jnp.bfloat16
F32 = jnp.float32
MESH_ID = pl.DeviceIdType.MESH
ALL = slice(None)
LINKS = ("z1", "z2", "z3", "x", "y", "c")
VMEM_CAP = 63 * 2**20
SLOT = 128
KINDS = (0, 2, 2, 1, 1, 1)
FF_ROWS = 512


def nn(lhs, rhs):
    return lax.dot_general(lhs, rhs, (((1,), (0,)), ((), ())), preferred_element_type=F32)


def nt(lhs, rhs):
    return lax.dot_general(lhs, rhs, (((1,), (1,)), ((), ())), preferred_element_type=F32)


def tn(lhs, rhs):
    return lax.dot_general(lhs, rhs, (((0,), (0,)), ((), ())), preferred_element_type=F32)


def gelu_pair(v):
    size = jnp.abs(v)
    t = 1.0 / (1.0 + (ERFC_P * 0.7071067811865476) * size)
    q = ERFC_Q[-1]
    for coef in ERFC_Q[-2::-1]:
        q = q * t + coef
    bell = jnp.exp(-0.5 * (v * v))
    tail = (HALF * bell) * (q * t)
    phi = jnp.where(v >= 0, 1.0 - tail, tail)
    return v * phi, phi + v * (bell * 0.3989422804014327)


def norm_stats(v):
    mean = jnp.mean(v, axis=-1, keepdims=True)
    cen = v - mean
    r = lax.rsqrt(jnp.mean(cen * cen, axis=-1, keepdims=True) + layer_eps)
    return cen * r, r


def norm_grad(vhat, r, t):
    m1 = jnp.mean(t, axis=-1, keepdims=True)
    m2 = jnp.mean(t * vhat, axis=-1, keepdims=True)
    return r * (t - m1 - vhat * m2)


def head_masks(rows, scale):
    lane = lax.broadcasted_iota(jnp.int32, (rows, 128), 1)
    low = jnp.where(lane < HDIM, scale, 0.0).astype(BF)
    high = jnp.where(lane < HDIM, 0.0, scale).astype(BF)
    return low, high


def split_heads(pair, masks):
    return jnp.concatenate([pair * masks[0], pair * masks[1]], axis=0)


def vector_masks(width, count, nrow):
    col = lax.broadcasted_iota(jnp.int32, (SLOT, width), 1).astype(F32)
    row = lax.broadcasted_iota(jnp.int32, (SLOT, width), 0).astype(F32)
    pick = jnp.where(col - jnp.floor((col + 0.5) * (1.0 / count)) * count == row, 1.0, 0.0).astype(BF)
    col = lax.broadcasted_iota(jnp.int32, (nrow, width), 1).astype(F32)
    row = lax.broadcasted_iota(jnp.int32, (nrow, width), 0).astype(F32)
    return pick, jnp.floor((col + 0.5) * (1.0 / count)) == row


class Place:
    def __init__(self):
        dp = lax.axis_index("dp")
        self.x = lax.axis_index("mp")
        self.z, self.y, self.c = lax.div(dp, 4), lax.rem(lax.div(dp, 2), 2), lax.rem(dp, 2)
        z, y, c, x = self.z, self.y, self.c, self.x
        self.nx, self.ny, self.nc = 1 - x, 1 - y, 1 - c
        self.at = [c * 0 + k for k in range(3)]
        self.far_z = {1: z + 1 - 2 * lax.rem(z, 2), 2: lax.rem(z + 2, 4), 3: 3 - z}
        at = lambda zz, yy, cc, xx: (zz * 4 + yy * 2 + cc, xx)
        self.peer = {
            "z1": at(self.far_z[1], y, c, x),
            "z2": at(self.far_z[2], y, c, x),
            "z3": at(self.far_z[3], y, c, x),
            "x": at(z, y, c, 1 - x),
            "y": at(z, 1 - y, c, x),
            "c": at(z, y, 1 - c, x),
            "d": at(z, 1 - y, c, 1 - x),
        }

    def barrier(self):
        sem = pltpu.get_barrier_semaphore()
        for peer in self.peer.values():
            pl.semaphore_signal(sem, inc=1, device_id=peer, device_id_type=MESH_ID)
        pl.semaphore_wait(sem, len(self.peer))


def rows_of(ref, xs):
    if isinstance(xs, slice):
        return xs
    half = ref.shape[-2] // 2
    return pl.ds(pl.multiple_of(xs * half, 8), half)


def block(ref, kind, zs, ys, cs, xs, cut):
    if kind == 0:
        return ref.at[(zs, ys, cs, xs) + cut]
    if kind == 1:
        return ref.at[(xs, zs, ys, cs) + cut]
    return ref.at[zs, ys, cs, rows_of(ref, xs), cut[1]]


class Sends:
    STEPS = ("z", "a", "b", "c", "w")

    def __init__(self, place, send_sem, recv_sem):
        self.place, self.send_sem, self.recv_sem = place, send_sem, recv_sem
        self.copies, self.waits = {}, {}
        self.live = False

    def copy(self, t, i, step, src, dst, link):
        out = self.STEPS.index("a" if step == "w" else step)
        return pltpu.make_async_remote_copy(
            src_ref=src,
            dst_ref=dst,
            send_sem=self.send_sem.at[4 * t + out],
            recv_sem=self.recv_sem.at[5 * i + self.STEPS.index(step)],
            device_id=self.place.peer[link],
            device_id_type=MESH_ID,
        )

    def go(self, t, i, step, part, src, dst, link):
        if self.live:
            self.copies[i, step, part].start()
        else:
            self.copies[i, step, part] = self.copy(t, i, step, src, dst, link)

    def got(self, t, i, step, all_of):
        if self.live:
            self.waits[i, step].wait_recv()
        else:
            self.waits[i, step] = self.copy(t, i, step, all_of, all_of, "c")

    def sent(self, t, sizes):
        for step, view in sizes.items():
            self.copy(t, 0, step, view, view, "c").wait_send()


def union(cuts):
    if cuts[1] is None:
        return cuts[0]
    return tuple(p if p == q else slice(p.start, q.stop) for p, q in zip(*cuts))


def order(half):
    return ("x", "y") if half == 0 else ("y", "x")


def gather_stage(sends, stage, i, t, kind, own, full, cuts, near_first):
    p = sends.place
    z, y, c, x = p.z, p.y, p.c, p.x
    whole = union(cuts)
    three = block(full, kind, slice(0, 3), y, c, x, whole)
    size = {
        "z": three,
        "w": three,
        "a": block(full, kind, z if near_first else ALL, y, c, x, whole),
        "b": block(full, kind, ALL, y, c, ALL, whole),
        "c": block(full, kind, ALL, ALL, c, ALL, whole),
    }
    waits = ((), ("a",), ("z",), ("w",), ("b",), ("c",)) if near_first else ((), ("z",), ("a",), ("b",), ("c",))
    if stage >= len(waits):
        return
    for step in waits[stage]:
        sends.got(t, i, step, size[step])
    for h, cut in enumerate(cuts):
        if cut is None:
            continue
        a, b = order(h)
        mine = block(full, kind, z, y, c, x, cut)
        line = block(full, kind, ALL, y, c, x, cut)
        if h == 0:
            next_one, next_line = block(full, kind, z, y, c, p.nx, cut), block(full, kind, ALL, y, c, p.nx, cut)
            far = block(full, kind, ALL, p.ny, c, ALL, cut)
        else:
            next_one, next_line = block(full, kind, z, p.ny, c, x, cut), block(full, kind, ALL, p.ny, c, x, cut)
            far = block(full, kind, ALL, ALL, c, p.nx, cut)
        own_z = [("z", k, own.at[cut], mine, k) for k in ("z1", "z2", "z3")]
        line_b, line_c = ("b", 1, line, line, b), ("c", 1, line, line, "c")
        next_bc = [("b", 2, next_line, next_line, b), ("c", 2, next_line, next_line, "c")]
        far_c = [("c", 3, far, far, "c")]
        if near_first:
            next_z = [("w", k, next_one, next_one, k) for k in ("z1", "z2", "z3")]
            steps = ([("a", 1, own.at[cut], mine, a)] + own_z, next_z, [line_b, line_c], next_bc, far_c, [])
        else:
            steps = (own_z, [("a", 1, line, line, a), line_b, line_c], next_bc, far_c, [])
        for step, part, src, dst, link in steps[stage]:
            sends.go(t, i, step, (h, part), src, dst, link)


def col_cuts(cols, parts):
    step = cols // (2 * parts)
    return [((ALL, slice(2 * step * i, 2 * step * i + step)), (ALL, slice(2 * step * i + step, 2 * step * (i + 1)))) for i in range(parts)]


def row_cuts(rows, parts):
    step = rows // (2 * parts)
    return [((slice(2 * step * i, 2 * step * i + step), ALL), (slice(2 * step * i + step, 2 * step * (i + 1)), ALL)) for i in range(parts)]


def block_cuts(rows, cols, col_parts, row_parts):
    step, width = rows // (2 * row_parts), cols // col_parts
    cuts = []
    for q in range(col_parts):
        lanes = slice(q * width, q * width + width)
        for r in range(row_parts):
            low = 2 * step * r
            cuts.append(((slice(low, low + step), lanes), (slice(low + step, low + 2 * step), lanes)))
    return cuts


def gather_plan(shapes):
    plan = [(0, 0, ((ALL, ALL), None))]
    plan += [(1, 2, c) for c in col_cuts(shapes[1][1], 3)]
    plan += [(2, 2, c) for c in col_cuts(shapes[2][1], 1)]
    plan += [(3, 1, c) for c in col_cuts(shapes[3][1], 6)]
    plan += [(4, 1, c) for c in col_cuts(shapes[4][1], 6)]
    plan += [(5, 1, c) for c in block_cuts(shapes[5][0], shapes[5][1], 3, 2)]
    return [piece + (near,) for piece, near in zip(plan, (False,) + NEAR_FIRST)]


class Ticks:
    def __init__(self, table, stage_fn):
        self.table, self.stage_fn, self.count = table, stage_fn, 0

    def run(self, k):
        for s, i in self.table[k]:
            self.stage_fn(s, i)

    def point(self):
        self.count += 1
        self.run(self.count - 1)

    def within(self, index, values):
        for value in values:
            if self.table[self.count]:
                pl.when(index == value)(functools.partial(self.run, self.count))
            self.count += 1


def forward_kernel(dims, sizes, *refs):
    (off_ref, seg_ref, x_i, dmol_i, vec_own, qkv_own, wo_own, wi_own, wf_own, cv_own) = refs[:10]
    outs = refs[10:28]
    (mol_out, vec_out, ln3_out, dcp_out, qkv_o, wo_o, wi_o, wf_o, cv_o, nst_o, proj_o, prob_o, headst_o, r1_o, n2t_o, act_o, gd_o, mit_o) = outs
    (vec_g, qkv_g, wo_g, wi_g, wf_g, cv_g, vec_f, vecs, pad, ns, proj, prob, heads, r1, n2, act, gd, r2, molin, x_ref, dmol_ref, local_sem, out_sem, send_sem, recv_sem) = refs[28:]
    tok, d, ff = dims
    win = WIN
    nw = tok // win + 1
    half_ff = ff // 2
    mols = tok // KER
    x_load = pltpu.make_async_copy(x_i, x_ref, local_sem.at[6])
    dmol_load = pltpu.make_async_copy(dmol_i, dmol_ref, local_sem.at[7])
    x_load.start()
    dmol_load.start()
    place = Place()
    owns = (vec_own, qkv_own, wo_own, wi_own, wf_own, cv_own)
    fulls = (vec_g, qkv_g, wo_g, wi_g, wf_g, cv_g)
    plan = gather_plan([o.shape for o in owns])
    kinds = KINDS
    place.barrier()
    sends = Sends(place, send_sem, recv_sem)
    local = []
    for i, (own, full, kind) in enumerate(zip(owns, fulls, kinds)):
        copy = pltpu.make_async_copy(own, block(full, kind, place.z, place.y, place.c, place.x, (ALL, ALL)), local_sem.at[i])
        copy.start()
        local.append(copy)

    def comm_stage(stage, i):
        t, kind, cuts, near_first = plan[i]
        if sends.live and stage == (2 if near_first else 1) and (i == 0 or plan[i - 1][0] != t):
            local[t].wait()
        gather_stage(sends, stage, i, t, kind, owns[t], fulls[t], cuts, near_first)

    for stage in range(6):
        for i in range(len(plan)):
            comm_stage(stage, i)
    sends.live = True
    ticks = Ticks(GATHER_TABLE, comm_stage)

    out_copies = []

    def flush(src, dst):
        copy = pltpu.make_async_copy(src, dst, out_sem.at[len(out_copies)])
        copy.start()
        out_copies.append(copy)
        return copy

    def unpack_vectors():
        nrow = vec_f.shape[0] // 16
        vec_f[...] = vec_g[...].reshape(vec_f.shape).astype(F32)
        for width, count in sorted(set(sizes)):
            pick, mine = vector_masks(width, count, nrow)
            for v in [i for i, s in enumerate(sizes) if s == (width, count)]:
                spread = nn(vec_f[pl.ds(v, nrow, stride=16), :].astype(BF), pick)
                vecs[v : v + 1, :width] = jnp.sum(jnp.where(mine, spread, 0.0), axis=0, keepdims=True)

    def vec(v, lo, hi):
        return vecs[v : v + 1, lo:hi]

    offset = off_ref[0]

    ticks.point()
    unpack_vectors()
    ticks.point()
    flush(vecs, vec_out)

    x_load.wait()
    pad[0:win, :] = jnp.zeros((win, d), BF)
    pad[win + tok : 2 * win + tok, :] = jnp.zeros((win, d), BF)

    @pl.loop(0, tok // 128)
    def _(b):
        rows = pl.ds(pl.multiple_of(b * 128, 128), 128)
        vhat, _ = norm_stats(x_ref[rows, :].astype(F32))
        pad[pl.ds(pl.multiple_of(b * 128 + win, 128), 128), :] = (vhat * vec(0, 0, d) + vec(1, 0, d)).astype(BF)
        ticks.within(b, (1, 3, 5, 7))

    ri = lax.broadcasted_iota(jnp.int32, (win, 2 * win), 0)
    rj = lax.broadcasted_iota(jnp.int32, (win, 2 * win), 1)
    shift_in = jnp.where(rj == ri + (win - offset), 1.0, 0.0).astype(BF)
    shift_out = jnp.where(rj == ri + offset, 1.0, 0.0).astype(BF)

    @pl.loop(0, nw)
    def _(w):
        at = pl.multiple_of(w * win, win)
        ns[pl.ds(at, win), :] = nn(shift_in, pad[pl.ds(at, 2 * win), :]).astype(BF)
        ticks.within(w, (4,))

    ns_t = act.at[0:d, 0 : nw * win]

    @pl.loop(0, nw // 3)
    def _(b):
        rows = pl.ds(pl.multiple_of(b * 384, 128), 384)
        ns_t[:, rows] = ns[rows, :].T

    ns_t_copy = flush(ns_t, nst_o)

    ticks.point()
    flush(qkv_g, qkv_o)
    wq = qkv_g.reshape(d, 3 * d)
    for blk3 in range(3):
        bias_row = None if blk3 == 1 else vec(2, (blk3 // 2) * d, (blk3 // 2) * d + d)

        @pl.loop(0, nw // 3)
        def _(b):
            rows = pl.ds(pl.multiple_of(b * 384, 128), 384)
            for n0 in range(0, d, 256):
                val = nn(ns[rows, :], wq[:, blk3 * d + n0 : blk3 * d + n0 + 256])
                if bias_row is not None:
                    val = val + bias_row[:, n0 : n0 + 256]
                proj[rows, blk3 * d + n0 : blk3 * d + n0 + 256] = val.astype(BF)

        ticks.point()

    proj_copy = flush(proj, proj_o)

    qmask = head_masks(win, HDIM**-0.5)
    vmask = head_masks(win, 1.0)
    seg_row = jnp.concatenate([seg_ref[0:1, :].astype(F32), jnp.full((1, win), -1.0, F32)], axis=1)
    seg_row = pltpu.roll(jnp.broadcast_to(seg_row, (8, tok + win)), offset, axis=1)
    segs = vec_f
    for w in range(nw):
        segs[w * 8 : w * 8 + 8, 0:win] = seg_row[:, w * win : (w + 1) * win]

    @pl.loop(0, nw)
    def _(w):
        rows = pl.ds(pl.multiple_of(w * win, win), win)
        seg_q = jnp.broadcast_to(segs[pl.ds(pl.multiple_of(w * 8, 8), 8), 0:win][0:1], (win, win))
        same = seg_q == seg_q.T
        same2 = jnp.concatenate([same, same], axis=1)
        for pr in range(HEADS // 2):
            lanes = slice(pr * 128, pr * 128 + 128)
            q2 = proj[rows, pr * 128 : pr * 128 + 128]
            k2 = proj[rows, d + pr * 128 : d + pr * 128 + 128]
            v2 = proj[rows, 2 * d + pr * 128 : 2 * d + pr * 128 + 128]
            s = jnp.where(same2, nt(k2, split_heads(q2, qmask)), -1e30)
            e = jnp.exp(s - jnp.max(s, axis=0, keepdims=True))
            pb = (e * (1.0 / jnp.sum(e, axis=0, keepdims=True))).astype(BF)
            prob[w, pr] = pb
            stacked = jnp.concatenate([pb[:, :win], pb[:, win:]], axis=0)
            pad[rows, lanes] = tn(stacked, split_heads(v2, vmask)).astype(BF)
        ticks.within(w, range(nw))

    prob_copy = flush(prob, prob_o)

    flush(wo_g, wo_o)
    wo = wo_g.reshape(d, d)
    proj_copy.wait()
    heads_t = proj.at[0:d, 0:tok]
    n2_t = proj.at[0:d, tok : 2 * tok]

    @pl.loop(0, tok // 128)
    def _(b):
        at = pl.multiple_of(b * 128, 128)
        hb = nn(shift_out, pad[pl.ds(at, 2 * win), :]).astype(BF)
        heads[pl.ds(at, 128), :] = hb
        heads_t[:, pl.ds(at, 128)] = hb.T

    ticks.point()

    @pl.loop(0, tok // 256)
    def _(b):
        rows = pl.ds(pl.multiple_of(b * 256, 256), 256)
        val = x_ref[rows, :].astype(F32) + nn(heads[rows, :], wo[...]) + vec(3, 0, d)
        r1[rows, :] = val
        vhat, _ = norm_stats(val)
        low = (vhat * vec(4, 0, d) + vec(5, 0, d)).astype(BF)
        n2[rows, :] = low
        n2_t[:, rows] = low.T
        ticks.within(b, (0, 1, 2))

    flush(heads_t, headst_o)
    flush(r1, r1_o)
    flush(n2_t, n2t_o)
    ns_t_copy.wait()

    wi = wi_g.reshape(2, d, half_ff)

    @pl.loop(0, half_ff // 256)
    def _(j):
        cols = pl.ds(pl.multiple_of(j * 256, 256), 256)
        base = ticks.count
        for hx in range(2):
            for q in range(half_ff // 256):
                if ticks.table[base + 2 * q + hx]:
                    pl.when(j == q)(functools.partial(ticks.run, base + 2 * q + hx))
            ocols = pl.ds(pl.multiple_of(hx * half_ff + j * 256, 256), 256)
            bias_row = vecs[6:7, ocols]
            for m in range(0, tok, 256):
                pre = nn(n2[m : m + 256, :], wi[hx, :, cols]) + bias_row
                g, dg = gelu_pair(pre)
                act[m : m + 256, ocols] = g.astype(BF)
                gd[m : m + 256, ocols] = dg.astype(BF)
        ticks.count = base + 2 * (half_ff // 256)

    flush(act, act_o)
    flush(gd, gd_o)

    ticks.point()
    flush(wi_g, wi_o)
    flush(wf_g, wf_o)
    wf = wf_g.reshape(2, d, half_ff)

    @pl.loop(0, tok // 256)
    def _(b):
        rows = pl.ds(pl.multiple_of(b * 256, 256), 256)
        for n0 in range(0, d, 256):
            cols = slice(n0, n0 + 256)
            val = nt(act[rows, 0:half_ff], wf[0, cols, :]) + nt(act[rows, half_ff:], wf[1, cols, :])
            val = r1[rows, cols] + val + vec(7, n0, n0 + 256)
            r2[n0 // 128, rows, :] = val[:, :128]
            r2[n0 // 128 + 1, rows, :] = val[:, 128:]
        ticks.within(b, range(4))

    for k in range(KER):
        for q in range(d // 128):
            molin[:, k * d + q * 128 : k * d + q * 128 + 128] = r2[q, pl.ds(k, mols, stride=KER), :].astype(BF)

    prob_copy.wait()
    for k in range(KER):
        for q in range(d // 128):
            prob[k, q] = molin[:, k * d + q * 128 : k * d + q * 128 + 128].T
    flush(prob.at[0:KER], mit_o)
    cv = cv_g.reshape(2, KER * d, d // 2)
    parts = {}
    for q in range(3):
        ticks.point()
        for hx in range(2):
            at = hx * (d // 2) + q * 128
            pre = nn(molin[...], cv[hx, :, q * 128 : q * 128 + 128]) + vec(8, at, at + 128)
            parts[at] = gelu_pair(pre)
        flush(cv_g.at[:, :, :, :, :, q * 128 : q * 128 + 128], cv_o.at[:, :, :, :, :, q * 128 : q * 128 + 128])
    dmol_load.wait()
    g = jnp.concatenate([parts[at][0] for at in range(0, d, 128)], axis=1)
    dg = jnp.concatenate([parts[at][1] for at in range(0, d, 128)], axis=1)
    vhat, r = norm_stats(g.astype(BF).astype(F32))
    mol_out[...] = vhat * vec(9, 0, d) + vec(10, 0, d)
    cot = dmol_ref[...].astype(F32)
    ln3_out[0:1, :] = jnp.sum(cot * vhat, axis=0, keepdims=True)
    ln3_out[1:2, :] = jnp.sum(cot, axis=0, keepdims=True)
    da = norm_grad(vhat, r, cot * vec(9, 0, d)).astype(BF).astype(F32)
    dcp_out[...] = (da * dg).astype(BF)
    for t, (full, kind) in enumerate(zip(fulls, kinds)):
        pick = functools.partial(block, full, kind, cut=(ALL, ALL))
        z, y, c, x = place.z, place.y, place.c, place.x
        sends.sent(t, {"z": pick(slice(0, 3), y, c, x), "a": pick(ALL, y, c, x), "b": pick(ALL, y, c, ALL), "c": pick(ALL, ALL, c, ALL)})
    for copy in out_copies:
        if not any(copy is early for early in (ns_t_copy, proj_copy, prob_copy)):
            copy.wait()


def scatter_plan(shapes):
    plan = [(5, 1, c) for c in row_cuts(shapes[5][0], 6)]
    for wf_cut, wi_cut in zip(col_cuts(shapes[4][1], 6), col_cuts(shapes[3][1], 6)):
        plan += [(4, 1, wf_cut), (3, 1, wi_cut)]
    plan += [(2, 2, c) for c in col_cuts(shapes[2][1], 1)]
    plan += [(1, 2, c) for c in col_cuts(shapes[1][1], 3)]
    plan += [(0, 0, ((ALL, ALL), None))]
    return plan


def backward_kernel(dims, sizes, *refs):
    (off_ref, x_i, dcp_ref, vecs, ln3_ref, qkv_i, wo_i, wi_i, wf_i, cv_i, nst_i, proj_i, prob_i, headst_i, r1_i, n2t_i, act_i, gd_i, mit_i) = refs[:19]
    dch_out = refs[19]
    own_dst = refs[20:26]
    grads = refs[26:32]
    from_core = refs[32:38]
    from_b = refs[38:44]
    from_a = refs[44:50]
    from_z = refs[50:56]
    own_outs = refs[56:62]
    sums, res_sem, tile_sem, load_sem, out_sem, own_sem, send_sem, recv_sem = refs[62:]
    tok, d, ff = dims
    win = WIN
    nw = tok // win + 1
    half_ff = ff // 2
    mols = tok // KER
    place = Place()
    z, y, c, x = place.z, place.y, place.c, place.x
    plan = scatter_plan([o.shape for o in own_outs])
    place.barrier()
    sends = Sends(place, send_sem, recv_sem)

    def add_blocks(dst_of, src_of):
        if not sends.live:
            return

        dst, src = dst_of(ALL), src_of(ALL)
        dst[...] = dst[...] + src[...]

    def vector_stage(stage, i, kind, g, rc, rb, ra, rz, own):
        both, mine = (ALL, ALL), block(g, kind, ALL, y, c, x, (ALL, ALL))
        if stage == 0:
            sends.go(0, i, "c", 0, block(g, kind, ALL, ALL, place.nc, ALL, both), rc, "c")
        elif stage == 1:
            sends.got(0, i, "c", rc)
            for q in range(2):
                add_blocks(lambda zz: block(g, kind, zz, ALL, c, place.at[q], both), lambda zz: rc.at[zz, :, place.at[q]])
            sends.go(0, i, "b", 0, block(g, kind, ALL, y, c, place.nx, both), rb.at[place.at[0]], "x")
            sends.go(0, i, "b", 1, block(g, kind, ALL, place.ny, c, x, both), rb.at[place.at[1]], "y")
            sends.go(0, i, "a", 0, block(g, kind, ALL, place.ny, c, place.nx, both), ra, "d")
        elif stage == 2:
            sends.got(0, i, "b", rb)
            sends.got(0, i, "a", ra)
            if sends.live:
                mine[...] = (mine[...] + rb[0]) + (rb[1] + ra[...])
            for q in (1, 2, 3):
                sends.go(0, i, "z", q, block(g, kind, place.far_z[q], y, c, x, both), rz.at[place.at[q - 1]], "z%d" % q)
        elif stage == 3:
            sends.got(0, i, "z", rz)
            if sends.live:
                own[...] = (block(g, kind, z, y, c, x, both)[...] + rz[0]) + (rz[1] + rz[2])

    own_copies = [pltpu.make_async_copy(o, p, own_sem.at[q]) for q, (o, p) in enumerate(zip(own_outs, own_dst))]
    last_piece = {plan[i][0]: i for row in SCATTER_TABLE for step, i in row if step == (3 if plan[i][0] == 0 else 4)}

    def comm_stage(stage, i):
        work_stage(stage, i)
        t = plan[i][0]
        if sends.live and last_piece[t] == i and stage == (3 if t == 0 else 4):
            own_copies[t].start()

    def work_stage(stage, i):
        t, kind, cuts = plan[i]
        g, rc, rb, ra, rz, own = grads[t], from_core[t], from_b[t], from_a[t], from_z[t], own_outs[t]

        def core_blk(zs, ys, xs, cut):
            if kind == 2:
                return rc.at[zs, ys, rows_of(rc, xs), cut[1]]
            return rc.at[(zs, ys, xs) + cut] if kind == 0 else rc.at[(xs, zs, ys) + cut]

        if t == 0:
            vector_stage(stage, i, kind, g, rc, rb, ra, rz, own)
            return
        whole = union(cuts)
        waits = {
            1: ("c", core_blk(ALL, ALL, ALL, whole)),
            2: ("b", rb.at[(ALL, ALL) + whole]),
            3: ("a", ra.at[(ALL,) + whole]),
            4: ("z", rz.at[(ALL,) + whole]),
        }
        if stage > 0:
            sends.got(t, i, *waits[stage])
        for h, cut in enumerate(cuts):
            if cut is None:
                continue
            a, b = order(h)
            if stage == 0:
                sends.go(t, i, "c", h, block(g, kind, ALL, ALL, place.nc, ALL, cut), core_blk(ALL, ALL, ALL, cut), "c")
            elif stage == 1:
                for far in (1, 0):
                    for o in range(2):
                        ys, xs = (place.ny if far else y, place.at[o]) if h == 0 else (place.at[o], place.nx if far else x)
                        add_blocks(lambda zz: block(g, kind, zz, ys, c, xs, cut), lambda zz: core_blk(zz, ys, xs, cut))
                        if far:
                            sends.go(t, i, "b", (h, o), block(g, kind, ALL, ys, c, xs, cut), rb.at[(place.at[o], ALL) + cut], b)
            elif stage == 2:
                near, other = (x, place.nx) if h == 0 else (y, place.ny)
                for far in (1, 0):
                    o = other if far else near
                    ys, xs = (y, o) if h == 0 else (o, x)
                    add_blocks(lambda zz: block(g, kind, zz, ys, c, xs, cut), lambda zz: rb.at[(o, zz) + cut])
                    if far:
                        sends.go(t, i, "a", h, block(g, kind, ALL, ys, c, xs, cut), ra.at[(ALL,) + cut], a)
            elif stage == 3:
                add_blocks(lambda zz: block(g, kind, zz, y, c, x, cut), lambda zz: ra.at[(zz,) + cut])
                for q in (1, 2, 3):
                    sends.go(t, i, "z", (h, q), block(g, kind, place.far_z[q], y, c, x, cut), rz.at[(place.at[q - 1],) + cut], "z%d" % q)
            elif sends.live:
                total = block(g, kind, z, y, c, x, cut)[...].astype(F32)
                for q in range(3):
                    total = total + rz.at[(place.at[q],) + cut][...].astype(F32)
                if t != 1:
                    own[cut] = total
                    continue
                for q in range(0, cut[1].stop - cut[1].start, 128):
                    part, r = divmod(cut[1].start + q, d)
                    to = (r // 256) * d + part * 256 + r % 256
                    own[:, to : to + 128] = total[:, q : q + 128]

    for stage in range(5):
        for i in range(len(plan)):
            comm_stage(stage, i)
    sends.live = True
    ticks = Ticks(SCATTER_TABLE, comm_stage)
    state = {"load": 0}

    def load(src, dst):
        copy = pltpu.make_async_copy(src, dst, load_sem.at[state["load"]])
        state["load"] += 1
        copy.start()
        return copy

    def vec(v, lo, hi):
        return vecs[v : v + 1, lo:hi]

    offset = off_ref[0]
    ri = lax.broadcasted_iota(jnp.int32, (win, 2 * win), 0)
    rj = lax.broadcasted_iota(jnp.int32, (win, 2 * win), 1)
    shift_in = jnp.where(rj == ri + (win - offset), 1.0, 0.0).astype(BF)
    shift_out = jnp.where(rj == ri + offset, 1.0, 0.0).astype(BF)
    sums[...] = jnp.zeros_like(sums)
    sums[9:10, 0:d] = ln3_ref[0:1, :]
    sums[10:11, 0:d] = ln3_ref[1:2, :]
    sums[8:9, 0:d] = jnp.sum(dcp_ref[...].astype(F32), axis=0, keepdims=True)
    g_vec, g_qkv, g_wo, g_wi, g_wf, g_cv = grads
    g_cv2 = g_cv.reshape(2, KER * d, d // 2)
    g_wi2 = g_wi.reshape(2, d, half_ff)
    g_wf2 = g_wf.reshape(2, d, half_ff)

    def rows_of_dres(dres, rows):
        return jnp.concatenate([dres[q, rows, :] for q in range(d // 128)], axis=1)

    def set_dres(dres, rows, val):
        for q in range(d // 128):
            dres[q, rows, :] = val[:, q * 128 : q * 128 + 128]

    def whole(dres, dpad):
        def conv_part(cv, mi):
            loads = [load(mit_i, mi), load(cv_i, cv)]
            cv2 = cv.reshape(2, KER * d, d // 2)
            loads[0].wait()
            for kk in range(KER):
                val = nn(mi[kk].reshape(d, mols), dcp_ref[...]).astype(BF)
                g_cv2[0, kk * d : kk * d + d, :] = val[:, : d // 2]
                g_cv2[1, kk * d : kk * d + d, :] = val[:, d // 2 :]

            ticks.point()
            loads[1].wait()
            for kk in range(KER):
                for n0 in range(0, d, 256):
                    rows = slice(kk * d + n0, kk * d + n0 + 256)
                    val = nt(dcp_ref[:, : d // 2], cv2[0, rows, :]) + nt(dcp_ref[:, d // 2 :], cv2[1, rows, :])
                    dres[n0 // 128, pl.ds(kk, mols, stride=KER), :] = val[:, :128]
                    dres[n0 // 128 + 1, pl.ds(kk, mols, stride=KER), :] = val[:, 128:]
                ticks.point()

        pl.run_scoped(conv_part, pltpu.VMEM(cv_i.shape, BF), pltpu.VMEM(mit_i.shape, BF))

        def pack_vectors():
            g_vec2 = g_vec.reshape(-1, SLOT)
            nrow = g_vec2.shape[0] // 16
            g_vec[...] = jnp.zeros_like(g_vec)
            for width, count in sorted(set(sizes)):
                pick, mine = vector_masks(width, count, nrow)
                for v in [i for i, s in enumerate(sizes) if s == (width, count)]:
                    spread = jnp.where(mine, sums[v : v + 1, :width], 0.0)
                    top = spread.astype(BF)
                    rest = (spread - top.astype(F32)).astype(BF)
                    g_vec2[pl.ds(v, nrow, stride=16), :] = nt(top, pick) + nt(rest, pick)

        def attn_part(proj, ns_t, dn1, loads, wqkv):
            proj_loads, ns_load = loads[:-1], loads[-1]
            qkv_load = load(qkv_i, wqkv)
            qmask = head_masks(win, HDIM**-0.5)
            vmask = head_masks(win, 1.0)
            g_qkv2 = g_qkv.reshape(d, 3 * d)
            wqkv2 = wqkv.reshape(d, 3 * d)

            def core_part(prob):
                n3 = nw // 3

                def prob_copy(i):
                    g, b, slot = lax.div(i, n3), lax.rem(i, n3), lax.rem(i, 2)
                    return pltpu.make_async_copy(prob_i.at[pl.ds(3 * b, 3), pl.ds(2 * g, 2)], prob.at[slot], res_sem.at[slot])

                prob_copy(0).start()
                ns_load.wait()
                base = ticks.count

                @pl.loop(0, d // 256)
                def _(g):
                    lq, lk, lv = [pl.ds(pl.multiple_of(r * d + g * 256, 256), 256) for r in range(3)]

                    @pl.loop(0, n3)
                    def _(b):
                        i = g * n3 + b
                        for q in range(n3):
                            pl.when(i == q)(proj_loads[q].wait)
                        prob_copy(i).wait()

                        @pl.when(i + 1 < n3 * (d // 256))
                        def _():
                            prob_copy(i + 1).start()

                        for u in range(3):
                            at = pl.multiple_of(b * (3 * win) + u * win, win)
                            rows = pl.ds(at, win)
                            dhw = nn(shift_in, dpad[pl.ds(at, 2 * win), lq]).astype(BF)
                            q4, k4, v4 = proj[rows, lq], proj[rows, lk], proj[rows, lv]
                            new = [[], [], []]
                            for pr in range(2):
                                lanes = slice(pr * 128, pr * 128 + 128)
                                q2, k2, v2 = q4[:, lanes], k4[:, lanes], v4[:, lanes]
                                pb = prob[lax.rem(i, 2), u, pr]
                                dbd = split_heads(dhw[:, lanes], vmask)
                                dp = nt(v2, dbd)
                                pf = pb.astype(F32)
                                ds = (pf * (dp - jnp.sum(pf * dp, axis=0, keepdims=True))).astype(BF)
                                stacked = jnp.concatenate([ds[:, :win], ds[:, win:]], axis=0)
                                new[0].append(tn(stacked, split_heads(k2, qmask)).astype(BF))
                                new[1].append(nn(ds, split_heads(q2, qmask)).astype(BF))
                                new[2].append(nn(pb, dbd).astype(BF))
                            for lanes, parts in zip((lq, lk, lv), new):
                                proj[rows, lanes] = jnp.concatenate(parts, axis=1)
                        for q in range(3):
                            for bb in range(n3):
                                if ticks.table[base + q * (n3 + 1) + bb]:
                                    pl.when(i == q * n3 + bb)(functools.partial(ticks.run, base + q * (n3 + 1) + bb))

                    for r, cols in enumerate((lq, lk, lv)):
                        to = pl.ds(pl.multiple_of(g * d + r * 256, 256), 256)
                        part = proj[:, cols]
                        if r != 1:
                            into = pl.ds(pl.multiple_of((r // 2) * d + g * 256, 256), 256)
                            sums[2:3, into] = jnp.sum(part.astype(F32), axis=0, keepdims=True)
                        g_qkv2[:, to] = nn(ns_t[...], part).astype(BF)
                    for q in range(3):
                        pl.when(g == q)(functools.partial(ticks.run, base + q * (n3 + 1) + n3))

                ticks.count = base + 3 * (n3 + 1)

            pl.run_scoped(core_part, pltpu.VMEM((2, 3, 2, win, 2 * win), BF))
            x_rows = dpad.at[0:tok]
            x_load = load(x_i, x_rows)
            qkv_load.wait()

            @pl.loop(0, nw // 3)
            def _(b):
                rows = pl.ds(pl.multiple_of(b * 384, 128), 384)
                for n0 in range(0, d, 256):
                    dn1[rows, n0 : n0 + 256] = nt(proj[rows, :], wqkv2[n0 : n0 + 256, :])
                ticks.within(b, range(3))

            x_load.wait()

            @pl.loop(0, tok // 128)
            def _(b):
                at = pl.multiple_of(b * 128, 128)
                rows = pl.ds(at, 128)
                both = pl.ds(at, 2 * win)
                high = dn1[both, :].astype(BF)
                cot = nn(shift_out, high) + nn(shift_out, (dn1[both, :] - high.astype(F32)).astype(BF))
                vhat, _ = norm_stats(x_rows[rows, :].astype(F32))
                sums[0:1, 0:d] += jnp.sum(cot * vhat, axis=0, keepdims=True)
                sums[1:2, 0:d] += jnp.sum(cot, axis=0, keepdims=True)
                dn1[rows, :] = cot
                ticks.within(b, range(8))

            pack_vectors()
            ticks.point()

            @pl.loop(0, tok // 128)
            def _(b):
                rows = pl.ds(pl.multiple_of(b * 128, 128), 128)
                vhat, r = norm_stats(x_rows[rows, :].astype(F32))
                set_dres(dres, rows, rows_of_dres(dres, rows) + norm_grad(vhat, r, dn1[rows, :] * vec(0, 0, d)))
                ticks.within(b, range(8))

        def ff_part(dn2_rows, r1):
            dn2 = dn2_rows.at[0:tok]
            r1_load = pltpu.make_async_copy(r1_i, r1, out_sem.at[1])
            def inner(act, gd, wf, wi, dff, dff_t, n2_t, dh):
                n2_load = load(n2t_i, n2_t)

                def tile_copies(j):
                    slot, hx, jj = lax.rem(j, 2), lax.rem(j, 2), lax.div(j, 2)
                    cols = pl.ds(pl.multiple_of(hx * half_ff + jj * 256, 256), 256)
                    wcols = pl.ds(pl.multiple_of(jj * 256, 256), 256)
                    pairs = (
                        (act_i.at[:, cols], act),
                        (gd_i.at[:, cols], gd),
                        (wf_i.at[hx, :, :, :, :, wcols], wf),
                        (wi_i.at[hx, :, :, :, :, wcols], wi),
                    )
                    slots = (slot, slot, slot, lax.rem(j, 4))
                    return [pltpu.make_async_copy(s, b.at[slots[q]], tile_sem.at[slot, q]) for q, (s, b) in enumerate(pairs)]

                for copy in tile_copies(0):
                    copy.start()
                r1_load.start()
                ticks.point()

                @pl.loop(0, tok // 256)
                def _(b):
                    rows = pl.ds(pl.multiple_of(b * 256, 256), 256)
                    val = rows_of_dres(dres, rows).astype(BF)
                    dff[rows, :] = val
                    sums[7:8, 0:d] += jnp.sum(val.astype(F32), axis=0, keepdims=True)
                    dff_t[:, rows] = val.T
                    ticks.within(b, range(4))

                dn2[...] = jnp.zeros(dn2.shape, F32)
                n2_load.wait()
                n_tiles = ff // 256

                @pl.loop(0, n_tiles)
                def _(j):
                    slot, hx, jj = lax.rem(j, 2), lax.rem(j, 2), lax.div(j, 2)
                    for copy in tile_copies(j):
                        copy.wait()

                    @pl.when(j + 1 < n_tiles)
                    def _():
                        for copy in tile_copies(j + 1):
                            copy.start()

                    wcols = pl.ds(pl.multiple_of(jj * 256, 256), 256)
                    wf_j = wf.at[slot].reshape(d, 256)
                    wi_j = wi.at[lax.rem(j, 4)].reshape(d, 256)
                    wi_before = wi.at[lax.rem(j + 3, 4)].reshape(d, 256)
                    total = jnp.zeros((1, 256), F32)
                    for m in range(0, tok, FF_ROWS):
                        val = (nn(dff[m : m + FF_ROWS, :], wf_j[...]) * gd[slot, m : m + FF_ROWS, :].astype(F32)).astype(BF)
                        dh[slot, m : m + FF_ROWS, :] = val
                        total = total + jnp.sum(val.astype(F32), axis=0, keepdims=True)
                    sums[6:7, pl.ds(pl.multiple_of(hx * half_ff + jj * 256, 256), 256)] = total
                    g_wf2[hx, :, wcols] = nn(dff_t[...], act[slot]).astype(BF)
                    g_wi2[hx, :, wcols] = nn(n2_t[...], dh[slot]).astype(BF)

                    @pl.when(hx == 1)
                    def _():
                        for m in range(0, tok, 512):
                            rows = slice(m, m + 512)
                            dn2[rows, :] = dn2[rows, :] + (nt(dh[0, rows], wi_before[...]) + nt(dh[1, rows], wi_j[...]))

                    ticks.within(j, range(12))

            pl.run_scoped(
                inner,
                pltpu.VMEM((2, tok, 256), BF),
                pltpu.VMEM((2, tok, 256), BF),
                pltpu.VMEM((2, 4, 2, 2, d // 16, 256), BF),
                pltpu.VMEM((4, 4, 2, 2, d // 16, 256), BF),
                pltpu.VMEM((tok, d), BF),
                pltpu.VMEM((d, tok), BF),
                pltpu.VMEM((d, tok), BF),
                pltpu.VMEM((2, tok, 256), BF),
            )

            def out_part(heads_t, wo, dattn):
                loads = [load(headst_i, heads_t), load(wo_i, wo)]
                wo2 = wo.reshape(d, d)
                g_wo2 = g_wo.reshape(d, d)
                r1_load.wait()

                @pl.loop(0, tok // 128)
                def _(b):
                    rows = pl.ds(pl.multiple_of(b * 128, 128), 128)
                    vhat, r = norm_stats(r1[rows, :])
                    cot = dn2[rows, :]
                    sums[4:5, 0:d] += jnp.sum(cot * vhat, axis=0, keepdims=True)
                    sums[5:6, 0:d] += jnp.sum(cot, axis=0, keepdims=True)
                    val = rows_of_dres(dres, rows) + norm_grad(vhat, r, cot * vec(4, 0, d))
                    set_dres(dres, rows, val)
                    low = val.astype(BF)
                    dattn[rows, :] = low
                    sums[3:4, 0:d] += jnp.sum(low.astype(F32), axis=0, keepdims=True)
                    ticks.within(b, range(8))

                for copy in loads:
                    copy.wait()
                g_wo2[...] = nn(heads_t[...], dattn[...]).astype(BF)
                ticks.point()
                dpad[0:win, :] = jnp.zeros((win, d), BF)
                dpad[win + tok : 2 * win + tok, :] = jnp.zeros((win, d), BF)

                @pl.loop(0, tok // 512)
                def _(b):
                    at = pl.multiple_of(b * 512, 256)
                    dpad[pl.ds(at + win, 512), :] = nt(dattn[pl.ds(at, 512), :], wo2[...]).astype(BF)
                    ticks.within(b, (0, 1))

            def rest(proj, ns_t):
                loads = [load(proj_i.at[pl.ds(b * 384, 384)], proj.at[pl.ds(b * 384, 384)]) for b in range(nw // 3)]
                loads.append(load(nst_i, ns_t))
                pl.run_scoped(out_part, pltpu.VMEM((d, tok), BF), pltpu.VMEM(wo_i.shape, BF), pltpu.VMEM((tok, d), BF))
                pl.run_scoped(functools.partial(attn_part, proj, ns_t, dn2_rows, loads), pltpu.VMEM(qkv_i.shape, BF))

            pl.run_scoped(rest, pltpu.VMEM(proj_i.shape, BF), pltpu.VMEM(nst_i.shape, BF))

        pl.run_scoped(ff_part, pltpu.VMEM((nw * win, d), F32), pltpu.VMEM((tok, d), F32))
        done = pltpu.make_async_copy(dres, dch_out, out_sem.at[0])
        done.start()

        ticks.point()
        for t, g in enumerate(grads):
            pick = functools.partial(block, g, KINDS[t], cut=(ALL, ALL))
            sends.sent(t, {"z": pick(slice(0, 3), y, c, x), "a": pick(ALL, y, c, x), "b": pick(ALL, y, c, ALL), "c": pick(ALL, ALL, c, ALL)})
        done.wait()
        for copy in own_copies:
            copy.wait()

    pl.run_scoped(whole, pltpu.VMEM((d // 128, tok, 128), F32), pltpu.VMEM((tok + 2 * win, d), BF))


def quick_mesh(mesh):
    return mesh.shape["dp"] == 16 and mesh.shape["mp"] == 2


def gathered_shape(shape, kind):
    if kind == 2:
        return (4, 2, 2, 2 * shape[0], shape[1])
    return ((4, 2, 2, 2) if kind == 0 else (2, 4, 2, 2)) + shape


def place_kernel(widths, *refs):
    n = (len(refs) - 3 - 2 * len(widths)) // 3
    sources, vec_ref, outs, vec_outs = refs[:n], refs[n], refs[n + 1 : 2 * n + 1], refs[2 * n + 1 : 2 * n + 1 + len(widths)]
    rest = refs[2 * n + 1 + len(widths) :]
    held, rows, in_sem, out_sem = rest[:n], rest[n : n + len(widths)], rest[-2], rest[-1]
    parts = held[-1].shape[0]
    pairs = [(sources[-1].at[q], held[-1].at[q], outs[-1].at[:, q * SLOT : q * SLOT + SLOT]) for q in range(parts)]
    pairs += list(zip(sources[:-1], held[:-1], outs[:-1]))
    loads = [pltpu.make_async_copy(s, h, in_sem.at[i]) for i, (s, h, _) in enumerate(pairs)]
    stores = [pltpu.make_async_copy(h, o, out_sem.at[i]) for i, (_, h, o) in enumerate(pairs)]
    for copy in loads:
        copy.start()
    for v, width in enumerate(widths):
        rows[v][...] = vec_ref[v, :width]
        stores.append(pltpu.make_async_copy(rows[v], vec_outs[v], out_sem.at[len(pairs) + v]))
        stores[-1].start()
    for load, store in zip(loads, stores):
        load.wait()
        store.start()
    for copy in stores:
        copy.wait()


def fast_shards(*args):
    (chars, seg, offs, l1g, l1b, wqkv, qvb, wo, aob, l2g, l2b, wi, fib, wf, fob, cv, cvb, l3g, l3b, dmol) = args
    tok, d = chars.shape
    mols = dmol.shape[0]
    vectors = (l1g, l1b, qvb, aob, l2g, l2b, fib, fob, cvb, l3g, l3b)
    sizes = tuple((v.shape[0] * 32, v.shape[0]) for v in vectors)
    ff = sizes[6][0]
    dims = (tok, d, ff)
    nw = tok // WIN + 1
    vec_own = sum(jnp.pad(v[None], ((i, 15 - i), (0, SLOT - v.shape[0]))) for i, v in enumerate(vectors))
    owns = (vec_own, wqkv, wo, wi, wf.T, cv)
    kinds = KINDS
    full = [gathered_shape(o.shape, k) for o, k in zip(owns, kinds)]
    plan = gather_plan([o.shape for o in owns])
    n_wait = 5 * len(plan)
    on_chip = pl.BlockSpec(memory_space=pltpu.VMEM)
    scalar = pl.BlockSpec(memory_space=pltpu.SMEM)
    any_mem = pl.BlockSpec(memory_space=pl.ANY)
    bf = lambda *s: jax.ShapeDtypeStruct(s, BF)
    f32 = lambda *s: jax.ShapeDtypeStruct(s, F32)
    prob_shape = (nw, HEADS // 2, WIN, 2 * WIN)
    saved = pl.pallas_call(
        functools.partial(forward_kernel, dims, sizes),
        out_shape=[
            f32(mols, d),
            f32(16, ff),
            f32(8, d),
            bf(mols, d),
            *[bf(*s) for s in full[1:]],
            bf(d, nw * WIN),
            bf(nw * WIN, 3 * d),
            bf(*prob_shape),
            bf(d, tok),
            f32(tok, d),
            bf(d, tok),
            bf(tok, ff),
            bf(tok, ff),
            bf(KER, d // SLOT, SLOT, mols),
        ],
        in_specs=[scalar, on_chip, any_mem, any_mem] + [on_chip] * 6,
        out_specs=[on_chip, any_mem, on_chip, on_chip] + [any_mem] * 14,
        scratch_shapes=[
            *[pltpu.VMEM(s, BF) for s in full],
            pltpu.VMEM((512, SLOT), F32),
            pltpu.VMEM((16, ff), F32),
            pltpu.VMEM((tok + 2 * WIN, d), BF),
            pltpu.VMEM((nw * WIN, d), BF),
            pltpu.VMEM((nw * WIN, 3 * d), BF),
            pltpu.VMEM(prob_shape, BF),
            pltpu.VMEM((tok, d), BF),
            pltpu.VMEM((tok, d), F32),
            pltpu.VMEM((tok, d), BF),
            pltpu.VMEM((tok, ff), BF),
            pltpu.VMEM((tok, ff), BF),
            pltpu.VMEM((d // 128, tok, 128), F32),
            pltpu.VMEM((mols, KER * d), BF),
            pltpu.VMEM((tok, d), BF),
            pltpu.VMEM((mols, d), BF),
            pltpu.SemaphoreType.DMA((8,)),
            pltpu.SemaphoreType.DMA((20,)),
            pltpu.SemaphoreType.DMA((24,)),
            pltpu.SemaphoreType.DMA((n_wait,)),
        ],
        compiler_params=pltpu.CompilerParams(collective_id=1, has_side_effects=True, vmem_limit_bytes=VMEM_CAP),
        name="gather_forward",
    )(offs, seg, chars, dmol, *owns)
    (mol, vecs, ln3, dcp, qkv_f, wo_f, wi_f, wf_f, cv_f, ns, proj, prob, heads, r1, n2, act, gd, mi) = saved

    own_shapes = [o.shape for o in owns]
    kind_core = lambda s, k: (4, 2, 2 * s[0], s[1]) if k == 2 else ((4, 2, 2) if k == 0 else (2, 4, 2)) + s
    types = [F32] + [BF] * 5
    plan = scatter_plan(own_shapes)
    n_back = 5 * len(plan)
    back = pl.pallas_call(
        functools.partial(backward_kernel, dims, sizes),
        out_shape=[f32(d // SLOT, tok, SLOT)] + [f32(*s) for s in own_shapes],
        in_specs=[scalar, any_mem] + [on_chip] * 3 + [any_mem] * 14,
        out_specs=[any_mem] * 7,
        scratch_shapes=[
            *[pltpu.VMEM(s, t) for s, t in zip(full, types)],
            *[pltpu.VMEM(kind_core(s, k), t) for s, k, t in zip(own_shapes, kinds, types)],
            *[pltpu.VMEM((2, 4) + s, t) for s, t in zip(own_shapes, types)],
            *[pltpu.VMEM((4,) + s, t) for s, t in zip(own_shapes, types)],
            *[pltpu.VMEM((3,) + s, t) for s, t in zip(own_shapes, types)],
            *[pltpu.VMEM(s, F32) for s in own_shapes],
            pltpu.VMEM((16, ff), F32),
            pltpu.SemaphoreType.DMA((2,)),
            pltpu.SemaphoreType.DMA((2, 4)),
            pltpu.SemaphoreType.DMA((16,)),
            pltpu.SemaphoreType.DMA((2,)),
            pltpu.SemaphoreType.DMA((6,)),
            pltpu.SemaphoreType.DMA((24,)),
            pltpu.SemaphoreType.DMA((n_back,)),
        ],
        compiler_params=pltpu.CompilerParams(collective_id=2, has_side_effects=True, vmem_limit_bytes=VMEM_CAP),
        name="backward_scatter",
    )(offs, chars, dcp, vecs, ln3, qkv_f, wo_f, wi_f, wf_f, cv_f, ns, proj, prob, heads, r1, n2, act, gd, mi)
    d_chars, d_vec, d_qkv, d_wo, d_wi, d_wf, d_cv = back
    large = (d_wo, d_qkv, d_wi, d_wf, d_cv, mol, d_chars)
    done = pl.pallas_call(
        functools.partial(place_kernel, tuple(v.shape[0] for v in vectors)),
        out_shape=[f32(*a.shape) for a in large[:-1]] + [f32(tok, d)] + [f32(v.shape[0]) for v in vectors],
        in_specs=[any_mem] * len(large) + [on_chip],
        out_specs=[any_mem] * (len(large) + len(vectors)),
        scratch_shapes=[
            *[pltpu.VMEM(a.shape, F32) for a in large],
            *[pltpu.VMEM(v.shape, F32) for v in vectors],
            pltpu.SemaphoreType.DMA((len(large) - 1 + d // SLOT,)),
            pltpu.SemaphoreType.DMA((len(large) - 1 + d // SLOT + len(vectors),)),
        ],
        compiler_params=pltpu.CompilerParams(vmem_limit_bytes=VMEM_CAP),
        name="place",
    )(*large, d_vec)
    d_wo, d_qkv, d_wi, d_wf, d_cv, mol, d_chars = done[: len(large)]
    dv = done[len(large) :]
    return (
        mol,
        d_chars,
        dv[0],
        dv[1],
        d_qkv,
        dv[2],
        d_wo,
        dv[3],
        dv[4],
        dv[5],
        d_wi,
        dv[6],
        d_wf.T,
        dv[7],
        d_cv,
        dv[8],
        dv[9],
        dv[10],
    )


def solution(mesh):
    placed = (
        P(("dp", "mp"), None),
        P(("dp", "mp"), None),
        P(("dp", "mp")),
        P(("dp", "mp")),
        P(("dp", "mp")),
        P(("dp", "mp"), None),
        P(("dp", "mp")),
        P(("dp", "mp"), None),
        P(("dp", "mp")),
        P(("dp", "mp")),
        P(("dp", "mp")),
        P("dp", "mp"),
        P(("dp", "mp")),
        P("mp", "dp"),
        P(("dp", "mp")),
        P("dp", "mp"),
        P(("dp", "mp")),
        P(("dp", "mp")),
        P(("dp", "mp")),
        P(("dp", "mp"), None),
    )
    return jax.shard_map(
        fast_shards if quick_mesh(mesh) else shards,
        mesh=mesh,
        in_specs=placed,
        out_specs=(
            P(("dp", "mp"), None),
            P(("dp", "mp"), None),
            P(("dp", "mp")),
            P(("dp", "mp")),
            P(("dp", "mp"), None),
            P(("dp", "mp")),
            P(("dp", "mp"), None),
            P(("dp", "mp")),
            P(("dp", "mp")),
            P(("dp", "mp")),
            P("dp", "mp"),
            P(("dp", "mp")),
            P("mp", "dp"),
            P(("dp", "mp")),
            P("dp", "mp"),
            P(("dp", "mp")),
            P(("dp", "mp")),
            P(("dp", "mp")),
        ),
        check_vma=False,
    )
```
